32 devices in a mesh: dp: 8 (over z, core), group: 4 (over y, x).
Axes of the slice: x: 2, y: 2, z: 4, core: 2. Of those that a mesh axis runs over, the one named last changes fastest.
Arguments:
- tokens: bfloat16 [32768, 1024], P(('dp', 'group')), may hold values from -6 to 6
- cotangent: bfloat16 [32768, 1024], P(('dp', 'group')), may hold values from -6 to 6
- doc_ids: int32 [32768], P(('dp', 'group')), may hold values from -1 to 3, as said below
- master: float32 [12587008], P('group')
- moment_one: float32 [12587008], P('group'), may hold values from -2 to 2
- moment_two: float32 [12587008], P('group'), may hold values from 0.001 to 1
Outputs:
- mixed: bfloat16 [32768, 1024], P(('dp', 'group'))
- input_grad: bfloat16 [32768, 1024], P(('dp', 'group'))
- weight_grad: float32 [12587008], P('group')
- master_step: float32 [12587008], P('group')
- new_moment_one: float32 [12587008], P('group')
The draws below stay inside these ranges and needn't reach their ends.
Inputs may be any that keep to these rules, and one draw needn't show every extreme that they name: `doc_ids`: each device's block of 1024 slots holds one to four sequences numbered 0, 1, ... in order, each of 16 tokens or more, followed by padding slots of -1 at its end; some device holds a single sequence of 1024 tokens and some device holds four.
All inputs are finite; a program needn't handle non-finite values.
Results may differ from the reference program's by a relative error of at most 0.012.
Values may be sent and summed in bfloat16 or wider, within the bound.
A program may use at most 384 MiB of HBM per device.

```python
import math
import jax
import jax.numpy as jnp
from jax import lax

D = 1024
H = 16
FF = 4096
TOK_DEV = 1024
SEQ_MIN = 16
TOKENS = 32768
PARAMS = 12587008
N_GROUP = 4


def draw_doc_ids(key, part):
    block_count = TOKENS // TOK_DEV
    key_count, key_used, key_weights = jax.random.split(key, 3)
    device_index = jnp.arange(block_count, dtype=jnp.int32)
    counts = jax.random.randint(key_count, (block_count,), 1, 5)
    counts = jnp.where(device_index == 0, 1, jnp.where(device_index == 1, 4, counts))
    used = jax.random.randint(key_used, (block_count,), TOK_DEV // 2, TOK_DEV + 1)
    used = jnp.where(device_index == 0, TOK_DEV, jnp.where(device_index == 1, TOK_DEV // 2, used))
    live = jnp.arange(4, dtype=jnp.int32)[None, :] < counts[:, None]
    shares = jnp.where(live, jax.random.randint(key_weights, (block_count, 4), 1, 9), 0)
    spare = used - counts * SEQ_MIN
    extra = spare[:, None] * shares // jnp.sum(shares, axis=1, keepdims=True)
    lengths = jnp.where(live, SEQ_MIN + extra, 0)
    ends = jnp.cumsum(lengths, axis=1)
    filled = ends[:, 3]
    slots = jnp.arange(TOK_DEV, dtype=jnp.int32)
    number = jnp.sum((slots[None, :, None] >= ends[:, None, :]).astype(jnp.int32), axis=2)
    number = jnp.where(slots[None, :] < filled[:, None], number, -1)
    return number.reshape(-1).astype(jnp.int32)


def draw_master(key, part):
    keys = jax.random.split(key, 6)
    shapes = [(D, 3 * D), (D, D), (D, FF), (FF, D), (2, D)]
    bases = [jax.random.normal(keys[index], shapes[index], jnp.float32) for index in range(5)]
    w_qkv = bases[0] * D ** (-0.5)
    w_out = bases[1] * 4.0 * D ** (-0.5)
    w_in = bases[2] * D ** (-0.5)
    w_back = bases[3] * FF ** (-0.5)
    gains = jax.random.uniform(keys[5], (2, D), jnp.float32, 0.6, 1.4)
    biases = bases[4] * 0.2
    norms = jnp.stack([gains[0], biases[0], gains[1], biases[1]])
    tables = [tensor.reshape(N_GROUP, -1) for tensor in [w_qkv, w_out, w_in, w_back, norms]]
    return jnp.concatenate(tables, axis=1).reshape(-1)


def block_levels(stream_key, dims, pieces, low, high):
    factor_of, own = 1.0, jax.random.fold_in(stream_key, 6)
    for axis_at, shards_of in pieces:
        draws = jnp.exp(jax.random.uniform(jax.random.fold_in(own, axis_at), (shards_of,), jnp.float32, low / len(pieces), high / len(pieces)))
        factor_of = factor_of * jnp.repeat(draws, dims[axis_at] // shards_of).reshape([-1 if axis == axis_at else 1 for axis in range(len(dims))])
    return factor_of


def centred(stream_key, shape, width, reach, cuts=(), kind=jnp.bfloat16):
    array = width * jax.random.normal(stream_key, shape, jnp.float32)
    if cuts:
        array = array * block_levels(stream_key, shape, cuts, -0.22, 0.18)
    return jnp.clip(array, -reach, reach).astype(kind)


def setup_inputs(seed: int = 0) -> dict:
    splits = jax.random.split(jax.random.key(seed), 7)
    return {
        "tokens": centred(splits[0], (TOKENS, D), 1.0, 6.0, ((0, 32),)),
        "cotangent": centred(splits[1], (TOKENS, D), 1.0, 6.0, ((0, 32),)),
        "doc_ids": draw_doc_ids(jax.random.fold_in(splits[6], 71), 0),
        "master": draw_master(jax.random.fold_in(splits[6], 71), 0),
        "moment_one": centred(splits[4], (PARAMS,), 0.3, 2.0, ((0, 4),), jnp.float32),
        "moment_two": jnp.clip(jnp.exp(math.log(1.0) - 6.9077552 * jax.random.uniform(splits[5], (PARAMS,), jnp.float32) ** block_levels(splits[5], (PARAMS,), ((0, 4),), -0.2, 0.2)), 0.001, 1.0),
    }


norm_eps = 1e-05
mask_fill = -1e+30
highest = lax.Precision.HIGHEST
beta_first = 0.9
beta_second = 0.999
learn_rate = 0.001
adam_eps = 1e-08
adam_steps = 100.0

@jax.custom_vjp
def low(v):
    return lax.optimization_barrier(v.astype(jnp.bfloat16)).astype(jnp.float32)

@jax.custom_vjp
def low_back(v):
    return v

def low_keep(v):
    return (low(v), None)

def low_pass(kept, grad):
    return (grad,)

def back_keep(v):
    return (v, None)

def back_low(kept, grad):
    return (low(grad),)
low.defvjp(low_keep, low_pass)
low_back.defvjp(back_keep, back_low)

def param_shapes():
    return [(D, 3 * D), (D, D), (D, FF), (FF, D), (4, D)]

def unpack(flat, group_count):
    table = flat.reshape(group_count, -1)
    tensors = []
    offset = 0
    for shape in param_shapes():
        length = shape[0] * shape[1] // group_count
        tensors.append(table[:, offset:offset + length].reshape(shape))
        offset = offset + length
    return tensors

def pack(tensors, group_count):
    return jnp.concatenate([tensor.reshape(group_count, -1) for tensor in tensors], axis=1).reshape(-1)

def layer_norm(values, gain, bias):
    centre = values - lax.optimization_barrier(jnp.mean(values, axis=-1, keepdims=True))
    spread = lax.optimization_barrier(jnp.mean(centre * centre, axis=-1, keepdims=True))
    return centre * lax.rsqrt(spread + norm_eps) * gain + bias

def attend(qkv, doc_ids):
    token_count = qkv.shape[0]
    head_size = D // H
    queries = qkv[:, :D].reshape(token_count, H, head_size)
    keys_all = qkv[:, D:2 * D].reshape(token_count, H, head_size)
    values_all = qkv[:, 2 * D:].reshape(token_count, H, head_size)
    block = min(512, token_count)
    factor = head_size ** (-0.5)

    def one_block(blk_index):
        start = blk_index * block
        query_blk = lax.dynamic_slice_in_dim(queries, start, block, 0)
        query_doc = lax.dynamic_slice_in_dim(doc_ids, start, block, 0)
        query_pos = start + jnp.arange(block, dtype=jnp.int32)
        key_pos = jnp.arange(token_count, dtype=jnp.int32)
        allowed = (query_doc[:, None] == doc_ids[None, :]) & (key_pos[None, :] <= query_pos[:, None])
        scores = low_back(jnp.einsum('qhd,khd->hqk', query_blk, keys_all, precision=highest) * factor)
        scores = jnp.where(allowed[None], scores, mask_fill)
        top_score = lax.optimization_barrier(jnp.max(scores, axis=-1, keepdims=True))
        exp_scores = jnp.exp(scores - top_score)
        prob_low = low(exp_scores / lax.optimization_barrier(jnp.sum(exp_scores, axis=-1, keepdims=True)))
        return jnp.einsum('hqk,khd->qhd', prob_low, values_all, precision=highest)
    outputs = lax.map(jax.checkpoint(one_block), jnp.arange(token_count // block, dtype=jnp.int32))
    return outputs.reshape(token_count, D)

def forward(token_in, w_qkv, w_out, w_in, w_back, norms, doc_ids):
    a_one = low(layer_norm(token_in, norms[0], norms[1]))
    qkv = low(low_back(jnp.dot(a_one, w_qkv, precision=highest)))
    att = low(low_back(attend(qkv, doc_ids)))
    resid = token_in + low_back(jnp.dot(att, w_out, precision=highest))
    a_two = low(layer_norm(resid, norms[2], norms[3]))
    hidden = low(jax.nn.gelu(low_back(jnp.dot(a_two, w_in, precision=highest)), approximate=False))
    return resid + low_back(jnp.dot(hidden, w_back, precision=highest))

def reference(tokens, cotangent, doc_ids, master, moment_one, moment_two):
    group_count = N_GROUP
    block_count = TOKENS // TOK_DEV
    weights = [low(tensor) for tensor in unpack(master, group_count)]
    token_blocks = tokens.astype(jnp.float32).reshape(block_count, TOK_DEV, D)
    cot_blocks = cotangent.astype(jnp.float32).reshape(block_count, TOK_DEV, D)
    doc_blocks = doc_ids.astype(jnp.int32).reshape(block_count, TOK_DEV)

    def one_device(totals, item):
        token_blk, cot_blk, doc_blk = item
        valid = (doc_blk >= 0)[:, None]

        def run(token_in, w_qkv, w_out, w_in, w_back, norms):
            return forward(token_in, w_qkv, w_out, w_in, w_back, norms, doc_blk)
        output, pull = jax.vjp(run, token_blk, weights[0], weights[1], weights[2], weights[3], weights[4])
        grads = pull(jnp.where(valid, cot_blk, 0.0))
        mixed_blk = jnp.where(valid, output, 0.0).astype(jnp.bfloat16)
        totals = tuple((total + piece_grad for total, piece_grad in zip(totals, grads[1:])))
        return (totals, (mixed_blk, grads[0].astype(jnp.bfloat16)))
    zeros = tuple((jnp.zeros(tensor.shape, jnp.float32) for tensor in weights))
    totals, (mixed, input_grad) = lax.scan(one_device, zeros, (token_blocks, cot_blocks, doc_blocks))
    inv_root = float(TOKENS) ** (-0.5)
    weight_grad = pack([total * inv_root for total in totals], group_count)
    first_new = beta_first * moment_one + (1.0 - beta_first) * weight_grad
    second_new = beta_second * moment_two + (1.0 - beta_second) * weight_grad * weight_grad
    first_hat = first_new / (1.0 - beta_first ** adam_steps)
    second_hat = second_new / (1.0 - beta_second ** adam_steps)
    step_taken = -learn_rate * first_hat / (jnp.sqrt(second_hat) + adam_eps)
    return (mixed.reshape(TOKENS, D), input_grad.reshape(TOKENS, D), weight_grad, step_taken, first_new)
```

```python
import functools

import jax
import jax.numpy as jnp
from jax import lax
from jax.experimental import pallas as pl
from jax.experimental.pallas import tpu as pltpu
from jax.sharding import Mesh
from jax.sharding import PartitionSpec as P

HEADS = 16
EPS = 1e-05
FILL = -1e30
BETA_ONE = 0.9
BETA_TWO = 0.999
RATE = 0.001
ADAM_EPS = 1e-08
STEPS = 100.0
VMEM_MB = 60

f32 = jnp.float32
bf16 = jnp.bfloat16
ANY = pl.BlockSpec(memory_space=pl.ANY)


def params(limit=VMEM_MB):
    return pltpu.CompilerParams(vmem_limit_bytes=limit << 20)


def cost(flops, nbytes, trans=0):
    return pl.CostEstimate(flops=int(flops), bytes_accessed=int(nbytes), transcendentals=int(trans))


def sds(shape, dtype):
    return jax.ShapeDtypeStruct(shape, dtype)


def dot_nn(a, b):
    return jnp.dot(a, b, preferred_element_type=f32)


def dot_nt(a, b):
    return lax.dot_general(a, b, (((1,), (1,)), ((), ())), preferred_element_type=f32)


def dot_tn(a, b):
    return lax.dot_general(a, b, (((0,), (0,)), ((), ())), preferred_element_type=f32)


def pick(flag, a, b):
    return jnp.where(flag, a, b)


def unpack_kernel(dims, ids, m_qkv, m_out, m_in, m_back, own_qkv, oth_qkv, own_oi, oth_oi, own_bk, oth_bk):
    n, d, ff = dims
    c = ids[1]
    first = c == 0
    rows = d // n
    nb = d // 128

    def put(ref, own, oth, dst, lo, hi, stride, count):
        a = ref[pl.ds(lo, count, stride=stride), :].astype(bf16)
        b = ref[pl.ds(hi, count, stride=stride), :].astype(bf16)
        own[:, dst : dst + 128] = pick(first, a, b)
        oth[:, dst : dst + 128] = pick(first, b, a)

    half = nb // 2
    for part in range(3):
        for w in range(half):
            lo = part * nb + w
            put(m_qkv, own_qkv, oth_qkv, (part * half + w) * 128, lo, lo + half, 3 * nb, rows)
    for w in range(half):
        put(m_out, own_oi, oth_oi, w * 128, w, w + half, nb, rows)
    share = ff // n
    hs = share // 2
    for j in range(n):
        for q in range(hs // 128):
            lo = (share * j) // 128 + q
            put(m_in, own_oi, oth_oi, d // 2 + hs * j + q * 128, lo, lo + hs // 128, ff // 128, rows)
    for w in range(nb):
        put(m_back, own_bk, oth_bk, w * 128, w, hs * nb + w, nb, hs)


def unpack(ids, flat, n, d, ff):
    rows = d // n
    hs = ff // n // 2
    lanes = flat.reshape(-1, 128)
    r1, r2, r3, r4 = rows * 3 * d // 128, rows * d // 128, rows * ff // 128, ff // n * d // 128
    assert r1 % r2 == 0 and (r1 + r2) % r3 == 0 and (r1 + r2 + r3) % r4 == 0
    spec = lambda r, i: pl.BlockSpec((r, 128), lambda g, ids: (i, 0))
    full = lambda s: pl.BlockSpec(s, lambda g, ids: (0, 0))
    s1, s2, s3 = (rows, 3 * d // 2), (rows, d // 2 + ff // 2), (hs, d)
    shapes = [s1, s1, s2, s2, s3, s3]
    return pl.pallas_call(
        functools.partial(unpack_kernel, (n, d, ff)),
        out_shape=[sds(s, bf16) for s in shapes],
        grid_spec=pltpu.PrefetchScalarGridSpec(
            num_scalar_prefetch=1,
            grid=(1,),
            in_specs=[spec(r1, 0), spec(r2, r1 // r2), spec(r3, (r1 + r2) // r3), spec(r4, (r1 + r2 + r3) // r4)],
            out_specs=[full(s) for s in shapes],
        ),
        compiler_params=params(),
        name="unpack",
    )(ids, lanes, lanes, lanes, lanes)


def gather_halves(h, n):
    rows = h.shape[0]
    if n == 4:
        hx = lax.ppermute(h, "x", [(0, 1), (1, 0)])
        hy = lax.ppermute(h, "y", [(0, 1), (1, 0)])
        da = lax.ppermute(hx[: rows // 2], "y", [(0, 1), (1, 0)])
        db = lax.ppermute(hy[rows // 2 :], "x", [(0, 1), (1, 0)])
        return [(0, 0, h), (1, 0, hx), (2, 0, hy), (3, 0, da), (3, rows // 2, db)]
    full = lax.all_gather(h, ("y", "x"), axis=0)
    me = lax.axis_index(("y", "x"))
    return [(k, 0, lax.dynamic_index_in_dim(full, me ^ k, 0, keepdims=False)) for k in range(n)]


def swap_core(v):
    return lax.ppermute(v, "core", [(0, 1), (1, 0)])


def piece_layout(pieces):
    return tuple((k, off, p.shape[0]) for k, off, p in pieces)


def start_pieces(layout, refs, dst, rows, base, cols, me, sems, first_sem, src_cols=None):
    copies = []
    for s, ((k, off, count), ref) in enumerate(zip(layout, refs)):
        start = pl.multiple_of(base + (me ^ k) * rows + off, 8)
        src = ref if src_cols is None else ref.at[:, src_cols]
        copies.append(pltpu.make_async_copy(src, dst.at[pl.ds(start, count), cols], sems.at[first_sem + s]))
    for cp in copies:
        cp.start()
    return copies


def layer_norm_parts(v):
    centre = v - jnp.mean(v, axis=-1, keepdims=True)
    r = lax.rsqrt(jnp.mean(centre * centre, axis=-1, keepdims=True) + EPS)
    return centre * r, r


def layer_norm_back(v, gain, dz):
    xhat, r = layer_norm_parts(v)
    dg = jnp.sum(dz * xhat, axis=0, keepdims=True)
    db = jnp.sum(dz, axis=0, keepdims=True)
    t = dz * gain
    dv = r * (t - jnp.mean(t, axis=-1, keepdims=True) - xhat * jnp.mean(t * xhat, axis=-1, keepdims=True))
    return dv, dg, db


def qkv_kernel(lay, ids, tok, norms, *refs):
    pieces, (a_out, own_out, oth_out, w, sems) = refs[: 2 * len(lay)], refs[2 * len(lay) :]
    d = tok.shape[1]
    rows = d // ids_n(lay)
    half = 3 * d // 2

    @pl.when(pl.program_id(0) == 0)
    def _():
        me = ids[0]
        cps = start_pieces(lay, pieces[: len(lay)], w, rows, 0, pl.ds(0, half), me, sems, 0)
        cps += start_pieces(lay, pieces[len(lay) :], w, rows, 0, pl.ds(half, half), me, sems, len(lay))
        for cp in cps:
            cp.wait()

    xhat, _ = layer_norm_parts(tok[...].astype(f32))
    a = (xhat * norms[0:1, :] + norms[1:2, :]).astype(bf16)
    a_out[...] = a
    acc = dot_nn(a, w[...])
    scale = (d // HEADS) ** (-0.5)
    q = d // 2
    own_out[:, :q] = (acc[:, :q].astype(bf16).astype(f32) * scale).astype(bf16)
    own_out[:, q:] = acc[:, q:half].astype(bf16)
    oth_out[:, :q] = (acc[:, half : half + q].astype(bf16).astype(f32) * scale).astype(bf16)
    oth_out[:, q:] = acc[:, half + q :].astype(bf16)


def ids_n(lay):
    return max(k for k, _, _ in lay) + 1


def project_qkv(ids, tok, norms, own, oth, tm=256):
    lay = piece_layout(own)
    t, d = tok.shape
    blk = lambda w: pl.BlockSpec((tm, w), lambda i, ids: (i, 0))
    return pl.pallas_call(
        functools.partial(qkv_kernel, lay),
        out_shape=[sds((t, d), bf16), sds((t, 3 * d // 2), bf16), sds((t, 3 * d // 2), bf16)],
        grid_spec=pltpu.PrefetchScalarGridSpec(
            num_scalar_prefetch=1,
            grid=(t // tm,),
            in_specs=[blk(d), pl.BlockSpec((4, d), lambda i, ids: (0, 0))] + [ANY] * (2 * len(lay)),
            out_specs=[blk(d), blk(3 * d // 2), blk(3 * d // 2)],
            scratch_shapes=[pltpu.VMEM((d, 3 * d), bf16), pltpu.SemaphoreType.DMA((2 * len(lay),))],
        ),
        compiler_params=params(),
        cost_estimate=cost(2 * t * d * 3 * d, 16e6),
        name="qkv",
    )(ids, tok, norms, *[p for _, _, p in own], *[p for _, _, p in oth])


QB = 256


def fill_bias(bias, doc_row, doc_col):
    t = bias.shape[0]
    for r in range(0, t, QB):
        key = r + lax.broadcasted_iota(jnp.int32, (QB, t), 0)
        query = lax.broadcasted_iota(jnp.int32, (QB, t), 1)
        ok = (doc_col[r : r + QB, :] == doc_row[...]) & (key <= query)
        bias[r : r + QB, :] = jnp.where(ok, 0.0, FILL)


def head_lanes(v, h, hd):
    lane = lax.broadcasted_iota(jnp.int32, v.shape, 1)
    return jnp.where((lane >= h * hd) & (lane < (h + 1) * hd), v, jnp.zeros_like(v))


def attend_kernel(hd, q, k, v, doc_row, doc_col, out, lse, bias):
    @pl.when(pl.program_id(0) == 0)
    def _():
        fill_bias(bias, doc_row, doc_col)

    t = q.shape[0]
    vt = v[...].T
    per = 128 // hd
    qs = [head_lanes(q[...], h, hd) for h in range(per)]
    for i in range(t // QB):
        n = (i + 1) * QB
        cols = slice(i * QB, n)
        outs = []
        for h in range(per):
            s = dot_nt(k[:n, :], qs[h][cols, :]) + bias[:n, cols]
            top = jnp.max(s, axis=0, keepdims=True)
            e = jnp.exp(s - top)
            total = jnp.sum(e, axis=0, keepdims=True)
            lse[0, h : h + 1, cols] = top + jnp.log(total)
            o = dot_nn(vt[h * hd : (h + 1) * hd, :n], e.astype(bf16))
            outs.append(o / total)
        out[cols, :] = jnp.concatenate(outs, axis=0).T.astype(bf16)


def attend(qkv, doc_row, doc_col, d):
    t = qkv.shape[0]
    half = d // 2
    pairs = half // 128
    hd = d // HEADS
    per = 128 // hd
    col = lambda part: pl.BlockSpec((t, 128), lambda p: (0, part * pairs + p))
    return pl.pallas_call(
        functools.partial(attend_kernel, hd),
        grid=(pairs,),
        out_shape=[sds((t, half), bf16), sds((pairs, per, t), f32)],
        in_specs=[col(0), col(1), col(2), pl.BlockSpec((1, t), lambda p: (0, 0)), pl.BlockSpec((t, 1), lambda p: (0, 0))],
        out_specs=[pl.BlockSpec((t, 128), lambda p: (0, p)), pl.BlockSpec((1, per, t), lambda p: (p, 0, 0))],
        scratch_shapes=[pltpu.VMEM((t, t), f32)],
        compiler_params=params(),
        cost_estimate=cost(8 * t * t * half, 5e6, t * t * half // hd),
        name="attend",
    )(qkv, qkv, qkv, doc_row, doc_col)


def attend_back_kernel(hd, q, k, v, dout, att, lse, doc_row, doc_col, dq, dk, dv, bias, dk_acc, dv_acc):
    @pl.when(pl.program_id(0) == 0)
    def _():
        fill_bias(bias, doc_row, doc_col)

    t = q.shape[0]
    per = 128 // hd
    scale = hd ** (-0.5)
    kt = k[...].T
    prod = (dout[...].astype(f32) * att[...].astype(f32)).T
    inner = [jnp.sum(prod[h * hd : (h + 1) * hd, :], axis=0, keepdims=True) for h in range(per)]
    qs = [head_lanes(q[...], h, hd) for h in range(per)]
    ds_ = [head_lanes(dout[...], h, hd) for h in range(per)]
    dk_acc[...] = jnp.zeros_like(dk_acc)
    dv_acc[...] = jnp.zeros_like(dv_acc)
    for i in range(t // QB):
        n = (i + 1) * QB
        cols = slice(i * QB, n)
        dqs = []
        for h in range(per):
            qh, dh = qs[h][cols, :], ds_[h][cols, :]
            s = dot_nt(k[:n, :], qh) + bias[:n, cols]
            p = jnp.exp(s - lse[0, h : h + 1, cols])
            dp = dot_nt(v[:n, :], dh)
            g = (p * (dp - inner[h][:, cols])).astype(bf16)
            dv_acc[:n, :] += dot_nn(p.astype(bf16), dh)
            dk_acc[:n, :] += dot_nn(g, qh)
            dqs.append(dot_nn(kt[h * hd : (h + 1) * hd, :n], g))
        dq[cols, :] = (jnp.concatenate(dqs, axis=0).T * scale).astype(bf16)
    dk[...] = dk_acc[...].astype(bf16)
    dv[...] = dv_acc[...].astype(bf16)


def attend_back(qkv, dout, att, lse, doc_row, doc_col, d):
    t = qkv.shape[0]
    half = d // 2
    pairs = half // 128
    hd = d // HEADS
    per = 128 // hd
    col = lambda part: pl.BlockSpec((t, 128), lambda p: (0, part * pairs + p))
    one = pl.BlockSpec((t, 128), lambda p: (0, p))
    return pl.pallas_call(
        functools.partial(attend_back_kernel, hd),
        grid=(pairs,),
        out_shape=[sds((t, half), bf16)] * 3,
        in_specs=[col(0), col(1), col(2), one, one, pl.BlockSpec((1, per, t), lambda p: (p, 0, 0)),
                  pl.BlockSpec((1, t), lambda p: (0, 0)), pl.BlockSpec((t, 1), lambda p: (0, 0))],
        out_specs=[one, one, one],
        scratch_shapes=[pltpu.VMEM((t, t), f32), pltpu.VMEM((t, 128), f32), pltpu.VMEM((t, 128), f32)],
        compiler_params=params(),
        cost_estimate=cost(20 * t * t * half, 8e6, t * t * half // hd),
        name="attend_back",
    )(qkv, qkv, qkv, dout, att, lse, doc_row, doc_col)


def out_proj_kernel(lay, ids, att_own, att_oth, tok, norms, *refs):
    pieces, (resid, a_two, w, sems) = refs[: 2 * len(lay)], refs[2 * len(lay) :]
    d = tok.shape[1]
    half = d // 2
    c = ids[1]

    @pl.when(pl.program_id(0) == 0)
    def _():
        load_out(lay, ids, pieces, w, sems)

    lo = pl.multiple_of(c * half, half)
    hi = pl.multiple_of((1 - c) * half, half)
    y = dot_nn(att_own[...], w[pl.ds(lo, half), :]) + dot_nn(att_oth[...], w[pl.ds(hi, half), :])
    r = tok[...].astype(f32) + y
    resid[...] = r
    xhat, _ = layer_norm_parts(r)
    a_two[...] = (xhat * norms[2:3, :] + norms[3:4, :]).astype(bf16)


def load_out(lay, ids, pieces, w, sems):
    d = w.shape[1]
    half = d // 2
    rows = d // ids_n(lay)
    me, c = ids[0], ids[1]
    cols = pl.ds(0, half)
    lo = pl.multiple_of(c * half, half)
    hi = pl.multiple_of((1 - c) * half, half)
    cps = start_pieces(lay, pieces[: len(lay)], w, rows, 0, pl.ds(lo, half), me, sems, 0, cols)
    cps += start_pieces(lay, pieces[len(lay) :], w, rows, 0, pl.ds(hi, half), me, sems, len(lay), cols)
    for cp in cps:
        cp.wait()


def out_proj(ids, att_own, att_oth, tok, norms, own, oth, tm=256):
    lay = piece_layout(own)
    t, d = tok.shape
    blk = lambda w: pl.BlockSpec((tm, w), lambda i, ids: (i, 0))
    return pl.pallas_call(
        functools.partial(out_proj_kernel, lay),
        out_shape=[sds((t, d), f32), sds((t, d), bf16)],
        grid_spec=pltpu.PrefetchScalarGridSpec(
            num_scalar_prefetch=1,
            grid=(t // tm,),
            in_specs=[blk(d // 2), blk(d // 2), blk(d), pl.BlockSpec((4, d), lambda i, ids: (0, 0))] + [ANY] * (2 * len(lay)),
            out_specs=[blk(d), blk(d)],
            scratch_shapes=[pltpu.VMEM((d, d), bf16), pltpu.SemaphoreType.DMA((2 * len(lay),))],
        ),
        compiler_params=params(),
        cost_estimate=cost(2 * t * d * d, 14e6),
        name="out_proj",
    )(ids, att_own, att_oth, tok, norms, *[p for _, _, p in own], *[p for _, _, p in oth])


def ffn_in_kernel(lay, ids, a_two, *refs):
    pieces, (hidden, slope, w, sems) = refs[: len(lay)], refs[len(lay) :]
    d = a_two.shape[1]
    wide = w.shape[1]
    blk = hidden.shape[1]

    @pl.when(pl.program_id(0) == 0)
    def _():
        cps = start_pieces(lay, pieces, w, d // ids_n(lay), 0, pl.ds(0, wide), ids[0], sems, 0, pl.ds(d // 2, wide))
        for cp in cps:
            cp.wait()

    cols = pl.ds(pl.multiple_of(pl.program_id(0) * blk, blk), blk)
    pre = dot_nn(a_two[...], w[:, cols])
    cdf = 0.5 + 0.5 * lax.erf(pre * (0.5**0.5))
    pdf = jnp.exp(-0.5 * pre * pre) * 0.3989422804014327
    hidden[...] = (pre * cdf).astype(bf16)
    slope[...] = (cdf + pre * pdf).astype(bf16)


def ffn_in(ids, a_two, pieces, ff, blk=512):
    lay = piece_layout(pieces)
    t, d = a_two.shape
    wide = ff // 2
    out = pl.BlockSpec((t, blk), lambda j, ids: (0, j))
    return pl.pallas_call(
        functools.partial(ffn_in_kernel, lay),
        out_shape=[sds((t, wide), bf16)] * 2,
        grid_spec=pltpu.PrefetchScalarGridSpec(
            num_scalar_prefetch=1,
            grid=(wide // blk,),
            in_specs=[pl.BlockSpec((t, d), lambda j, ids: (0, 0))] + [ANY] * len(lay),
            out_specs=[out, out],
            scratch_shapes=[pltpu.VMEM((d, wide), bf16), pltpu.SemaphoreType.DMA((len(lay),))],
        ),
        compiler_params=params(),
        cost_estimate=cost(2 * t * d * wide, 14e6, 2 * t * wide),
        name="ffn_in",
    )(ids, a_two, *[p for _, _, p in pieces])


def ffn_out_kernel(lay, ids, h_own, h_oth, resid, doc, *refs):
    pieces, (mixed, w, sems) = refs[: 2 * len(lay)], refs[2 * len(lay) :]
    half = h_own.shape[1]
    d = resid.shape[1]

    @pl.when(pl.program_id(0) == 0)
    def _():
        rows = half // ids_n(lay)
        cps = start_pieces(lay, pieces[: len(lay)], w, rows, 0, pl.ds(0, d), ids[0], sems, 0)
        cps += start_pieces(lay, pieces[len(lay) :], w, rows, half, pl.ds(0, d), ids[0], sems, len(lay))
        for cp in cps:
            cp.wait()

    y = dot_nn(h_own[...], w[:half, :]) + dot_nn(h_oth[...], w[half:, :]) + resid[...]
    mixed[...] = jnp.where(doc[...] >= 0, y, 0.0).astype(bf16)


def ffn_out(ids, h_own, h_oth, resid, doc_col, own, oth, tm=256):
    lay = piece_layout(own)
    t, half = h_own.shape
    d = resid.shape[1]
    blk = lambda w: pl.BlockSpec((tm, w), lambda i, ids: (i, 0))
    return pl.pallas_call(
        functools.partial(ffn_out_kernel, lay),
        out_shape=sds((t, d), bf16),
        grid_spec=pltpu.PrefetchScalarGridSpec(
            num_scalar_prefetch=1,
            grid=(t // tm,),
            in_specs=[blk(half), blk(half), blk(d), blk(1)] + [ANY] * (2 * len(lay)),
            out_specs=blk(d),
            scratch_shapes=[pltpu.VMEM((2 * half, d), bf16), pltpu.SemaphoreType.DMA((2 * len(lay),))],
        ),
        compiler_params=params(),
        cost_estimate=cost(4 * t * d * half, 23e6),
        name="ffn_out",
    )(ids, h_own, h_oth, resid, doc_col, *[p for _, _, p in own], *[p for _, _, p in oth])


def d_pre_kernel(lay, ids, d_out, slope, *refs):
    pieces, (d_pre, w, sems) = refs[: len(lay)], refs[len(lay) :]
    d = d_out.shape[1]
    blk = slope.shape[1]
    half = w.shape[0]

    @pl.when(pl.program_id(0) == 0)
    def _():
        cps = start_pieces(lay, pieces, w, half // ids_n(lay), 0, pl.ds(0, d), ids[0], sems, 0)
        for cp in cps:
            cp.wait()

    rows = pl.ds(pl.multiple_of(pl.program_id(0) * blk, blk), blk)
    d_pre[...] = (dot_nt(d_out[...], w[rows, :]) * slope[...].astype(f32)).astype(bf16)


def pre_grad(ids, d_out, slope, pieces, blk=512):
    lay = piece_layout(pieces)
    t, d = d_out.shape
    half = slope.shape[1]
    col = pl.BlockSpec((t, blk), lambda j, ids: (0, j))
    return pl.pallas_call(
        functools.partial(d_pre_kernel, lay),
        out_shape=sds((t, half), bf16),
        grid_spec=pltpu.PrefetchScalarGridSpec(
            num_scalar_prefetch=1,
            grid=(half // blk,),
            in_specs=[pl.BlockSpec((t, d), lambda j, ids: (0, 0)), col] + [ANY] * len(lay),
            out_specs=col,
            scratch_shapes=[pltpu.VMEM((half, d), bf16), pltpu.SemaphoreType.DMA((len(lay),))],
        ),
        compiler_params=params(),
        cost_estimate=cost(2 * t * d * half, 14e6),
        name="pre_grad",
    )(ids, d_out, slope, *[p for _, _, p in pieces])


def d_two_kernel(lay, ids, p_own, p_oth, resid, d_out, norms, *refs):
    pieces = refs[: 2 * len(lay)]
    d_resid, low, low_oth, dg, db, w, sems = refs[2 * len(lay) :]
    half = p_own.shape[1]
    d = resid.shape[1]

    @pl.when(pl.program_id(0) == 0)
    def _():
        rows = d // ids_n(lay)
        cols = pl.ds(d // 2, half)
        cps = start_pieces(lay, pieces[: len(lay)], w, rows, 0, pl.ds(0, half), ids[0], sems, 0, cols)
        cps += start_pieces(lay, pieces[len(lay) :], w, rows, 0, pl.ds(half, half), ids[0], sems, len(lay), cols)
        for cp in cps:
            cp.wait()
        dg[...] = jnp.zeros_like(dg)
        db[...] = jnp.zeros_like(db)

    dz = dot_nt(p_own[...], w[:, :half]) + dot_nt(p_oth[...], w[:, half:])
    dv, g, b = layer_norm_back(resid[...], norms[2:3, :], dz)
    dg[...] += g
    db[...] += b
    dr = d_out[...].astype(f32) + dv
    d_resid[...] = dr
    dl = dr.astype(bf16)
    low[...] = dl
    low_oth[...] = pick(ids[1] == 0, dl[:, d // 2 :], dl[:, : d // 2])


def two_grad(ids, p_own, p_oth, resid, d_out, norms, own, oth, tm=256):
    lay = piece_layout(own)
    t, half = p_own.shape
    d = resid.shape[1]
    blk = lambda w: pl.BlockSpec((tm, w), lambda i, ids: (i, 0))
    row = pl.BlockSpec((1, d), lambda i, ids: (0, 0))
    return pl.pallas_call(
        functools.partial(d_two_kernel, lay),
        out_shape=[sds((t, d), f32), sds((t, d), bf16), sds((t, d // 2), bf16), sds((1, d), f32), sds((1, d), f32)],
        grid_spec=pltpu.PrefetchScalarGridSpec(
            num_scalar_prefetch=1,
            grid=(t // tm,),
            in_specs=[blk(half), blk(half), blk(d), blk(d), pl.BlockSpec((4, d), lambda i, ids: (0, 0))] + [ANY] * (2 * len(lay)),
            out_specs=[blk(d), blk(d), blk(d // 2), row, row],
            scratch_shapes=[pltpu.VMEM((d, 2 * half), bf16), pltpu.SemaphoreType.DMA((2 * len(lay),))],
        ),
        compiler_params=params(),
        cost_estimate=cost(4 * t * d * half, 30e6),
        name="two_grad",
    )(ids, p_own, p_oth, resid, d_out, norms, *[p for _, _, p in own], *[p for _, _, p in oth])


def d_att_kernel(lay, ids, low, *refs):
    pieces, (own, oth, w, sems) = refs[: 2 * len(lay)], refs[2 * len(lay) :]
    half = own.shape[1]

    @pl.when(pl.program_id(0) == 0)
    def _():
        load_out(lay, ids, pieces, w, sems)

    lo = pl.multiple_of(ids[1] * half, half)
    hi = pl.multiple_of((1 - ids[1]) * half, half)
    own[...] = dot_nt(low[...], w[pl.ds(lo, half), :]).astype(bf16)
    oth[...] = dot_nt(low[...], w[pl.ds(hi, half), :]).astype(bf16)


def att_grad(ids, low, own, oth, tm=512):
    lay = piece_layout(own)
    t, d = low.shape
    blk = lambda w: pl.BlockSpec((tm, w), lambda i, ids: (i, 0))
    return pl.pallas_call(
        functools.partial(d_att_kernel, lay),
        out_shape=[sds((t, d // 2), bf16)] * 2,
        grid_spec=pltpu.PrefetchScalarGridSpec(
            num_scalar_prefetch=1,
            grid=(t // tm,),
            in_specs=[blk(d)] + [ANY] * (2 * len(lay)),
            out_specs=[blk(d // 2), blk(d // 2)],
            scratch_shapes=[pltpu.VMEM((d, d), bf16), pltpu.SemaphoreType.DMA((2 * len(lay),))],
        ),
        compiler_params=params(),
        cost_estimate=cost(2 * t * d * d, 6e6),
        name="att_grad",
    )(ids, low, *[p for _, _, p in own], *[p for _, _, p in oth])


def d_one_kernel(lay, ids, *refs):
    grads, (tok, d_resid, norms), refs = refs[:6], refs[6:9], refs[9:]
    pieces, (out, dg, db, w, sems) = refs[: 2 * len(lay)], refs[2 * len(lay) :]
    d = tok.shape[1]
    half = 3 * d // 2

    @pl.when(pl.program_id(0) == 0)
    def _():
        rows = d // ids_n(lay)
        cps = start_pieces(lay, pieces[: len(lay)], w, rows, 0, pl.ds(0, half), ids[0], sems, 0)
        cps += start_pieces(lay, pieces[len(lay) :], w, rows, 0, pl.ds(half, half), ids[0], sems, len(lay))
        for cp in cps:
            cp.wait()
        dg[...] = jnp.zeros_like(dg)
        db[...] = jnp.zeros_like(db)

    both = jnp.concatenate([g[...] for g in grads], axis=1)
    dz = dot_nt(both, w[...])
    dv, g, b = layer_norm_back(tok[...].astype(f32), norms[0:1, :], dz)
    dg[...] += g
    db[...] += b
    out[...] = (d_resid[...] + dv).astype(bf16)


def one_grad(ids, g_own, g_oth, tok, d_resid, norms, own, oth, tm=256):
    lay = piece_layout(own)
    t, d = tok.shape
    blk = lambda w: pl.BlockSpec((tm, w), lambda i, ids: (i, 0))
    row = pl.BlockSpec((1, d), lambda i, ids: (0, 0))
    return pl.pallas_call(
        functools.partial(d_one_kernel, lay),
        out_shape=[sds((t, d), bf16), sds((1, d), f32), sds((1, d), f32)],
        grid_spec=pltpu.PrefetchScalarGridSpec(
            num_scalar_prefetch=1,
            grid=(t // tm,),
            in_specs=[blk(d // 2)] * 6 + [blk(d), blk(d), pl.BlockSpec((4, d), lambda i, ids: (0, 0))] + [ANY] * (2 * len(lay)),
            out_specs=[blk(d), row, row],
            scratch_shapes=[pltpu.VMEM((d, 3 * d), bf16), pltpu.SemaphoreType.DMA((2 * len(lay),))],
        ),
        compiler_params=params(),
        cost_estimate=cost(6 * t * d * d, 22e6),
        name="one_grad",
    )(ids, *g_own, *g_oth, tok, d_resid, norms, *[p for _, _, p in own], *[p for _, _, p in oth])


def pair_kernel(nb, a_mine, a_theirs, *refs):
    mine, theirs, out = refs[:nb], refs[nb : 2 * nb], refs[2 * nb]
    wide = mine[0].shape[1]
    for j in range(nb):
        acc = dot_tn(a_mine[...], mine[j][...]) + dot_tn(a_theirs[...], theirs[j][...])
        out[:, j * wide : (j + 1) * wide] = acc.astype(bf16)


def pair_grad(a_mine, a_theirs, mine, theirs, name, tm=256):
    t, m = a_mine.shape
    wide = mine[0].shape[1]
    nb = len(mine)
    a_spec = pl.BlockSpec((t, tm), lambda i: (0, i))
    b_spec = pl.BlockSpec((t, wide), lambda i: (0, 0))
    return pl.pallas_call(
        functools.partial(pair_kernel, nb),
        grid=(m // tm,),
        out_shape=sds((m, nb * wide), bf16),
        in_specs=[a_spec, a_spec] + [b_spec] * (2 * nb),
        out_specs=pl.BlockSpec((tm, nb * wide), lambda i: (i, 0)),
        compiler_params=params(),
        cost_estimate=cost(4 * t * m * wide * nb, 14e6),
        name=name,
    )(a_mine, a_theirs, *mine, *theirs)


def out_grad_kernel(ids, a_own, a_oth, t_own, t_oth, low, theirs, out):
    half = a_own.shape[1]
    c = ids[1]
    lo = pl.multiple_of(c * half, half)
    hi = pl.multiple_of((1 - c) * half, half)
    out[pl.ds(lo, half), :] = (dot_tn(a_own[...], low[...]) + dot_tn(t_oth[...], theirs[...])).astype(bf16)
    out[pl.ds(hi, half), :] = (dot_tn(a_oth[...], low[...]) + dot_tn(t_own[...], theirs[...])).astype(bf16)


def out_grad(ids, att_own, att_oth, their_own, their_oth, low, theirs):
    t, half = att_own.shape
    full = pl.BlockSpec((t, half), lambda i, ids: (0, 0))
    return pl.pallas_call(
        out_grad_kernel,
        out_shape=sds((2 * half, half), bf16),
        grid_spec=pltpu.PrefetchScalarGridSpec(
            num_scalar_prefetch=1,
            grid=(1,),
            in_specs=[full] * 4 + [pl.BlockSpec((t, half), lambda i, ids: (0, ids[1])), full],
            out_specs=pl.BlockSpec((2 * half, half), lambda i, ids: (0, 0)),
        ),
        compiler_params=params(),
        cost_estimate=cost(8 * t * half * half, 8e6),
        name="out_grad",
    )(ids, att_own, att_oth, their_own, their_oth, low, theirs)


def reduce_depth(v, nz):
    if nz != 4:
        return lax.psum(v.astype(f32), "z").astype(bf16)
    z = lax.axis_index("z")
    near = [(0, 1), (1, 0), (2, 3), (3, 2)]
    far = [(0, 2), (2, 0), (1, 3), (3, 1)]

    def split(u, bit):
        h = u.shape[0] // 2
        a, b = u[:h], u[h:]
        return jnp.where(bit == 0, a, b), jnp.where(bit == 0, b, a)

    def join(mine, theirs, bit):
        return jnp.where(bit == 0, jnp.concatenate([mine, theirs]), jnp.concatenate([theirs, mine]))

    b0, b1 = z % 2, z // 2
    keep, send = split(v, b0)
    keep = keep + lax.ppermute(send, "z", near)
    keep, send = split(keep, b1)
    keep = keep + lax.ppermute(send, "z", far)
    keep = join(keep, lax.ppermute(keep, "z", far), b1)
    return join(keep, lax.ppermute(keep, "z", near), b0)


def adam_rows(g, m1, m2):
    first = BETA_ONE * m1 + (1.0 - BETA_ONE) * g
    second = BETA_TWO * m2 + (1.0 - BETA_TWO) * g * g
    first_hat = first / (1.0 - BETA_ONE**STEPS)
    second_hat = second / (1.0 - BETA_TWO**STEPS)
    return -RATE * first_hat / (jnp.sqrt(second_hat) + ADAM_EPS), first


def adam_kernel(plan, inv_root, ids, own, oth, m1, m2, *refs):
    wg, st, mn = refs[-3:]
    rows, stride, places = plan
    first = ids[1] == 0
    for col, lo, hi in places:
        a = own[:, col : col + 128].astype(f32)
        b = oth[:, col : col + 128].astype(f32)
        for at, g in ((lo, pick(first, a, b)), (hi, pick(first, b, a))):
            where = pl.ds(at, rows, stride=stride)
            g = g * inv_root
            step, moment = adam_rows(g, m1[where, :], m2[where, :])
            wg[where, :] = g
            st[where, :] = step
            mn[where, :] = moment


def adam_columns(ids, own, oth, m1, m2, prev, inv_root, first_row, rows, places, width):
    count = own.shape[0]
    nb = width // 128
    blk = rows * nb
    assert first_row % blk == 0
    base = first_row // blk
    half = pl.BlockSpec((rows, own.shape[1]), lambda i, ids: (i, 0))
    flat = pl.BlockSpec((blk, 128), lambda i, ids: (base + i, 0))
    plan = (rows, nb, places)
    return adam_call(plan, ids, own, oth, m1, m2, prev, inv_root, count // rows, half, flat)


def adam_call(plan, ids, own, oth, m1, m2, prev, inv_root, steps, half, flat):
    return pl.pallas_call(
        functools.partial(adam_kernel, plan, inv_root),
        out_shape=[sds(m1.shape, f32)] * 3,
        grid_spec=pltpu.PrefetchScalarGridSpec(
            num_scalar_prefetch=1,
            grid=(steps,),
            in_specs=[half, half, flat, flat] + [ANY] * len(prev),
            out_specs=[flat] * 3,
        ),
        input_output_aliases={5 + i: i for i in range(len(prev))},
        compiler_params=params(),
        cost_estimate=cost(0, own.size * 2 * 22),
        name="adam",
    )(ids, own, oth, m1, m2, *prev)


def adam_back_kernel(inv_root, ids, own, oth, m1, m2, *refs):
    wg, st, mn = refs[-3:]
    g = pick(pl.program_id(0) == ids[1], own[...], oth[...]).astype(f32) * inv_root
    rows, width = g.shape
    nb = width // 128
    for w in range(nb):
        where = pl.ds(w, rows, stride=nb)
        gw = g[:, w * 128 : (w + 1) * 128]
        step, moment = adam_rows(gw, m1[where, :], m2[where, :])
        wg[where, :] = gw
        st[where, :] = step
        mn[where, :] = moment


def adam_back(ids, own, oth, m1, m2, prev, inv_root, first_row):
    count, width = own.shape
    rows = count // 4
    blk = rows * width // 128
    base = first_row // blk
    half = pl.BlockSpec((rows, width), lambda h, i, ids: (i, 0))
    flat = pl.BlockSpec((blk, 128), lambda h, i, ids: (base + h * 4 + i, 0))
    return pl.pallas_call(
        functools.partial(adam_back_kernel, inv_root),
        out_shape=[sds(m1.shape, f32)] * 3,
        grid_spec=pltpu.PrefetchScalarGridSpec(
            num_scalar_prefetch=1,
            grid=(2, 4),
            in_specs=[half, half, flat, flat] + [ANY] * len(prev),
            out_specs=[flat] * 3,
        ),
        input_output_aliases={5 + i: i for i in range(len(prev))},
        compiler_params=params(),
        cost_estimate=cost(0, own.size * 2 * 22),
        name="adam_back",
    )(ids, own, oth, m1, m2, *prev)


def adam_tail_kernel(g, m1, m2, p1, p2, p3, wg, st, mn):
    step, moment = adam_rows(g[...], m1[...], m2[...])
    wg[...] = g[...]
    st[...] = step
    mn[...] = moment


def adam_tail(g, m1, m2, prev, first_row):
    rows = 8
    assert first_row % rows == 0 and g.shape[0] <= rows
    g = jnp.pad(g, ((0, rows - g.shape[0]), (0, 0)))
    flat = pl.BlockSpec((rows, 128), lambda i: (first_row // rows, 0))
    return pl.pallas_call(
        adam_tail_kernel,
        grid=(1,),
        out_shape=[sds(m1.shape, f32)] * 3,
        in_specs=[pl.BlockSpec((rows, 128), lambda i: (0, 0)), flat, flat] + [ANY] * 3,
        out_specs=[flat] * 3,
        input_output_aliases={3: 0, 4: 1, 5: 2},
        name="adam_norms",
    )(g, m1, m2, *prev)


def body(n, nz, tokens, cotangent, doc_ids, master, moment_one, moment_two):
    t, d = tokens.shape
    ff = (master.shape[0] * n - 4 * d) // (2 * d) - 2 * d
    me = lax.axis_index(("y", "x"))
    core = lax.axis_index("core")
    ids = jnp.stack([me, core]).astype(jnp.int32)
    rows = d // n

    own_qkv, oth_qkv, own_oi, oth_oi, own_bk, oth_bk = unpack(ids, master, n, d, ff)
    norm_share = master[-(4 * d // n) :].astype(bf16)
    norms = lax.all_gather(norm_share, ("y", "x"), axis=0, tiled=True).reshape(4, d).astype(f32)

    def fetch(own, oth):
        pieces = gather_halves(own, n)
        others = [(0, 0, oth)] + [(k, off, swap_core(p)) for k, off, p in pieces[1:]]
        return pieces, others

    w_qkv = fetch(own_qkv, oth_qkv)
    own_oi, _ = lax.optimization_barrier((own_oi, w_qkv[0][-1][2]))
    w_oi = fetch(own_oi, oth_oi)
    own_bk, _ = lax.optimization_barrier((own_bk, w_oi[0][-1][2]))
    w_bk = fetch(own_bk, oth_bk)

    doc_row = doc_ids.reshape(1, t)
    doc_col = doc_ids.reshape(t, 1)
    d_out = jnp.where(doc_col >= 0, cotangent, jnp.zeros((), bf16))

    a_one, qkv_own, qkv_oth = project_qkv(ids, tokens, norms, *w_qkv)
    att_own, lse_own = attend(qkv_own, doc_row, doc_col, d)
    att_oth, lse_oth = attend(qkv_oth, doc_row, doc_col, d)
    resid, a_two = out_proj(ids, att_own, att_oth, tokens, norms, *w_oi)
    hid_oth, slope_oth = ffn_in(ids, a_two, w_oi[1], ff)
    hid_own, slope_own = ffn_in(ids, a_two, w_oi[0], ff)

    d_out_p = swap_core(d_out)
    a_one_p = swap_core(a_one)
    a_two_p = swap_core(a_two)
    att_own_p, att_oth_p = swap_core(att_own), swap_core(att_oth)
    hid_p = swap_core(hid_oth)

    scatter = lambda g: lax.psum_scatter(g, ("y", "x"), scatter_dimension=0, tiled=True)

    grad_back = scatter(pair_grad(hid_own, hid_p, [d_out], [d_out_p], "grad_back"))
    mixed = ffn_out(ids, hid_own, hid_oth, resid, doc_col, *w_bk)
    dp_oth = pre_grad(ids, d_out, slope_oth, w_bk[1])
    dp_p = swap_core(dp_oth)
    dp_own = pre_grad(ids, d_out, slope_own, w_bk[0])
    grad_in = scatter(pair_grad(a_two, a_two_p, [dp_own], [dp_p], "grad_in"))
    d_resid, low, low_oth, gain_two, bias_two = two_grad(ids, dp_own, dp_oth, resid, d_out, norms, *w_oi)
    low_p = swap_core(low_oth)
    datt_own, datt_oth = att_grad(ids, low, *w_oi)
    grad_out = scatter(out_grad(ids, att_own, att_oth, att_own_p, att_oth_p, low, low_p))
    dqkv_oth = attend_back(qkv_oth, datt_oth, att_oth, lse_oth, doc_row, doc_col, d)
    dqkv_p = [swap_core(g) for g in dqkv_oth]
    dqkv_own = attend_back(qkv_own, datt_own, att_own, lse_own, doc_row, doc_col, d)
    grad_qkv = scatter(pair_grad(a_one, a_one_p, dqkv_own, dqkv_p, "grad_qkv"))
    input_grad, gain_one, bias_one = one_grad(ids, dqkv_own, dqkv_oth, tokens, d_resid, norms, *w_qkv)

    norm_grads = lax.psum(jnp.concatenate([gain_one, bias_one, gain_two, bias_two]), ("z", "core", "y", "x"))
    inv_root = float(t * n * nz * 2) ** (-0.5)
    share = 4 * d // n
    norm_share = lax.dynamic_slice_in_dim(norm_grads.reshape(-1), me * share, share, 0) * inv_root

    m1, m2 = moment_one.reshape(-1, 128), moment_two.reshape(-1, 128)

    def finish(g):
        g = reduce_depth(g, nz)
        return g, swap_core(g)

    nb = d // 128
    half = nb // 2
    hs = ff // n // 2
    r_qkv, r_out, r_in = rows * 3 * nb, rows * nb, rows * ff // 128
    back_at = r_qkv + r_out + r_in
    outs = adam_back(ids, *finish(grad_back), m1, m2, [], inv_root, back_at)
    places = [(hs * j + q * 128, (2 * hs * j) // 128 + q, (2 * hs * j + hs) // 128 + q) for j in range(n) for q in range(hs // 128)]
    outs = adam_columns(ids, *finish(grad_in), m1, m2, outs, inv_root, r_qkv + r_out, rows // 8, places, ff)
    places = [(w * 128, w, w + half) for w in range(half)]
    outs = adam_columns(ids, *finish(grad_out), m1, m2, outs, inv_root, r_qkv, rows // 2, places, d)
    places = [((p * half + w) * 128, p * nb + w, p * nb + w + half) for p in range(3) for w in range(half)]
    outs = adam_columns(ids, *finish(grad_qkv), m1, m2, outs, inv_root, 0, rows // 8, places, 3 * d)
    outs = adam_tail(norm_share.reshape(-1, 128), m1, m2, outs, back_at + ff // n * nb)
    weight_grad, step, moment = [o.reshape(-1) for o in outs]
    return mixed, input_grad, weight_grad, step, moment


def solution(mesh):
    dp, n = mesh.shape["dp"], mesh.shape["group"]
    fine = Mesh(mesh.devices.reshape(dp // 2, 2, n // 2, 2), ("z", "core", "y", "x"))
    tok = ("z", "core", "y", "x")
    flat = P(("y", "x"))
    in_specs = (P(tok, None), P(tok, None), P(tok), flat, flat, flat)
    out_specs = (P(tok, None), P(tok, None), flat, flat, flat)
    return jax.shard_map(
        functools.partial(body, n, dp // 2), mesh=fine, in_specs=in_specs, out_specs=out_specs, check_vma=False
    )
```

```python
import functools

import jax
import jax.numpy as jnp
from jax import lax
from jax.experimental import pallas as pl
from jax.experimental.pallas import tpu as pltpu
from jax.sharding import Mesh
from jax.sharding import PartitionSpec as P

HEADS = 16
EPS = 1e-05
FILL = -1e30
BETA_ONE = 0.9
BETA_TWO = 0.999
RATE = 0.001
ADAM_EPS = 1e-08
STEPS = 100.0
VMEM_MB = 60

f32 = jnp.float32
bf16 = jnp.bfloat16
ANY = pl.BlockSpec(memory_space=pl.ANY)


def params(limit=VMEM_MB):
    return pltpu.CompilerParams(vmem_limit_bytes=limit << 20)


def cost(flops, nbytes, trans=0):
    return pl.CostEstimate(flops=int(flops), bytes_accessed=int(nbytes), transcendentals=int(trans))


def sds(shape, dtype):
    return jax.ShapeDtypeStruct(shape, dtype)


def dot_nn(a, b):
    return jnp.dot(a, b, preferred_element_type=f32)


def dot_nt(a, b):
    return lax.dot_general(a, b, (((1,), (1,)), ((), ())), preferred_element_type=f32)


def dot_tn(a, b):
    return lax.dot_general(a, b, (((0,), (0,)), ((), ())), preferred_element_type=f32)


def pick(flag, a, b):
    return jnp.where(flag, a, b)


MESH = pl.DeviceIdType.MESH


def peer(*axes):
    return {a: 1 - lax.axis_index(a) for a in axes}


def greet(peers):
    barrier = pltpu.get_barrier_semaphore()
    for p in peers:
        pl.semaphore_signal(barrier, inc=1, device_id=p, device_id_type=MESH)
    pl.semaphore_wait(barrier, len(peers))


def member():
    return lax.axis_index("y") * 2 + lax.axis_index("x")


class Gather:
    COUNT = 9

    def __init__(self, own, oth, send, recv, base):
        rows = own.shape[0] // 4
        half = rows // 2
        x, y = lax.axis_index("x"), lax.axis_index("y")
        share = [y * 2 + x, y * 2 + 1 - x, (1 - y) * 2 + x, (1 - y) * 2 + 1 - x]

        def at(ref, k, off, count):
            return ref.at[pl.ds(pl.multiple_of(share[k] * rows + off, 8), count), :]

        def move(i, k, off, count, dst, to):
            return pltpu.make_async_remote_copy(
                src_ref=at(own, k, off, count), dst_ref=at(dst, k, off, count),
                send_sem=send.at[base + i], recv_sem=recv.at[base + i], device_id=peer(to), device_id_type=MESH,
            )

        self.moves = [
            move(0, 0, 0, rows, own, "x"),
            move(1, 0, 0, rows, own, "y"),
            move(2, 0, 0, rows, oth, "core"),
            move(3, 1, 0, half, own, "y"),
            move(4, 2, half, half, own, "x"),
            move(5, 1, 0, rows, oth, "core"),
            move(6, 2, 0, rows, oth, "core"),
            move(7, 3, 0, half, oth, "core"),
            move(8, 3, half, half, oth, "core"),
        ]

    def begin(self):
        for i in (0, 1, 2):
            self.moves[i].start()

    def relay(self):
        self.moves[0].wait_recv()
        self.moves[3].start()
        self.moves[5].start()
        self.moves[1].wait_recv()
        self.moves[4].start()
        self.moves[6].start()

    def finish(self):
        self.moves[3].wait_recv()
        self.moves[7].start()
        self.moves[4].wait_recv()
        self.moves[8].start()
        for i in (2, 5, 6, 7, 8):
            self.moves[i].wait_recv()
        for m in self.moves:
            m.wait_send()


def hand_over(src, dst, send, recv):
    return pltpu.make_async_remote_copy(
        src_ref=src, dst_ref=dst, send_sem=send, recv_sem=recv, device_id=peer("core"), device_id_type=MESH
    )


class Fold:
    def __init__(self, pieces, source, mine, inbox, cross, stage, total, theirs, send, recv, base):
        self.pieces = pieces
        z = lax.axis_index("z")
        self.end = (z == 0) | (z == 3)
        self.mid = (z == 1) | (z == 2)
        near, far = self.peers()
        rows = mine.shape[0] // pieces
        self.mine, self.inbox, self.across, self.stage, self.total = mine, inbox, cross, stage, total
        self.rows = [pl.ds(s * rows, rows) for s in range(pieces)]

        def move(kind, src, dst, to):
            i = base + kind
            return pltpu.make_async_remote_copy(
                src_ref=src, dst_ref=dst, send_sem=send.at[i], recv_sem=recv.at[i], device_id=to, device_id_type=MESH
            )

        self.fold = [move(4 * s, source.at[r, :], inbox.at[s], near) for s, r in enumerate(self.rows)]
        self.cross = [move(4 * s + 1, stage.at[s], cross.at[s], far) for s, r in enumerate(self.rows)]
        self.unfold = [move(4 * s + 2, total.at[r, :], total.at[r, :], near) for s, r in enumerate(self.rows)]
        self.core = [move(4 * s + 3, total.at[r, :], theirs.at[r, :], peer("core")) for s, r in enumerate(self.rows)]

    @staticmethod
    def peers():
        z = lax.axis_index("z")
        return [{"z": z + 1 - 2 * (z % 2)}, {"z": 3 - z}]

    def begin(self, s=None):
        @pl.when(self.end)
        def _():
            for m in self.fold if s is None else [self.fold[s]]:
                m.start()

    def inner(self, s):
        @pl.when(self.mid)
        def _():
            self.fold[s].wait_recv()
            both = self.mine[self.rows[s], :].astype(f32) + self.inbox[s].astype(f32)
            self.stage[s] = both.astype(bf16)
            self.cross[s].start()

    def outer(self, s):
        @pl.when(self.mid)
        def _():
            self.cross[s].wait_recv()
            both = self.stage[s].astype(f32) + self.across[s].astype(f32)
            self.total[self.rows[s], :] = both.astype(bf16)
            self.unfold[s].start()
            self.core[s].start()

    def land(self, s):
        @pl.when(self.end)
        def _():
            self.unfold[s].wait_recv()
            self.core[s].start()

    def tick(self, k):
        if 0 <= k < self.pieces:
            self.inner(k)
        if 0 <= k - 1 < self.pieces:
            self.outer(k - 1)
        if 0 <= k - 2 < self.pieces:
            self.land(k - 2)

    def finish(self):
        @pl.when(self.end)
        def _():
            for m in self.fold:
                m.wait_send()

        @pl.when(self.mid)
        def _():
            for m in self.cross + self.unfold:
                m.wait_send()

        for m in self.core:
            m.wait()


def fold_scratch(rows, cols, pieces):
    block = pltpu.VMEM((pieces, rows // pieces, cols), bf16)
    whole = pltpu.VMEM((rows, cols), bf16)
    return [whole, block, block, block, whole, whole]


class Scatter:
    COUNT = 6

    def __init__(self, pieces, grads, held, far, near, mid, total, send, recv, base):
        self.pieces = pieces
        share_rows = grads.shape[0] // 4
        rows = share_rows // pieces
        half = rows // 2
        x, y = lax.axis_index("x"), lax.axis_index("y")
        me, over_x, over_y, both = y * 2 + x, y * 2 + 1 - x, (1 - y) * 2 + x, (1 - y) * 2 + 1 - x
        self.held, self.far, self.near, self.mid, self.total = held, far, near, mid, total
        self.half = half

        def at(share, s, part):
            return pl.ds(pl.multiple_of(share * share_rows + s * rows + part * half, half), half)

        def move(i, src, dst, to):
            return pltpu.make_async_remote_copy(
                src_ref=src, dst_ref=dst, send_sem=send.at[base + i], recv_sem=recv.at[base + i],
                device_id=peer(to), device_id_type=MESH,
            )

        self.first, self.second, self.keep = [], [], []
        for s in range(pieces):
            b = 6 * s
            self.first.append([
                move(b, grads.at[at(over_x, s, 0), :], far.at[s, 0], "x"),
                move(b + 1, grads.at[at(both, s, 0), :], far.at[s, 1], "x"),
                move(b + 2, grads.at[at(over_y, s, 1), :], far.at[s, 2], "y"),
                move(b + 3, grads.at[at(both, s, 1), :], far.at[s, 3], "y"),
            ])
            self.second.append([
                move(b + 4, mid.at[s, 1], near.at[s, 0], "y"),
                move(b + 5, mid.at[s, 3], near.at[s, 1], "x"),
            ])
            self.keep.append([at(me, s, 0), at(over_y, s, 0), at(me, s, 1), at(over_x, s, 1)])

    def begin(self, s):
        for m in self.first[s]:
            m.start()

    def turn(self, s):
        for k in (1, 0, 3, 2):
            self.first[s][k].wait_recv()
            both = self.held[self.keep[s][k], :].astype(f32) + self.far[s, k].astype(f32)
            self.mid[s, k] = both.astype(bf16)
            if k == 1:
                self.second[s][0].start()
            if k == 3:
                self.second[s][1].start()

    def close(self, s):
        for part in range(2):
            self.second[s][part].wait_recv()
            both = self.mid[s, 2 * part].astype(f32) + self.near[s, part].astype(f32)
            self.total[pl.ds((2 * s + part) * self.half, self.half), :] = both.astype(bf16)

    def finish(self):
        for s in range(self.pieces):
            for m in self.first[s] + self.second[s]:
                m.wait_send()


def scatter_scratch(rows, cols, pieces):
    half = rows // 4 // pieces // 2
    four = pltpu.VMEM((pieces, 4, half, cols), bf16)
    return [pltpu.VMEM((rows, cols), bf16), four, pltpu.VMEM((pieces, 2, half, cols), bf16), four]


def swap_core(v):
    return lax.ppermute(v, "core", [(0, 1), (1, 0)])


def comm_params(cid, limit=VMEM_MB):
    if cid is None:
        return params(limit)
    return pltpu.CompilerParams(vmem_limit_bytes=limit << 20, collective_id=cid, has_side_effects=True)


def dma(count):
    return pltpu.SemaphoreType.DMA((count,))


def gain_row(norms, r, d):
    nb = d // 128
    return jnp.concatenate([norms[r * nb + i : r * nb + i + 1, :] for i in range(nb)], axis=1)


def layer_norm_parts(v):
    centre = v - jnp.mean(v, axis=-1, keepdims=True)
    r = lax.rsqrt(jnp.mean(centre * centre, axis=-1, keepdims=True) + EPS)
    return centre * r, r


def layer_norm_back(v, gain, dz):
    xhat, r = layer_norm_parts(v)
    dg = jnp.sum(dz * xhat, axis=0, keepdims=True)
    db = jnp.sum(dz, axis=0, keepdims=True)
    t = dz * gain
    dv = r * (t - jnp.mean(t, axis=-1, keepdims=True) - xhat * jnp.mean(t * xhat, axis=-1, keepdims=True))
    return dv, dg, db


def unpack_kernel(dims, m_qkv, m_out, m_norm, own_qkv, own_out, norm):
    n, d = dims
    first = lax.axis_index("core") == 0
    nb = d // 128
    half = nb // 2
    rows = own_qkv.shape[0]

    def put(ref, own, dst, lo, stride):
        a = ref[pl.ds(lo, rows, stride=stride), :]
        b = ref[pl.ds(lo + half, rows, stride=stride), :]
        own[:, dst : dst + 128] = pick(first, a, b).astype(bf16)

    for part in range(3):
        for w in range(half):
            put(m_qkv, own_qkv, (part * half + w) * 128, part * nb + w, 3 * nb)
    for w in range(half):
        put(m_out, own_out, w * 128, w, nb)
    norm[...] = m_norm[...].astype(bf16).astype(f32)


def group_index(n):
    return lax.axis_index(("y", "x"))


def unpack_first(lanes, n, d, ff):
    rows = d // n
    nb = d // 128
    r1, r2, r3, r4 = rows * 3 * nb, rows * nb, rows * ff // 128, ff // n * nb
    steps = 4 if n == 4 else 2
    sr = rows // steps
    me = lambda: group_index(n)
    return pl.pallas_call(
        functools.partial(unpack_kernel, (n, d)),
        grid=(steps,),
        out_shape=[sds((d, 3 * d // 2), bf16), sds((d, d // 2), bf16), sds((8, 128), f32)],
        in_specs=[
            pl.BlockSpec((r1 // steps, 128), lambda i: (i, 0)),
            pl.BlockSpec((r2 // steps, 128), lambda i: (r1 // (r2 // steps) + i, 0)),
            pl.BlockSpec((8, 128), lambda i: ((r1 + r2 + r3 + r4) // 8, 0)),
        ],
        out_specs=[
            pl.BlockSpec((sr, 3 * d // 2), lambda i: (me() * steps + i, 0)),
            pl.BlockSpec((sr, d // 2), lambda i: (me() * steps + i, 0)),
            pl.BlockSpec((8, 128), lambda i: (0, 0)),
        ],
        compiler_params=params(),
        name="unpack",
    )(lanes, lanes, lanes)


UNPACK_STEPS = 8


def qkv_kernel(cfg, tok, norm_share, m_in, m_back, w_own_in, w_oth_in, o_own_in, o_oth_in, *refs):
    n, d, comm = cfg
    (a_out, qkv, own_in, own_bk, w_own, w_oth, o_own, o_oth, norms_out, norms, w, lsem, send, recv) = refs
    if not comm:
        w_own, w_oth = w_own_in, w_oth_in
    step = pl.program_id(0)
    nb = d // 128
    half = 3 * d // 2

    if comm:
        me = member()
        near = [peer("x"), peer("y"), peer("x", "y")]
        mine = pl.ds(pl.multiple_of(me * 8, 8), 8)
        notes = [
            pltpu.make_async_remote_copy(
                src_ref=norm_share, dst_ref=norms.at[mine, :], send_sem=send.at[18 + i], recv_sem=recv.at[18 + i],
                device_id=p, device_id_type=MESH,
            )
            for i, p in enumerate(near)
        ]
        first = Gather(w_own, w_oth, send, recv, 0)
        second = Gather(o_own, o_oth, send, recv, 9)

        @pl.when(step == 0)
        def _():
            greet(near + [peer("core")])
            for m in notes:
                m.start()
            first.begin()
            norms[mine, :] = norm_share[...]

    @pl.when(step < UNPACK_STEPS)
    def _():
        core = lax.axis_index("core") == 0
        rows = own_in.shape[0]
        hs = own_in.shape[1] // n
        for j in range(n):
            for q in range(hs // 128):
                lo = (2 * hs * j) // 128 + q
                stride = m_in.shape[0] // rows
                a = m_in[pl.ds(lo, rows, stride=stride), :]
                b = m_in[pl.ds(lo + hs // 128, rows, stride=stride), :]
                at = hs * j + q * 128
                own_in[:, at : at + 128] = pick(core, a, b).astype(bf16)
        for q in range(nb):
            own_bk[:, q * 128 : (q + 1) * 128] = m_back[pl.ds(q, own_bk.shape[0], stride=nb), :].astype(bf16)

    @pl.when(step == UNPACK_STEPS)
    def _():
        if comm:
            for m in notes:
                m.wait()
            first.relay()
            second.begin()
            first.finish()
            norms_out[...] = norms[...]
        else:
            norms[...] = norm_share[...]
            norms_out[...] = norms[...]
        cps = [
            pltpu.make_async_copy(w_own, w.at[:, pl.ds(0, half)], lsem.at[0]),
            pltpu.make_async_copy(w_oth, w.at[:, pl.ds(half, half)], lsem.at[1]),
        ]
        for cp in cps:
            cp.start()
        for cp in cps:
            cp.wait()

    @pl.when(step >= UNPACK_STEPS)
    def _():
        xhat, _ = layer_norm_parts(tok[...].astype(f32))
        a = (xhat * gain_row(norms, 0, d) + gain_row(norms, 1, d)).astype(bf16)
        a_out[...] = a
        acc = dot_nn(a, w[...])
        scale = (d // HEADS) ** (-0.5)
        q = d // 2
        for o in (0, half):
            qkv[:, o : o + q] = (acc[:, o : o + q].astype(bf16).astype(f32) * scale).astype(bf16)
            qkv[:, o + q : o + half] = acc[:, o + q : o + half].astype(bf16)

    if comm:

        @pl.when(step == UNPACK_STEPS + 2)
        def _():
            second.relay()

        @pl.when(step == pl.num_programs(0) - 1)
        def _():
            second.finish()


def project_qkv(lanes, tok, norm_share, w, o, n, ff, comm, tm=256):
    t, d = tok.shape
    rows = d // n
    nb = d // 128
    hs = ff // n // 2
    r_in, r_bk = rows * ff // 128, ff // n * nb
    at_in, at_bk = rows * 4 * nb, rows * 4 * nb + r_in
    b_in, b_bk = r_in // UNPACK_STEPS, hs * nb // UNPACK_STEPS
    assert at_in % b_in == 0 and at_bk % b_bk == 0
    up = lambda i: jnp.minimum(i, UNPACK_STEPS - 1)
    tk = lambda i: jnp.maximum(i - UNPACK_STEPS, 0)
    me = lambda: group_index(n)
    blk = lambda wd: pl.BlockSpec((tm, wd), lambda i: (tk(i), 0))
    whole = lambda a: pl.BlockSpec(a.shape, lambda i: (0, 0))
    half = 3 * d // 2
    w_oth = [] if comm else [w[1], o[1]]
    shapes = [sds((t, d), bf16), sds((t, 3 * d), bf16), sds((d, ff // 2), bf16), sds((ff // 2, d), bf16),
              sds((d, half), bf16), sds((d, half), bf16), sds((d, d // 2), bf16), sds((d, d // 2), bf16), sds((4 * nb, 128), f32)]
    if not comm:
        w_args = [w[0], w[1], o[0], o[1]]
    else:
        w_args = [w, norm_share, o, norm_share]
    outs = pl.pallas_call(
        functools.partial(qkv_kernel, (n, d, comm)),
        grid=(UNPACK_STEPS + t // tm,),
        out_shape=shapes,
        in_specs=[
            blk(d), whole(norm_share),
            pl.BlockSpec((b_in, 128), lambda i: (at_in // b_in + up(i), 0)),
            pl.BlockSpec((b_bk, 128), lambda i: (at_bk // b_bk + lax.axis_index("core") * UNPACK_STEPS + up(i), 0)),
            ANY, ANY, ANY, ANY,
        ],
        out_specs=[
            blk(d), blk(3 * d),
            pl.BlockSpec((rows // UNPACK_STEPS, ff // 2), lambda i: (me() * UNPACK_STEPS + up(i), 0)),
            pl.BlockSpec((hs // UNPACK_STEPS, d), lambda i: (me() * UNPACK_STEPS + up(i), 0)),
            ANY, ANY, ANY, ANY, pl.BlockSpec((4 * nb, 128), lambda i: (0, 0)),
        ],
        scratch_shapes=[pltpu.VMEM((4 * nb, 128), f32), pltpu.VMEM((d, 3 * d), bf16), dma(2), dma(21), dma(21)],
        input_output_aliases={4: 4, 6: 6},
        compiler_params=comm_params(1 if comm else None),
        cost_estimate=cost(2 * t * d * 3 * d, 40e6),
        name="qkv",
    )(tok, norm_share, lanes, lanes, *w_args)
    if comm:
        return outs
    return [*outs[:4], w[0], w[1], o[0], o[1], outs[8]]


QB = 256


def fill_bias(bias, doc_row, doc_col):
    t = bias.shape[0]
    for r in range(0, t, QB):
        key = r + lax.broadcasted_iota(jnp.int32, (QB, t), 0)
        query = lax.broadcasted_iota(jnp.int32, (QB, t), 1)
        ok = (doc_col[r : r + QB, :] == doc_row[...]) & (key <= query)
        bias[r : r + QB, :] = jnp.where(ok, 0.0, FILL)


def head_lanes(v, h, hd):
    lane = lax.broadcasted_iota(jnp.int32, v.shape, 1)
    return jnp.where((lane >= h * hd) & (lane < (h + 1) * hd), v, jnp.zeros_like(v))


def attend_kernel(cfg, q, k, v, doc_row, doc_col, w_own_in, a_one, d_out, out, lse, w_own, w_oth, a_p, d_p, bias, send, recv):
    hd, comm = cfg
    step = pl.program_id(0)
    last = pl.num_programs(0) - 1
    if comm:
        gather = Gather(w_own, w_oth, send, recv, 0)
        swaps = [hand_over(a_one, a_p, send.at[9], recv.at[9]), hand_over(d_out, d_p, send.at[10], recv.at[10])]

        @pl.when(step == 0)
        def _():
            greet([peer("x"), peer("y"), peer("core")])
            gather.begin()
            for s in swaps:
                s.start()

        @pl.when(step == 5)
        def _():
            gather.relay()

    @pl.when(step == 0)
    def _():
        fill_bias(bias, doc_row, doc_col)

    t = q.shape[0]
    vt = v[...].T
    per = 128 // hd
    qs = [head_lanes(q[...], h, hd) for h in range(per)]
    for i in range(t // QB):
        n = (i + 1) * QB
        cols = slice(i * QB, n)
        outs = []
        for h in range(per):
            s = dot_nt(k[:n, :], qs[h][cols, :]) + bias[:n, cols]
            top = jnp.max(s, axis=0, keepdims=True)
            e = jnp.exp(s - top)
            total = jnp.sum(e, axis=0, keepdims=True)
            lse[0, h : h + 1, cols] = top + jnp.log(total)
            o = dot_nn(vt[h * hd : (h + 1) * hd, :n], e.astype(bf16))
            outs.append(o / total)
        out[cols, :] = jnp.concatenate(outs, axis=0).T.astype(bf16)

    if comm:

        @pl.when(step == last)
        def _():
            gather.finish()
            for s in swaps:
                s.wait()


def head_column(d, part):
    pairs = d // 256
    return lambda p: (0, (p // pairs) * 3 * pairs + part * pairs + p % pairs)


def attend(qkv, doc_row, doc_col, w_own, a_one, d_out, d, comm):
    t = qkv.shape[0]
    pairs = d // 128
    hd = d // HEADS
    per = 128 // hd
    col = lambda part: pl.BlockSpec((t, 128), head_column(d, part))
    outs = pl.pallas_call(
        functools.partial(attend_kernel, (hd, comm)),
        grid=(pairs,),
        out_shape=[sds((t, d), bf16), sds((pairs, per, t), f32), sds(w_own.shape, bf16), sds(w_own.shape, bf16),
                   sds((t, d), bf16), sds((t, d), bf16)],
        in_specs=[col(0), col(1), col(2), pl.BlockSpec((1, t), lambda p: (0, 0)), pl.BlockSpec((t, 1), lambda p: (0, 0)),
                  ANY, ANY, ANY],
        out_specs=[pl.BlockSpec((t, 128), lambda p: (0, p)), pl.BlockSpec((1, per, t), lambda p: (p, 0, 0)), ANY, ANY, ANY, ANY],
        scratch_shapes=[pltpu.VMEM((t, t), f32), dma(11), dma(11)],
        input_output_aliases={5: 2},
        compiler_params=comm_params(2 if comm else None),
        cost_estimate=cost(8 * t * t * d, 10e6, t * t * HEADS),
        name="attend",
    )(qkv, qkv, qkv, doc_row, doc_col, w_own, a_one, d_out)
    if comm:
        return outs
    full, oth = spread(w_own)
    return outs[0], outs[1], full, oth, swap_core(a_one), swap_core(d_out)


def spread(own):
    n = lax.axis_size("y") * lax.axis_size("x")
    rows = own.shape[0] // n
    mine = lax.dynamic_slice_in_dim(own, lax.axis_index(("y", "x")) * rows, rows, 0)
    full = lax.all_gather(mine, ("y", "x"), axis=0, tiled=True)
    return full, swap_core(full)


def attend_back_kernel(cfg, q, k, v, dout, att, lse, doc_row, doc_col, part_sum, dq, dk, dv, sent, red, red_p, *refs):
    hd, comm, deep = cfg
    bias, dk_acc, dv_acc, stage, lsem, send, recv = refs[:7]
    step = pl.program_id(0)
    pairs = q_pairs(stage)

    def hand(p, part):
        wide = 128 * pairs
        cols = pl.ds(pl.multiple_of(part * wide + p * 128, 128), 128)
        i = p * 3 + part
        return hand_over(stage.at[i], sent.at[:, cols], send.at[i], recv.at[i])

    if comm:

        if deep:
            fold = Fold(PIECES, part_sum, refs[7], *refs[8:13], send, recv, 3 * pairs)

        @pl.when(step == 0)
        def _():
            greet([peer("core")] + (Fold.peers() if deep else []))
            if deep:
                load = pltpu.make_async_copy(part_sum, refs[7], lsem.at[0])
                load.start()
                fold.begin()
                load.wait()

        @pl.when((step > 0) & (step <= pairs))
        def _():
            for part in range(3):
                hand(step - 1, part).start()

    @pl.when(step == 0)
    def _():
        fill_bias(bias, doc_row, doc_col)

    t = q.shape[0]
    per = 128 // hd
    scale = hd ** (-0.5)
    kt = k[...].T
    prod = (dout[...].astype(f32) * att[...].astype(f32)).T
    inner = [jnp.sum(prod[h * hd : (h + 1) * hd, :], axis=0, keepdims=True) for h in range(per)]
    qs = [head_lanes(q[...], h, hd) for h in range(per)]
    ds_ = [head_lanes(dout[...], h, hd) for h in range(per)]
    dk_acc[...] = jnp.zeros_like(dk_acc)
    dv_acc[...] = jnp.zeros_like(dv_acc)
    for i in range(t // QB):
        if deep and i % 2 == 0:
            for at in range(2 * pairs):
                beat = 2 * at + i // 2 - 3
                if 0 <= beat < PIECES + 2:

                    @pl.when(step == at)
                    def _():
                        fold.tick(beat)

        n = (i + 1) * QB
        cols = slice(i * QB, n)
        dqs = []
        for h in range(per):
            qh, dh = qs[h][cols, :], ds_[h][cols, :]
            s = dot_nt(k[:n, :], qh) + bias[:n, cols]
            p = jnp.exp(s - lse[0, h : h + 1, cols])
            dp = dot_nt(v[:n, :], dh)
            g = (p * (dp - inner[h][:, cols])).astype(bf16)
            dv_acc[:n, :] += dot_nn(p.astype(bf16), dh)
            dk_acc[:n, :] += dot_nn(g, qh)
            dqs.append(dot_nn(kt[h * hd : (h + 1) * hd, :n], g))
        dq[cols, :] = (jnp.concatenate(dqs, axis=0).T * scale).astype(bf16)
    dk[...] = dk_acc[...].astype(bf16)
    dv[...] = dv_acc[...].astype(bf16)

    if comm:

        @pl.when(step < pairs)
        def _():
            stage[step * 3] = dq[...]
            stage[step * 3 + 1] = dk[...]
            stage[step * 3 + 2] = dv[...]

        @pl.when(step == 2 * pairs - 1)
        def _():
            for p in range(pairs):
                for part in range(3):
                    hand(p, part).wait()
            if deep:
                fold.finish()
                put_away(refs[11], red, refs[12], red_p, lsem)


def q_pairs(stage):
    return stage.shape[0] // 3


def put_away(total, red, theirs, red_p, lsem):
    cps = [pltpu.make_async_copy(total, red, lsem.at[0]), pltpu.make_async_copy(theirs, red_p, lsem.at[1])]
    for cp in cps:
        cp.start()
    for cp in cps:
        cp.wait()


PIECES = 8


def attend_back(qkv, dout, att, lse, doc_row, doc_col, part_sum, d, comm, deep):
    t = qkv.shape[0]
    pairs = d // 128
    half = pairs // 2
    hd = d // HEADS
    per = 128 // hd
    turn = lambda p: (p + half) % pairs
    col = lambda part: pl.BlockSpec((t, 128), lambda p: head_column(d, part)(turn(p)))
    one = pl.BlockSpec((t, 128), lambda p: (0, turn(p)))
    outs = pl.pallas_call(
        functools.partial(attend_back_kernel, (hd, comm, deep)),
        grid=(pairs,),
        out_shape=[sds((t, d), bf16)] * 3 + [sds((t, 3 * d // 2), bf16)] + [sds(part_sum.shape, bf16)] * 2,
        in_specs=[col(0), col(1), col(2), one, one, pl.BlockSpec((1, per, t), lambda p: (turn(p), 0, 0)),
                  pl.BlockSpec((1, t), lambda p: (0, 0)), pl.BlockSpec((t, 1), lambda p: (0, 0)), ANY],
        out_specs=[one, one, one, ANY, ANY, ANY],
        scratch_shapes=[pltpu.VMEM((t, t), f32), pltpu.VMEM((t, 128), f32), pltpu.VMEM((t, 128), f32),
                        pltpu.VMEM((3 * half, t, 128), bf16), dma(2), dma(3 * half + 4 * PIECES), dma(3 * half + 4 * PIECES)]
        + (fold_scratch(*part_sum.shape, PIECES) if deep else []),
        compiler_params=comm_params(6 if comm else None),
        cost_estimate=cost(20 * t * t * d, 16e6, t * t * HEADS),
        name="attend_back",
    )(qkv, qkv, qkv, dout, att, lse, doc_row, doc_col, part_sum)
    sent = outs[3] if comm else swap_core(jnp.concatenate([g[:, d // 2 :] for g in outs[:3]], axis=1))
    return outs[0], outs[1], outs[2], sent, both_halves(part_sum, outs[4], outs[5], comm and deep)


def both_halves(part_sum, red, red_p, done):
    if done:
        return red, red_p
    full = lax.psum(part_sum.astype(f32), "z").astype(bf16)
    return full, swap_core(full)


def middle_kernel(cfg, att_rows, tok, norms, o_own, o_oth, w_own, w_oth, att_all, bk_own_in, *refs):
    d, tm, blk, comm = cfg
    (resid, a_two_out, hidden, slope, bk_own, bk_oth, hid_p, att_p, w, a_two, stage, lsem, send, recv) = refs
    step = pl.program_id(0)
    last = pl.num_programs(0) - 1
    t = a_two.shape[0]
    pro = t // tm
    half = d // 2
    wide = hid_p.shape[1]
    nb = wide // blk
    core = lax.axis_index("core")

    def hand(j):
        cols = pl.ds(pl.multiple_of(j * blk, blk), blk)
        return hand_over(stage.at[j], hid_p.at[:, cols], send.at[10 + j], recv.at[10 + j])

    if comm:
        gather = Gather(bk_own, bk_oth, send, recv, 0)
        swap = hand_over(att_all, att_p, send.at[9], recv.at[9])

        @pl.when(step == 0)
        def _():
            greet([peer("x"), peer("y"), peer("core")])
            gather.begin()
            swap.start()

        @pl.when(step == pro + nb + 1)
        def _():
            gather.relay()

        @pl.when((step > pro) & (step <= pro + nb))
        def _():
            hand(step - pro - 1).start()

    @pl.when(step == 0)
    def _():
        lo = pl.multiple_of(core * half, half)
        hi = pl.multiple_of((1 - core) * half, half)
        cps = [
            pltpu.make_async_copy(o_own, w.at[:, pl.ds(lo, half)], lsem.at[0]),
            pltpu.make_async_copy(o_oth, w.at[:, pl.ds(hi, half)], lsem.at[1]),
        ]
        for cp in cps:
            cp.start()
        for cp in cps:
            cp.wait()

    @pl.when(step < pro)
    def _():
        lo = pl.multiple_of(core * half, half)
        hi = pl.multiple_of((1 - core) * half, half)
        y = dot_nn(att_rows[:, :half], w[pl.ds(lo, half), :]) + dot_nn(att_rows[:, half:], w[pl.ds(hi, half), :])
        r = tok[...].astype(f32) + y
        resid[...] = r
        xhat, _ = layer_norm_parts(r)
        a = (xhat * gain_row(norms, 2, d) + gain_row(norms, 3, d)).astype(bf16)
        a_two_out[...] = a
        a_two[pl.ds(pl.multiple_of(step * tm, tm), tm), :] = a

    def unit(w_blk):
        pre = dot_nn(a_two[...], w_blk)
        cdf = 0.5 + 0.5 * lax.erf(pre * (0.5**0.5))
        pdf = jnp.exp(-0.5 * pre * pre) * 0.3989422804014327
        h = (pre * cdf).astype(bf16)
        hidden[...] = h
        slope[...] = (cdf + pre * pdf).astype(bf16)
        return h

    @pl.when((step >= pro) & (step < pro + nb))
    def _():
        h = unit(w_oth[...])
        if comm:
            stage[step - pro] = h

    @pl.when(step >= pro + nb)
    def _():
        unit(w_own[...])

    if comm:

        @pl.when(step == last)
        def _():
            gather.finish()
            swap.wait()
            for j in range(nb):
                hand(j).wait()


def middle(att, tok, norms, o_own, o_oth, w_own, w_oth, bk_own, comm, tm=256, blk=512):
    t, d = tok.shape
    wide = w_own.shape[1]
    pro, nb = t // tm, wide // blk
    rowi = lambda i: jnp.minimum(i, pro - 1)
    oth = lambda i: jnp.clip(i - pro, 0, nb - 1)
    own = lambda i: jnp.clip(i - pro - nb, 0, nb - 1)
    both = lambda i: jnp.where(i < pro + nb, nb + oth(i), own(i))
    rows = lambda wd: pl.BlockSpec((tm, wd), lambda i: (rowi(i), 0))
    outs = pl.pallas_call(
        functools.partial(middle_kernel, (d, tm, blk, comm)),
        grid=(pro + 2 * nb,),
        out_shape=[sds((t, d), f32), sds((t, d), bf16), sds((t, 2 * wide), bf16), sds((t, 2 * wide), bf16),
                   sds(bk_own.shape, bf16), sds(bk_own.shape, bf16), sds((t, wide), bf16), sds((t, d), bf16)],
        in_specs=[rows(d), rows(d), pl.BlockSpec(norms.shape, lambda i: (0, 0)), ANY, ANY,
                  pl.BlockSpec((d, blk), lambda i: (0, own(i))), pl.BlockSpec((d, blk), lambda i: (0, oth(i))), ANY, ANY],
        out_specs=[rows(d), rows(d), pl.BlockSpec((t, blk), lambda i: (0, both(i))), pl.BlockSpec((t, blk), lambda i: (0, both(i))),
                   ANY, ANY, ANY, ANY],
        scratch_shapes=[pltpu.VMEM((d, d), bf16), pltpu.VMEM((t, d), bf16), pltpu.VMEM((nb, t, blk), bf16), dma(2), dma(10 + nb), dma(10 + nb)],
        input_output_aliases={8: 4},
        compiler_params=comm_params(3 if comm else None),
        cost_estimate=cost(2 * t * d * d + 4 * t * d * wide, 44e6, 4 * t * wide),
        name="middle",
    )(att, tok, norms, o_own, o_oth, w_own, w_oth, att, bk_own)
    if comm:
        return outs
    full, other = spread(bk_own)
    return [*outs[:4], full, other, swap_core(outs[2][:, wide:]), swap_core(att)]


def pre_grad_kernel(comm, d_out, slope, w_own, w_oth, a_two, d_pre, sent, a_p, stage, send, recv):
    step = pl.program_id(0)
    nb = pl.num_programs(0) // 2
    blk = slope.shape[1]

    def hand(j):
        cols = pl.ds(pl.multiple_of(j * blk, blk), blk)
        return hand_over(stage.at[j], sent.at[:, cols], send.at[1 + j], recv.at[1 + j])

    if comm:
        swap = hand_over(a_two, a_p, send.at[0], recv.at[0])

        @pl.when(step == 0)
        def _():
            greet([peer("core")])
            swap.start()

        @pl.when((step > 0) & (step <= nb))
        def _():
            hand(step - 1).start()

    @pl.when(step < nb)
    def _():
        g = (dot_nt(d_out[...], w_oth[...]) * slope[...].astype(f32)).astype(bf16)
        d_pre[...] = g
        if comm:
            stage[step] = g

    @pl.when(step >= nb)
    def _():
        d_pre[...] = (dot_nt(d_out[...], w_own[...]) * slope[...].astype(f32)).astype(bf16)

    if comm:

        @pl.when(step == 2 * nb - 1)
        def _():
            swap.wait()
            for j in range(nb):
                hand(j).wait()


def pre_grad(d_out, slope, own, oth, a_two, comm, blk=512):
    t, d = d_out.shape
    half = own.shape[0]
    nb = half // blk
    col = pl.BlockSpec((t, blk), lambda i: (0, (i + nb) % (2 * nb)))
    outs = pl.pallas_call(
        functools.partial(pre_grad_kernel, comm),
        grid=(2 * nb,),
        out_shape=[sds((t, 2 * half), bf16), sds((t, half), bf16), sds((t, d), bf16)],
        in_specs=[pl.BlockSpec((t, d), lambda i: (0, 0)), col,
                  pl.BlockSpec((blk, d), lambda i: (jnp.maximum(i - nb, 0), 0)),
                  pl.BlockSpec((blk, d), lambda i: (jnp.minimum(i, nb - 1), 0)), ANY],
        out_specs=[col, ANY, ANY],
        scratch_shapes=[pltpu.VMEM((nb, t, blk), bf16), dma(1 + nb), dma(1 + nb)],
        compiler_params=comm_params(4 if comm else None),
        cost_estimate=cost(4 * t * d * half, 28e6),
        name="pre_grad",
    )(d_out, slope, own, oth, a_two)
    if comm:
        return outs
    return outs[0], swap_core(outs[0][:, half:]), swap_core(a_two)


def two_grad_kernel(comm, d_pre, resid, d_out, norms, w_own, w_oth, o_own, o_oth, *refs):
    d_resid, low, d_att, dg, db, sent, w, wo, stage, lsem, send, recv = refs
    step = pl.program_id(0)
    tm, d = resid.shape
    half = d // 2
    wide = w_own.shape[1]
    core = lax.axis_index("core")
    here = pl.ds(pl.multiple_of(step * tm, tm), tm)

    def hand():
        return hand_over(stage.at[here, :], sent.at[here, :], send.at[step], recv.at[step])

    @pl.when(step == 0)
    def _():
        if comm:
            greet([peer("core")])
        lo = pl.multiple_of(core * half, half)
        hi = pl.multiple_of((1 - core) * half, half)
        cps = [
            pltpu.make_async_copy(w_own, w.at[:, pl.ds(0, wide)], lsem.at[0]),
            pltpu.make_async_copy(w_oth, w.at[:, pl.ds(wide, wide)], lsem.at[1]),
            pltpu.make_async_copy(o_own, wo.at[:, pl.ds(lo, half)], lsem.at[2]),
            pltpu.make_async_copy(o_oth, wo.at[:, pl.ds(hi, half)], lsem.at[3]),
        ]
        for cp in cps:
            cp.start()
        for cp in cps:
            cp.wait()
        dg[...] = jnp.zeros_like(dg)
        db[...] = jnp.zeros_like(db)

    dz = dot_nt(d_pre[...], w[...])
    dv, g, b = layer_norm_back(resid[...], gain_row(norms, 2, d), dz)
    dg[...] += g
    db[...] += b
    dr = d_out[...].astype(f32) + dv
    d_resid[...] = dr
    dl = dr.astype(bf16)
    low[...] = dl
    stage[here, :] = pick(core == 0, dl[:, half:], dl[:, :half])
    lo = pl.multiple_of(core * half, half)
    hi = pl.multiple_of((1 - core) * half, half)
    d_att[:, :half] = dot_nt(dl, wo[pl.ds(lo, half), :]).astype(bf16)
    d_att[:, half:] = dot_nt(dl, wo[pl.ds(hi, half), :]).astype(bf16)
    if comm:
        hand().start()

        @pl.when(step == pl.num_programs(0) - 1)
        def _():
            for s in range(stage.shape[0] // tm):
                rows = pl.ds(s * tm, tm)
                hand_over(stage.at[rows, :], sent.at[rows, :], send.at[s], recv.at[s]).wait()


def two_grad(d_pre, resid, d_out, norms, w_own, w_oth, o_own, o_oth, comm, tm=256):
    t, wide = d_pre.shape
    d = resid.shape[1]
    blk = lambda w: pl.BlockSpec((tm, w), lambda i: (i, 0))
    row = pl.BlockSpec((1, d), lambda i: (0, 0))
    outs = pl.pallas_call(
        functools.partial(two_grad_kernel, comm),
        grid=(t // tm,),
        out_shape=[sds((t, d), f32), sds((t, d), bf16), sds((t, d), bf16), sds((1, d), f32), sds((1, d), f32), sds((t, d // 2), bf16)],
        in_specs=[blk(wide), blk(d), blk(d), pl.BlockSpec(norms.shape, lambda i: (0, 0)), ANY, ANY, ANY, ANY],
        out_specs=[blk(d), blk(d), blk(d), row, row, ANY],
        scratch_shapes=[pltpu.VMEM((d, wide), bf16), pltpu.VMEM((d, d), bf16), pltpu.VMEM((t, d // 2), bf16),
                        dma(4), dma(t // tm), dma(t // tm)],
        compiler_params=comm_params(5 if comm else None),
        cost_estimate=cost(2 * t * d * (wide + d), 34e6),
        name="two_grad",
    )(d_pre, resid, d_out, norms, w_own, w_oth, o_own, o_oth)
    if comm:
        return outs
    core = lax.axis_index("core")
    other = lax.dynamic_slice_in_dim(outs[1], (1 - core) * (d // 2), d // 2, 1)
    return [*outs[:5], swap_core(other)]


LEAD = 2


def last_kernel(cfg, dq, dk, dv, tok, d_resid, norms, h_own, h_oth, resid, doc, two_norm, w_own, w_oth, b_own, b_oth, part_in, grads, *refs):
    d, comm = cfg
    out, mixed, red_in, red_in_p, red_at, red_at_p, sums, w, wb, parts, lsem = refs[:11]
    step = pl.program_id(0)
    last = pl.num_programs(0) - 1
    pro = last // 2
    half = 3 * d // 2
    q = d // 2
    hb = b_own.shape[0]
    nb = d // 128
    late = [
        pltpu.make_async_copy(b_own, wb.at[pl.ds(0, hb), :], lsem.at[2]),
        pltpu.make_async_copy(b_oth, wb.at[pl.ds(hb, hb), :], lsem.at[3]),
    ]
    if comm:
        send, recv, fi, sc, fa, vec, box = refs[11], refs[12], refs[13:19], refs[19:23], refs[23:29], refs[29], refs[30]
        fold_in = Fold(PIECES, part_in, fi[0], *fi[1:6], send, recv, 0)
        scat = Scatter(PIECES, grads, sc[0], sc[1], sc[2], sc[3], fa[0], send, recv, 4 * PIECES)
        fold_at = Fold(PIECES, fa[0], fa[0], *fa[1:6], send, recv, 10 * PIECES)
        base = 14 * PIECES

        def note(i, src, dst, to):
            return pltpu.make_async_remote_copy(
                src_ref=src, dst_ref=dst, send_sem=send.at[base + i], recv_sem=recv.at[base + i], device_id=to, device_id_type=MESH
            )

        near, far = Fold.peers()
        notes = [
            note(0, vec.at[0], box.at[0], peer("x")),
            note(1, vec.at[1], box.at[1], peer("y")),
            note(2, vec.at[2], box.at[2], peer("core")),
            note(3, vec.at[3], box.at[3], near),
            note(4, vec.at[4], box.at[4], far),
            note(5, vec.at[5], vec.at[5], near),
        ]

        def tick(k):
            if LEAD <= k + LEAD - 1 < PIECES:
                scat.begin(k + LEAD - 1)
            if 0 <= k - 1 < PIECES:
                scat.turn(k - 1)
            if 0 <= k - 2 < PIECES:
                scat.close(k - 2)
                fold_at.begin(k - 2)
            fold_in.tick(k - 1)
            fold_at.tick(k - 3)

        def norm_sum(k):
            if k < 3:
                notes[k].wait_recv()
                vec[k + 1] = vec[k] + box[k]
                if k < 2:
                    notes[k + 1].start()
                else:
                    pl.when(fold_in.end)(notes[3].start)
            elif k < 5:

                @pl.when(fold_in.mid)
                def _():
                    notes[k].wait_recv()
                    vec[k + 1] = vec[k] + box[k]
                    notes[k + 1].start()

            else:
                pl.when(fold_in.end)(notes[5].wait_recv)

    @pl.when(step == 0)
    def _():
        cps = [
            pltpu.make_async_copy(w_own, w.at[:, pl.ds(0, half)], lsem.at[0]),
            pltpu.make_async_copy(w_oth, w.at[:, pl.ds(half, half)], lsem.at[1]),
        ]
        for cp in cps:
            cp.start()
        if comm:
            loads = [pltpu.make_async_copy(part_in, fi[0], lsem.at[4]), pltpu.make_async_copy(grads, sc[0], lsem.at[5])]
            for cp in loads:
                cp.start()
            greet([peer("core"), peer("x"), peer("y")] + Fold.peers())
            for s in range(LEAD):
                scat.begin(s)
            fold_in.begin()
            for cp in loads:
                cp.wait()
        for cp in cps:
            cp.wait()
        for cp in late:
            cp.start()
        parts[0 : 2 * nb, :] = jnp.zeros((2 * nb, 128), f32)
        parts[2 * nb :, :] = two_norm[...]

    if comm:
        for k in range(1, last):

            @pl.when(step == k)
            def _():
                tick(k)

    @pl.when(step < pro)
    def _():
        both = jnp.concatenate([g[:, :q] for g in (dq, dk, dv)] + [g[:, q:] for g in (dq, dk, dv)], axis=1)
        dz = dot_nt(both, w[...])
        grad, g, b = layer_norm_back(tok[...].astype(f32), gain_row(norms, 0, d), dz)
        parts[0:nb, :] += flat_row(g)
        parts[nb : 2 * nb, :] += flat_row(b)
        out[...] = (d_resid[...] + grad).astype(bf16)

    @pl.when(step == pro)
    def _():
        for cp in late:
            cp.wait()
        if comm:
            vec[0] = parts[...]
            notes[0].start()

    @pl.when((step >= pro) & (step < last))
    def _():
        y = dot_nn(h_own[...], wb[:hb, :]) + dot_nn(h_oth[...], wb[hb:, :]) + resid[...]
        mixed[...] = jnp.where(doc[...] >= 0, y, 0.0).astype(bf16)

    @pl.when(step == last)
    def _():
        if comm:
            for k in range(2 * pro, PIECES + 6):
                tick(k)
                if k - 2 * pro < 6:
                    norm_sum(k - 2 * pro)
            fold_in.finish()
            scat.finish()
            fold_at.finish()
            for i in (0, 1, 2):
                notes[i].wait_send()
            pl.when(fold_in.end)(notes[3].wait_send)

            @pl.when(fold_in.mid)
            def _():
                notes[4].wait_send()
                notes[5].wait_send()

            sums[...] = vec[5]
            put_away(fi[4], red_in, fi[5], red_in_p, lsem)
            put_away(fa[4], red_at, fa[5], red_at_p, lsem)
        else:
            sums[...] = parts[...]


def flat_row(v):
    return jnp.concatenate([v[:, i * 128 : (i + 1) * 128] for i in range(v.shape[1] // 128)], axis=0)


def last_grad(grads3, tok, d_resid, norms, hidden, resid, doc_col, two_norm, own, oth, b_own, b_oth, part_in, grads, comm, tm=256):
    t, d = tok.shape
    pro = t // tm
    half = b_own.shape[0]
    one = lambda w, c=0: pl.BlockSpec((tm, w), lambda i: (jnp.minimum(i, pro - 1), c))
    two = lambda w, c=0: pl.BlockSpec((tm, w), lambda i: (jnp.clip(i - pro, 0, pro - 1), c))
    whole = lambda a: pl.BlockSpec(a.shape, lambda i: (0, 0))
    nv = 4 * d // 128
    share = (grads.shape[0] // 4, grads.shape[1])
    slots = 14 * PIECES + 6
    extra = []
    if comm:
        extra = [dma(slots), dma(slots)] + fold_scratch(*part_in.shape, PIECES) + scatter_scratch(*grads.shape, PIECES)
        extra += fold_scratch(*share, PIECES) + [pltpu.VMEM((6, nv, 128), f32), pltpu.VMEM((5, nv, 128), f32)]
    return pl.pallas_call(
        functools.partial(last_kernel, (d, comm)),
        grid=(2 * pro + 1,),
        out_shape=[sds((t, d), bf16), sds((t, d), bf16)] + [sds(part_in.shape, bf16)] * 2 + [sds(share, bf16)] * 2 + [sds((nv, 128), f32)],
        in_specs=[one(d)] * 5 + [whole(norms), two(half), two(half, 1), two(d), two(1), whole(two_norm)] + [ANY] * 6,
        out_specs=[one(d), two(d), ANY, ANY, ANY, ANY, pl.BlockSpec((nv, 128), lambda i: (0, 0))],
        scratch_shapes=[pltpu.VMEM((d, 3 * d), bf16), pltpu.VMEM((2 * half, d), bf16), pltpu.VMEM((nv, 128), f32), dma(6)] + extra,
        compiler_params=comm_params(7 if comm else None, 62),
        cost_estimate=cost(6 * t * d * d + 4 * t * d * half, 45e6),
        name="last_grad",
    )(*grads3, tok, d_resid, norms, hidden, hidden, resid, doc_col, two_norm, own, oth, b_own, b_oth, part_in, grads)


def pair_kernel(nb, a_mine, a_theirs, *refs):
    mine, theirs, out = refs[:nb], refs[nb], refs[nb + 1]
    wide = mine[0].shape[1]
    for j in range(nb):
        cols = slice(j * wide, (j + 1) * wide)
        acc = dot_tn(a_mine[...], mine[j][...]) + dot_tn(a_theirs[...], theirs[:, cols])
        out[:, cols] = acc.astype(bf16)


def pair_grad(a_mine, m, a_theirs, mine, wide, theirs, name, tm=256):
    t = a_mine.shape[0]
    nb = len(mine)
    a_spec = pl.BlockSpec((t, tm), lambda i: (0, i))
    b_spec = pl.BlockSpec((t, wide), lambda i: (0, 0))
    return pl.pallas_call(
        functools.partial(pair_kernel, nb),
        grid=(m // tm,),
        out_shape=sds((m, nb * wide), bf16),
        in_specs=[a_spec, a_spec] + [b_spec] * nb + [pl.BlockSpec((t, nb * wide), lambda i: (0, 0))],
        out_specs=pl.BlockSpec((tm, nb * wide), lambda i: (i, 0)),
        compiler_params=params(),
        cost_estimate=cost(4 * t * m * wide * nb, 14e6),
        name=name,
    )(a_mine, a_theirs, *mine, theirs)


def attention_grad_kernel(a, a_p, g1, g2, g3, theirs, att, att_p, low, low_p, out):
    wide = g1.shape[1]
    for j, g in enumerate((g1, g2, g3)):
        cols = slice(j * wide, (j + 1) * wide)
        out[:, cols] = (dot_tn(a[...], g[...]) + dot_tn(a_p[...], theirs[:, cols])).astype(bf16)
    out[:, 3 * wide :] = (dot_tn(att[...], low[...]) + dot_tn(att_p[...], low_p[...])).astype(bf16)


def attention_grads(a_one, a_one_p, mine, theirs, att, att_p, low, low_p, tm=256):
    t, d = a_one.shape
    half = d // 2
    nh = half // tm
    core = lambda: lax.axis_index("core")
    col = lambda f: pl.BlockSpec((t, tm), lambda i: (0, f(i)))
    held = lambda wd, f: pl.BlockSpec((t, wd), lambda i: (0, f()))
    own = lambda i: (i + core() * nh) % (2 * nh)
    theirs_at = lambda i: (i + (1 - core()) * nh) % (2 * nh)
    zero = lambda: 0
    return pl.pallas_call(
        attention_grad_kernel,
        grid=(d // tm,),
        out_shape=sds((d, 2 * d), bf16),
        in_specs=[col(lambda i: i), col(lambda i: i)] + [held(half, zero)] * 3 + [held(3 * half, zero)]
        + [col(own), col(theirs_at), held(half, core), held(half, zero)],
        out_specs=pl.BlockSpec((tm, 2 * d), lambda i: (i, 0)),
        compiler_params=params(),
        cost_estimate=cost(8 * t * d * d, 20e6),
        name="attention_grads",
    )(a_one, a_one_p, *mine, theirs, att, att_p, low, low_p)


def adam_update(g, m1, m2, wg, st, mn):
    first = BETA_ONE * m1[...] + (1.0 - BETA_ONE) * g
    second_hat = (BETA_TWO / (1.0 - BETA_TWO**STEPS)) * m2[...] + ((1.0 - BETA_TWO) / (1.0 - BETA_TWO**STEPS)) * g * g
    wg[...] = g
    st[...] = (-RATE / (1.0 - BETA_ONE**STEPS)) * first / (jnp.sqrt(second_hat) + ADAM_EPS)
    mn[...] = first


def flatten_columns(flat, own, oth, take, rows, stride, places, inv_root):
    first = lax.axis_index("core") == 0
    for col, lo, hi in places:
        a = own[take, col : col + 128].astype(f32) * inv_root
        b = oth[take, col : col + 128].astype(f32) * inv_root
        flat[pl.ds(lo, rows, stride=stride), :] = pick(first, a, b)
        flat[pl.ds(hi, rows, stride=stride), :] = pick(first, b, a)


def adam_kernel(plan, inv_root, own, oth, m1, m2, *refs):
    wg, st, mn, flat = refs[-4:]
    rows, stride, places = plan
    flatten_columns(flat, own, oth, slice(None), rows, stride, places, inv_root)
    adam_update(flat[...], m1, m2, wg, st, mn)


def adam_columns(own, oth, at, wide, m1, m2, prev, inv_root, first_row, rows, places):
    count = own.shape[0]
    nb = 2 * wide // 128
    blk = rows * nb
    assert first_row % blk == 0
    base = first_row // blk
    half = pl.BlockSpec((rows, wide), lambda i: (i, at))
    flat = pl.BlockSpec((blk, 128), lambda i: (base + i, 0))
    kernel = functools.partial(adam_kernel, (rows, nb, places), inv_root)
    return adam_call(kernel, (count // rows,), own, oth, m1, m2, prev, half, flat, blk, "adam")


def adam_call(kernel, grid, own, oth, m1, m2, prev, half, flat, blk, name):
    return pl.pallas_call(
        kernel,
        grid=grid,
        out_shape=[sds(m1.shape, f32)] * 3,
        in_specs=[half, half, flat, flat] + [ANY] * len(prev),
        out_specs=[flat] * 3,
        scratch_shapes=[pltpu.VMEM((blk, 128), f32)],
        input_output_aliases={4 + i: i for i in range(len(prev))},
        compiler_params=params(),
        cost_estimate=cost(0, own.size * 2 * 22),
        name=name,
    )(own, oth, m1, m2, *prev)


def adam_rows_kernel(inv_root, own, oth, m1, m2, *refs):
    wg, st, mn, flat = refs[-4:]
    g = pick(pl.program_id(0) == lax.axis_index("core"), own[...], oth[...]).astype(f32) * inv_root
    rows, width = g.shape
    nb = width // 128
    for w in range(nb):
        flat[pl.ds(w, rows, stride=nb), :] = g[:, w * 128 : (w + 1) * 128]
    adam_update(flat[...], m1, m2, wg, st, mn)


def adam_rows_halves(own, oth, m1, m2, prev, inv_root, first_row):
    count, width = own.shape
    rows = count // 4
    blk = rows * width // 128
    base = first_row // blk
    half = pl.BlockSpec((rows, width), lambda h, i: (i, 0))
    flat = pl.BlockSpec((blk, 128), lambda h, i: (base + h * 4 + i, 0))
    kernel = functools.partial(adam_rows_kernel, inv_root)
    return adam_call(kernel, (2, 4), own, oth, m1, m2, prev, half, flat, blk, "adam_rows")


def adam_tail_kernel(g, m1, m2, p1, p2, p3, wg, st, mn):
    adam_update(g[...], m1, m2, wg, st, mn)


def adam_tail(g, m1, m2, prev, first_row):
    rows = 8
    assert first_row % rows == 0 and g.shape[0] <= rows
    g = jnp.pad(g, ((0, rows - g.shape[0]), (0, 0)))
    flat = pl.BlockSpec((rows, 128), lambda i: (first_row // rows, 0))
    return pl.pallas_call(
        adam_tail_kernel,
        grid=(1,),
        out_shape=[sds(m1.shape, f32)] * 3,
        in_specs=[pl.BlockSpec((rows, 128), lambda i: (0, 0)), flat, flat] + [ANY] * 3,
        out_specs=[flat] * 3,
        input_output_aliases={3: 0, 4: 1, 5: 2},
        name="adam_norms",
    )(g, m1, m2, *prev)


def after(x, *deps):
    return lax.optimization_barrier((x, deps))[0]


def body(n, nz, tokens, cotangent, doc_ids, master, moment_one, moment_two):
    t, d = tokens.shape
    ff = (master.shape[0] * n - 4 * d) // (2 * d) - 2 * d
    me = lax.axis_index(("y", "x"))
    rows = d // n
    comm = n == 4

    lanes = master.reshape(-1, 128)
    w, o, norm_share = unpack_first(lanes, n, d, ff)
    doc_row = doc_ids.reshape(1, t)
    doc_col = doc_ids.reshape(t, 1)
    d_out = jnp.where(doc_col >= 0, cotangent, jnp.zeros((), bf16))
    if not comm:
        w, o = spread(w), spread(o)
        norm_share = lax.all_gather(master[-(4 * d // n) :].astype(bf16), ("y", "x"), axis=0, tiled=True)
        norm_share = norm_share.astype(f32).reshape(-1, 128)
    a_one, qkv, in_own, bk_own, w_own, w_oth, o_own, o_oth, norms = project_qkv(lanes, tokens, norm_share, w, o, n, ff, comm)
    att, lse, in_own, in_oth, a_one_p, d_out_p = attend(qkv, doc_row, doc_col, in_own, a_one, d_out, d, comm)
    resid, a_two, hidden, slope, bk_own, bk_oth, hid_p, att_p = middle(
        att, tokens, norms, o_own, o_oth, in_own, in_oth, bk_own, comm
    )
    scatter = lambda g: lax.psum_scatter(g, ("y", "x"), scatter_dimension=0, tiled=True)
    g_back = pair_grad(hidden, ff // 2, hid_p, [d_out], d, d_out_p, "grad_back")
    grad_back = scatter(g_back)
    d_pre, dp_p, a_two_p = pre_grad(after(d_out, g_back), slope, bk_own, bk_oth, a_two, comm)
    g_in = pair_grad(a_two, d, a_two_p, [d_pre], ff // 2, dp_p, "grad_in")
    grad_in = scatter(g_in)
    d_resid, low, d_att, gain_two, bias_two, low_p = two_grad(
        after(d_pre, g_in), resid, d_out, norms, in_own, in_oth, o_own, o_oth, comm
    )
    deep = nz == 4
    dq, dk, dv, dqkv_p, red_back = attend_back(
        qkv, d_att, att, lse, doc_row, doc_col, grad_back, d, comm, deep
    )
    g_at = attention_grads(a_one, a_one_p, [dq, dk, dv], dqkv_p, att, att_p, low, low_p)
    two_norm = jnp.concatenate([gain_two, bias_two]).reshape(-1, 128)
    full = comm and deep
    input_grad, mixed, red_in, red_in_p, red_at, red_at_p, sums = last_grad(
        [after(dq, g_at), dk, dv], tokens, d_resid, norms, hidden, resid, doc_col, two_norm, w_own, w_oth, bk_own, bk_oth,
        grad_in, g_at, full,
    )
    if not full:
        red_in, red_in_p = both_halves(grad_in, None, None, False)
        red_at, red_at_p = both_halves(scatter(g_at), None, None, False)
        sums = lax.psum(sums, ("z", "core", "y", "x"))

    inv_root = float(t * n * nz * 2) ** (-0.5)
    m1, m2 = moment_one.reshape(-1, 128), moment_two.reshape(-1, 128)
    nb = d // 128
    half = nb // 2
    hs = ff // n // 2
    r_qkv, r_out, r_in = rows * 3 * nb, rows * nb, rows * ff // 128
    back_at = r_qkv + r_out + r_in
    outs = adam_rows_halves(*red_back, m1, m2, [], inv_root, back_at)
    places = [(hs * j + q * 128, (2 * hs * j) // 128 + q, (2 * hs * j + hs) // 128 + q) for j in range(n) for q in range(hs // 128)]
    outs = adam_columns(red_in, red_in_p, 0, ff // 2, m1, m2, outs, inv_root, r_qkv + r_out, rows // 8, places)
    places = [((p * half + w) * 128, p * nb + w, p * nb + w + half) for p in range(3) for w in range(half)]
    outs = adam_columns(red_at, red_at_p, 0, 3 * d // 2, m1, m2, outs, inv_root, 0, rows // 8, places)
    places = [(w * 128, w, w + half) for w in range(half)]
    outs = adam_columns(red_at, red_at_p, 3, d // 2, m1, m2, outs, inv_root, r_qkv, rows // 2, places)
    per = 4 * nb // n
    norm_part = lax.dynamic_slice_in_dim(sums, group_index(n) * per, per, 0) * inv_root
    outs = adam_tail(norm_part, m1, m2, outs, back_at + ff // n * nb)
    weight_grad, step, moment = [o.reshape(-1) for o in outs]
    return mixed, input_grad, weight_grad, step, moment


def solution(mesh):
    dp, n = mesh.shape["dp"], mesh.shape["group"]
    fine = Mesh(mesh.devices.reshape(dp // 2, 2, n // 2, 2), ("z", "core", "y", "x"))
    tok = ("z", "core", "y", "x")
    flat = P(("y", "x"))
    in_specs = (P(tok, None), P(tok, None), P(tok), flat, flat, flat)
    out_specs = (P(tok, None), P(tok, None), flat, flat, flat)
    return jax.shard_map(
        functools.partial(body, n, dp // 2), mesh=fine, in_specs=in_specs, out_specs=out_specs, check_vma=False
    )
```

```python
import functools

import jax
import jax.numpy as jnp
from jax import lax
from jax.experimental import pallas as pl
from jax.experimental.pallas import tpu as pltpu
from jax.sharding import Mesh
from jax.sharding import PartitionSpec as P

HEADS = 16
EPS = 1e-05
FILL = -1e30
BETA_ONE = 0.9
BETA_TWO = 0.999
RATE = 0.001
ADAM_EPS = 1e-08
STEPS = 100.0
VMEM_MB = 60

f32 = jnp.float32
bf16 = jnp.bfloat16
ANY = pl.BlockSpec(memory_space=pl.ANY)


def params(limit=VMEM_MB):
    return pltpu.CompilerParams(vmem_limit_bytes=limit << 20)


def cost(flops, nbytes, trans=0):
    return pl.CostEstimate(flops=int(flops), bytes_accessed=int(nbytes), transcendentals=int(trans))


def sds(shape, dtype):
    return jax.ShapeDtypeStruct(shape, dtype)


def dot_nn(a, b):
    return jnp.dot(a, b, preferred_element_type=f32)


def dot_nt(a, b):
    return lax.dot_general(a, b, (((1,), (1,)), ((), ())), preferred_element_type=f32)


def dot_tn(a, b):
    return lax.dot_general(a, b, (((0,), (0,)), ((), ())), preferred_element_type=f32)


def pick(flag, a, b):
    return jnp.where(flag, a, b)


MESH = pl.DeviceIdType.MESH


def peer(*axes):
    return {a: 1 - lax.axis_index(a) for a in axes}


def greet(peers):
    barrier = pltpu.get_barrier_semaphore()
    for p in peers:
        pl.semaphore_signal(barrier, inc=1, device_id=p, device_id_type=MESH)
    pl.semaphore_wait(barrier, len(peers))


def member():
    return lax.axis_index("y") * 2 + lax.axis_index("x")


class Gather:
    COUNT = 11

    def __init__(self, own, oth, send, recv, base):
        rows = own.shape[0] // 4
        half = rows // 2
        x, y = lax.axis_index("x"), lax.axis_index("y")
        share = [y * 2 + x, y * 2 + 1 - x, (1 - y) * 2 + x, (1 - y) * 2 + 1 - x]
        self.rows = [pl.ds(pl.multiple_of(k * rows, 8), rows) for k in share]

        def move(i, k, off, count, dst, to):
            at = pl.ds(pl.multiple_of(share[k] * rows + off, 8), count)
            return pltpu.make_async_remote_copy(
                src_ref=own.at[at, :], dst_ref=dst.at[at, :],
                send_sem=send.at[base + i], recv_sem=recv.at[base + i], device_id=peer(to), device_id_type=MESH,
            )

        self.moves = [
            move(0, 0, 0, half, own, "x"),
            move(1, 0, half, half, own, "x"),
            move(2, 0, half, half, own, "y"),
            move(3, 0, 0, half, own, "y"),
            move(4, 0, 0, rows, oth, "core"),
            move(5, 1, 0, half, own, "y"),
            move(6, 2, half, half, own, "x"),
            move(7, 1, 0, rows, oth, "core"),
            move(8, 2, 0, rows, oth, "core"),
            move(9, 3, 0, half, oth, "core"),
            move(10, 3, half, half, oth, "core"),
        ]

    def begin(self):
        for i in (0, 2, 1, 3, 4):
            self.moves[i].start()

    def relay(self):
        self.moves[0].wait_recv()
        self.moves[5].start()
        self.moves[2].wait_recv()
        self.moves[6].start()

    def forward(self):
        self.moves[1].wait_recv()
        self.moves[7].start()
        self.moves[3].wait_recv()
        self.moves[8].start()

    def close(self):
        self.moves[5].wait_recv()
        self.moves[9].start()
        self.moves[6].wait_recv()
        self.moves[10].start()

    def arrive(self, *which):
        for i in which:
            self.moves[i].wait_recv()

    def sent(self):
        for m in self.moves:
            m.wait_send()

    def finish(self):
        self.close()
        self.arrive(4, 7, 8, 9, 10)
        self.sent()


def hand_over(src, dst, send, recv):
    return pltpu.make_async_remote_copy(
        src_ref=src, dst_ref=dst, send_sem=send, recv_sem=recv, device_id=peer("core"), device_id_type=MESH
    )


class Fold:
    def __init__(self, source, mine, inbox, cross, stage, total, red, theirs, keep, send, recv, base):
        self.pieces = len(mine)
        self.out = [pltpu.make_async_copy(total.at[s], red.at[s], keep.at[s]) for s in range(self.pieces)]
        z = lax.axis_index("z")
        self.end = (z == 0) | (z == 3)
        self.mid = (z == 1) | (z == 2)
        near, far = self.peers()
        self.mine, self.inbox, self.across, self.stage, self.total = mine, inbox, cross, stage, total

        def move(s, kind, src, dst, to):
            i = base + 4 * s + kind
            return pltpu.make_async_remote_copy(
                src_ref=src, dst_ref=dst, send_sem=send.at[i], recv_sem=recv.at[i], device_id=to, device_id_type=MESH
            )

        every = range(self.pieces)
        self.fold = [move(s, 0, source[s], inbox.at[s], near) for s in every]
        self.cross = [move(s, 1, stage.at[s], cross.at[s], far) for s in every]
        self.unfold = [move(s, 2, total.at[s], total.at[s], near) for s in every]
        self.core = [move(s, 3, total.at[s], theirs.at[s], peer("core")) for s in every]

    @staticmethod
    def peers():
        z = lax.axis_index("z")
        return [{"z": z + 1 - 2 * (z % 2)}, {"z": 3 - z}]

    def begin(self, s):
        pl.when(self.end)(self.fold[s].start)

    def inner(self, s):
        @pl.when(self.mid)
        def _():
            self.fold[s].wait_recv()
            both = self.mine[s][...].astype(f32) + self.inbox[s].astype(f32)
            self.stage[s] = both.astype(bf16)
            self.cross[s].start()

    def outer(self, s):
        @pl.when(self.mid)
        def _():
            self.cross[s].wait_recv()
            both = self.stage[s].astype(f32) + self.across[s].astype(f32)
            self.total[s] = both.astype(bf16)
            self.unfold[s].start()
            self.core[s].start()
            self.out[s].start()

    def land(self, s):
        @pl.when(self.end)
        def _():
            self.unfold[s].wait_recv()
            self.core[s].start()
            self.out[s].start()

    def finish(self):
        @pl.when(self.end)
        def _():
            for m in self.fold:
                m.wait_send()

        @pl.when(self.mid)
        def _():
            for m in self.cross + self.unfold:
                m.wait_send()

        for m in self.core + self.out:
            m.wait()


def row_pieces(ref, pieces):
    rows = ref.shape[0] // pieces
    return [ref.at[pl.ds(s * rows, rows), :] for s in range(pieces)]


def fold_scratch(rows, cols, pieces):
    return [pltpu.VMEM((pieces, rows // pieces, cols), bf16)] * 4


class Scatter:
    def __init__(self, held, far, near, mid, total, send, recv, base):
        pieces, rows, _ = held.shape
        block = rows // 4
        half = block // 2
        x, y = lax.axis_index("x"), lax.axis_index("y")
        me, over_x, over_y, both = y * 2 + x, y * 2 + 1 - x, (1 - y) * 2 + x, (1 - y) * 2 + 1 - x
        self.pieces, self.held, self.far, self.near, self.mid, self.total, self.half = pieces, held, far, near, mid, total, half

        def at(share, part):
            return pl.ds(pl.multiple_of(share * block + part * half, half), half)

        def move(i, src, dst, to):
            return pltpu.make_async_remote_copy(
                src_ref=src, dst_ref=dst, send_sem=send.at[base + i], recv_sem=recv.at[base + i],
                device_id=peer(to), device_id_type=MESH,
            )

        self.first, self.second = [], []
        for s in range(pieces):
            b = 6 * s
            self.first.append([
                move(b, held.at[s, at(over_x, 0), :], far.at[s, 0], "x"),
                move(b + 1, held.at[s, at(both, 0), :], far.at[s, 1], "x"),
                move(b + 2, held.at[s, at(over_y, 1), :], far.at[s, 2], "y"),
                move(b + 3, held.at[s, at(both, 1), :], far.at[s, 3], "y"),
            ])
            self.second.append([move(b + 4, mid.at[s, 1], near.at[s, 0], "y"), move(b + 5, mid.at[s, 3], near.at[s, 1], "x")])
        self.keep = [at(me, 0), at(over_y, 0), at(me, 1), at(over_x, 1)]

    def begin(self, s):
        for k in (1, 3, 0, 2):
            self.first[s][k].start()

    def turn(self, s):
        for k in (1, 3, 0, 2):
            self.first[s][k].wait_recv()
            both = self.held[s, self.keep[k], :].astype(f32) + self.far[s, k].astype(f32)
            self.mid[s, k] = both.astype(bf16)
            if k in (1, 3):
                self.second[s][k // 2].start()

    def close(self, s):
        for part in range(2):
            self.second[s][part].wait_recv()
            both = self.mid[s, 2 * part].astype(f32) + self.near[s, part].astype(f32)
            self.total[s, part * self.half : (part + 1) * self.half, :] = both.astype(bf16)

    def finish(self):
        for s in range(self.pieces):
            for m in self.first[s] + self.second[s]:
                m.wait_send()


def scatter_scratch(rows, cols, pieces):
    half = rows // 8
    four = pltpu.VMEM((pieces, 4, half, cols), bf16)
    return [pltpu.VMEM((pieces, rows, cols), bf16), four, pltpu.VMEM((pieces, 2, half, cols), bf16), four]


def swap_core(v):
    return lax.ppermute(v, "core", [(0, 1), (1, 0)])


def comm_params(cid, limit=VMEM_MB):
    if cid is None:
        return params(limit)
    return pltpu.CompilerParams(vmem_limit_bytes=limit << 20, collective_id=cid, has_side_effects=True)


def dma(count):
    return pltpu.SemaphoreType.DMA((count,))


def gain_row(norms, r, d):
    nb = d // 128
    return jnp.concatenate([norms[r * nb + i : r * nb + i + 1, :] for i in range(nb)], axis=1)


def layer_norm_parts(v):
    centre = v - jnp.mean(v, axis=-1, keepdims=True)
    r = lax.rsqrt(jnp.mean(centre * centre, axis=-1, keepdims=True) + EPS)
    return centre * r, r


def layer_norm_back(v, gain, dz):
    xhat, r = layer_norm_parts(v)
    dg = jnp.sum(dz * xhat, axis=0, keepdims=True)
    db = jnp.sum(dz, axis=0, keepdims=True)
    t = dz * gain
    dv = r * (t - jnp.mean(t, axis=-1, keepdims=True) - xhat * jnp.mean(t * xhat, axis=-1, keepdims=True))
    return dv, dg, db


def unpack_kernel(dims, m_qkv, m_out, m_norm, own_qkv, own_out, norm):
    n, d = dims
    core = lax.axis_index("core")
    nb = d // 128
    half = nb // 2
    rows = own_qkv.shape[0]

    def put(ref, own, dst, lo, stride):
        own[:, dst : dst + 128] = ref[pl.ds(lo + core * half, rows, stride=stride), :].astype(bf16)

    for part in range(3):
        for w in range(half):
            put(m_qkv, own_qkv, (part * half + w) * 128, part * nb + w, 3 * nb)
    for w in range(half):
        put(m_out, own_out, w * 128, w, nb)
    norm[...] = m_norm[...].astype(bf16).astype(f32)


def group_index(n):
    return lax.axis_index(("y", "x"))


def unpack_first(lanes, n, d, ff):
    rows = d // n
    nb = d // 128
    r1, r2, r3, r4 = rows * 3 * nb, rows * nb, rows * ff // 128, ff // n * nb
    steps = 4 if n == 4 else 2
    sr = rows // steps
    me = lambda: group_index(n)
    return pl.pallas_call(
        functools.partial(unpack_kernel, (n, d)),
        grid=(steps,),
        out_shape=[sds((d, 3 * d // 2), bf16), sds((d, d // 2), bf16), sds((8, 128), f32)],
        in_specs=[
            pl.BlockSpec((r1 // steps, 128), lambda i: (i, 0)),
            pl.BlockSpec((r2 // steps, 128), lambda i: (r1 // (r2 // steps) + i, 0)),
            pl.BlockSpec((8, 128), lambda i: ((r1 + r2 + r3 + r4) // 8, 0)),
        ],
        out_specs=[
            pl.BlockSpec((sr, 3 * d // 2), lambda i: (me() * steps + i, 0)),
            pl.BlockSpec((sr, d // 2), lambda i: (me() * steps + i, 0)),
            pl.BlockSpec((8, 128), lambda i: (0, 0)),
        ],
        compiler_params=params(),
        name="unpack",
    )(lanes, lanes, lanes)


UNPACK_STEPS = 8


def qkv_kernel(cfg, tok, norm_share, m_in, m_back, w_own_in, w_oth_in, o_own_in, o_oth_in, *refs):
    n, comm = cfg
    (a_out, qkv, own_in, own_bk, w_own, w_oth, o_own, o_oth, norms_out, norms, w, toks, acc, lsem, send, recv) = refs
    if not comm:
        w_own, w_oth = w_own_in, w_oth_in
    t, d = toks.shape
    step = pl.program_id(0)
    nb = d // 128
    half = 3 * d // 2
    share = d // n
    tm = min(256, t)
    tok_copy = pltpu.make_async_copy(tok, toks, lsem.at[0])

    if comm:
        me = member()
        near = [peer("x"), peer("y"), peer("x", "y")]
        mine = pl.ds(pl.multiple_of(me * 8, 8), 8)
        notes = [
            pltpu.make_async_remote_copy(
                src_ref=norm_share, dst_ref=norms.at[mine, :], send_sem=send.at[22 + i], recv_sem=recv.at[22 + i],
                device_id=p, device_id_type=MESH,
            )
            for i, p in enumerate(near)
        ]
        first = Gather(w_own, w_oth, send, recv, 0)
        second = Gather(o_own, o_oth, send, recv, 11)
        rows = first.rows
    else:
        rows = [pl.ds(k * share, share) for k in range(n)]

    @pl.when(step == 0)
    def _():
        tok_copy.start()
        if comm:
            greet(near + [peer("core")])
            for m in notes:
                m.start()
            first.begin()
            norms[mine, :] = norm_share[...]

    @pl.when(step < UNPACK_STEPS)
    def _():
        core = lax.axis_index("core")
        rows_in = own_in.shape[0]
        hs = own_in.shape[1] // n
        stride = m_in.shape[0] // rows_in
        for j in range(n):
            for q in range(hs // 128):
                lo = (2 * hs * j) // 128 + q + core * (hs // 128)
                at = hs * j + q * 128
                own_in[:, at : at + 128] = m_in[pl.ds(lo, rows_in, stride=stride), :].astype(bf16)
        for q in range(nb):
            own_bk[:, q * 128 : (q + 1) * 128] = m_back[pl.ds(q, own_bk.shape[0], stride=nb), :].astype(bf16)

    def load(*which):
        cps = []
        for k in which:
            cps.append(pltpu.make_async_copy(w_own.at[rows[k], :], w.at[k, :, pl.ds(0, half)], lsem.at[1 + 2 * k]))
            cps.append(pltpu.make_async_copy(w_oth.at[rows[k], :], w.at[k, :, pl.ds(half, half)], lsem.at[2 + 2 * k]))
        for cp in cps:
            cp.start()
        for cp in cps:
            cp.wait()

    def product(at, *which):
        return sum(dot_nn(a_out[at, cols_of(k)], w[k]) for k in which)

    def cols_of(k):
        if comm:
            return rows[k]
        return slice(k * share, (k + 1) * share)

    def each_block(fn):
        @pl.loop(0, t // tm)
        def _(i):
            fn(pl.ds(pl.multiple_of(i * tm, tm), tm))

    @pl.when(step == UNPACK_STEPS)
    def _():
        if comm:
            for m in notes:
                m.wait()
            first.relay()
            second.begin()
        else:
            norms[...] = norm_share[...]
        norms_out[...] = norms[...]
        tok_copy.wait()
        gain, bias = gain_row(norms, 0, d), gain_row(norms, 1, d)

        def norm(at):
            xhat, _ = layer_norm_parts(toks[at, :].astype(f32))
            a_out[at, :] = (xhat * gain + bias).astype(bf16)

        each_block(norm)
        if comm:
            first.arrive(4)
        load(0)

        def start(at):
            acc[at, :] = product(at, 0)

        each_block(start)

    @pl.when(step == UNPACK_STEPS + 1)
    def _():
        if comm:
            first.forward()
            first.arrive(7, 8)
        load(*range(1, n - 1))

        def more(at):
            acc[at, :] += product(at, *range(1, n - 1))

        each_block(more)

    @pl.when(step == UNPACK_STEPS + 2)
    def _():
        if comm:
            first.close()
            second.relay()
            first.arrive(9, 10)
        load(n - 1)
        scale = (d // HEADS) ** (-0.5)
        q = d // 2

        def last(at):
            total = acc[at, :] + product(at, n - 1)
            for o in (0, half):
                qkv[at, o : o + q] = (total[:, o : o + q].astype(bf16).astype(f32) * scale).astype(bf16)
                qkv[at, o + q : o + half] = total[:, o + q : o + half].astype(bf16)

        each_block(last)
        if comm:
            second.forward()
            second.finish()
            first.sent()


def project_qkv(lanes, tok, norm_share, w, o, n, ff, comm):
    t, d = tok.shape
    rows = d // n
    nb = d // 128
    hs = ff // n // 2
    r_in, r_bk = rows * ff // 128, ff // n * nb
    at_in, at_bk = rows * 4 * nb, rows * 4 * nb + r_in
    b_in, b_bk = r_in // UNPACK_STEPS, hs * nb // UNPACK_STEPS
    assert at_in % b_in == 0 and at_bk % b_bk == 0
    up = lambda i: jnp.minimum(i, UNPACK_STEPS - 1)
    me = lambda: group_index(n)
    whole = lambda s: pl.BlockSpec(s, lambda i: (0, 0))
    half = 3 * d // 2
    shapes = [sds((t, d), bf16), sds((t, 3 * d), bf16), sds((d, ff // 2), bf16), sds((ff // 2, d), bf16),
              sds((d, half), bf16), sds((d, half), bf16), sds((d, d // 2), bf16), sds((d, d // 2), bf16), sds((4 * nb, 128), f32)]
    w_args = [w, norm_share, o, norm_share] if comm else [w[0], w[1], o[0], o[1]]
    outs = pl.pallas_call(
        functools.partial(qkv_kernel, (n, comm)),
        grid=(UNPACK_STEPS + 3,),
        out_shape=shapes,
        in_specs=[
            ANY, whole(norm_share.shape),
            pl.BlockSpec((b_in, 128), lambda i: (at_in // b_in + up(i), 0)),
            pl.BlockSpec((b_bk, 128), lambda i: (at_bk // b_bk + lax.axis_index("core") * UNPACK_STEPS + up(i), 0)),
            ANY, ANY, ANY, ANY,
        ],
        out_specs=[
            whole((t, d)), whole((t, 3 * d)),
            pl.BlockSpec((rows // UNPACK_STEPS, ff // 2), lambda i: (me() * UNPACK_STEPS + up(i), 0)),
            pl.BlockSpec((hs // UNPACK_STEPS, d), lambda i: (me() * UNPACK_STEPS + up(i), 0)),
            ANY, ANY, ANY, ANY, whole((4 * nb, 128)),
        ],
        scratch_shapes=[pltpu.VMEM((4 * nb, 128), f32), pltpu.VMEM((n, rows, 3 * d), bf16), pltpu.VMEM((t, d), bf16),
                        pltpu.VMEM((t, 3 * d), f32), dma(1 + 2 * n), dma(25), dma(25)],
        input_output_aliases={4: 4, 6: 6},
        compiler_params=comm_params(1 if comm else None),
        cost_estimate=cost(2 * t * d * 3 * d, 40e6),
        name="qkv",
    )(tok, norm_share, lanes, lanes, *w_args)
    if comm:
        return outs
    return [*outs[:4], w[0], w[1], o[0], o[1], outs[8]]


QB = 256


def fill_bias(bias, doc_row, doc_col):
    t = bias.shape[0]
    for r in range(0, t, QB):
        key = r + lax.broadcasted_iota(jnp.int32, (QB, t), 0)
        query = lax.broadcasted_iota(jnp.int32, (QB, t), 1)
        ok = (doc_col[r : r + QB, :] == doc_row[...]) & (key <= query)
        bias[r : r + QB, :] = jnp.where(ok, 0.0, FILL)


def head_lanes(v, h, hd):
    lane = lax.broadcasted_iota(jnp.int32, v.shape, 1)
    return jnp.where((lane >= h * hd) & (lane < (h + 1) * hd), v, jnp.zeros_like(v))


def attend_kernel(cfg, q, k, v, doc_row, doc_col, w_own_in, a_one, d_out, out, lse, w_own, w_oth, a_p, d_p, bias, send, recv):
    hd, comm = cfg
    step = pl.program_id(0)
    last = pl.num_programs(0) - 1
    if comm:
        gather = Gather(w_own, w_oth, send, recv, 0)
        swaps = [hand_over(a_one, a_p, send.at[11], recv.at[11]), hand_over(d_out, d_p, send.at[12], recv.at[12])]

        @pl.when(step == 0)
        def _():
            greet([peer("x"), peer("y"), peer("core")])
            gather.begin()
            for s in swaps:
                s.start()

        @pl.when(step == 4)
        def _():
            gather.relay()

        @pl.when(step == 6)
        def _():
            gather.forward()

    @pl.when(step == 0)
    def _():
        fill_bias(bias, doc_row, doc_col)

    t = q.shape[0]
    vt = v[...].T
    per = 128 // hd
    qs = [head_lanes(q[...], h, hd) for h in range(per)]
    for i in range(t // QB):
        n = (i + 1) * QB
        cols = slice(i * QB, n)
        outs = []
        for h in range(per):
            s = dot_nt(k[:n, :], qs[h][cols, :]) + bias[:n, cols]
            top = jnp.max(s, axis=0, keepdims=True)
            e = jnp.exp(s - top)
            total = jnp.sum(e, axis=0, keepdims=True)
            lse[0, h : h + 1, cols] = top + jnp.log(total)
            o = dot_nn(vt[h * hd : (h + 1) * hd, :n], e.astype(bf16))
            outs.append(o * (1.0 / total))
        out[cols, :] = jnp.concatenate(outs, axis=0).T.astype(bf16)

    if comm:

        @pl.when(step == last)
        def _():
            gather.finish()
            for s in swaps:
                s.wait()


def head_column(d, part):
    pairs = d // 256
    return lambda p: (0, (p // pairs) * 3 * pairs + part * pairs + p % pairs)


def attend(qkv, doc_row, doc_col, w_own, a_one, d_out, d, comm):
    t = qkv.shape[0]
    pairs = d // 128
    hd = d // HEADS
    per = 128 // hd
    col = lambda part: pl.BlockSpec((t, 128), head_column(d, part))
    outs = pl.pallas_call(
        functools.partial(attend_kernel, (hd, comm)),
        grid=(pairs,),
        out_shape=[sds((t, d), bf16), sds((pairs, per, t), f32), sds(w_own.shape, bf16), sds(w_own.shape, bf16),
                   sds((t, d), bf16), sds((t, d), bf16)],
        in_specs=[col(0), col(1), col(2), pl.BlockSpec((1, t), lambda p: (0, 0)), pl.BlockSpec((t, 1), lambda p: (0, 0)),
                  ANY, ANY, ANY],
        out_specs=[pl.BlockSpec((t, 128), lambda p: (0, p)), pl.BlockSpec((1, per, t), lambda p: (p, 0, 0)), ANY, ANY, ANY, ANY],
        scratch_shapes=[pltpu.VMEM((t, t), f32), dma(13), dma(13)],
        input_output_aliases={5: 2},
        compiler_params=comm_params(2 if comm else None),
        cost_estimate=cost(8 * t * t * d, 10e6, t * t * HEADS),
        name="attend",
    )(qkv, qkv, qkv, doc_row, doc_col, w_own, a_one, d_out)
    if comm:
        return outs
    full, oth = spread(w_own)
    return outs[0], outs[1], full, oth, swap_core(a_one), swap_core(d_out)


def spread(own):
    n = lax.axis_size("y") * lax.axis_size("x")
    rows = own.shape[0] // n
    mine = lax.dynamic_slice_in_dim(own, lax.axis_index(("y", "x")) * rows, rows, 0)
    full = lax.all_gather(mine, ("y", "x"), axis=0, tiled=True)
    return full, swap_core(full)


def attend_back_kernel(cfg, q, k, v, dout, att, lse, doc_row, doc_col, part_sum, dq, dk, dv, sent, red, red_p, *refs):
    hd, comm, deep = cfg
    bias, dk_acc, dv_acc, stage, lsem, send, recv = refs[:7]
    step = pl.program_id(0)
    pairs = stage.shape[0] // 3

    def hand(p, part):
        wide = 128 * pairs
        cols = pl.ds(pl.multiple_of(part * wide + p * 128, 128), 128)
        i = p * 3 + part
        return hand_over(stage.at[i], sent.at[:, cols], send.at[i], recv.at[i])

    if comm:

        if deep:
            fold = Fold(
                row_pieces(part_sum, PIECES), row_pieces(refs[7], PIECES), *refs[8:12], red, red_p, refs[12], send, recv, 3 * pairs
            )
            acts = (fold.inner, fold.outer, fold.land)

        @pl.when(step == 0)
        def _():
            greet([peer("core")] + (Fold.peers() if deep else []))
            if deep:
                load = pltpu.make_async_copy(part_sum, refs[7], lsem.at[0])
                load.start()
                for s in range(PIECES):
                    fold.begin(s)
                load.wait()

        @pl.when((step > 0) & (step <= pairs))
        def _():
            for part in range(3):
                hand(step - 1, part).start()

    @pl.when(step == 0)
    def _():
        fill_bias(bias, doc_row, doc_col)

    if comm and deep:
        for at, codes in enumerate(BACK_PLAN[:-1]):
            if codes:
                pl.when(step == at)(functools.partial(run_plan, acts, codes))

    t = q.shape[0]
    per = 128 // hd
    scale = hd ** (-0.5)
    kt = k[...].T
    prod = (dout[...].astype(f32) * att[...].astype(f32)).T
    inner = [jnp.sum(prod[h * hd : (h + 1) * hd, :], axis=0, keepdims=True) for h in range(per)]
    qs = [head_lanes(q[...], h, hd) for h in range(per)]
    ds_ = [head_lanes(dout[...], h, hd) for h in range(per)]
    dk_acc[...] = jnp.zeros_like(dk_acc)
    dv_acc[...] = jnp.zeros_like(dv_acc)
    for i in range(t // QB):
        n = (i + 1) * QB
        cols = slice(i * QB, n)
        dqs = []
        for h in range(per):
            qh, dh = qs[h][cols, :], ds_[h][cols, :]
            s = dot_nt(k[:n, :], qh) + bias[:n, cols]
            p = jnp.exp(s - lse[0, h : h + 1, cols])
            dp = dot_nt(v[:n, :], dh)
            g = (p * (dp - inner[h][:, cols])).astype(bf16)
            dv_acc[:n, :] += dot_nn(p.astype(bf16), dh)
            dk_acc[:n, :] += dot_nn(g, qh)
            dqs.append(dot_nn(kt[h * hd : (h + 1) * hd, :n], g))
        dq[cols, :] = (jnp.concatenate(dqs, axis=0).T * scale).astype(bf16)
    dk[...] = dk_acc[...].astype(bf16)
    dv[...] = dv_acc[...].astype(bf16)

    if comm:

        @pl.when(step < pairs)
        def _():
            stage[step * 3] = dq[...]
            stage[step * 3 + 1] = dk[...]
            stage[step * 3 + 2] = dv[...]

        @pl.when(step == 2 * pairs - 1)
        def _():
            for p in range(pairs):
                for part in range(3):
                    hand(p, part).wait()
            if deep:
                run_plan(acts, BACK_PLAN[-1])
                fold.finish()


def run_plan(acts, codes):
    for code in codes:
        acts[code // 10](code % 10)


BACK_PLAN = (
    (),
    (0,),
    (1, 10, 2),
    (3, 11),
    (4, 5, 12, 13, 20),
    (6, 7, 14, 21),
    (15, 16, 22),
    (17, 23),
    (24, 25, 26, 27),
)
LAST_PLAN = (
    (),
    (0,),
    (1,),
    (30,),
    (10, 2, 31),
    (11, 3, 32, 40),
    (20, 33, 41),
    (12, 4, 34, 42),
    (21, 35, 43, 50),
    (13, 5, 22, 36, 44, 45, 37, 51),
    (14, 6, 23, 60, 46, 52, 53),
    (15, 7, 24, 61, 62, 70, 47, 54),
    (16, 25, 63, 64, 71, 55),
    (17, 26, 65, 72, 73, 66, 56, 90),
    (27, 67, 74, 75, 80, 91),
    (76, 81, 57, 92),
    (77, 93, 82, 94, 83, 95, 84, 85, 86, 87),
)
PIECES = 8


def attend_back(qkv, dout, att, lse, doc_row, doc_col, part_sum, d, comm, deep):
    t = qkv.shape[0]
    pairs = d // 128
    half = pairs // 2
    hd = d // HEADS
    per = 128 // hd
    turn = lambda p: (p + half) % pairs
    pieced = (PIECES, part_sum.shape[0] // PIECES, part_sum.shape[1])
    col = lambda part: pl.BlockSpec((t, 128), lambda p: head_column(d, part)(turn(p)))
    one = pl.BlockSpec((t, 128), lambda p: (0, turn(p)))
    outs = pl.pallas_call(
        functools.partial(attend_back_kernel, (hd, comm, deep)),
        grid=(pairs,),
        out_shape=[sds((t, d), bf16)] * 3 + [sds((t, 3 * d // 2), bf16)] + [sds(pieced, bf16)] * 2,
        in_specs=[col(0), col(1), col(2), one, one, pl.BlockSpec((1, per, t), lambda p: (turn(p), 0, 0)),
                  pl.BlockSpec((1, t), lambda p: (0, 0)), pl.BlockSpec((t, 1), lambda p: (0, 0)), ANY],
        out_specs=[one, one, one, ANY, ANY, ANY],
        scratch_shapes=[pltpu.VMEM((t, t), f32), pltpu.VMEM((t, 128), f32), pltpu.VMEM((t, 128), f32),
                        pltpu.VMEM((3 * half, t, 128), bf16), dma(2), dma(3 * half + 4 * PIECES), dma(3 * half + 4 * PIECES)]
        + ([pltpu.VMEM(part_sum.shape, bf16)] + fold_scratch(*part_sum.shape, PIECES) + [dma(PIECES)] if deep else []),
        compiler_params=comm_params(6 if comm else None),
        cost_estimate=cost(20 * t * t * d, 16e6, t * t * HEADS),
        name="attend_back",
    )(qkv, qkv, qkv, dout, att, lse, doc_row, doc_col, part_sum)
    sent = outs[3] if comm else swap_core(jnp.concatenate([g[:, d // 2 :] for g in outs[:3]], axis=1))
    return outs[0], outs[1], outs[2], sent, both_halves(part_sum, outs[4], outs[5], comm and deep)


def both_halves(part_sum, red, red_p, done):
    if done:
        return red.reshape(part_sum.shape), red_p.reshape(part_sum.shape)
    full = lax.psum(part_sum.astype(f32), "z").astype(bf16)
    return full, swap_core(full)


def middle_kernel(cfg, att_rows, tok, norms, o_own, o_oth, w_own, w_oth, att_all, bk_own_in, *refs):
    d, tm, blk, comm = cfg
    (resid, a_two_out, hidden, slope, bk_own, bk_oth, hid_p, att_p, w, a_two, stage, lsem, send, recv) = refs
    step = pl.program_id(0)
    last = pl.num_programs(0) - 1
    t = a_two.shape[0]
    pro = t // tm
    half = d // 2
    wide = hid_p.shape[1]
    nb = wide // blk
    core = lax.axis_index("core")

    def hand(j):
        cols = pl.ds(pl.multiple_of(j * blk, blk), blk)
        return hand_over(stage.at[j], hid_p.at[:, cols], send.at[12 + j], recv.at[12 + j])

    if comm:
        gather = Gather(bk_own, bk_oth, send, recv, 0)
        swap = hand_over(att_all, att_p, send.at[11], recv.at[11])

        @pl.when(step == 0)
        def _():
            greet([peer("x"), peer("y"), peer("core")])
            gather.begin()
            swap.start()

        @pl.when(step == pro + 4)
        def _():
            gather.relay()

        @pl.when((step > pro) & (step <= pro + nb))
        def _():
            hand(step - pro - 1).start()

    @pl.when(step == 0)
    def _():
        lo = pl.multiple_of(core * half, half)
        hi = pl.multiple_of((1 - core) * half, half)
        cps = [
            pltpu.make_async_copy(o_own, w.at[:, pl.ds(lo, half)], lsem.at[0]),
            pltpu.make_async_copy(o_oth, w.at[:, pl.ds(hi, half)], lsem.at[1]),
        ]
        for cp in cps:
            cp.start()
        for cp in cps:
            cp.wait()

    @pl.when(step < pro)
    def _():
        lo = pl.multiple_of(core * half, half)
        hi = pl.multiple_of((1 - core) * half, half)
        y = dot_nn(att_rows[:, :half], w[pl.ds(lo, half), :]) + dot_nn(att_rows[:, half:], w[pl.ds(hi, half), :])
        r = tok[...].astype(f32) + y
        resid[...] = r
        xhat, _ = layer_norm_parts(r)
        a = (xhat * gain_row(norms, 2, d) + gain_row(norms, 3, d)).astype(bf16)
        a_two_out[...] = a
        a_two[pl.ds(pl.multiple_of(step * tm, tm), tm), :] = a

    def unit(w_blk):
        pre = dot_nn(a_two[...], w_blk)
        cdf = 0.5 + 0.5 * lax.erf(pre * (0.5**0.5))
        pdf = jnp.exp(-0.5 * pre * pre) * 0.3989422804014327
        h = (pre * cdf).astype(bf16)
        hidden[...] = h
        slope[...] = (cdf + pre * pdf).astype(bf16)
        return h

    @pl.when((step >= pro) & (step < pro + nb))
    def _():
        h = unit(w_oth[...])
        if comm:
            stage[step - pro] = h

    @pl.when(step >= pro + nb)
    def _():
        unit(w_own[...])

    if comm:

        @pl.when(step == last)
        def _():
            gather.forward()
            gather.finish()
            swap.wait()
            for j in range(nb):
                hand(j).wait()


def middle(att, tok, norms, o_own, o_oth, w_own, w_oth, bk_own, comm, tm=256, blk=512):
    t, d = tok.shape
    wide = w_own.shape[1]
    pro, nb = t // tm, wide // blk
    rowi = lambda i: jnp.minimum(i, pro - 1)
    oth = lambda i: jnp.clip(i - pro, 0, nb - 1)
    own = lambda i: jnp.clip(i - pro - nb, 0, nb - 1)
    both = lambda i: jnp.where(i < pro + nb, nb + oth(i), own(i))
    rows = lambda wd: pl.BlockSpec((tm, wd), lambda i: (rowi(i), 0))
    outs = pl.pallas_call(
        functools.partial(middle_kernel, (d, tm, blk, comm)),
        grid=(pro + 2 * nb,),
        out_shape=[sds((t, d), f32), sds((t, d), bf16), sds((t, 2 * wide), bf16), sds((t, 2 * wide), bf16),
                   sds(bk_own.shape, bf16), sds(bk_own.shape, bf16), sds((t, wide), bf16), sds((t, d), bf16)],
        in_specs=[rows(d), rows(d), pl.BlockSpec(norms.shape, lambda i: (0, 0)), ANY, ANY,
                  pl.BlockSpec((d, blk), lambda i: (0, own(i))), pl.BlockSpec((d, blk), lambda i: (0, oth(i))), ANY, ANY],
        out_specs=[rows(d), rows(d), pl.BlockSpec((t, blk), lambda i: (0, both(i))), pl.BlockSpec((t, blk), lambda i: (0, both(i))),
                   ANY, ANY, ANY, ANY],
        scratch_shapes=[pltpu.VMEM((d, d), bf16), pltpu.VMEM((t, d), bf16), pltpu.VMEM((nb, t, blk), bf16), dma(2), dma(12 + nb), dma(12 + nb)],
        input_output_aliases={8: 4},
        compiler_params=comm_params(3 if comm else None),
        cost_estimate=cost(2 * t * d * d + 4 * t * d * wide, 44e6, 4 * t * wide),
        name="middle",
    )(att, tok, norms, o_own, o_oth, w_own, w_oth, att, bk_own)
    if comm:
        return outs
    full, other = spread(bk_own)
    return [*outs[:4], full, other, swap_core(outs[2][:, wide:]), swap_core(att)]


def pre_grad_kernel(comm, d_out, slope, w_own, w_oth, a_two, d_pre, sent, a_p, stage, send, recv):
    step = pl.program_id(0)
    nb = pl.num_programs(0) // 2
    blk = slope.shape[1]

    def hand(j):
        cols = pl.ds(pl.multiple_of(j * blk, blk), blk)
        return hand_over(stage.at[j], sent.at[:, cols], send.at[1 + j], recv.at[1 + j])

    if comm:
        swap = hand_over(a_two, a_p, send.at[0], recv.at[0])

        @pl.when(step == 0)
        def _():
            greet([peer("core")])
            swap.start()

        @pl.when((step > 0) & (step <= nb))
        def _():
            hand(step - 1).start()

    @pl.when(step < nb)
    def _():
        g = (dot_nt(d_out[...], w_oth[...]) * slope[...].astype(f32)).astype(bf16)
        d_pre[...] = g
        if comm:
            stage[step] = g

    @pl.when(step >= nb)
    def _():
        d_pre[...] = (dot_nt(d_out[...], w_own[...]) * slope[...].astype(f32)).astype(bf16)

    if comm:

        @pl.when(step == 2 * nb - 1)
        def _():
            swap.wait()
            for j in range(nb):
                hand(j).wait()


def pre_grad(d_out, slope, own, oth, a_two, comm, blk=512):
    t, d = d_out.shape
    half = own.shape[0]
    nb = half // blk
    col = pl.BlockSpec((t, blk), lambda i: (0, (i + nb) % (2 * nb)))
    outs = pl.pallas_call(
        functools.partial(pre_grad_kernel, comm),
        grid=(2 * nb,),
        out_shape=[sds((t, 2 * half), bf16), sds((t, half), bf16), sds((t, d), bf16)],
        in_specs=[pl.BlockSpec((t, d), lambda i: (0, 0)), col,
                  pl.BlockSpec((blk, d), lambda i: (jnp.maximum(i - nb, 0), 0)),
                  pl.BlockSpec((blk, d), lambda i: (jnp.minimum(i, nb - 1), 0)), ANY],
        out_specs=[col, ANY, ANY],
        scratch_shapes=[pltpu.VMEM((nb, t, blk), bf16), dma(1 + nb), dma(1 + nb)],
        compiler_params=comm_params(4 if comm else None),
        cost_estimate=cost(4 * t * d * half, 28e6),
        name="pre_grad",
    )(d_out, slope, own, oth, a_two)
    if comm:
        return outs
    return outs[0], swap_core(outs[0][:, half:]), swap_core(a_two)


def two_grad_kernel(comm, d_pre, resid, d_out, norms, w_own, w_oth, o_own, o_oth, *refs):
    d_resid, low, d_att, dg, db, sent, w, wo, stage, lsem, send, recv = refs
    step = pl.program_id(0)
    tm, d = resid.shape
    half = d // 2
    wide = w_own.shape[1]
    core = lax.axis_index("core")
    here = pl.ds(pl.multiple_of(step * tm, tm), tm)

    def hand():
        return hand_over(stage.at[here, :], sent.at[here, :], send.at[step], recv.at[step])

    @pl.when(step == 0)
    def _():
        if comm:
            greet([peer("core")])
        lo = pl.multiple_of(core * half, half)
        hi = pl.multiple_of((1 - core) * half, half)
        cps = [
            pltpu.make_async_copy(w_own, w.at[:, pl.ds(0, wide)], lsem.at[0]),
            pltpu.make_async_copy(w_oth, w.at[:, pl.ds(wide, wide)], lsem.at[1]),
            pltpu.make_async_copy(o_own, wo.at[:, pl.ds(lo, half)], lsem.at[2]),
            pltpu.make_async_copy(o_oth, wo.at[:, pl.ds(hi, half)], lsem.at[3]),
        ]
        for cp in cps:
            cp.start()
        for cp in cps:
            cp.wait()
        dg[...] = jnp.zeros_like(dg)
        db[...] = jnp.zeros_like(db)

    dz = dot_nt(d_pre[...], w[...])
    dv, g, b = layer_norm_back(resid[...], gain_row(norms, 2, d), dz)
    dg[...] += g
    db[...] += b
    dr = d_out[...].astype(f32) + dv
    d_resid[...] = dr
    dl = dr.astype(bf16)
    low[...] = dl
    stage[here, :] = pick(core == 0, dl[:, half:], dl[:, :half])
    lo = pl.multiple_of(core * half, half)
    hi = pl.multiple_of((1 - core) * half, half)
    d_att[:, :half] = dot_nt(dl, wo[pl.ds(lo, half), :]).astype(bf16)
    d_att[:, half:] = dot_nt(dl, wo[pl.ds(hi, half), :]).astype(bf16)
    if comm:
        hand().start()

        @pl.when(step == pl.num_programs(0) - 1)
        def _():
            for s in range(stage.shape[0] // tm):
                rows = pl.ds(s * tm, tm)
                hand_over(stage.at[rows, :], sent.at[rows, :], send.at[s], recv.at[s]).wait()


def two_grad(d_pre, resid, d_out, norms, w_own, w_oth, o_own, o_oth, comm, tm=256):
    t, wide = d_pre.shape
    d = resid.shape[1]
    blk = lambda w: pl.BlockSpec((tm, w), lambda i: (i, 0))
    row = pl.BlockSpec((1, d), lambda i: (0, 0))
    outs = pl.pallas_call(
        functools.partial(two_grad_kernel, comm),
        grid=(t // tm,),
        out_shape=[sds((t, d), f32), sds((t, d), bf16), sds((t, d), bf16), sds((1, d), f32), sds((1, d), f32), sds((t, d // 2), bf16)],
        in_specs=[blk(wide), blk(d), blk(d), pl.BlockSpec(norms.shape, lambda i: (0, 0)), ANY, ANY, ANY, ANY],
        out_specs=[blk(d), blk(d), blk(d), row, row, ANY],
        scratch_shapes=[pltpu.VMEM((d, wide), bf16), pltpu.VMEM((d, d), bf16), pltpu.VMEM((t, d // 2), bf16),
                        dma(4), dma(t // tm), dma(t // tm)],
        compiler_params=comm_params(5 if comm else None),
        cost_estimate=cost(2 * t * d * (wide + d), 34e6),
        name="two_grad",
    )(d_pre, resid, d_out, norms, w_own, w_oth, o_own, o_oth)
    if comm:
        return outs
    core = lax.axis_index("core")
    other = lax.dynamic_slice_in_dim(outs[1], (1 - core) * (d // 2), d // 2, 1)
    return [*outs[:5], swap_core(other)]


def last_kernel(cfg, g1, g2, g3, theirs, low, low_p, dq, dk, dv, tok, d_resid, norms, h_own, h_oth, resid, doc, two_norm,
                a_one, a_one_p, att, att_p, w_own, w_oth, b_own, b_oth, part_in, *refs):
    d, comm = cfg
    out, mixed, red_in, red_in_p, red_at, red_at_p, sums, w, wb, parts, held, lsem = refs[:12]
    step = pl.program_id(0)
    last = pl.num_programs(0) - 1
    np_ = held.shape[0]
    pro = (last - np_) // 2
    half = 3 * d // 2
    q = d // 2
    hb = b_own.shape[0]
    nb = d // 128
    core = lax.axis_index("core")
    early = [pltpu.make_async_copy(a, wb.at[pl.ds(i * d, d), :], lsem.at[i]) for i, a in enumerate((a_one, a_one_p, att, att_p))]
    mids = [
        pltpu.make_async_copy(w_own, w.at[:, pl.ds(0, half)], lsem.at[4]),
        pltpu.make_async_copy(w_oth, w.at[:, pl.ds(half, half)], lsem.at[5]),
    ]
    late = [
        pltpu.make_async_copy(b_own, wb.at[pl.ds(0, hb), :], lsem.at[6]),
        pltpu.make_async_copy(b_oth, wb.at[pl.ds(hb, hb), :], lsem.at[7]),
    ]
    if comm:
        send, recv, mine_in, fi, sc, fa, vec, box, k_in, k_at = (
            refs[12], refs[13], refs[14], refs[15:19], refs[19:22], refs[22:27], refs[27], refs[28], refs[29], refs[30]
        )
        fold_in = Fold(
            row_pieces(part_in, PIECES), row_pieces(mine_in, PIECES), *fi, red_in, red_in_p, k_in, send, recv, 0
        )
        scat = Scatter(held, *sc, fa[0], send, recv, 4 * PIECES)
        mine_at = [fa[0].at[s] for s in range(np_)]
        fold_at = Fold(mine_at, mine_at, *fa[1:5], red_at, red_at_p, k_at, send, recv, 4 * PIECES + 6 * np_)
        base = 4 * PIECES + 10 * np_

        def note(i, src, dst, to):
            return pltpu.make_async_remote_copy(
                src_ref=src, dst_ref=dst, send_sem=send.at[base + i], recv_sem=recv.at[base + i], device_id=to, device_id_type=MESH
            )

        near, far = Fold.peers()
        notes = [
            note(0, vec.at[0], box.at[0], peer("x")),
            note(1, vec.at[1], box.at[1], peer("y")),
            note(2, vec.at[2], box.at[2], peer("core")),
            note(3, vec.at[3], box.at[3], near),
            note(4, vec.at[4], box.at[4], far),
            note(5, vec.at[5], vec.at[5], near),
        ]

        def norm_sum(k):
            if k < 3:
                notes[k].wait_recv()
                vec[k + 1] = vec[k] + box[k]
                if k < 2:
                    notes[k + 1].start()
                else:
                    pl.when(fold_in.end)(notes[3].start)
            elif k < 5:

                @pl.when(fold_in.mid)
                def _():
                    notes[k].wait_recv()
                    vec[k + 1] = vec[k] + box[k]
                    notes[k + 1].start()

            else:
                pl.when(fold_in.end)(notes[5].wait_recv)

        def settle(s):
            scat.close(s)
            fold_at.begin(s)

        acts = (scat.begin, scat.turn, settle, fold_in.inner, fold_in.outer, fold_in.land, fold_at.inner, fold_at.outer,
                fold_at.land, norm_sum)

    @pl.when(step == 0)
    def _():
        for cp in early + mids:
            cp.start()
        if comm:
            load = pltpu.make_async_copy(part_in, mine_in, lsem.at[8])
            load.start()
            greet([peer("core"), peer("x"), peer("y")] + Fold.peers())
            for s in range(PIECES):
                fold_in.begin(s)
            load.wait()
        for cp in early:
            cp.wait()
        parts[0 : 2 * nb, :] = jnp.zeros((2 * nb, 128), f32)
        parts[2 * nb :, :] = two_norm[...]

    if comm:
        for k, codes in enumerate(LAST_PLAN[:-1]):
            if codes:
                pl.when(step == k)(functools.partial(run_plan, acts, codes))

    per = q // g1.shape[1]
    for k, g in enumerate((g1, g2, g3)):

        @pl.when((step >= k * per) & (step < (k + 1) * per))
        def _():
            acc = dot_tn(wb[0:d, :], g[...]) + dot_tn(wb[d : 2 * d, :], theirs[...])
            held[step] = acc.astype(bf16)

    @pl.when((step >= 3 * per) & (step < np_))
    def _():
        lo = pl.ds(pl.multiple_of(core * q, q), q)
        hi = pl.ds(pl.multiple_of((1 - core) * q, q), q)
        own = dot_tn(wb[2 * d : 3 * d, :q], low[...]) + dot_tn(wb[3 * d :, q:], low_p[...])
        held[step, lo, :] = own.astype(bf16)
        other = dot_tn(wb[2 * d : 3 * d, q:], low[...]) + dot_tn(wb[3 * d :, :q], low_p[...])
        held[step, hi, :] = other.astype(bf16)

    @pl.when(step == np_)
    def _():
        for cp in late:
            cp.start()
        for cp in mids:
            cp.wait()

    @pl.when((step >= np_) & (step < np_ + pro))
    def _():
        both = jnp.concatenate([g[:, :q] for g in (dq, dk, dv)] + [g[:, q:] for g in (dq, dk, dv)], axis=1)
        dz = dot_nt(both, w[...])
        grad, g, b = layer_norm_back(tok[...].astype(f32), gain_row(norms, 0, d), dz)
        parts[0:nb, :] += flat_row(g)
        parts[nb : 2 * nb, :] += flat_row(b)
        out[...] = (d_resid[...] + grad).astype(bf16)

    @pl.when(step == np_ + pro)
    def _():
        for cp in late:
            cp.wait()
        if comm:
            vec[0] = parts[...]
            notes[0].start()

    @pl.when((step >= np_ + pro) & (step < last))
    def _():
        y = dot_nn(h_own[...], wb[:hb, :]) + dot_nn(h_oth[...], wb[hb:, :]) + resid[...]
        mixed[...] = jnp.where(doc[...] >= 0, y, 0.0).astype(bf16)

    @pl.when(step == last)
    def _():
        if comm:
            run_plan(acts, LAST_PLAN[-1])
            fold_in.finish()
            scat.finish()
            fold_at.finish()
            for i in (0, 1, 2):
                notes[i].wait_send()
            pl.when(fold_in.end)(notes[3].wait_send)

            @pl.when(fold_in.mid)
            def _():
                notes[4].wait_send()
                notes[5].wait_send()

            sums[...] = vec[5]
        else:
            sums[...] = parts[...]
            cp = pltpu.make_async_copy(held, red_at, lsem.at[0])
            cp.start()
            cp.wait()


def flat_row(v):
    return jnp.concatenate([v[:, i * 128 : (i + 1) * 128] for i in range(v.shape[1] // 128)], axis=0)


def last_grad(grads3, theirs, low, low_p, tok, d_resid, norms, hidden, resid, doc_col, two_norm, a_one, a_one_p, att, att_p,
              own, oth, b_own, b_oth, part_in, n, comm, tm=256, wide=256):
    t, d = tok.shape
    pro = t // tm
    half = b_own.shape[0]
    q = d // 2
    per = q // wide
    np_ = 4 * per
    one = lambda w, c=0: pl.BlockSpec((tm, w), lambda i: (jnp.clip(i - np_, 0, pro - 1), c))
    two = lambda w, c=0: pl.BlockSpec((tm, w), lambda i: (jnp.clip(i - np_ - pro, 0, pro - 1), c))
    whole = lambda a: pl.BlockSpec(a.shape, lambda i: (0, 0))
    col = lambda k, count: pl.BlockSpec((t, wide), lambda i: (0, jnp.clip(i - k * per, 0, count - 1)))
    low_col = pl.BlockSpec((t, wide), lambda i: (0, lax.axis_index("core") * per + jnp.clip(i - 3 * per, 0, per - 1)))
    nv = 4 * d // 128
    pieced = (PIECES, part_in.shape[0] // PIECES, part_in.shape[1])
    share = (np_, d // n if comm else d, wide)
    slots = 4 * PIECES + 10 * np_ + 6
    extra = []
    if comm:
        extra = [dma(slots), dma(slots), pltpu.VMEM(part_in.shape, bf16)] + fold_scratch(*part_in.shape, PIECES)
        extra += scatter_scratch(d, wide, np_)[1:] + [pltpu.VMEM(share, bf16)] * 5
        extra += [pltpu.VMEM((6, nv, 128), f32), pltpu.VMEM((5, nv, 128), f32), dma(PIECES), dma(np_)]
    return pl.pallas_call(
        functools.partial(last_kernel, (d, comm)),
        grid=(np_ + 2 * pro + 1,),
        out_shape=[sds((t, d), bf16), sds((t, d), bf16)] + [sds(pieced, bf16)] * 2 + [sds(share, bf16)] * 2 + [sds((nv, 128), f32)],
        in_specs=[col(0, per), col(1, per), col(2, per), col(0, 3 * per), low_col, col(3, per)]
        + [one(d)] * 5 + [whole(norms), two(half), two(half, 1), two(d), two(1), whole(two_norm)] + [ANY] * 9,
        out_specs=[one(d), two(d), ANY, ANY, ANY, ANY, pl.BlockSpec((nv, 128), lambda i: (0, 0))],
        scratch_shapes=[pltpu.VMEM((d, 3 * d), bf16), pltpu.VMEM((4 * d, d), bf16), pltpu.VMEM((nv, 128), f32),
                        pltpu.VMEM((np_, d, wide), bf16), dma(9)] + extra,
        compiler_params=comm_params(7 if comm else None, 63),
        cost_estimate=cost(14 * t * d * d + 4 * t * d * half, 60e6),
        name="last_grad",
    )(*grads3, theirs, low, low_p, *grads3, tok, d_resid, norms, hidden, hidden, resid, doc_col, two_norm,
      a_one, a_one_p, att, att_p, own, oth, b_own, b_oth, part_in)


def pair_kernel(nb, a_mine, a_theirs, *refs):
    mine, theirs, out = refs[:nb], refs[nb], refs[nb + 1]
    wide = mine[0].shape[1]
    for j in range(nb):
        cols = slice(j * wide, (j + 1) * wide)
        acc = dot_tn(a_mine[...], mine[j][...]) + dot_tn(a_theirs[...], theirs[:, cols])
        out[:, cols] = acc.astype(bf16)


def pair_grad(a_mine, m, a_theirs, mine, wide, theirs, name, tm=256):
    t = a_mine.shape[0]
    nb = len(mine)
    a_spec = pl.BlockSpec((t, tm), lambda i: (0, i))
    b_spec = pl.BlockSpec((t, wide), lambda i: (0, 0))
    return pl.pallas_call(
        functools.partial(pair_kernel, nb),
        grid=(m // tm,),
        out_shape=sds((m, nb * wide), bf16),
        in_specs=[a_spec, a_spec] + [b_spec] * nb + [pl.BlockSpec((t, nb * wide), lambda i: (0, 0))],
        out_specs=pl.BlockSpec((tm, nb * wide), lambda i: (i, 0)),
        compiler_params=params(),
        cost_estimate=cost(4 * t * m * wide * nb, 14e6),
        name=name,
    )(a_mine, a_theirs, *mine, theirs)


def adam_update(g, m1, m2, wg, st, mn):
    first = BETA_ONE * m1[...] + (1.0 - BETA_ONE) * g
    second_hat = (BETA_TWO / (1.0 - BETA_TWO**STEPS)) * m2[...] + ((1.0 - BETA_TWO) / (1.0 - BETA_TWO**STEPS)) * g * g
    wg[...] = g
    st[...] = (-RATE / (1.0 - BETA_ONE**STEPS)) * first / (jnp.sqrt(second_hat) + ADAM_EPS)
    mn[...] = first


def adam_kernel(plan, inv_root, own, oth, m1, m2, *refs):
    wg, st, mn, flat = refs[-4:]
    rows, stride, places = plan
    first = lax.axis_index("core") == 0
    wide = own.shape[2]
    for col, lo, hi in places:
        p, c = col // wide, col % wide
        a = own[p, :, c : c + 128].astype(f32) * inv_root
        b = oth[p, :, c : c + 128].astype(f32) * inv_root
        flat[pl.ds(lo, rows, stride=stride), :] = pick(first, a, b)
        flat[pl.ds(hi, rows, stride=stride), :] = pick(first, b, a)
    adam_update(flat[...], m1, m2, wg, st, mn)


def adam_columns(own, oth, at, count, m1, m2, prev, inv_root, first_row, rows, places):
    total, wide = own.shape[1:]
    nb = 2 * count * wide // 128
    blk = rows * nb
    assert first_row % blk == 0
    base = first_row // blk
    half = pl.BlockSpec((count, rows, wide), lambda i: (at, i, 0))
    flat = pl.BlockSpec((blk, 128), lambda i: (base + i, 0))
    kernel = functools.partial(adam_kernel, (rows, nb, places), inv_root)
    return adam_call(kernel, (total // rows,), own, oth, m1, m2, prev, half, flat, blk, "adam")


def adam_call(kernel, grid, own, oth, m1, m2, prev, half, flat, blk, name):
    return pl.pallas_call(
        kernel,
        grid=grid,
        out_shape=[sds(m1.shape, f32)] * 3,
        in_specs=[half, half, flat, flat] + [ANY] * len(prev),
        out_specs=[flat] * 3,
        scratch_shapes=[pltpu.VMEM((blk, 128), f32)],
        input_output_aliases={4 + i: i for i in range(len(prev))},
        compiler_params=params(),
        cost_estimate=cost(0, own.size * 2 * 22),
        name=name,
    )(own, oth, m1, m2, *prev)


def adam_rows_kernel(inv_root, own, oth, m1, m2, *refs):
    wg, st, mn, flat = refs[-4:]
    g = pick(pl.program_id(0) == lax.axis_index("core"), own[...], oth[...]).astype(f32) * inv_root
    rows, width = g.shape
    nb = width // 128
    for w in range(nb):
        flat[pl.ds(w, rows, stride=nb), :] = g[:, w * 128 : (w + 1) * 128]
    adam_update(flat[...], m1, m2, wg, st, mn)


def adam_rows_halves(own, oth, m1, m2, prev, inv_root, first_row):
    count, width = own.shape
    rows = count // 4
    blk = rows * width // 128
    base = first_row // blk
    half = pl.BlockSpec((rows, width), lambda h, i: (i, 0))
    flat = pl.BlockSpec((blk, 128), lambda h, i: (base + h * 4 + i, 0))
    kernel = functools.partial(adam_rows_kernel, inv_root)
    return adam_call(kernel, (2, 4), own, oth, m1, m2, prev, half, flat, blk, "adam_rows")


def adam_tail_kernel(g, m1, m2, p1, p2, p3, wg, st, mn):
    adam_update(g[...], m1, m2, wg, st, mn)


def adam_tail(g, m1, m2, prev, first_row):
    rows = 8
    assert first_row % rows == 0 and g.shape[0] <= rows
    g = jnp.pad(g, ((0, rows - g.shape[0]), (0, 0)))
    flat = pl.BlockSpec((rows, 128), lambda i: (first_row // rows, 0))
    return pl.pallas_call(
        adam_tail_kernel,
        grid=(1,),
        out_shape=[sds(m1.shape, f32)] * 3,
        in_specs=[pl.BlockSpec((rows, 128), lambda i: (0, 0)), flat, flat] + [ANY] * 3,
        out_specs=[flat] * 3,
        input_output_aliases={3: 0, 4: 1, 5: 2},
        name="adam_norms",
    )(g, m1, m2, *prev)


BLOCK = 2048


def adam_all_kernel(cfg, b_own, b_oth, i_own, i_oth, a_own, a_oth, norm, m1, m2, wg, st, mn, flat, later):
    inv_root, at_in, at_at, counts = cfg
    step = pl.program_id(0)
    core = lax.axis_index("core")
    first = core == 0
    n_back, n_in, n_at = counts

    @pl.when(step < n_back)
    def _():
        g = pick(step // (n_back // 2) == core, b_own[...], b_oth[...]).astype(f32) * inv_root
        nb = g.shape[1] // 128
        for w in range(nb):
            flat[pl.ds(w, g.shape[0], stride=nb), :] = g[:, w * 128 : (w + 1) * 128]

    def spread_columns(dst, own, oth, places):
        rows = own.shape[0]
        for col, lo, hi, stride in places:
            a = own[:, col : col + 128].astype(f32) * inv_root
            b = oth[:, col : col + 128].astype(f32) * inv_root
            dst[pl.ds(lo, rows, stride=stride), :] = pick(first, a, b)
            dst[pl.ds(hi, rows, stride=stride), :] = pick(first, b, a)

    @pl.when((step >= n_back) & (step < n_back + n_in))
    def _():
        spread_columns(flat, i_own, i_oth, at_in)

    for p, places in enumerate(at_at):

        @pl.when(step == p)
        def _():
            spread_columns(later, a_own.at[0], a_oth.at[0], places)

    @pl.when((step >= n_back + n_in) & (step < n_back + n_in + n_at))
    def _():
        at = pl.multiple_of((step - n_back - n_in) * BLOCK, BLOCK)
        flat[...] = later[pl.ds(at, BLOCK), :]

    @pl.when(step == n_back + n_in + n_at)
    def _():
        flat[0 : norm.shape[0], :] = norm[...]

    adam_update(flat[...], m1, m2, wg, st, mn)


def adam_all(back, inner, attention, norm, m1, m2, inv_root, places):
    at_in, at_qkv, at_out = places
    b_rows, b_cols = back[0].shape
    i_rows, i_cols = inner[0].shape
    np_, a_rows, wide = attention[0].shape
    n_back = 2 * b_rows * b_cols // 128 // BLOCK
    n_in = 2 * i_rows * i_cols // 128 // BLOCK
    n_at = 2 * np_ * a_rows * wide // 128 // BLOCK
    assert np_ <= n_back + n_in and m1.shape[0] == (n_back + n_in + n_at) * BLOCK + 8
    s_in, s_qkv, s_out = 2 * i_cols // 128, 2 * len(at_qkv), 2 * len(at_out)
    edge = a_rows * s_qkv
    at_at = [[] for _ in range(np_)]
    for col, lo, hi in at_qkv:
        at_at[col // wide].append((col % wide, lo, hi, s_qkv))
    for col, lo, hi in at_out:
        at_at[(len(at_qkv) * 128 + col) // wide].append((col % wide, edge + lo, edge + hi, s_out))
    cfg = (inv_root, [(c, lo, hi, s_in) for c, lo, hi in at_in], at_at, (n_back, n_in, n_at))
    after_at, after_in = n_at, n_at + n_in

    def where(i):
        back_or_in = jnp.where(i < n_back, after_in + i, after_at + i - n_back)
        return jnp.where(i < n_back + n_in, back_or_in, jnp.where(i < n_back + n_in + n_at, i - n_back - n_in, i))

    flat = pl.BlockSpec((BLOCK, 128), lambda i: (where(i), 0))
    b_spec = pl.BlockSpec((2 * b_rows // n_back, b_cols), lambda i: (jnp.minimum(i, n_back - 1) % (n_back // 2), 0))
    i_spec = pl.BlockSpec((i_rows // n_in, i_cols), lambda i: (jnp.clip(i - n_back, 0, n_in - 1), 0))
    a_spec = pl.BlockSpec((1, a_rows, wide), lambda i: (jnp.minimum(i, np_ - 1), 0, 0))
    return pl.pallas_call(
        functools.partial(adam_all_kernel, cfg),
        grid=(n_back + n_in + n_at + 1,),
        out_shape=[sds(m1.shape, f32)] * 3,
        in_specs=[b_spec, b_spec, i_spec, i_spec, a_spec, a_spec, pl.BlockSpec(norm.shape, lambda i: (0, 0)), flat, flat],
        out_specs=[flat] * 3,
        scratch_shapes=[pltpu.VMEM((BLOCK, 128), f32), pltpu.VMEM((n_at * BLOCK, 128), f32)],
        compiler_params=params(),
        cost_estimate=cost(0, m1.size * 22),
        name="adam_all",
    )(*back, *inner, *attention, norm, m1, m2)


def after(x, *deps):
    return lax.optimization_barrier((x, deps))[0]


def body(n, nz, tokens, cotangent, doc_ids, master, moment_one, moment_two):
    t, d = tokens.shape
    ff = (master.shape[0] * n - 4 * d) // (2 * d) - 2 * d
    me = lax.axis_index(("y", "x"))
    rows = d // n
    comm = n == 4

    lanes = master.reshape(-1, 128)
    w, o, norm_share = unpack_first(lanes, n, d, ff)
    doc_row = doc_ids.reshape(1, t)
    doc_col = doc_ids.reshape(t, 1)
    d_out = jnp.where(doc_col >= 0, cotangent, jnp.zeros((), bf16))
    if not comm:
        w, o = spread(w), spread(o)
        norm_share = lax.all_gather(master[-(4 * d // n) :].astype(bf16), ("y", "x"), axis=0, tiled=True)
        norm_share = norm_share.astype(f32).reshape(-1, 128)
    a_one, qkv, in_own, bk_own, w_own, w_oth, o_own, o_oth, norms = project_qkv(lanes, tokens, norm_share, w, o, n, ff, comm)
    att, lse, in_own, in_oth, a_one_p, d_out_p = attend(qkv, doc_row, doc_col, in_own, a_one, d_out, d, comm)
    resid, a_two, hidden, slope, bk_own, bk_oth, hid_p, att_p = middle(
        att, tokens, norms, o_own, o_oth, in_own, in_oth, bk_own, comm
    )
    scatter = lambda g: lax.psum_scatter(g, ("y", "x"), scatter_dimension=0, tiled=True)
    g_back = pair_grad(hidden, ff // 2, hid_p, [d_out], d, d_out_p, "grad_back")
    grad_back = scatter(g_back)
    d_pre, dp_p, a_two_p = pre_grad(after(d_out, g_back), slope, bk_own, bk_oth, a_two, comm)
    g_in = pair_grad(a_two, d, a_two_p, [d_pre], ff // 2, dp_p, "grad_in")
    grad_in = scatter(g_in)
    d_resid, low, d_att, gain_two, bias_two, low_p = two_grad(
        after(d_pre, g_in), resid, d_out, norms, in_own, in_oth, o_own, o_oth, comm
    )
    deep = nz == 4
    dq, dk, dv, dqkv_p, red_back = attend_back(
        qkv, d_att, att, lse, doc_row, doc_col, grad_back, d, comm, deep
    )
    two_norm = jnp.concatenate([gain_two, bias_two]).reshape(-1, 128)
    full = comm and deep
    input_grad, mixed, red_in, red_in_p, red_at, red_at_p, sums = last_grad(
        [dq, dk, dv], dqkv_p, low, low_p, tokens, d_resid, norms, hidden, resid, doc_col, two_norm, a_one, a_one_p, att, att_p,
        w_own, w_oth, bk_own, bk_oth, grad_in, n, full,
    )
    if full:
        red_in, red_in_p = red_in.reshape(grad_in.shape), red_in_p.reshape(grad_in.shape)
    else:
        red_in, red_in_p = both_halves(grad_in, None, None, False)
        part = lax.psum_scatter(red_at, ("y", "x"), scatter_dimension=1, tiled=True)
        red_at, red_at_p = both_halves(part, None, None, False)
        sums = lax.psum(sums, ("z", "core", "y", "x"))

    inv_root = float(t * n * nz * 2) ** (-0.5)
    m1, m2 = moment_one.reshape(-1, 128), moment_two.reshape(-1, 128)
    nb = d // 128
    half = nb // 2
    hs = ff // n // 2
    r_qkv, r_out, r_in = rows * 3 * nb, rows * nb, rows * ff // 128
    back_at = r_qkv + r_out + r_in
    at_in = [(hs * j + q * 128, (2 * hs * j) // 128 + q, (2 * hs * j + hs) // 128 + q) for j in range(n) for q in range(hs // 128)]
    at_qkv = [((p * half + w) * 128, p * nb + w, p * nb + w + half) for p in range(3) for w in range(half)]
    at_out = [(w * 128, w, w + half) for w in range(half)]
    per = 4 * nb // n
    norm_part = lax.dynamic_slice_in_dim(sums, group_index(n) * per, per, 0) * inv_root
    if full:
        outs = adam_all(red_back, (red_in, red_in_p), (red_at, red_at_p), norm_part, m1, m2, inv_root, (at_in, at_qkv, at_out))
    else:
        outs = adam_rows_halves(*red_back, m1, m2, [], inv_root, back_at)
        outs = adam_columns(red_in[None], red_in_p[None], 0, 1, m1, m2, outs, inv_root, r_qkv + r_out, rows // 8, at_in)
        outs = adam_columns(red_at, red_at_p, 0, 3 * red_at.shape[0] // 4, m1, m2, outs, inv_root, 0, rows // 8, at_qkv)
        outs = adam_columns(red_at, red_at_p, 3, red_at.shape[0] // 4, m1, m2, outs, inv_root, r_qkv, rows // 2, at_out)
        outs = adam_tail(norm_part, m1, m2, outs, back_at + ff // n * nb)
    weight_grad, step, moment = [o.reshape(-1) for o in outs]
    return mixed, input_grad, weight_grad, step, moment


def solution(mesh):
    dp, n = mesh.shape["dp"], mesh.shape["group"]
    fine = Mesh(mesh.devices.reshape(dp // 2, 2, n // 2, 2), ("z", "core", "y", "x"))
    tok = ("z", "core", "y", "x")
    flat = P(("y", "x"))
    in_specs = (P(tok, None), P(tok, None), P(tok), flat, flat, flat)
    out_specs = (P(tok, None), P(tok, None), flat, flat, flat)
    return jax.shard_map(
        functools.partial(body, n, dp // 2), mesh=fine, in_specs=in_specs, out_specs=out_specs, check_vma=False
    )
```

```python
import functools

import jax
import jax.numpy as jnp
from jax import lax
from jax.experimental import pallas as pl
from jax.experimental.pallas import tpu as pltpu
from jax.sharding import Mesh
from jax.sharding import PartitionSpec as P

HEADS = 16
EPS = 1e-05
FILL = -1e30
BETA_ONE = 0.9
BETA_TWO = 0.999
RATE = 0.001
ADAM_EPS = 1e-08
STEPS = 100.0
VMEM_MB = 60

f32 = jnp.float32
bf16 = jnp.bfloat16
ANY = pl.BlockSpec(memory_space=pl.ANY)


def params(limit=VMEM_MB):
    return pltpu.CompilerParams(vmem_limit_bytes=limit << 20)


def cost(flops, nbytes, trans=0):
    return pl.CostEstimate(flops=int(flops), bytes_accessed=int(nbytes), transcendentals=int(trans))


def sds(shape, dtype):
    return jax.ShapeDtypeStruct(shape, dtype)


def dot_nn(a, b):
    return jnp.dot(a, b, preferred_element_type=f32)


def dot_nt(a, b):
    return lax.dot_general(a, b, (((1,), (1,)), ((), ())), preferred_element_type=f32)


def dot_tn(a, b):
    return lax.dot_general(a, b, (((0,), (0,)), ((), ())), preferred_element_type=f32)


def pick(flag, a, b):
    return jnp.where(flag, a, b)


MESH = pl.DeviceIdType.MESH


def peer(*axes):
    return {a: 1 - lax.axis_index(a) for a in axes}


def greet(peers):
    barrier = pltpu.get_barrier_semaphore()
    for p in peers:
        pl.semaphore_signal(barrier, inc=1, device_id=p, device_id_type=MESH)
    pl.semaphore_wait(barrier, len(peers))


def member():
    return lax.axis_index("y") * 2 + lax.axis_index("x")


class Gather:
    COUNT = 11

    def __init__(self, own, oth, send, recv, base):
        rows = own.shape[0] // 4
        half = rows // 2
        x, y = lax.axis_index("x"), lax.axis_index("y")
        share = [y * 2 + x, y * 2 + 1 - x, (1 - y) * 2 + x, (1 - y) * 2 + 1 - x]
        self.rows = [pl.ds(pl.multiple_of(k * rows, 8), rows) for k in share]

        def move(i, k, off, count, dst, to):
            at = pl.ds(pl.multiple_of(share[k] * rows + off, 8), count)
            return pltpu.make_async_remote_copy(
                src_ref=own.at[at, :], dst_ref=dst.at[at, :],
                send_sem=send.at[base + i], recv_sem=recv.at[base + i], device_id=peer(to), device_id_type=MESH,
            )

        self.moves = [
            move(0, 0, 0, half, own, "x"),
            move(1, 0, half, half, own, "x"),
            move(2, 0, half, half, own, "y"),
            move(3, 0, 0, half, own, "y"),
            move(4, 0, 0, rows, oth, "core"),
            move(5, 1, 0, half, own, "y"),
            move(6, 2, half, half, own, "x"),
            move(7, 1, 0, rows, oth, "core"),
            move(8, 2, 0, rows, oth, "core"),
            move(9, 3, 0, half, oth, "core"),
            move(10, 3, half, half, oth, "core"),
        ]

    def begin(self):
        for i in (0, 2, 1, 3, 4):
            self.moves[i].start()

    def relay(self):
        self.moves[0].wait_recv()
        self.moves[5].start()
        self.moves[2].wait_recv()
        self.moves[6].start()

    def forward(self):
        self.moves[1].wait_recv()
        self.moves[7].start()
        self.moves[3].wait_recv()
        self.moves[8].start()

    def close(self):
        self.moves[5].wait_recv()
        self.moves[9].start()
        self.moves[6].wait_recv()
        self.moves[10].start()

    def arrive(self, *which):
        for i in which:
            self.moves[i].wait_recv()

    def sent(self):
        for m in self.moves:
            m.wait_send()

    def finish(self):
        self.close()
        self.arrive(4, 7, 8, 9, 10)
        self.sent()


def hand_over(src, dst, send, recv):
    return pltpu.make_async_remote_copy(
        src_ref=src, dst_ref=dst, send_sem=send, recv_sem=recv, device_id=peer("core"), device_id_type=MESH
    )


def add_up(dst, a, b):
    rows, cols = dst.shape
    step = max(8, 16384 // cols)

    @pl.loop(0, rows // step)
    def _(i):
        at = pl.ds(pl.multiple_of(i * step, 8), step)
        dst[at, :] = (a[at, :].astype(f32) + b[at, :].astype(f32)).astype(bf16)


class Fold:
    def __init__(self, source, mine, inbox, cross, stage, total, red, theirs, keep, send, recv, base):
        self.pieces = len(mine)
        self.out = [pltpu.make_async_copy(total.at[s], red.at[s], keep.at[s]) for s in range(self.pieces)]
        z = lax.axis_index("z")
        self.end = (z == 0) | (z == 3)
        self.mid = (z == 1) | (z == 2)
        near, far = self.peers()
        self.mine, self.inbox, self.across, self.stage, self.total = mine, inbox, cross, stage, total

        def move(s, kind, src, dst, to):
            i = base + 4 * s + kind
            return pltpu.make_async_remote_copy(
                src_ref=src, dst_ref=dst, send_sem=send.at[i], recv_sem=recv.at[i], device_id=to, device_id_type=MESH
            )

        every = range(self.pieces)
        self.fold = [move(s, 0, source[s], inbox.at[s], near) for s in every]
        self.cross = [move(s, 1, stage.at[s], cross.at[s], far) for s in every]
        self.unfold = [move(s, 2, total.at[s], total.at[s], near) for s in every]
        self.core = [move(s, 3, total.at[s], theirs.at[s], peer("core")) for s in every]

    @staticmethod
    def peers():
        z = lax.axis_index("z")
        return [{"z": z + 1 - 2 * (z % 2)}, {"z": 3 - z}]

    def begin(self, s):
        pl.when(self.end)(self.fold[s].start)

    def inner(self, s):
        @pl.when(self.mid)
        def _():
            self.fold[s].wait_recv()
            add_up(self.stage.at[s], self.mine[s], self.inbox.at[s])
            self.cross[s].start()

    def outer(self, s):
        @pl.when(self.mid)
        def _():
            self.cross[s].wait_recv()
            add_up(self.total.at[s], self.stage.at[s], self.across.at[s])
            self.unfold[s].start()
            self.core[s].start()
            self.out[s].start()

    def land(self, s):
        @pl.when(self.end)
        def _():
            self.unfold[s].wait_recv()
            self.core[s].start()
            self.out[s].start()

    def finish(self):
        @pl.when(self.end)
        def _():
            for m in self.fold:
                m.wait_send()

        @pl.when(self.mid)
        def _():
            for m in self.cross + self.unfold:
                m.wait_send()

        for m in self.core + self.out:
            m.wait()


def pieces_of(ref):
    return [ref.at[i] for i in range(ref.shape[0])]


def fold_scratch(pieces, rows, cols):
    return [pltpu.VMEM((pieces, rows, cols), bf16)] * 4


class Scatter:
    def __init__(self, source, held, far, near, mid, total, send, recv, base, out=None, keep=None):
        pieces, rows, _ = held.shape
        self.out = [] if out is None else [pltpu.make_async_copy(total.at[s], out.at[s], keep.at[s]) for s in range(pieces)]
        block = rows // 4
        half = block // 2
        x, y = lax.axis_index("x"), lax.axis_index("y")
        me, over_x, over_y, both = y * 2 + x, y * 2 + 1 - x, (1 - y) * 2 + x, (1 - y) * 2 + 1 - x
        self.pieces, self.held, self.far, self.near, self.mid, self.total, self.half = pieces, held, far, near, mid, total, half

        def at(share, part):
            return pl.ds(pl.multiple_of(share * block + part * half, half), half)

        def move(i, src, dst, to):
            return pltpu.make_async_remote_copy(
                src_ref=src, dst_ref=dst, send_sem=send.at[base + i], recv_sem=recv.at[base + i],
                device_id=peer(to), device_id_type=MESH,
            )

        self.first, self.second = [], []
        for s in range(pieces):
            b = 6 * s
            self.first.append([
                move(b, source.at[s, at(over_x, 0), :], far.at[s, 0], "x"),
                move(b + 1, source.at[s, at(both, 0), :], far.at[s, 1], "x"),
                move(b + 2, source.at[s, at(over_y, 1), :], far.at[s, 2], "y"),
                move(b + 3, source.at[s, at(both, 1), :], far.at[s, 3], "y"),
            ])
            self.second.append([move(b + 4, mid.at[s, 1], near.at[s, 0], "y"), move(b + 5, mid.at[s, 3], near.at[s, 1], "x")])
        self.keep = [at(me, 0), at(over_y, 0), at(me, 1), at(over_x, 1)]

    def begin(self, s):
        for k in (1, 3, 0, 2):
            self.first[s][k].start()

    def turn(self, s):
        for k in (1, 3, 0, 2):
            self.first[s][k].wait_recv()
            add_up(self.mid.at[s, k], self.held.at[s, self.keep[k], :], self.far.at[s, k])
            if k in (1, 3):
                self.second[s][k // 2].start()

    def close(self, s):
        for part in range(2):
            self.second[s][part].wait_recv()
            at = pl.ds(part * self.half, self.half)
            add_up(self.total.at[s, at, :], self.mid.at[s, 2 * part], self.near.at[s, part])
        if self.out:
            self.out[s].start()

    def finish(self):
        for s in range(self.pieces):
            for m in self.first[s] + self.second[s]:
                m.wait_send()
        for m in self.out:
            m.wait()


def scatter_scratch(pieces, rows, cols):
    half = rows // 8
    four = pltpu.VMEM((pieces, 4, half, cols), bf16)
    return [pltpu.VMEM((pieces, rows, cols), bf16), four, pltpu.VMEM((pieces, 2, half, cols), bf16), four]


def swap_core(v):
    return lax.ppermute(v, "core", [(0, 1), (1, 0)])


def comm_params(cid, limit=VMEM_MB):
    if cid is None:
        return params(limit)
    return pltpu.CompilerParams(vmem_limit_bytes=limit << 20, collective_id=cid, has_side_effects=True)


def dma(count):
    return pltpu.SemaphoreType.DMA((count,))


def gain_row(norms, r, d):
    nb = d // 128
    return jnp.concatenate([norms[r * nb + i : r * nb + i + 1, :] for i in range(nb)], axis=1)


def layer_norm_parts(v):
    centre = v - jnp.mean(v, axis=-1, keepdims=True)
    r = lax.rsqrt(jnp.mean(centre * centre, axis=-1, keepdims=True) + EPS)
    return centre * r, r


def layer_norm_back(v, gain, dz):
    xhat, r = layer_norm_parts(v)
    dg = jnp.sum(dz * xhat, axis=0, keepdims=True)
    db = jnp.sum(dz, axis=0, keepdims=True)
    t = dz * gain
    dv = r * (t - jnp.mean(t, axis=-1, keepdims=True) - xhat * jnp.mean(t * xhat, axis=-1, keepdims=True))
    return dv, dg, db


def unpack_kernel(dims, m_qkv, m_out, m_norm, own_qkv, own_out, norm):
    n, d = dims
    core = lax.axis_index("core")
    nb = d // 128
    half = nb // 2
    rows = own_qkv.shape[0]

    def put(ref, own, dst, lo, stride):
        own[:, dst : dst + 128] = ref[pl.ds(lo + core * half, rows, stride=stride), :].astype(bf16)

    for part in range(3):
        for w in range(half):
            put(m_qkv, own_qkv, (part * half + w) * 128, part * nb + w, 3 * nb)
    for w in range(half):
        put(m_out, own_out, w * 128, w, nb)
    norm[...] = m_norm[...].astype(bf16).astype(f32)


def group_index(n):
    return lax.axis_index(("y", "x"))


def unpack_first(lanes, n, d, ff):
    rows = d // n
    nb = d // 128
    r1, r2, r3, r4 = rows * 3 * nb, rows * nb, rows * ff // 128, ff // n * nb
    steps = 4 if n == 4 else 2
    sr = rows // steps
    me = lambda: group_index(n)
    return pl.pallas_call(
        functools.partial(unpack_kernel, (n, d)),
        grid=(steps,),
        out_shape=[sds((d, 3 * d // 2), bf16), sds((d, d // 2), bf16), sds((8, 128), f32)],
        in_specs=[
            pl.BlockSpec((r1 // steps, 128), lambda i: (i, 0)),
            pl.BlockSpec((r2 // steps, 128), lambda i: (r1 // (r2 // steps) + i, 0)),
            pl.BlockSpec((8, 128), lambda i: ((r1 + r2 + r3 + r4) // 8, 0)),
        ],
        out_specs=[
            pl.BlockSpec((sr, 3 * d // 2), lambda i: (me() * steps + i, 0)),
            pl.BlockSpec((sr, d // 2), lambda i: (me() * steps + i, 0)),
            pl.BlockSpec((8, 128), lambda i: (0, 0)),
        ],
        compiler_params=params(),
        name="unpack",
    )(lanes, lanes, lanes)


UNPACK_STEPS = 8


def qkv_kernel(cfg, tok, norm_share, m_in, m_back, w_own_in, w_oth_in, o_own_in, o_oth_in, *refs):
    n, comm = cfg
    (a_out, qkv, own_in, own_bk, w_own, w_oth, o_own, o_oth, norms_out, norms, w, toks, acc, lsem, send, recv) = refs
    if not comm:
        w_own, w_oth = w_own_in, w_oth_in
    t, d = toks.shape
    step = pl.program_id(0)
    nb = d // 128
    half = 3 * d // 2
    share = d // n
    tm = min(256, t)
    tok_copy = pltpu.make_async_copy(tok, toks, lsem.at[0])

    if comm:
        me = member()
        near = [peer("x"), peer("y"), peer("x", "y")]
        mine = pl.ds(pl.multiple_of(me * 8, 8), 8)
        notes = [
            pltpu.make_async_remote_copy(
                src_ref=norm_share, dst_ref=norms.at[mine, :], send_sem=send.at[22 + i], recv_sem=recv.at[22 + i],
                device_id=p, device_id_type=MESH,
            )
            for i, p in enumerate(near)
        ]
        first = Gather(w_own, w_oth, send, recv, 0)
        second = Gather(o_own, o_oth, send, recv, 11)
        rows = first.rows
    else:
        rows = [pl.ds(k * share, share) for k in range(n)]

    @pl.when(step == 0)
    def _():
        tok_copy.start()
        if comm:
            greet(near + [peer("core")])
            for m in notes:
                m.start()
            first.begin()
            norms[mine, :] = norm_share[...]

    @pl.when(step < UNPACK_STEPS)
    def _():
        core = lax.axis_index("core")
        rows_in = own_in.shape[0]
        hs = own_in.shape[1] // n
        stride = m_in.shape[0] // rows_in
        for j in range(n):
            for q in range(hs // 128):
                lo = (2 * hs * j) // 128 + q + core * (hs // 128)
                at = hs * j + q * 128
                own_in[:, at : at + 128] = m_in[pl.ds(lo, rows_in, stride=stride), :].astype(bf16)
        for q in range(nb):
            own_bk[:, q * 128 : (q + 1) * 128] = m_back[pl.ds(q, own_bk.shape[0], stride=nb), :].astype(bf16)

    def load(*which):
        cps = []
        for k in which:
            cps.append(pltpu.make_async_copy(w_own.at[rows[k], :], w.at[k, :, pl.ds(0, half)], lsem.at[1 + 2 * k]))
            cps.append(pltpu.make_async_copy(w_oth.at[rows[k], :], w.at[k, :, pl.ds(half, half)], lsem.at[2 + 2 * k]))
        for cp in cps:
            cp.start()
        for cp in cps:
            cp.wait()

    def product(at, *which):
        return sum(dot_nn(a_out[at, cols_of(k)], w[k]) for k in which)

    def cols_of(k):
        if comm:
            return rows[k]
        return slice(k * share, (k + 1) * share)

    def each_block(fn):
        @pl.loop(0, t // tm)
        def _(i):
            fn(pl.ds(pl.multiple_of(i * tm, tm), tm))

    @pl.when(step == UNPACK_STEPS)
    def _():
        if comm:
            for m in notes:
                m.wait()
            first.relay()
            second.begin()
        else:
            norms[...] = norm_share[...]
        norms_out[...] = norms[...]
        tok_copy.wait()
        gain, bias = gain_row(norms, 0, d), gain_row(norms, 1, d)

        def norm(at):
            xhat, _ = layer_norm_parts(toks[at, :].astype(f32))
            a_out[at, :] = (xhat * gain + bias).astype(bf16)

        each_block(norm)
        if comm:
            first.arrive(4)
        load(0)

        def start(at):
            acc[at, :] = product(at, 0)

        each_block(start)

    @pl.when(step == UNPACK_STEPS + 1)
    def _():
        if comm:
            first.forward()
            first.arrive(7, 8)
        load(*range(1, n - 1))

        def more(at):
            acc[at, :] += product(at, *range(1, n - 1))

        each_block(more)

    @pl.when(step == UNPACK_STEPS + 2)
    def _():
        if comm:
            first.close()
            second.relay()
            first.arrive(9, 10)
        load(n - 1)
        scale = (d // HEADS) ** (-0.5)
        q = d // 2

        def last(at):
            total = acc[at, :] + product(at, n - 1)
            for o in (0, half):
                qkv[at, o : o + q] = (total[:, o : o + q].astype(bf16).astype(f32) * scale).astype(bf16)
                qkv[at, o + q : o + half] = total[:, o + q : o + half].astype(bf16)

        each_block(last)
        if comm:
            second.forward()
            second.finish()
            first.sent()


def project_qkv(lanes, tok, norm_share, w, o, n, ff, comm):
    t, d = tok.shape
    rows = d // n
    nb = d // 128
    hs = ff // n // 2
    r_in, r_bk = rows * ff // 128, ff // n * nb
    at_in, at_bk = rows * 4 * nb, rows * 4 * nb + r_in
    b_in, b_bk = r_in // UNPACK_STEPS, hs * nb // UNPACK_STEPS
    assert at_in % b_in == 0 and at_bk % b_bk == 0
    up = lambda i: jnp.minimum(i, UNPACK_STEPS - 1)
    me = lambda: group_index(n)
    whole = lambda s: pl.BlockSpec(s, lambda i: (0, 0))
    half = 3 * d // 2
    shapes = [sds((t, d), bf16), sds((t, 3 * d), bf16), sds((d, ff // 2), bf16), sds((ff // 2, d), bf16),
              sds((d, half), bf16), sds((d, half), bf16), sds((d, d // 2), bf16), sds((d, d // 2), bf16), sds((4 * nb, 128), f32)]
    w_args = [w, norm_share, o, norm_share] if comm else [w[0], w[1], o[0], o[1]]
    outs = pl.pallas_call(
        functools.partial(qkv_kernel, (n, comm)),
        grid=(UNPACK_STEPS + 3,),
        out_shape=shapes,
        in_specs=[
            ANY, whole(norm_share.shape),
            pl.BlockSpec((b_in, 128), lambda i: (at_in // b_in + up(i), 0)),
            pl.BlockSpec((b_bk, 128), lambda i: (at_bk // b_bk + lax.axis_index("core") * UNPACK_STEPS + up(i), 0)),
            ANY, ANY, ANY, ANY,
        ],
        out_specs=[
            whole((t, d)), whole((t, 3 * d)),
            pl.BlockSpec((rows // UNPACK_STEPS, ff // 2), lambda i: (me() * UNPACK_STEPS + up(i), 0)),
            pl.BlockSpec((hs // UNPACK_STEPS, d), lambda i: (me() * UNPACK_STEPS + up(i), 0)),
            ANY, ANY, ANY, ANY, whole((4 * nb, 128)),
        ],
        scratch_shapes=[pltpu.VMEM((4 * nb, 128), f32), pltpu.VMEM((n, rows, 3 * d), bf16), pltpu.VMEM((t, d), bf16),
                        pltpu.VMEM((t, 3 * d), f32), dma(1 + 2 * n), dma(25), dma(25)],
        input_output_aliases={4: 4, 6: 6},
        compiler_params=comm_params(1 if comm else None),
        cost_estimate=cost(2 * t * d * 3 * d, 40e6),
        name="qkv",
    )(tok, norm_share, lanes, lanes, *w_args)
    if comm:
        return outs
    return [*outs[:4], w[0], w[1], o[0], o[1], outs[8]]


QB = 256


def fill_bias(bias, doc_row, doc_col):
    t = bias.shape[0]
    for r in range(0, t, QB):
        key = r + lax.broadcasted_iota(jnp.int32, (QB, t), 0)
        query = lax.broadcasted_iota(jnp.int32, (QB, t), 1)
        ok = (doc_col[r : r + QB, :] == doc_row[...]) & (key <= query)
        bias[r : r + QB, :] = jnp.where(ok, 0.0, FILL)


def head_lanes(v, h, hd):
    lane = lax.broadcasted_iota(jnp.int32, v.shape, 1)
    return jnp.where((lane >= h * hd) & (lane < (h + 1) * hd), v, jnp.zeros_like(v))


def attend_kernel(cfg, q, k, v, doc_row, doc_col, w_own_in, a_one, d_out, out, lse, w_own, w_oth, a_p, d_p, bias, send, recv):
    hd, comm = cfg
    step = pl.program_id(0)
    last = pl.num_programs(0) - 1
    if comm:
        gather = Gather(w_own, w_oth, send, recv, 0)
        swaps = [hand_over(a_one, a_p, send.at[11], recv.at[11]), hand_over(d_out, d_p, send.at[12], recv.at[12])]

        @pl.when(step == 0)
        def _():
            greet([peer("x"), peer("y"), peer("core")])
            gather.begin()
            for s in swaps:
                s.start()

        @pl.when(step == 4)
        def _():
            gather.relay()

        @pl.when(step == 6)
        def _():
            gather.forward()

    @pl.when(step == 0)
    def _():
        fill_bias(bias, doc_row, doc_col)

    t = q.shape[0]
    vt = v[...].T
    per = 128 // hd
    qs = [head_lanes(q[...], h, hd) for h in range(per)]
    for i in range(t // QB):
        n = (i + 1) * QB
        cols = slice(i * QB, n)
        outs = []
        for h in range(per):
            s = dot_nt(k[:n, :], qs[h][cols, :]) + bias[:n, cols]
            top = jnp.max(s, axis=0, keepdims=True)
            e = jnp.exp(s - top)
            total = jnp.sum(e, axis=0, keepdims=True)
            lse[0, h : h + 1, cols] = top + jnp.log(total)
            o = dot_nn(vt[h * hd : (h + 1) * hd, :n], e.astype(bf16))
            outs.append(o * (1.0 / total))
        out[cols, :] = jnp.concatenate(outs, axis=0).T.astype(bf16)

    if comm:

        @pl.when(step == last)
        def _():
            gather.finish()
            for s in swaps:
                s.wait()


def head_column(d, part):
    pairs = d // 256
    return lambda p: (0, (p // pairs) * 3 * pairs + part * pairs + p % pairs)


def attend(qkv, doc_row, doc_col, w_own, a_one, d_out, d, comm):
    t = qkv.shape[0]
    pairs = d // 128
    hd = d // HEADS
    per = 128 // hd
    col = lambda part: pl.BlockSpec((t, 128), head_column(d, part))
    outs = pl.pallas_call(
        functools.partial(attend_kernel, (hd, comm)),
        grid=(pairs,),
        out_shape=[sds((t, d), bf16), sds((pairs, per, t), f32), sds(w_own.shape, bf16), sds(w_own.shape, bf16),
                   sds((t, d), bf16), sds((t, d), bf16)],
        in_specs=[col(0), col(1), col(2), pl.BlockSpec((1, t), lambda p: (0, 0)), pl.BlockSpec((t, 1), lambda p: (0, 0)),
                  ANY, ANY, ANY],
        out_specs=[pl.BlockSpec((t, 128), lambda p: (0, p)), pl.BlockSpec((1, per, t), lambda p: (p, 0, 0)), ANY, ANY, ANY, ANY],
        scratch_shapes=[pltpu.VMEM((t, t), f32), dma(13), dma(13)],
        input_output_aliases={5: 2},
        compiler_params=comm_params(2 if comm else None),
        cost_estimate=cost(8 * t * t * d, 10e6, t * t * HEADS),
        name="attend",
    )(qkv, qkv, qkv, doc_row, doc_col, w_own, a_one, d_out)
    if comm:
        return outs
    full, oth = spread(w_own)
    return outs[0], outs[1], full, oth, swap_core(a_one), swap_core(d_out)


def spread(own):
    n = lax.axis_size("y") * lax.axis_size("x")
    rows = own.shape[0] // n
    mine = lax.dynamic_slice_in_dim(own, lax.axis_index(("y", "x")) * rows, rows, 0)
    full = lax.all_gather(mine, ("y", "x"), axis=0, tiled=True)
    return full, swap_core(full)


def attend_back_kernel(cfg, q, k, v, dout, att, lse, doc_row, doc_col, part_sum, g_in, dq, dk, dv, sent, red, red_p, part_in, *refs):
    hd, comm = cfg
    bias, dk_acc, dv_acc, stage, lsem, send, recv = refs[:7]
    step = pl.program_id(0)
    pairs = stage.shape[0] // 3

    def hand(p, part):
        wide = 128 * pairs
        cols = pl.ds(pl.multiple_of(part * wide + p * 128, 128), 128)
        i = p * 3 + part
        return hand_over(stage.at[i], sent.at[:, cols], send.at[i], recv.at[i])

    if comm:

        base = 3 * pairs
        mine, keep, held, far, near, mid, total, keep_in = refs[7], refs[12], *refs[13:19]
        fold = Fold(pieces_of(part_sum), pieces_of(mine), *refs[8:12], red, red_p, keep, send, recv, base)
        scat = Scatter(g_in, held, far, near, mid, total, send, recv, base + 4 * PIECES, part_in, keep_in)
        acts = (scat.begin, scat.turn, scat.close, fold.inner, fold.outer, fold.land)

        @pl.when(step == 0)
        def _():
            loads = [pltpu.make_async_copy(part_sum, mine, lsem.at[0]), pltpu.make_async_copy(g_in, held, lsem.at[1])]
            for cp in loads:
                cp.start()
            greet([peer("core"), peer("x"), peer("y")] + Fold.peers())
            run_plan(acts, BACK_PLAN[0])
            for s in range(PIECES):
                fold.begin(s)
            for cp in loads:
                cp.wait()

        @pl.when((step > 0) & (step <= pairs))
        def _():
            for part in range(3):
                hand(step - 1, part).start()

    @pl.when(step == 0)
    def _():
        fill_bias(bias, doc_row, doc_col)

    if comm:
        for at, codes in enumerate(BACK_PLAN[:-1]):
            if codes and at > 0:
                pl.when(step == at)(functools.partial(run_plan, acts, codes))

    t = q.shape[0]
    per = 128 // hd
    scale = hd ** (-0.5)
    kt = k[...].T
    prod = (dout[...].astype(f32) * att[...].astype(f32)).T
    inner = [jnp.sum(prod[h * hd : (h + 1) * hd, :], axis=0, keepdims=True) for h in range(per)]
    qs = [head_lanes(q[...], h, hd) for h in range(per)]
    ds_ = [head_lanes(dout[...], h, hd) for h in range(per)]
    dk_acc[...] = jnp.zeros_like(dk_acc)
    dv_acc[...] = jnp.zeros_like(dv_acc)
    for i in range(t // QB):
        n = (i + 1) * QB
        cols = slice(i * QB, n)
        dqs = []
        for h in range(per):
            qh, dh = qs[h][cols, :], ds_[h][cols, :]
            s = dot_nt(k[:n, :], qh) + bias[:n, cols]
            p = jnp.exp(s - lse[0, h : h + 1, cols])
            dp = dot_nt(v[:n, :], dh)
            g = (p * (dp - inner[h][:, cols])).astype(bf16)
            dv_acc[:n, :] += dot_nn(p.astype(bf16), dh)
            dk_acc[:n, :] += dot_nn(g, qh)
            dqs.append(dot_nn(kt[h * hd : (h + 1) * hd, :n], g))
        dq[cols, :] = (jnp.concatenate(dqs, axis=0).T * scale).astype(bf16)
    dk[...] = dk_acc[...].astype(bf16)
    dv[...] = dv_acc[...].astype(bf16)

    if comm:

        @pl.when(step < pairs)
        def _():
            stage[step * 3] = dq[...]
            stage[step * 3 + 1] = dk[...]
            stage[step * 3 + 2] = dv[...]

        @pl.when(step == 2 * pairs - 1)
        def _():
            for p in range(pairs):
                for part in range(3):
                    hand(p, part).wait()
            run_plan(acts, BACK_PLAN[-1])
            fold.finish()
            scat.finish()


def run_plan(acts, codes):
    for code in codes:
        acts[code // 10](code % 10)


FEED_PLAN = (
    (0, 1),
    (),
    (10, 2),
    (11, 3, 20),
    (12, 4),
    (21, 13, 5),
    (22,),
    (14, 6, 23),
    (15, 7, 24),
    (16,),
    (25,),
    (17, 26),
    (),
    (27,),
    (),
    (),
    (),
)
BACK_PLAN = (
    (0, 1, 2),
    (),
    (10, 3, 11, 4, 30, 31),
    (12, 5, 20, 32, 33, 40),
    (13, 6, 21, 34, 35, 41, 42),
    (14, 7, 22, 36, 37, 43, 44, 50),
    (15, 23, 45, 51, 52, 16, 46),
    (17, 24, 47, 53, 54, 25),
    (26, 27, 55, 56, 57),
)
LAST_PLAN = (
    (),
    (0,),
    (1,),
    (30,),
    (10, 2, 31),
    (11, 3, 32, 40),
    (20, 33, 41),
    (12, 4, 34, 42),
    (21, 35, 43, 50),
    (13, 5, 22, 36, 44, 45, 37, 51),
    (14, 6, 23, 60, 46, 52, 53),
    (15, 7, 24, 61, 62, 70, 47, 54),
    (16, 25, 63, 64, 71, 55),
    (17, 26, 65, 72, 73, 66, 56, 90),
    (27, 67, 74, 75, 80, 91),
    (76, 81, 57, 92),
    (77, 93, 82, 94, 83, 95, 84, 85, 86, 87),
)
PIECES = 8


def attend_back(qkv, dout, att, lse, doc_row, doc_col, part_sum, g_in, d, n, comm):
    t = qkv.shape[0]
    pairs = d // 128
    half = pairs // 2
    hd = d // HEADS
    per = 128 // hd
    turn = lambda p: (p + half) % pairs
    part_in = (g_in.shape[0], g_in.shape[1] // n, g_in.shape[2])
    col = lambda part: pl.BlockSpec((t, 128), lambda p: head_column(d, part)(turn(p)))
    one = pl.BlockSpec((t, 128), lambda p: (0, turn(p)))
    sems = 3 * half + 10 * PIECES
    extra = []
    if comm:
        extra = [pltpu.VMEM(part_sum.shape, bf16)] + fold_scratch(*part_sum.shape) + [dma(PIECES)]
        extra += scatter_scratch(*g_in.shape) + [pltpu.VMEM(part_in, bf16), dma(PIECES)]
    outs = pl.pallas_call(
        functools.partial(attend_back_kernel, (hd, comm)),
        grid=(pairs,),
        out_shape=[sds((t, d), bf16)] * 3 + [sds((t, 3 * d // 2), bf16)] + [sds(part_sum.shape, bf16)] * 2 + [sds(part_in, bf16)],
        in_specs=[col(0), col(1), col(2), one, one, pl.BlockSpec((1, per, t), lambda p: (turn(p), 0, 0)),
                  pl.BlockSpec((1, t), lambda p: (0, 0)), pl.BlockSpec((t, 1), lambda p: (0, 0)), ANY, ANY],
        out_specs=[one, one, one, ANY, ANY, ANY, ANY],
        scratch_shapes=[pltpu.VMEM((t, t), f32), pltpu.VMEM((t, 128), f32), pltpu.VMEM((t, 128), f32),
                        pltpu.VMEM((3 * half, t, 128), bf16), dma(2), dma(sems), dma(sems)] + extra,
        compiler_params=comm_params(6 if comm else None),
        cost_estimate=cost(20 * t * t * d, 16e6, t * t * HEADS),
        name="attend_back",
    )(qkv, qkv, qkv, dout, att, lse, doc_row, doc_col, part_sum, g_in)
    if comm:
        return outs[0], outs[1], outs[2], outs[3], (outs[4], outs[5]), outs[6]
    sent = swap_core(jnp.concatenate([g[:, d // 2 :] for g in outs[:3]], axis=1))
    return outs[0], outs[1], outs[2], sent, both_halves(part_sum), scatter_pieces(g_in)


def both_halves(part_sum):
    full = lax.psum(part_sum.astype(f32), "z").astype(bf16)
    return full, swap_core(full)


def middle_kernel(cfg, att_rows, tok, norms, o_own, o_oth, w_own, w_oth, att_all, bk_own_in, d_out, d_out_p, *refs):
    d, tm, blk, comm = cfg
    (resid, a_two_out, hidden, slope, bk_own, bk_oth, att_p, grad, w, a_two, stage, theirs, douts, lsem, send, recv) = refs
    step = pl.program_id(0)
    last = pl.num_programs(0) - 1
    t = a_two.shape[0]
    pro = t // tm
    half = d // 2
    nb = theirs.shape[0]
    core = lax.axis_index("core")
    loads = [pltpu.make_async_copy(v, douts.at[i], lsem.at[2 + i]) for i, v in enumerate((d_out, d_out_p))]

    def hand(j):
        return hand_over(stage.at[j], theirs.at[j], send.at[12 + j], recv.at[12 + j])

    if comm:
        gather = Gather(bk_own, bk_oth, send, recv, 0)
        swap = hand_over(att_all, att_p, send.at[11], recv.at[11])

        @pl.when(step == 0)
        def _():
            greet([peer("x"), peer("y"), peer("core")])
            gather.begin()
            swap.start()

        @pl.when(step == pro + 4)
        def _():
            gather.relay()

        @pl.when((step > pro) & (step <= pro + nb))
        def _():
            hand(step - pro - 1).start()

    @pl.when(step == 0)
    def _():
        lo = pl.multiple_of(core * half, half)
        hi = pl.multiple_of((1 - core) * half, half)
        cps = [
            pltpu.make_async_copy(o_own, w.at[:, pl.ds(lo, half)], lsem.at[0]),
            pltpu.make_async_copy(o_oth, w.at[:, pl.ds(hi, half)], lsem.at[1]),
        ]
        for cp in cps + loads:
            cp.start()
        for cp in cps:
            cp.wait()

    @pl.when(step < pro)
    def _():
        lo = pl.multiple_of(core * half, half)
        hi = pl.multiple_of((1 - core) * half, half)
        y = dot_nn(att_rows[:, :half], w[pl.ds(lo, half), :]) + dot_nn(att_rows[:, half:], w[pl.ds(hi, half), :])
        r = tok[...].astype(f32) + y
        resid[...] = r
        xhat, _ = layer_norm_parts(r)
        a = (xhat * gain_row(norms, 2, d) + gain_row(norms, 3, d)).astype(bf16)
        a_two_out[...] = a
        a_two[pl.ds(pl.multiple_of(step * tm, tm), tm), :] = a

    @pl.when((step >= pro) & (step < pro + 2 * nb))
    def _():
        pre = dot_nn(a_two[...], pick(step < pro + nb, w_oth[...], w_own[...]))
        cdf = 0.5 + 0.5 * lax.erf(pre * (0.5**0.5))
        pdf = jnp.exp(-0.5 * pre * pre) * 0.3989422804014327
        h = (pre * cdf).astype(bf16)
        hidden[...] = h
        slope[...] = (cdf + pre * pdf).astype(bf16)
        stage[step - pro] = h

    @pl.when(step == pro + 2 * nb)
    def _():
        for cp in loads:
            cp.wait()

    if comm:
        for j in range(nb):

            @pl.when(step == pro + 2 * nb + j)
            def _():
                hand(j).wait_recv()

        @pl.when(step == pro + 2 * nb)
        def _():
            gather.forward()

    @pl.when(step >= pro + 2 * nb)
    def _():
        j = step - pro - 2 * nb
        g = dot_tn(stage[nb + j], douts[0])
        if comm:
            g = g + dot_tn(theirs[j], douts[1])
        store_columns(grad, g)

    if comm:

        @pl.when(step == last)
        def _():
            gather.finish()
            swap.wait()
            for j in range(nb):
                hand(j).wait_send()


def store_columns(ref, g):
    wide = ref.shape[2]
    for p in range(ref.shape[0]):
        ref[p] = g[:, p * wide : (p + 1) * wide].astype(bf16)


def middle(att, tok, norms, o_own, o_oth, w_own, w_oth, bk_own, d_out, d_out_p, comm, tm=256, blk=512):
    t, d = tok.shape
    wide = w_own.shape[1]
    pro, nb = t // tm, wide // blk
    rowi = lambda i: jnp.minimum(i, pro - 1)
    oth = lambda i: jnp.clip(i - pro, 0, nb - 1)
    own = lambda i: jnp.clip(i - pro - nb, 0, nb - 1)
    both = lambda i: jnp.where(i < pro + nb, nb + oth(i), own(i))
    rows = lambda wd: pl.BlockSpec((tm, wd), lambda i: (rowi(i), 0))
    part = lambda count: pltpu.VMEM((count, t, blk), bf16)
    outs = pl.pallas_call(
        functools.partial(middle_kernel, (d, tm, blk, comm)),
        grid=(pro + 3 * nb,),
        out_shape=[sds((t, d), f32), sds((t, d), bf16), sds((t, 2 * wide), bf16), sds((t, 2 * wide), bf16),
                   sds(bk_own.shape, bf16), sds(bk_own.shape, bf16), sds((t, d), bf16), sds((PIECES, wide, d // PIECES), bf16)],
        in_specs=[rows(d), rows(d), pl.BlockSpec(norms.shape, lambda i: (0, 0)), ANY, ANY,
                  pl.BlockSpec((d, blk), lambda i: (0, own(i))), pl.BlockSpec((d, blk), lambda i: (0, oth(i))), ANY, ANY, ANY, ANY],
        out_specs=[rows(d), rows(d), pl.BlockSpec((t, blk), lambda i: (0, both(i))), pl.BlockSpec((t, blk), lambda i: (0, both(i))),
                   ANY, ANY, ANY, pl.BlockSpec((PIECES, blk, d // PIECES), lambda i: (0, jnp.maximum(i - pro - 2 * nb, 0), 0))],
        scratch_shapes=[pltpu.VMEM((d, d), bf16), pltpu.VMEM((t, d), bf16), part(2 * nb), part(nb), pltpu.VMEM((2, t, d), bf16),
                        dma(4), dma(12 + nb), dma(12 + nb)],
        input_output_aliases={8: 4},
        compiler_params=comm_params(3 if comm else None),
        cost_estimate=cost(2 * t * d * d + 8 * t * d * wide, 60e6, 4 * t * wide),
        name="middle",
    )(att, tok, norms, o_own, o_oth, w_own, w_oth, att, bk_own, d_out, d_out_p)
    if comm:
        return outs
    full, other = spread(bk_own)
    hid_p = swap_core(outs[2][:, wide:])
    grad = (dot_tn(outs[2][:, :wide], d_out) + dot_tn(hid_p, d_out_p)).astype(bf16)
    return [*outs[:4], full, other, swap_core(att), in_columns(grad)]


def in_columns(g):
    rows, cols = g.shape
    return g.reshape(rows, PIECES, cols // PIECES).transpose(1, 0, 2)


def feed_kernel(comm, d_out, slope, b_own, b_oth, i_own, i_oth, resid, dout_rows, norms, o_own, o_oth, a_two, g_back, *refs):
    (grad, d_resid, low, d_att, two_norm, sent, part_back, stage, theirs, lhs, dz, wo, lows, lsem, send, recv) = refs[:16]
    step = pl.program_id(0)
    nb = theirs.shape[0]
    tm, d = resid.shape
    pro = dz.shape[0] // tm
    half = d // 2
    np_ = d // 128
    core = lax.axis_index("core")
    lo = pl.multiple_of(core * half, half)
    hi = pl.multiple_of((1 - core) * half, half)
    loads = [
        pltpu.make_async_copy(a_two, lhs.at[0], lsem.at[0]),
        pltpu.make_async_copy(o_own, wo.at[:, pl.ds(lo, half)], lsem.at[1]),
        pltpu.make_async_copy(o_oth, wo.at[:, pl.ds(hi, half)], lsem.at[2]),
    ]

    def hand(j):
        return hand_over(stage.at[j], theirs.at[j], send.at[1 + j], recv.at[1 + j])

    def hand_low(r):
        at = pl.ds(pl.multiple_of(r * tm, tm), tm)
        return hand_over(lows.at[at, :], sent.at[at, :], send.at[1 + nb + r], recv.at[1 + nb + r])

    @pl.when(step == 0)
    def _():
        for cp in loads:
            cp.start()

    if comm:
        swap = hand_over(a_two, lhs.at[1], send.at[0], recv.at[0])
        held, far, near, mid, total, keep = refs[16:22]
        scat = Scatter(g_back, held, far, near, mid, total, send, recv, 1 + nb + pro, part_back, keep)
        acts = (scat.begin, scat.turn, scat.close)

        @pl.when(step == 0)
        def _():
            load = pltpu.make_async_copy(g_back, held, lsem.at[3])
            load.start()
            greet([peer("core"), peer("x"), peer("y")])
            run_plan(acts, FEED_PLAN[0])
            swap.start()
            load.wait()

        for at, codes in enumerate(FEED_PLAN[:-1]):
            if codes and at > 0:
                pl.when(step == at)(functools.partial(run_plan, acts, codes))

        @pl.when((step > 0) & (step <= nb))
        def _():
            hand(step - 1).start()

    @pl.when(step < 2 * nb)
    def _():
        first = step < nb
        g = (dot_nt(d_out[...], pick(first, b_oth[...], b_own[...])) * slope[...].astype(f32)).astype(bf16)
        stage[step] = g
        more = dot_nt(g, pick(first, i_oth[...], i_own[...]))

        @pl.when(step == 0)
        def _():
            dz[...] = more

        @pl.when(step > 0)
        def _():
            dz[...] += more

    @pl.when(step == 2 * nb)
    def _():
        loads[0].wait()
        if comm:
            swap.wait()

    if comm:
        for j in range(nb):

            @pl.when(step == 2 * nb + j)
            def _():
                hand(j).wait()

    @pl.when((step >= 2 * nb) & (step < 3 * nb))
    def _():
        j = step - 2 * nb
        g = dot_tn(lhs[0], stage[nb + j])
        if comm:
            g = g + dot_tn(lhs[1], theirs[j])
        store_columns(grad, g)

    @pl.when(step == 3 * nb)
    def _():
        loads[1].wait()
        loads[2].wait()
        two_norm[...] = jnp.zeros_like(two_norm)

    @pl.when(step >= 3 * nb)
    def _():
        here = pl.ds(pl.multiple_of((step - 3 * nb) * tm, tm), tm)
        dv, g, b = layer_norm_back(resid[...], gain_row(norms, 2, d), dz[here, :])
        two_norm[0:np_, :] += flat_row(g)
        two_norm[np_:, :] += flat_row(b)
        dr = dout_rows[...].astype(f32) + dv
        d_resid[...] = dr
        dl = dr.astype(bf16)
        low[...] = dl
        lows[here, :] = pick(core == 0, dl[:, half:], dl[:, :half])
        d_att[:, :half] = dot_nt(dl, wo[pl.ds(lo, half), :]).astype(bf16)
        d_att[:, half:] = dot_nt(dl, wo[pl.ds(hi, half), :]).astype(bf16)
        if comm:
            hand_low(step - 3 * nb).start()

    if comm:

        @pl.when(step == pl.num_programs(0) - 1)
        def _():
            run_plan(acts, FEED_PLAN[-1])
            scat.finish()
            for r in range(pro):
                hand_low(r).wait()


def feed_back(d_out, slope, b_own, b_oth, i_own, i_oth, resid, norms, o_own, o_oth, a_two, g_back, n, comm, tm=256, blk=512):
    t, d = d_out.shape
    half = b_own.shape[0]
    nb = half // blk
    pro = t // tm
    oth = lambda i: jnp.minimum(i, nb - 1)
    own = lambda i: jnp.clip(i - nb, 0, nb - 1)
    row = lambda i: jnp.clip(i - 3 * nb, 0, pro - 1)
    rows = lambda w: pl.BlockSpec((tm, w), lambda i: (row(i), 0))
    whole = lambda s: pl.BlockSpec(s, lambda i: (0, 0))
    pieces, g_rows, g_cols = g_back.shape
    part = (pieces, g_rows // n, g_cols)
    per = half // PIECES
    extra = scatter_scratch(*g_back.shape) + [pltpu.VMEM(part, bf16), dma(pieces)] if comm else []
    sems = 1 + nb + pro + 6 * pieces
    outs = pl.pallas_call(
        functools.partial(feed_kernel, comm),
        grid=(3 * nb + pro,),
        out_shape=[sds((PIECES, d, per), bf16), sds((t, d), f32), sds((t, d), bf16), sds((t, d), bf16), sds((d // 64, 128), f32),
                   sds((t, d // 2), bf16), sds(part, bf16)],
        in_specs=[whole((t, d)), pl.BlockSpec((t, blk), lambda i: (0, jnp.where(i < nb, nb + i, own(i)))),
                  pl.BlockSpec((blk, d), lambda i: (own(i), 0)), pl.BlockSpec((blk, d), lambda i: (oth(i), 0)),
                  pl.BlockSpec((d, blk), lambda i: (0, own(i))), pl.BlockSpec((d, blk), lambda i: (0, oth(i))),
                  rows(d), rows(d), whole(norms.shape), ANY, ANY, ANY, ANY],
        out_specs=[pl.BlockSpec((blk // per, d, per), lambda i: (jnp.clip(i - 2 * nb, 0, nb - 1), 0, 0)), rows(d), rows(d), rows(d),
                   whole((d // 64, 128)), ANY, ANY],
        scratch_shapes=[pltpu.VMEM((2 * nb, t, blk), bf16), pltpu.VMEM((nb, t, blk), bf16), pltpu.VMEM((2, t, d), bf16),
                        pltpu.VMEM((t, d), f32), pltpu.VMEM((d, d), bf16), pltpu.VMEM((t, d // 2), bf16), dma(4), dma(sems), dma(sems)]
        + extra,
        compiler_params=comm_params(4 if comm else None, 62),
        cost_estimate=cost(12 * t * d * half + 2 * t * d * d, 60e6),
        name="feed_back",
    )(d_out, slope, b_own, b_oth, i_own, i_oth, resid, d_out, norms, o_own, o_oth, a_two, g_back)
    if comm:
        return outs
    core = lax.axis_index("core")
    other = lax.dynamic_slice_in_dim(outs[2], (1 - core) * (d // 2), d // 2, 1)
    d_pre = pre_values(d_out, slope, b_own, b_oth)
    g_in = dot_tn(a_two, d_pre[:, :half]) + dot_tn(swap_core(a_two), swap_core(d_pre[:, half:]))
    return [in_columns(g_in.astype(bf16)), *outs[1:5], swap_core(other), scatter_pieces(g_back)]


def pre_values(d_out, slope, own, oth):
    both = jnp.concatenate([dot_nt(d_out, own), dot_nt(d_out, oth)], axis=1)
    return (both * slope.astype(f32)).astype(bf16)


def scatter_pieces(g):
    return lax.psum_scatter(g, ("y", "x"), scatter_dimension=1, tiled=True)


def last_kernel(cfg, g1, g2, g3, theirs, low, low_p, dq, dk, dv, tok, d_resid, norms, h_own, h_oth, resid, doc, two_norm,
                a_one, a_one_p, att, att_p, w_own, w_oth, b_own, b_oth, part_in, *refs):
    d, comm = cfg
    out, mixed, red_in, red_in_p, red_at, red_at_p, sums, w, wb, parts, held, lsem = refs[:12]
    step = pl.program_id(0)
    last = pl.num_programs(0) - 1
    np_ = held.shape[0]
    pro = (last - np_) // 2
    half = 3 * d // 2
    q = d // 2
    hb = b_own.shape[0]
    nb = d // 128
    core = lax.axis_index("core")
    early = [pltpu.make_async_copy(a, wb.at[pl.ds(i * d, d), :], lsem.at[i]) for i, a in enumerate((a_one, a_one_p, att, att_p))]
    mids = [
        pltpu.make_async_copy(w_own, w.at[:, pl.ds(0, half)], lsem.at[4]),
        pltpu.make_async_copy(w_oth, w.at[:, pl.ds(half, half)], lsem.at[5]),
    ]
    late = [
        pltpu.make_async_copy(b_own, wb.at[pl.ds(0, hb), :], lsem.at[6]),
        pltpu.make_async_copy(b_oth, wb.at[pl.ds(hb, hb), :], lsem.at[7]),
    ]
    if comm:
        send, recv, mine_in, fi, sc, fa, vec, box, k_in, k_at = (
            refs[12], refs[13], refs[14], refs[15:19], refs[19:22], refs[22:27], refs[27], refs[28], refs[29], refs[30]
        )
        fold_in = Fold(
            pieces_of(part_in), pieces_of(mine_in), *fi, red_in, red_in_p, k_in, send, recv, 0
        )
        scat = Scatter(held, held, *sc, fa[0], send, recv, 4 * PIECES)
        mine_at = pieces_of(fa[0])
        fold_at = Fold(mine_at, mine_at, *fa[1:5], red_at, red_at_p, k_at, send, recv, 4 * PIECES + 6 * np_)
        base = 4 * PIECES + 10 * np_

        def note(i, src, dst, to):
            return pltpu.make_async_remote_copy(
                src_ref=src, dst_ref=dst, send_sem=send.at[base + i], recv_sem=recv.at[base + i], device_id=to, device_id_type=MESH
            )

        near, far = Fold.peers()
        notes = [
            note(0, vec.at[0], box.at[0], peer("x")),
            note(1, vec.at[1], box.at[1], peer("y")),
            note(2, vec.at[2], box.at[2], peer("core")),
            note(3, vec.at[3], box.at[3], near),
            note(4, vec.at[4], box.at[4], far),
            note(5, vec.at[5], vec.at[5], near),
        ]

        def norm_sum(k):
            if k < 3:
                notes[k].wait_recv()
                vec[k + 1] = vec[k] + box[k]
                if k < 2:
                    notes[k + 1].start()
                else:
                    pl.when(fold_in.end)(notes[3].start)
            elif k < 5:

                @pl.when(fold_in.mid)
                def _():
                    notes[k].wait_recv()
                    vec[k + 1] = vec[k] + box[k]
                    notes[k + 1].start()

            else:
                pl.when(fold_in.end)(notes[5].wait_recv)

        def settle(s):
            scat.close(s)
            fold_at.begin(s)

        acts = (scat.begin, scat.turn, settle, fold_in.inner, fold_in.outer, fold_in.land, fold_at.inner, fold_at.outer,
                fold_at.land, norm_sum)

    @pl.when(step == 0)
    def _():
        for cp in early + mids:
            cp.start()
        if comm:
            load = pltpu.make_async_copy(part_in, mine_in, lsem.at[8])
            load.start()
            greet([peer("core"), peer("x"), peer("y")] + Fold.peers())
            for s in range(PIECES):
                fold_in.begin(s)
            load.wait()
        for cp in early:
            cp.wait()
        parts[0 : 2 * nb, :] = jnp.zeros((2 * nb, 128), f32)
        parts[2 * nb :, :] = two_norm[...]

    if comm:
        for k, codes in enumerate(LAST_PLAN[:-1]):
            if codes:
                pl.when(step == k)(functools.partial(run_plan, acts, codes))

    per = q // g1.shape[1]

    @pl.when(step < 3 * per)
    def _():
        g = pick(step < per, g1[...], pick(step < 2 * per, g2[...], g3[...]))
        acc = dot_tn(wb[0:d, :], g) + dot_tn(wb[d : 2 * d, :], theirs[...])
        held[step] = acc.astype(bf16)

    @pl.when((step >= 3 * per) & (step < np_))
    def _():
        lo = pl.ds(pl.multiple_of(core * q, q), q)
        hi = pl.ds(pl.multiple_of((1 - core) * q, q), q)
        own = dot_tn(wb[2 * d : 3 * d, :q], low[...]) + dot_tn(wb[3 * d :, q:], low_p[...])
        held[step, lo, :] = own.astype(bf16)
        other = dot_tn(wb[2 * d : 3 * d, q:], low[...]) + dot_tn(wb[3 * d :, :q], low_p[...])
        held[step, hi, :] = other.astype(bf16)

    @pl.when(step == np_)
    def _():
        for cp in late:
            cp.start()
        for cp in mids:
            cp.wait()

    @pl.when((step >= np_) & (step < np_ + pro))
    def _():
        both = jnp.concatenate([g[:, :q] for g in (dq, dk, dv)] + [g[:, q:] for g in (dq, dk, dv)], axis=1)
        dz = dot_nt(both, w[...])
        grad, g, b = layer_norm_back(tok[...].astype(f32), gain_row(norms, 0, d), dz)
        parts[0:nb, :] += flat_row(g)
        parts[nb : 2 * nb, :] += flat_row(b)
        out[...] = (d_resid[...] + grad).astype(bf16)

    @pl.when(step == np_ + pro)
    def _():
        for cp in late:
            cp.wait()
        if comm:
            vec[0] = parts[...]
            notes[0].start()

    @pl.when((step >= np_ + pro) & (step < last))
    def _():
        y = dot_nn(h_own[...], wb[:hb, :]) + dot_nn(h_oth[...], wb[hb:, :]) + resid[...]
        mixed[...] = jnp.where(doc[...] >= 0, y, 0.0).astype(bf16)

    @pl.when(step == last)
    def _():
        if comm:
            run_plan(acts, LAST_PLAN[-1])
            fold_in.finish()
            scat.finish()
            fold_at.finish()
            for i in (0, 1, 2):
                notes[i].wait_send()
            pl.when(fold_in.end)(notes[3].wait_send)

            @pl.when(fold_in.mid)
            def _():
                notes[4].wait_send()
                notes[5].wait_send()

            sums[...] = vec[5]
        else:
            sums[...] = parts[...]
            cp = pltpu.make_async_copy(held, red_at, lsem.at[0])
            cp.start()
            cp.wait()


def flat_row(v):
    return jnp.concatenate([v[:, i * 128 : (i + 1) * 128] for i in range(v.shape[1] // 128)], axis=0)


def last_grad(grads3, theirs, low, low_p, tok, d_resid, norms, hidden, resid, doc_col, two_norm, a_one, a_one_p, att, att_p,
              own, oth, b_own, b_oth, part_in, n, comm, tm=256, wide=256):
    t, d = tok.shape
    pro = t // tm
    half = b_own.shape[0]
    q = d // 2
    per = q // wide
    np_ = 4 * per
    one = lambda w, c=0: pl.BlockSpec((tm, w), lambda i: (jnp.clip(i - np_, 0, pro - 1), c))
    two = lambda w, c=0: pl.BlockSpec((tm, w), lambda i: (jnp.clip(i - np_ - pro, 0, pro - 1), c))
    whole = lambda a: pl.BlockSpec(a.shape, lambda i: (0, 0))
    col = lambda k, count: pl.BlockSpec((t, wide), lambda i: (0, jnp.clip(i - k * per, 0, count - 1)))
    low_col = pl.BlockSpec((t, wide), lambda i: (0, lax.axis_index("core") * per + jnp.clip(i - 3 * per, 0, per - 1)))
    nv = 4 * d // 128
    pieced = part_in.shape
    share = (np_, d // n if comm else d, wide)
    slots = 4 * PIECES + 10 * np_ + 6
    extra = []
    if comm:
        extra = [dma(slots), dma(slots), pltpu.VMEM(part_in.shape, bf16)] + fold_scratch(*part_in.shape)
        extra += scatter_scratch(np_, d, wide)[1:] + [pltpu.VMEM(share, bf16)] * 5
        extra += [pltpu.VMEM((6, nv, 128), f32), pltpu.VMEM((5, nv, 128), f32), dma(PIECES), dma(np_)]
    return pl.pallas_call(
        functools.partial(last_kernel, (d, comm)),
        grid=(np_ + 2 * pro + 1,),
        out_shape=[sds((t, d), bf16), sds((t, d), bf16)] + [sds(pieced, bf16)] * 2 + [sds(share, bf16)] * 2 + [sds((nv, 128), f32)],
        in_specs=[col(0, per), col(1, per), col(2, per), col(0, 3 * per), low_col, col(3, per)]
        + [one(d)] * 5 + [whole(norms), two(half), two(half, 1), two(d), two(1), whole(two_norm)] + [ANY] * 9,
        out_specs=[one(d), two(d), ANY, ANY, ANY, ANY, pl.BlockSpec((nv, 128), lambda i: (0, 0))],
        scratch_shapes=[pltpu.VMEM((d, 3 * d), bf16), pltpu.VMEM((4 * d, d), bf16), pltpu.VMEM((nv, 128), f32),
                        pltpu.VMEM((np_, d, wide), bf16), dma(9)] + extra,
        compiler_params=comm_params(7 if comm else None, 63),
        cost_estimate=cost(14 * t * d * d + 4 * t * d * half, 60e6),
        name="last_grad",
    )(*grads3, theirs, low, low_p, *grads3, tok, d_resid, norms, hidden, hidden, resid, doc_col, two_norm,
      a_one, a_one_p, att, att_p, own, oth, b_own, b_oth, part_in)


def adam_update(g_ref, m1, m2, wg, st, mn):
    rows = g_ref.shape[0]
    step = min(rows, 256)

    @pl.loop(0, rows // step)
    def _(i):
        at = pl.ds(pl.multiple_of(i * step, 8), step)
        g = g_ref[at, :]
        first = BETA_ONE * m1[at, :] + (1.0 - BETA_ONE) * g
        second_hat = (BETA_TWO / (1.0 - BETA_TWO**STEPS)) * m2[at, :] + ((1.0 - BETA_TWO) / (1.0 - BETA_TWO**STEPS)) * g * g
        wg[at, :] = g
        st[at, :] = (-RATE / (1.0 - BETA_ONE**STEPS)) * first / (second_hat * lax.rsqrt(second_hat) + ADAM_EPS)
        mn[at, :] = first


def adam_kernel(plan, inv_root, own, oth, m1, m2, *refs):
    wg, st, mn, flat = refs[-4:]
    rows, stride, places = plan
    first = lax.axis_index("core") == 0
    wide = own.shape[2]
    for col, lo, hi in places:
        p, c = col // wide, col % wide
        a = own[p, :, c : c + 128].astype(f32) * inv_root
        b = oth[p, :, c : c + 128].astype(f32) * inv_root
        flat[pl.ds(lo, rows, stride=stride), :] = pick(first, a, b)
        flat[pl.ds(hi, rows, stride=stride), :] = pick(first, b, a)
    adam_update(flat, m1, m2, wg, st, mn)


def adam_columns(own, oth, at, count, m1, m2, prev, inv_root, first_row, rows, places):
    total, wide = own.shape[1:]
    nb = 2 * count * wide // 128
    blk = rows * nb
    assert first_row % blk == 0
    base = first_row // blk
    half = pl.BlockSpec((count, rows, wide), lambda i: (at, i, 0))
    flat = pl.BlockSpec((blk, 128), lambda i: (base + i, 0))
    kernel = functools.partial(adam_kernel, (rows, nb, places), inv_root)
    return adam_call(kernel, (total // rows,), own, oth, m1, m2, prev, half, flat, blk, "adam")


def adam_call(kernel, grid, own, oth, m1, m2, prev, half, flat, blk, name):
    return pl.pallas_call(
        kernel,
        grid=grid,
        out_shape=[sds(m1.shape, f32)] * 3,
        in_specs=[half, half, flat, flat] + [ANY] * len(prev),
        out_specs=[flat] * 3,
        scratch_shapes=[pltpu.VMEM((blk, 128), f32)],
        input_output_aliases={4 + i: i for i in range(len(prev))},
        compiler_params=params(),
        cost_estimate=cost(0, own.size * 2 * 22),
        name=name,
    )(own, oth, m1, m2, *prev)


def adam_rows_kernel(inv_root, own, oth, m1, m2, *refs):
    wg, st, mn, flat = refs[-4:]
    g = pick(pl.program_id(0) == lax.axis_index("core"), own[...], oth[...]).astype(f32) * inv_root
    rows, width = g.shape
    nb = width // 128
    for w in range(nb):
        flat[pl.ds(w, rows, stride=nb), :] = g[:, w * 128 : (w + 1) * 128]
    adam_update(flat, m1, m2, wg, st, mn)


def adam_rows_halves(own, oth, m1, m2, prev, inv_root, first_row):
    count, width = own.shape
    rows = count // 4
    blk = rows * width // 128
    base = first_row // blk
    half = pl.BlockSpec((rows, width), lambda h, i: (i, 0))
    flat = pl.BlockSpec((blk, 128), lambda h, i: (base + h * 4 + i, 0))
    kernel = functools.partial(adam_rows_kernel, inv_root)
    return adam_call(kernel, (2, 4), own, oth, m1, m2, prev, half, flat, blk, "adam_rows")


def adam_tail_kernel(g, m1, m2, p1, p2, p3, wg, st, mn):
    adam_update(g, m1, m2, wg, st, mn)


def adam_tail(g, m1, m2, prev, first_row):
    rows = 8
    assert first_row % rows == 0 and g.shape[0] <= rows
    g = jnp.pad(g, ((0, rows - g.shape[0]), (0, 0)))
    flat = pl.BlockSpec((rows, 128), lambda i: (first_row // rows, 0))
    return pl.pallas_call(
        adam_tail_kernel,
        grid=(1,),
        out_shape=[sds(m1.shape, f32)] * 3,
        in_specs=[pl.BlockSpec((rows, 128), lambda i: (0, 0)), flat, flat] + [ANY] * 3,
        out_specs=[flat] * 3,
        input_output_aliases={3: 0, 4: 1, 5: 2},
        name="adam_norms",
    )(g, m1, m2, *prev)


BLOCK = 4096


def adam_all_kernel(cfg, b_own, b_oth, i_own, i_oth, a_own, a_oth, norm, m1, m2, wg, st, mn, flat, later):
    inv_root, at_in, at_at, counts = cfg
    step = pl.program_id(0)
    core = lax.axis_index("core")
    first = core == 0
    n_back, n_in, n_at = counts

    @pl.when(step < n_back)
    def _():
        mine = step // (n_back // 2) == core
        pieces, rows, wide = b_own.shape
        for w in range(pieces * wide // 128):
            p, c = w * 128 // wide, w * 128 % wide
            g = pick(mine, b_own[p, :, c : c + 128], b_oth[p, :, c : c + 128])
            flat[pl.ds(w, rows, stride=pieces * wide // 128), :] = g.astype(f32) * inv_root

    def spread_columns(dst, own, oth, places):
        rows, wide = own.shape[1:]
        for col, lo, hi, stride in places:
            p, c = col // wide, col % wide
            a = own[p, :, c : c + 128].astype(f32) * inv_root
            b = oth[p, :, c : c + 128].astype(f32) * inv_root
            dst[pl.ds(lo, rows, stride=stride), :] = pick(first, a, b)
            dst[pl.ds(hi, rows, stride=stride), :] = pick(first, b, a)

    @pl.when((step >= n_back) & (step < n_back + n_in))
    def _():
        spread_columns(flat, i_own, i_oth, at_in)

    for k, places in enumerate(at_at):
        pl.when(step == k)(functools.partial(spread_columns, later, a_own, a_oth, places))

    @pl.when((step >= n_back + n_in) & (step < n_back + n_in + n_at))
    def _():
        at = pl.multiple_of((step - n_back - n_in) * BLOCK, BLOCK)
        flat[...] = later[pl.ds(at, BLOCK), :]

    @pl.when(step == n_back + n_in + n_at)
    def _():
        per = norm.shape[0] // 4
        at = pl.multiple_of(lax.axis_index(("y", "x")) * per, per)
        flat[0:per, :] = norm[pl.ds(at, per), :] * inv_root

    adam_update(flat, m1, m2, wg, st, mn)


def adam_all(back, inner, attention, norm, m1, m2, inv_root, places):
    at_in, at_qkv, at_out = places
    b_np, b_rows, b_wide = back[0].shape
    i_np, i_rows, i_wide = inner[0].shape
    np_, a_rows, wide = attention[0].shape
    n_back = 2 * b_np * b_rows * b_wide // 128 // BLOCK
    n_in = 2 * i_np * i_rows * i_wide // 128 // BLOCK
    n_at = 2 * np_ * a_rows * wide // 128 // BLOCK
    lots = np_ // (n_back + n_in)
    assert np_ == lots * (n_back + n_in) and m1.shape[0] == (n_back + n_in + n_at) * BLOCK + 8
    s_in, s_qkv, s_out = 2 * i_np * i_wide // 128, 2 * len(at_qkv), 2 * len(at_out)
    edge = a_rows * s_qkv
    at_at = [[] for _ in range(n_back + n_in)]
    for col, lo, hi in at_qkv:
        at_at[col // wide // lots].append((col % (wide * lots), lo, hi, s_qkv))
    for col, lo, hi in at_out:
        col += len(at_qkv) * 128
        at_at[col // wide // lots].append((col % (wide * lots), edge + lo, edge + hi, s_out))
    cfg = (inv_root, [(c, lo, hi, s_in) for c, lo, hi in at_in], at_at, (n_back, n_in, n_at))
    after_at, after_in = n_at, n_at + n_in

    def where(i):
        back_or_in = jnp.where(i < n_back, after_in + i, after_at + i - n_back)
        return jnp.where(i < n_back + n_in, back_or_in, jnp.where(i < n_back + n_in + n_at, i - n_back - n_in, i))

    flat = pl.BlockSpec((BLOCK, 128), lambda i: (where(i), 0))
    b_spec = pl.BlockSpec((b_np, 2 * b_rows // n_back, b_wide), lambda i: (0, jnp.minimum(i, n_back - 1) % (n_back // 2), 0))
    i_spec = pl.BlockSpec((i_np, i_rows // n_in, i_wide), lambda i: (0, jnp.clip(i - n_back, 0, n_in - 1), 0))
    a_spec = pl.BlockSpec((lots, a_rows, wide), lambda i: (jnp.minimum(i, n_back + n_in - 1), 0, 0))
    return pl.pallas_call(
        functools.partial(adam_all_kernel, cfg),
        grid=(n_back + n_in + n_at + 1,),
        out_shape=[sds(m1.shape, f32)] * 3,
        in_specs=[b_spec, b_spec, i_spec, i_spec, a_spec, a_spec, pl.BlockSpec(norm.shape, lambda i: (0, 0)), flat, flat],
        out_specs=[flat] * 3,
        scratch_shapes=[pltpu.VMEM((BLOCK, 128), f32), pltpu.VMEM((n_at * BLOCK, 128), f32)],
        compiler_params=params(),
        cost_estimate=cost(0, m1.size * 22),
        name="adam_all",
    )(*back, *inner, *attention, norm, m1, m2)


def after(x, *deps):
    return lax.optimization_barrier((x, deps))[0]


def body(n, nz, tokens, cotangent, doc_ids, master, moment_one, moment_two):
    t, d = tokens.shape
    ff = (master.shape[0] * n - 4 * d) // (2 * d) - 2 * d
    me = lax.axis_index(("y", "x"))
    rows = d // n
    comm = n == 4 and nz == 4

    lanes = master.reshape(-1, 128)
    w, o, norm_share = unpack_first(lanes, n, d, ff)
    doc_row = doc_ids.reshape(1, t)
    doc_col = doc_ids.reshape(t, 1)
    d_out = jnp.where(doc_col >= 0, cotangent, jnp.zeros((), bf16))
    if not comm:
        w, o = spread(w), spread(o)
        norm_share = lax.all_gather(master[-(4 * d // n) :].astype(bf16), ("y", "x"), axis=0, tiled=True)
        norm_share = norm_share.astype(f32).reshape(-1, 128)
    a_one, qkv, in_own, bk_own, w_own, w_oth, o_own, o_oth, norms = project_qkv(lanes, tokens, norm_share, w, o, n, ff, comm)
    att, lse, in_own, in_oth, a_one_p, d_out_p = attend(qkv, doc_row, doc_col, in_own, a_one, d_out, d, comm)
    resid, a_two, hidden, slope, bk_own, bk_oth, att_p, g_back = middle(
        att, tokens, norms, o_own, o_oth, in_own, in_oth, bk_own, d_out, d_out_p, comm
    )
    g_in, d_resid, low, d_att, two_norm, low_p, part_back = feed_back(
        d_out, slope, bk_own, bk_oth, in_own, in_oth, resid, norms, o_own, o_oth, a_two, g_back, n, comm
    )
    dq, dk, dv, dqkv_p, red_back, part_in = attend_back(qkv, d_att, att, lse, doc_row, doc_col, part_back, g_in, d, n, comm)
    input_grad, mixed, red_in, red_in_p, red_at, red_at_p, sums = last_grad(
        [dq, dk, dv], dqkv_p, low, low_p, tokens, d_resid, norms, hidden, resid, doc_col, two_norm, a_one, a_one_p, att, att_p,
        w_own, w_oth, bk_own, bk_oth, part_in, n, comm,
    )
    red_in, red_at = (red_in, red_in_p), (red_at, red_at_p)
    if not comm:
        red_in, red_at = both_halves(part_in), both_halves(scatter_pieces(red_at[0]))
        sums = lax.psum(sums, ("z", "core", "y", "x"))

    inv_root = float(t * n * nz * 2) ** (-0.5)
    m1, m2 = moment_one.reshape(-1, 128), moment_two.reshape(-1, 128)
    nb = d // 128
    half = nb // 2
    hs = ff // n // 2
    r_qkv, r_out, r_in = rows * 3 * nb, rows * nb, rows * ff // 128
    back_at = r_qkv + r_out + r_in
    at_in = [(hs * j + q * 128, (2 * hs * j) // 128 + q, (2 * hs * j + hs) // 128 + q) for j in range(n) for q in range(hs // 128)]
    at_qkv = [((p * half + w) * 128, p * nb + w, p * nb + w + half) for p in range(3) for w in range(half)]
    at_out = [(w * 128, w, w + half) for w in range(half)]
    if comm:
        outs = adam_all(red_back, red_in, red_at, sums, m1, m2, inv_root, (at_in, at_qkv, at_out))
    else:
        plain = lambda v: v.transpose(1, 0, 2).reshape(v.shape[1], -1)
        count = red_at[0].shape[0]
        outs = adam_rows_halves(plain(red_back[0]), plain(red_back[1]), m1, m2, [], inv_root, back_at)
        outs = adam_columns(*red_in, 0, red_in[0].shape[0], m1, m2, outs, inv_root, r_qkv + r_out, rows // 8, at_in)
        outs = adam_columns(*red_at, 0, 3 * count // 4, m1, m2, outs, inv_root, 0, rows // 8, at_qkv)
        outs = adam_columns(*red_at, 3, count // 4, m1, m2, outs, inv_root, r_qkv, rows // 2, at_out)
        per = 4 * nb // n
        norm_part = lax.dynamic_slice_in_dim(sums, group_index(n) * per, per, 0) * inv_root
        outs = adam_tail(norm_part, m1, m2, outs, back_at + ff // n * nb)
    weight_grad, step, moment = [o.reshape(-1) for o in outs]
    return mixed, input_grad, weight_grad, step, moment


def solution(mesh):
    dp, n = mesh.shape["dp"], mesh.shape["group"]
    fine = Mesh(mesh.devices.reshape(dp // 2, 2, n // 2, 2), ("z", "core", "y", "x"))
    tok = ("z", "core", "y", "x")
    flat = P(("y", "x"))
    in_specs = (P(tok, None), P(tok, None), P(tok), flat, flat, flat)
    out_specs = (P(tok, None), P(tok, None), flat, flat, flat)
    return jax.shard_map(
        functools.partial(body, n, dp // 2), mesh=fine, in_specs=in_specs, out_specs=out_specs, check_vma=False
    )
```

```python
import functools

import jax
import jax.numpy as jnp
from jax import lax
from jax.experimental import pallas as pl
from jax.experimental.pallas import tpu as pltpu
from jax.sharding import Mesh
from jax.sharding import PartitionSpec as P

HEADS = 16
EPS = 1e-05
FILL = -1e30
BETA_ONE = 0.9
BETA_TWO = 0.999
RATE = 0.001
ADAM_EPS = 1e-08
STEPS = 100.0
VMEM_MB = 60

f32 = jnp.float32
bf16 = jnp.bfloat16
ANY = pl.BlockSpec(memory_space=pl.ANY)


def params(limit=VMEM_MB):
    return pltpu.CompilerParams(vmem_limit_bytes=limit << 20)


def cost(flops, nbytes, trans=0):
    return pl.CostEstimate(flops=int(flops), bytes_accessed=int(nbytes), transcendentals=int(trans))


def sds(shape, dtype):
    return jax.ShapeDtypeStruct(shape, dtype)


def dot_nn(a, b):
    return jnp.dot(a, b, preferred_element_type=f32)


def dot_nt(a, b):
    return lax.dot_general(a, b, (((1,), (1,)), ((), ())), preferred_element_type=f32)


def dot_tn(a, b):
    return lax.dot_general(a, b, (((0,), (0,)), ((), ())), preferred_element_type=f32)


def pick(flag, a, b):
    return jnp.where(flag, a, b)


MESH = pl.DeviceIdType.MESH


def peer(*axes):
    return {a: 1 - lax.axis_index(a) for a in axes}


def greet(peers):
    barrier = pltpu.get_barrier_semaphore()
    for p in peers:
        pl.semaphore_signal(barrier, inc=1, device_id=p, device_id_type=MESH)
    pl.semaphore_wait(barrier, len(peers))


def member():
    return lax.axis_index("y") * 2 + lax.axis_index("x")


class Gather:
    COUNT = 11

    def __init__(self, own, oth, send, recv, base):
        rows = own.shape[0] // 4
        half = rows // 2
        x, y = lax.axis_index("x"), lax.axis_index("y")
        share = [y * 2 + x, y * 2 + 1 - x, (1 - y) * 2 + x, (1 - y) * 2 + 1 - x]
        self.rows = [pl.ds(pl.multiple_of(k * rows, 8), rows) for k in share]

        def move(i, k, off, count, dst, to):
            at = pl.ds(pl.multiple_of(share[k] * rows + off, 8), count)
            return pltpu.make_async_remote_copy(
                src_ref=own.at[at, :], dst_ref=dst.at[at, :],
                send_sem=send.at[base + i], recv_sem=recv.at[base + i], device_id=peer(to), device_id_type=MESH,
            )

        self.moves = [
            move(0, 0, 0, half, own, "x"),
            move(1, 0, half, half, own, "x"),
            move(2, 0, half, half, own, "y"),
            move(3, 0, 0, half, own, "y"),
            move(4, 0, 0, rows, oth, "core"),
            move(5, 1, 0, half, own, "y"),
            move(6, 2, half, half, own, "x"),
            move(7, 1, 0, rows, oth, "core"),
            move(8, 2, 0, rows, oth, "core"),
            move(9, 3, 0, half, oth, "core"),
            move(10, 3, half, half, oth, "core"),
        ]

    def begin(self):
        for i in (0, 2, 1, 3, 4):
            self.moves[i].start()

    def relay(self):
        self.moves[0].wait_recv()
        self.moves[5].start()
        self.moves[2].wait_recv()
        self.moves[6].start()

    def forward(self):
        self.moves[1].wait_recv()
        self.moves[7].start()
        self.moves[3].wait_recv()
        self.moves[8].start()

    def close(self):
        self.moves[5].wait_recv()
        self.moves[9].start()
        self.moves[6].wait_recv()
        self.moves[10].start()

    def arrive(self, *which):
        for i in which:
            self.moves[i].wait_recv()

    def sent(self):
        for m in self.moves:
            m.wait_send()

    def finish(self):
        self.close()
        self.arrive(4, 7, 8, 9, 10)
        self.sent()


def hand_over(src, dst, send, recv):
    return pltpu.make_async_remote_copy(
        src_ref=src, dst_ref=dst, send_sem=send, recv_sem=recv, device_id=peer("core"), device_id_type=MESH
    )


def add_up(dst, a, b):
    dst[...] = a[...] + b[...]


class Fold:
    def __init__(self, source, mine, inbox, cross, stage, total, red, theirs, keep, send, recv, base):
        self.pieces = len(mine)
        self.out = [pltpu.make_async_copy(total.at[s], red.at[s], keep.at[s]) for s in range(self.pieces)]
        z = lax.axis_index("z")
        self.end = (z == 0) | (z == 3)
        self.mid = (z == 1) | (z == 2)
        near, far = self.peers()
        self.mine, self.inbox, self.across, self.stage, self.total = mine, inbox, cross, stage, total

        def move(s, kind, src, dst, to):
            i = base + 4 * s + kind
            return pltpu.make_async_remote_copy(
                src_ref=src, dst_ref=dst, send_sem=send.at[i], recv_sem=recv.at[i], device_id=to, device_id_type=MESH
            )

        every = range(self.pieces)
        self.fold = [move(s, 0, source[s], inbox.at[s], near) for s in every]
        self.cross = [move(s, 1, stage.at[s], cross.at[s], far) for s in every]
        self.unfold = [move(s, 2, total.at[s], total.at[s], near) for s in every]
        self.core = [move(s, 3, total.at[s], theirs.at[s], peer("core")) for s in every]

    @staticmethod
    def peers():
        z = lax.axis_index("z")
        return [{"z": z + 1 - 2 * (z % 2)}, {"z": 3 - z}]

    def begin(self, s):
        pl.when(self.end)(self.fold[s].start)

    def inner(self, s):
        @pl.when(self.mid)
        def _():
            self.fold[s].wait_recv()
            add_up(self.stage.at[s], self.mine[s], self.inbox.at[s])
            self.cross[s].start()

    def outer(self, s):
        @pl.when(self.mid)
        def _():
            self.cross[s].wait_recv()
            add_up(self.total.at[s], self.stage.at[s], self.across.at[s])
            self.unfold[s].start()
            self.core[s].start()
            self.out[s].start()

    def land(self, s):
        @pl.when(self.end)
        def _():
            self.unfold[s].wait_recv()
            self.core[s].start()
            self.out[s].start()

    def finish(self):
        @pl.when(self.end)
        def _():
            for m in self.fold:
                m.wait_send()

        @pl.when(self.mid)
        def _():
            for m in self.cross + self.unfold:
                m.wait_send()

        for m in self.core + self.out:
            m.wait()


def pieces_of(ref):
    return [ref.at[i] for i in range(ref.shape[0])]


def fold_scratch(pieces, rows, cols):
    return [pltpu.VMEM((pieces, rows, cols), bf16)] * 4


class Scatter:
    def __init__(self, source, held, far, near, mid, total, send, recv, base, out=None, keep=None):
        pieces, rows, _ = held.shape
        self.out = [] if out is None else [pltpu.make_async_copy(total.at[s], out.at[s], keep.at[s]) for s in range(pieces)]
        block = rows // 4
        half = block // 2
        x, y = lax.axis_index("x"), lax.axis_index("y")
        me, over_x, over_y, both = y * 2 + x, y * 2 + 1 - x, (1 - y) * 2 + x, (1 - y) * 2 + 1 - x
        self.pieces, self.held, self.far, self.near, self.mid, self.total, self.half = pieces, held, far, near, mid, total, half

        def at(share, part):
            return pl.ds(pl.multiple_of(share * block + part * half, half), half)

        def move(i, src, dst, to):
            return pltpu.make_async_remote_copy(
                src_ref=src, dst_ref=dst, send_sem=send.at[base + i], recv_sem=recv.at[base + i],
                device_id=peer(to), device_id_type=MESH,
            )

        self.first, self.second = [], []
        for s in range(pieces):
            b = 6 * s
            self.first.append([
                move(b, source.at[s, at(over_x, 0), :], far.at[s, 0], "x"),
                move(b + 1, source.at[s, at(both, 0), :], far.at[s, 1], "x"),
                move(b + 2, source.at[s, at(over_y, 1), :], far.at[s, 2], "y"),
                move(b + 3, source.at[s, at(both, 1), :], far.at[s, 3], "y"),
            ])
            self.second.append([move(b + 4, mid.at[s, 1], near.at[s, 0], "y"), move(b + 5, mid.at[s, 3], near.at[s, 1], "x")])
        self.keep = [at(me, 0), at(over_y, 0), at(me, 1), at(over_x, 1)]

    def begin(self, s):
        for k in (1, 3, 0, 2):
            self.first[s][k].start()

    def turn(self, s):
        for k in (1, 3, 0, 2):
            self.first[s][k].wait_recv()
            add_up(self.mid.at[s, k], self.held.at[s, self.keep[k], :], self.far.at[s, k])
            if k in (1, 3):
                self.second[s][k // 2].start()

    def close(self, s):
        for part in range(2):
            self.second[s][part].wait_recv()
            at = pl.ds(part * self.half, self.half)
            add_up(self.total.at[s, at, :], self.mid.at[s, 2 * part], self.near.at[s, part])
        if self.out:
            self.out[s].start()

    def finish(self):
        for s in range(self.pieces):
            for m in self.first[s] + self.second[s]:
                m.wait_send()
        for m in self.out:
            m.wait()


def scatter_scratch(pieces, rows, cols):
    half = rows // 8
    four = pltpu.VMEM((pieces, 4, half, cols), bf16)
    return [pltpu.VMEM((pieces, rows, cols), bf16), four, pltpu.VMEM((pieces, 2, half, cols), bf16), four]


def swap_core(v):
    return lax.ppermute(v, "core", [(0, 1), (1, 0)])


def comm_params(cid, limit=VMEM_MB):
    if cid is None:
        return params(limit)
    return pltpu.CompilerParams(vmem_limit_bytes=limit << 20, collective_id=cid, has_side_effects=True)


def dma(count):
    return pltpu.SemaphoreType.DMA((count,))


def gain_row(norms, r, d):
    nb = d // 128
    return jnp.concatenate([norms[r * nb + i : r * nb + i + 1, :] for i in range(nb)], axis=1)


def layer_norm_parts(v):
    centre = v - jnp.mean(v, axis=-1, keepdims=True)
    r = lax.rsqrt(jnp.mean(centre * centre, axis=-1, keepdims=True) + EPS)
    return centre * r, r


def layer_norm_back(v, gain, dz):
    xhat, r = layer_norm_parts(v)
    dg = jnp.sum(dz * xhat, axis=0, keepdims=True)
    db = jnp.sum(dz, axis=0, keepdims=True)
    t = dz * gain
    dv = r * (t - jnp.mean(t, axis=-1, keepdims=True) - xhat * jnp.mean(t * xhat, axis=-1, keepdims=True))
    return dv, dg, db


def unpack_kernel(dims, m_qkv, m_out, m_norm, own_qkv, own_out, norm):
    n, d = dims
    core = lax.axis_index("core")
    nb = d // 128
    half = nb // 2
    rows = own_qkv.shape[0]

    def put(ref, own, dst, lo, stride):
        own[:, dst : dst + 128] = ref[pl.ds(lo + core * half, rows, stride=stride), :].astype(bf16)

    for part in range(3):
        for w in range(half):
            put(m_qkv, own_qkv, (part * half + w) * 128, part * nb + w, 3 * nb)
    for w in range(half):
        put(m_out, own_out, w * 128, w, nb)
    norm[...] = m_norm[...].astype(bf16).astype(f32)


def group_index(n):
    return lax.axis_index(("y", "x"))


def unpack_first(lanes, n, d, ff):
    rows = d // n
    nb = d // 128
    r1, r2, r3, r4 = rows * 3 * nb, rows * nb, rows * ff // 128, ff // n * nb
    steps = 4 if n == 4 else 2
    sr = rows // steps
    me = lambda: group_index(n)
    return pl.pallas_call(
        functools.partial(unpack_kernel, (n, d)),
        grid=(steps,),
        out_shape=[sds((d, 3 * d // 2), bf16), sds((d, d // 2), bf16), sds((8, 128), f32)],
        in_specs=[
            pl.BlockSpec((r1 // steps, 128), lambda i: (i, 0)),
            pl.BlockSpec((r2 // steps, 128), lambda i: (r1 // (r2 // steps) + i, 0)),
            pl.BlockSpec((8, 128), lambda i: ((r1 + r2 + r3 + r4) // 8, 0)),
        ],
        out_specs=[
            pl.BlockSpec((sr, 3 * d // 2), lambda i: (me() * steps + i, 0)),
            pl.BlockSpec((sr, d // 2), lambda i: (me() * steps + i, 0)),
            pl.BlockSpec((8, 128), lambda i: (0, 0)),
        ],
        compiler_params=params(),
        name="unpack",
    )(lanes, lanes, lanes)


UNPACK_STEPS = 8


def qkv_kernel(cfg, tok, norm_share, m_in, m_back, w_own_in, w_oth_in, o_own_in, o_oth_in, cot, docs, *refs):
    n, comm = cfg
    (a_hbm, qkv_hbm, own_in, own_bk, w_own, w_oth, o_own, o_oth, norms_out, d_hbm, doc_col, norms, w, toks, acc, cots, qkv, a_out,
     lsem, send, recv) = refs
    if not comm:
        w_own, w_oth = w_own_in, w_oth_in
    t, d = toks.shape
    step = pl.program_id(0)
    nb = d // 128
    half = 3 * d // 2
    share = d // n
    tm = min(256, t)
    tok_copy = pltpu.make_async_copy(tok, toks, lsem.at[0])
    cot_copy = pltpu.make_async_copy(cot, cots, lsem.at[1 + 2 * n])
    a_copy = pltpu.make_async_copy(a_out, a_hbm, lsem.at[2 + 2 * n])
    d_copy = pltpu.make_async_copy(cots, d_hbm, lsem.at[3 + 2 * n])

    if comm:
        me = member()
        near = [peer("x"), peer("y"), peer("x", "y")]
        mine = pl.ds(pl.multiple_of(me * 8, 8), 8)
        notes = [
            pltpu.make_async_remote_copy(
                src_ref=norm_share, dst_ref=norms.at[mine, :], send_sem=send.at[22 + i], recv_sem=recv.at[22 + i],
                device_id=p, device_id_type=MESH,
            )
            for i, p in enumerate(near)
        ]
        first = Gather(w_own, w_oth, send, recv, 0)
        second = Gather(o_own, o_oth, send, recv, 11)
        rows = first.rows
    else:
        rows = [pl.ds(k * share, share) for k in range(n)]

    @pl.when(step == 0)
    def _():
        tok_copy.start()
        cot_copy.start()
        if comm:
            greet(near + [peer("core")])
            for m in notes:
                m.start()
            first.begin()
            norms[mine, :] = norm_share[...]

    @pl.when(step < UNPACK_STEPS)
    def _():
        core = lax.axis_index("core")
        rows_in = own_in.shape[0]
        hs = own_in.shape[1] // n
        stride = m_in.shape[0] // rows_in
        for j in range(n):
            for q in range(hs // 128):
                lo = (2 * hs * j) // 128 + q + core * (hs // 128)
                at = hs * j + q * 128
                own_in[:, at : at + 128] = m_in[pl.ds(lo, rows_in, stride=stride), :].astype(bf16)
        for q in range(nb):
            own_bk[:, q * 128 : (q + 1) * 128] = m_back[pl.ds(q, own_bk.shape[0], stride=nb), :].astype(bf16)

    def load(*which):
        cps = []
        for k in which:
            cps.append(pltpu.make_async_copy(w_own.at[rows[k], :], w.at[k, :, pl.ds(0, half)], lsem.at[1 + 2 * k]))
            cps.append(pltpu.make_async_copy(w_oth.at[rows[k], :], w.at[k, :, pl.ds(half, half)], lsem.at[2 + 2 * k]))
        for cp in cps:
            cp.start()
        for cp in cps:
            cp.wait()

    def product(at, *which):
        return sum(dot_nn(a_out[at, cols_of(k)], w[k]) for k in which)

    def cols_of(k):
        if comm:
            return rows[k]
        return slice(k * share, (k + 1) * share)

    def each_block(fn):
        @pl.loop(0, t // tm)
        def _(i):
            fn(pl.ds(pl.multiple_of(i * tm, tm), tm))

    @pl.when(step == UNPACK_STEPS)
    def _():
        if comm:
            for m in notes:
                m.wait()
            first.relay()
            second.begin()
        else:
            norms[...] = norm_share[...]
        norms_out[...] = norms[...]
        tok_copy.wait()
        gain, bias = gain_row(norms, 0, d), gain_row(norms, 1, d)

        def norm(at):
            xhat, _ = layer_norm_parts(toks[at, :].astype(f32))
            a_out[at, :] = (xhat * gain + bias).astype(bf16)

        each_block(norm)
        cot_copy.wait()
        doc_col[...] = jnp.broadcast_to(docs[...].astype(f32), (128, t)).T[:, :1].astype(jnp.int32)

        def mask(at):
            cots[at, :] = jnp.where(doc_col[at, :] >= 0, cots[at, :].astype(f32), 0.0).astype(bf16)

        each_block(mask)
        a_copy.start()
        d_copy.start()
        if comm:
            first.arrive(4)
        load(0)

        def start(at):
            acc[at, :] = product(at, 0)

        each_block(start)

    @pl.when(step == UNPACK_STEPS + 1)
    def _():
        if comm:
            first.forward()
            first.arrive(7, 8)
        load(*range(1, n - 1))

        def more(at):
            acc[at, :] += product(at, *range(1, n - 1))

        each_block(more)

    @pl.when(step == UNPACK_STEPS + 2)
    def _():
        if comm:
            first.close()
            second.relay()
            first.arrive(9, 10)
        load(n - 1)
        scale = (d // HEADS) ** (-0.5)
        q = d // 2

        def last(at):
            total = acc[at, :] + product(at, n - 1)
            for o in (0, half):
                qkv[at, o : o + q] = (total[:, o : o + q].astype(bf16).astype(f32) * scale).astype(bf16)
                qkv[at, o + q : o + half] = total[:, o + q : o + half].astype(bf16)

        each_block(last)
        out = pltpu.make_async_copy(qkv, qkv_hbm, lsem.at[4 + 2 * n])
        out.start()
        if comm:
            second.forward()
            second.finish()
            first.sent()
        for cp in (a_copy, d_copy, out):
            cp.wait()


def project_qkv(lanes, tok, cot, docs, norm_share, w, o, n, ff, comm):
    t, d = tok.shape
    rows = d // n
    nb = d // 128
    hs = ff // n // 2
    r_in, r_bk = rows * ff // 128, ff // n * nb
    at_in, at_bk = rows * 4 * nb, rows * 4 * nb + r_in
    b_in, b_bk = r_in // UNPACK_STEPS, hs * nb // UNPACK_STEPS
    assert at_in % b_in == 0 and at_bk % b_bk == 0
    up = lambda i: jnp.minimum(i, UNPACK_STEPS - 1)
    me = lambda: group_index(n)
    whole = lambda s: pl.BlockSpec(s, lambda i: (0, 0))
    half = 3 * d // 2
    shapes = [sds((t, d), bf16), sds((t, 3 * d), bf16), sds((d, ff // 2), bf16), sds((ff // 2, d), bf16),
              sds((d, half), bf16), sds((d, half), bf16), sds((d, d // 2), bf16), sds((d, d // 2), bf16), sds((4 * nb, 128), f32),
              sds((t, d), bf16), sds((t, 1), jnp.int32)]
    w_args = [w, norm_share, o, norm_share] if comm else [w[0], w[1], o[0], o[1]]
    outs = pl.pallas_call(
        functools.partial(qkv_kernel, (n, comm)),
        grid=(UNPACK_STEPS + 3,),
        out_shape=shapes,
        in_specs=[
            ANY, whole(norm_share.shape),
            pl.BlockSpec((b_in, 128), lambda i: (at_in // b_in + up(i), 0)),
            pl.BlockSpec((b_bk, 128), lambda i: (at_bk // b_bk + lax.axis_index("core") * UNPACK_STEPS + up(i), 0)),
            ANY, ANY, ANY, ANY, ANY, whole((1, t)),
        ],
        out_specs=[
            ANY, ANY,
            pl.BlockSpec((rows // UNPACK_STEPS, ff // 2), lambda i: (me() * UNPACK_STEPS + up(i), 0)),
            pl.BlockSpec((hs // UNPACK_STEPS, d), lambda i: (me() * UNPACK_STEPS + up(i), 0)),
            ANY, ANY, ANY, ANY, whole((4 * nb, 128)), ANY, whole((t, 1)),
        ],
        scratch_shapes=[pltpu.VMEM((4 * nb, 128), f32), pltpu.VMEM((n, rows, 3 * d), bf16), pltpu.VMEM((t, d), bf16),
                        pltpu.VMEM((t, 3 * d), f32), pltpu.VMEM((t, d), bf16), pltpu.VMEM((t, 3 * d), bf16), pltpu.VMEM((t, d), bf16),
                        dma(5 + 2 * n), dma(25), dma(25)],
        input_output_aliases={4: 4, 6: 6},
        compiler_params=comm_params(1 if comm else None),
        cost_estimate=cost(2 * t * d * 3 * d, 40e6),
        name="qkv",
    )(tok, norm_share, lanes, lanes, *w_args, cot, docs)
    if comm:
        return outs
    return [*outs[:4], w[0], w[1], o[0], o[1], *outs[8:]]


QB = 256


def fill_bias(bias, doc_row, doc_col):
    t = bias.shape[0]
    for r in range(0, t, QB):
        key = r + lax.broadcasted_iota(jnp.int32, (QB, t), 0)
        query = lax.broadcasted_iota(jnp.int32, (QB, t), 1)
        ok = (doc_col[r : r + QB, :] == doc_row[...]) & (key <= query)
        bias[r : r + QB, :] = jnp.where(ok, 0.0, FILL)


def head_lanes(v, h, hd):
    lane = lax.broadcasted_iota(jnp.int32, v.shape, 1)
    return jnp.where((lane >= h * hd) & (lane < (h + 1) * hd), v, jnp.zeros_like(v))


def attend_kernel(cfg, q, k, v, doc_row, doc_col, w_own_in, a_one, d_out, out, lse, w_own, w_oth, a_p, d_p, bias, send, recv):
    hd, comm = cfg
    step = pl.program_id(0)
    last = pl.num_programs(0) - 1
    if comm:
        gather = Gather(w_own, w_oth, send, recv, 0)
        swaps = [hand_over(a_one, a_p, send.at[11], recv.at[11]), hand_over(d_out, d_p, send.at[12], recv.at[12])]

        @pl.when(step == 0)
        def _():
            greet([peer("x"), peer("y"), peer("core")])
            gather.begin()
            for s in swaps:
                s.start()

        @pl.when(step == 4)
        def _():
            gather.relay()

        @pl.when(step == 6)
        def _():
            gather.forward()

    @pl.when(step == 0)
    def _():
        fill_bias(bias, doc_row, doc_col)

    t = q.shape[0]
    vt = v[...].T
    per = 128 // hd
    qs = [head_lanes(q[...], h, hd) for h in range(per)]
    for i in range(t // QB):
        n = (i + 1) * QB
        cols = slice(i * QB, n)
        outs = []
        for h in range(per):
            s = dot_nt(k[:n, :], qs[h][cols, :]) + bias[:n, cols]
            top = jnp.max(s, axis=0, keepdims=True)
            e = jnp.exp(s - top)
            total = jnp.sum(e, axis=0, keepdims=True)
            lse[0, h : h + 1, cols] = top + jnp.log(total)
            o = dot_nn(vt[h * hd : (h + 1) * hd, :n], e.astype(bf16))
            outs.append(o * (1.0 / total))
        out[cols, :] = jnp.concatenate(outs, axis=0).T.astype(bf16)

    if comm:

        @pl.when(step == last)
        def _():
            gather.finish()
            for s in swaps:
                s.wait()


def head_column(d, part):
    pairs = d // 256
    return lambda p: (0, (p // pairs) * 3 * pairs + part * pairs + p % pairs)


def attend(qkv, doc_row, doc_col, w_own, a_one, d_out, d, comm):
    t = qkv.shape[0]
    pairs = d // 128
    hd = d // HEADS
    per = 128 // hd
    col = lambda part: pl.BlockSpec((t, 128), head_column(d, part))
    outs = pl.pallas_call(
        functools.partial(attend_kernel, (hd, comm)),
        grid=(pairs,),
        out_shape=[sds((t, d), bf16), sds((pairs, per, t), f32), sds(w_own.shape, bf16), sds(w_own.shape, bf16),
                   sds((t, d), bf16), sds((t, d), bf16)],
        in_specs=[col(0), col(1), col(2), pl.BlockSpec((1, t), lambda p: (0, 0)), pl.BlockSpec((t, 1), lambda p: (0, 0)),
                  ANY, ANY, ANY],
        out_specs=[pl.BlockSpec((t, 128), lambda p: (0, p)), pl.BlockSpec((1, per, t), lambda p: (p, 0, 0)), ANY, ANY, ANY, ANY],
        scratch_shapes=[pltpu.VMEM((t, t), f32), dma(13), dma(13)],
        input_output_aliases={5: 2},
        compiler_params=comm_params(2 if comm else None),
        cost_estimate=cost(8 * t * t * d, 10e6, t * t * HEADS),
        name="attend",
    )(qkv, qkv, qkv, doc_row, doc_col, w_own, a_one, d_out)
    if comm:
        return outs
    full, oth = spread(w_own)
    return outs[0], outs[1], full, oth, swap_core(a_one), swap_core(d_out)


def spread(own):
    n = lax.axis_size("y") * lax.axis_size("x")
    rows = own.shape[0] // n
    mine = lax.dynamic_slice_in_dim(own, lax.axis_index(("y", "x")) * rows, rows, 0)
    full = lax.all_gather(mine, ("y", "x"), axis=0, tiled=True)
    return full, swap_core(full)


def attend_back_kernel(cfg, q, k, v, dout, att, lse, doc_row, doc_col, part_sum, g_in, dq, dk, dv, sent, red, red_p, part_in, *refs):
    hd, comm = cfg
    bias, dk_acc, dv_acc, stage, lsem, send, recv = refs[:7]
    step = pl.program_id(0)
    pairs = stage.shape[0] // 3

    def hand(p, part):
        wide = 128 * pairs
        cols = pl.ds(pl.multiple_of(part * wide + p * 128, 128), 128)
        i = p * 3 + part
        return hand_over(stage.at[i], sent.at[:, cols], send.at[i], recv.at[i])

    if comm:

        base = 3 * pairs
        mine, keep, held, far, near, mid, total, keep_in = refs[7], refs[12], *refs[13:19]
        fold = Fold(pieces_of(part_sum), pieces_of(mine), *refs[8:12], red, red_p, keep, send, recv, base)
        scat = Scatter(g_in, held, far, near, mid, total, send, recv, base + 4 * PIECES, part_in, keep_in)
        acts = (scat.begin, scat.turn, scat.close, fold.inner, fold.outer, fold.land)

        @pl.when(step == 0)
        def _():
            loads = [pltpu.make_async_copy(part_sum, mine, lsem.at[0]), pltpu.make_async_copy(g_in, held, lsem.at[1])]
            for cp in loads:
                cp.start()
            greet([peer("core"), peer("x"), peer("y")] + Fold.peers())
            run_plan(acts, BACK_PLAN[0])
            for s in range(PIECES):
                fold.begin(s)
            for cp in loads:
                cp.wait()

        @pl.when((step > 0) & (step <= pairs))
        def _():
            for part in range(3):
                hand(step - 1, part).start()

    @pl.when(step == 0)
    def _():
        fill_bias(bias, doc_row, doc_col)

    if comm:
        for at, codes in enumerate(BACK_PLAN[:-1]):
            if codes and at > 0:
                pl.when(step == at)(functools.partial(run_plan, acts, codes))

    t = q.shape[0]
    per = 128 // hd
    scale = hd ** (-0.5)
    kt = k[...].T
    prod = (dout[...].astype(f32) * att[...].astype(f32)).T
    inner = [jnp.sum(prod[h * hd : (h + 1) * hd, :], axis=0, keepdims=True) for h in range(per)]
    qs = [head_lanes(q[...], h, hd) for h in range(per)]
    ds_ = [head_lanes(dout[...], h, hd) for h in range(per)]
    dk_acc[...] = jnp.zeros_like(dk_acc)
    dv_acc[...] = jnp.zeros_like(dv_acc)
    for i in range(t // QB):
        n = (i + 1) * QB
        cols = slice(i * QB, n)
        dqs = []
        for h in range(per):
            qh, dh = qs[h][cols, :], ds_[h][cols, :]
            s = dot_nt(k[:n, :], qh) + bias[:n, cols]
            p = jnp.exp(s - lse[0, h : h + 1, cols])
            dp = dot_nt(v[:n, :], dh)
            g = (p * (dp - inner[h][:, cols])).astype(bf16)
            dv_acc[:n, :] += dot_nn(p.astype(bf16), dh)
            dk_acc[:n, :] += dot_nn(g, qh)
            dqs.append(dot_nn(kt[h * hd : (h + 1) * hd, :n], g))
        dq[cols, :] = (jnp.concatenate(dqs, axis=0).T * scale).astype(bf16)
    dk[...] = dk_acc[...].astype(bf16)
    dv[...] = dv_acc[...].astype(bf16)

    if comm:

        @pl.when(step < pairs)
        def _():
            stage[step * 3] = dq[...]
            stage[step * 3 + 1] = dk[...]
            stage[step * 3 + 2] = dv[...]

        @pl.when(step == 2 * pairs - 1)
        def _():
            for p in range(pairs):
                for part in range(3):
                    hand(p, part).wait()
            run_plan(acts, BACK_PLAN[-1])
            fold.finish()
            scat.finish()


def run_plan(acts, codes):
    for code in codes:
        acts[code // 10](code % 10)


FEED_PLAN = (
    (0, 1),
    (),
    (10, 2),
    (11, 3, 20),
    (12, 4),
    (21, 13, 5),
    (22,),
    (14, 6, 23),
    (15, 7, 24),
    (16,),
    (25,),
    (17, 26),
    (),
    (27,),
    (),
    (),
    (),
)
BACK_PLAN = (
    (0, 1, 2),
    (),
    (10, 3, 11, 4, 30, 31),
    (12, 5, 20, 32, 33, 40),
    (13, 6, 21, 34, 35, 41, 42),
    (14, 7, 22, 36, 37, 43, 44, 50),
    (15, 23, 45, 51, 52, 16, 46),
    (17, 24, 47, 53, 54, 25),
    (26, 27, 55, 56, 57),
)
LAST_PLAN = (
    (),
    (0,),
    (1,),
    (30,),
    (10, 2, 31),
    (11, 3, 32, 40),
    (20, 33, 41),
    (12, 4, 34, 42),
    (21, 35, 43, 50),
    (13, 5, 22, 36, 44, 45, 37, 51),
    (14, 6, 23, 60, 46, 52, 53),
    (15, 7, 24, 61, 62, 70, 47, 54),
    (16, 25, 63, 64, 71, 55),
    (17, 26, 65, 72, 73, 66, 56, 90),
    (27, 67, 74, 75, 80, 91),
    (76, 81, 57, 92),
    (77, 93, 82, 94, 83, 95, 84, 85, 86, 87),
)
PIECES = 8


def attend_back(qkv, dout, att, lse, doc_row, doc_col, part_sum, g_in, d, n, comm):
    t = qkv.shape[0]
    pairs = d // 128
    half = pairs // 2
    hd = d // HEADS
    per = 128 // hd
    turn = lambda p: (p + half) % pairs
    part_in = (g_in.shape[0], g_in.shape[1] // n, g_in.shape[2])
    col = lambda part: pl.BlockSpec((t, 128), lambda p: head_column(d, part)(turn(p)))
    one = pl.BlockSpec((t, 128), lambda p: (0, turn(p)))
    sems = 3 * half + 10 * PIECES
    extra = []
    if comm:
        extra = [pltpu.VMEM(part_sum.shape, bf16)] + fold_scratch(*part_sum.shape) + [dma(PIECES)]
        extra += scatter_scratch(*g_in.shape) + [pltpu.VMEM(part_in, bf16), dma(PIECES)]
    outs = pl.pallas_call(
        functools.partial(attend_back_kernel, (hd, comm)),
        grid=(pairs,),
        out_shape=[sds((t, d), bf16)] * 3 + [sds((t, 3 * d // 2), bf16)] + [sds(part_sum.shape, bf16)] * 2 + [sds(part_in, bf16)],
        in_specs=[col(0), col(1), col(2), one, one, pl.BlockSpec((1, per, t), lambda p: (turn(p), 0, 0)),
                  pl.BlockSpec((1, t), lambda p: (0, 0)), pl.BlockSpec((t, 1), lambda p: (0, 0)), ANY, ANY],
        out_specs=[one, one, one, ANY, ANY, ANY, ANY],
        scratch_shapes=[pltpu.VMEM((t, t), f32), pltpu.VMEM((t, 128), f32), pltpu.VMEM((t, 128), f32),
                        pltpu.VMEM((3 * half, t, 128), bf16), dma(2), dma(sems), dma(sems)] + extra,
        compiler_params=comm_params(6 if comm else None),
        cost_estimate=cost(20 * t * t * d, 16e6, t * t * HEADS),
        name="attend_back",
    )(qkv, qkv, qkv, dout, att, lse, doc_row, doc_col, part_sum, g_in)
    if comm:
        return outs[0], outs[1], outs[2], outs[3], (outs[4], outs[5]), outs[6]
    sent = swap_core(jnp.concatenate([g[:, d // 2 :] for g in outs[:3]], axis=1))
    return outs[0], outs[1], outs[2], sent, both_halves(part_sum), scatter_pieces(g_in)


def both_halves(part_sum):
    full = lax.psum(part_sum.astype(f32), "z").astype(bf16)
    return full, swap_core(full)


def middle_kernel(cfg, att_rows, tok, norms, o_own, o_oth, w_own, w_oth, att_all, bk_own_in, d_out, d_out_p, *refs):
    d, tm, blk, comm = cfg
    (resid, a_two_out, hidden, slope, bk_own, bk_oth, att_p, grad, w, a_two, stage, theirs, douts, lsem, send, recv) = refs
    step = pl.program_id(0)
    last = pl.num_programs(0) - 1
    t = a_two.shape[0]
    pro = t // tm
    half = d // 2
    nb = theirs.shape[0]
    core = lax.axis_index("core")
    loads = [pltpu.make_async_copy(v, douts.at[i], lsem.at[2 + i]) for i, v in enumerate((d_out, d_out_p))]

    def hand(j):
        return hand_over(stage.at[j], theirs.at[j], send.at[12 + j], recv.at[12 + j])

    if comm:
        gather = Gather(bk_own, bk_oth, send, recv, 0)
        swap = hand_over(att_all, att_p, send.at[11], recv.at[11])

        @pl.when(step == 0)
        def _():
            greet([peer("x"), peer("y"), peer("core")])
            gather.begin()
            swap.start()

        @pl.when(step == pro + 4)
        def _():
            gather.relay()

        @pl.when((step > pro) & (step <= pro + nb))
        def _():
            hand(step - pro - 1).start()

    @pl.when(step == 0)
    def _():
        lo = pl.multiple_of(core * half, half)
        hi = pl.multiple_of((1 - core) * half, half)
        cps = [
            pltpu.make_async_copy(o_own, w.at[:, pl.ds(lo, half)], lsem.at[0]),
            pltpu.make_async_copy(o_oth, w.at[:, pl.ds(hi, half)], lsem.at[1]),
        ]
        for cp in cps + loads:
            cp.start()
        for cp in cps:
            cp.wait()

    @pl.when(step < pro)
    def _():
        lo = pl.multiple_of(core * half, half)
        hi = pl.multiple_of((1 - core) * half, half)
        y = dot_nn(att_rows[:, :half], w[pl.ds(lo, half), :]) + dot_nn(att_rows[:, half:], w[pl.ds(hi, half), :])
        r = tok[...].astype(f32) + y
        resid[...] = r
        xhat, _ = layer_norm_parts(r)
        a = (xhat * gain_row(norms, 2, d) + gain_row(norms, 3, d)).astype(bf16)
        a_two_out[...] = a
        a_two[pl.ds(pl.multiple_of(step * tm, tm), tm), :] = a

    @pl.when((step >= pro) & (step < pro + 2 * nb))
    def _():
        pre = dot_nn(a_two[...], pick(step < pro + nb, w_oth[...], w_own[...]))
        cdf = 0.5 + 0.5 * lax.erf(pre * (0.5**0.5))
        pdf = jnp.exp(-0.5 * pre * pre) * 0.3989422804014327
        h = (pre * cdf).astype(bf16)
        hidden[...] = h
        slope[...] = (cdf + pre * pdf).astype(bf16)
        stage[step - pro] = h

    @pl.when(step == pro + 2 * nb)
    def _():
        for cp in loads:
            cp.wait()

    if comm:
        for j in range(nb):

            @pl.when(step == pro + 2 * nb + j)
            def _():
                hand(j).wait_recv()

        @pl.when(step == pro + 2 * nb)
        def _():
            gather.forward()

    @pl.when(step >= pro + 2 * nb)
    def _():
        j = step - pro - 2 * nb
        g = dot_tn(stage[nb + j], douts[0])
        if comm:
            g = g + dot_tn(theirs[j], douts[1])
        store_columns(grad, g)

    if comm:

        @pl.when(step == last)
        def _():
            gather.finish()
            swap.wait()
            for j in range(nb):
                hand(j).wait_send()


def store_columns(ref, g):
    wide = ref.shape[2]
    for p in range(ref.shape[0]):
        ref[p] = g[:, p * wide : (p + 1) * wide].astype(bf16)


def middle(att, tok, norms, o_own, o_oth, w_own, w_oth, bk_own, d_out, d_out_p, comm, tm=256, blk=512):
    t, d = tok.shape
    wide = w_own.shape[1]
    pro, nb = t // tm, wide // blk
    rowi = lambda i: jnp.minimum(i, pro - 1)
    oth = lambda i: jnp.clip(i - pro, 0, nb - 1)
    own = lambda i: jnp.clip(i - pro - nb, 0, nb - 1)
    both = lambda i: jnp.where(i < pro + nb, nb + oth(i), own(i))
    rows = lambda wd: pl.BlockSpec((tm, wd), lambda i: (rowi(i), 0))
    part = lambda count: pltpu.VMEM((count, t, blk), bf16)
    outs = pl.pallas_call(
        functools.partial(middle_kernel, (d, tm, blk, comm)),
        grid=(pro + 3 * nb,),
        out_shape=[sds((t, d), f32), sds((t, d), bf16), sds((t, 2 * wide), bf16), sds((t, 2 * wide), bf16),
                   sds(bk_own.shape, bf16), sds(bk_own.shape, bf16), sds((t, d), bf16), sds((PIECES, wide, d // PIECES), bf16)],
        in_specs=[rows(d), rows(d), pl.BlockSpec(norms.shape, lambda i: (0, 0)), ANY, ANY,
                  pl.BlockSpec((d, blk), lambda i: (0, own(i))), pl.BlockSpec((d, blk), lambda i: (0, oth(i))), ANY, ANY, ANY, ANY],
        out_specs=[rows(d), rows(d), pl.BlockSpec((t, blk), lambda i: (0, both(i))), pl.BlockSpec((t, blk), lambda i: (0, both(i))),
                   ANY, ANY, ANY, pl.BlockSpec((PIECES, blk, d // PIECES), lambda i: (0, jnp.maximum(i - pro - 2 * nb, 0), 0))],
        scratch_shapes=[pltpu.VMEM((d, d), bf16), pltpu.VMEM((t, d), bf16), part(2 * nb), part(nb), pltpu.VMEM((2, t, d), bf16),
                        dma(4), dma(12 + nb), dma(12 + nb)],
        input_output_aliases={8: 4},
        compiler_params=comm_params(3 if comm else None),
        cost_estimate=cost(2 * t * d * d + 8 * t * d * wide, 60e6, 4 * t * wide),
        name="middle",
    )(att, tok, norms, o_own, o_oth, w_own, w_oth, att, bk_own, d_out, d_out_p)
    if comm:
        return outs
    full, other = spread(bk_own)
    hid_p = swap_core(outs[2][:, wide:])
    grad = (dot_tn(outs[2][:, :wide], d_out) + dot_tn(hid_p, d_out_p)).astype(bf16)
    return [*outs[:4], full, other, swap_core(att), in_columns(grad)]


def in_columns(g):
    rows, cols = g.shape
    return g.reshape(rows, PIECES, cols // PIECES).transpose(1, 0, 2)


def feed_kernel(comm, d_out, slope, b_own, b_oth, i_own, i_oth, resid, dout_rows, norms, o_own, o_oth, a_two, g_back, *refs):
    (grad, d_resid, low, d_att, two_norm, sent, part_back, stage, theirs, lhs, dz, wo, lows, lsem, send, recv) = refs[:16]
    step = pl.program_id(0)
    nb = theirs.shape[0]
    tm, d = resid.shape
    pro = dz.shape[0] // tm
    half = d // 2
    np_ = d // 128
    core = lax.axis_index("core")
    lo = pl.multiple_of(core * half, half)
    hi = pl.multiple_of((1 - core) * half, half)
    loads = [
        pltpu.make_async_copy(a_two, lhs.at[0], lsem.at[0]),
        pltpu.make_async_copy(o_own, wo.at[:, pl.ds(lo, half)], lsem.at[1]),
        pltpu.make_async_copy(o_oth, wo.at[:, pl.ds(hi, half)], lsem.at[2]),
    ]

    def hand(j):
        return hand_over(stage.at[j], theirs.at[j], send.at[1 + j], recv.at[1 + j])

    def hand_low(r):
        at = pl.ds(pl.multiple_of(r * tm, tm), tm)
        return hand_over(lows.at[at, :], sent.at[at, :], send.at[1 + nb + r], recv.at[1 + nb + r])

    @pl.when(step == 0)
    def _():
        for cp in loads:
            cp.start()

    if comm:
        swap = hand_over(a_two, lhs.at[1], send.at[0], recv.at[0])
        held, far, near, mid, total, keep = refs[16:22]
        scat = Scatter(g_back, held, far, near, mid, total, send, recv, 1 + nb + pro, part_back, keep)
        acts = (scat.begin, scat.turn, scat.close)

        @pl.when(step == 0)
        def _():
            load = pltpu.make_async_copy(g_back, held, lsem.at[3])
            load.start()
            greet([peer("core"), peer("x"), peer("y")])
            run_plan(acts, FEED_PLAN[0])
            swap.start()
            load.wait()

        for at, codes in enumerate(FEED_PLAN[:-1]):
            if codes and at > 0:
                pl.when(step == at)(functools.partial(run_plan, acts, codes))

        @pl.when((step > 0) & (step <= nb))
        def _():
            hand(step - 1).start()

    @pl.when(step < 2 * nb)
    def _():
        first = step < nb
        g = (dot_nt(d_out[...], pick(first, b_oth[...], b_own[...])) * slope[...].astype(f32)).astype(bf16)
        stage[step] = g
        more = dot_nt(g, pick(first, i_oth[...], i_own[...]))

        @pl.when(step == 0)
        def _():
            dz[...] = more

        @pl.when(step > 0)
        def _():
            dz[...] += more

    @pl.when(step == 2 * nb)
    def _():
        loads[0].wait()
        if comm:
            swap.wait()

    if comm:
        for j in range(nb):

            @pl.when(step == 2 * nb + j)
            def _():
                hand(j).wait()

    @pl.when((step >= 2 * nb) & (step < 3 * nb))
    def _():
        j = step - 2 * nb
        g = dot_tn(lhs[0], stage[nb + j])
        if comm:
            g = g + dot_tn(lhs[1], theirs[j])
        store_columns(grad, g)

    @pl.when(step == 3 * nb)
    def _():
        loads[1].wait()
        loads[2].wait()
        two_norm[...] = jnp.zeros_like(two_norm)

    @pl.when(step >= 3 * nb)
    def _():
        here = pl.ds(pl.multiple_of((step - 3 * nb) * tm, tm), tm)
        dv, g, b = layer_norm_back(resid[...], gain_row(norms, 2, d), dz[here, :])
        two_norm[0:np_, :] += flat_row(g)
        two_norm[np_:, :] += flat_row(b)
        dr = dout_rows[...].astype(f32) + dv
        d_resid[...] = dr
        dl = dr.astype(bf16)
        low[...] = dl
        lows[here, :] = pick(core == 0, dl[:, half:], dl[:, :half])
        d_att[:, :half] = dot_nt(dl, wo[pl.ds(lo, half), :]).astype(bf16)
        d_att[:, half:] = dot_nt(dl, wo[pl.ds(hi, half), :]).astype(bf16)
        if comm:
            hand_low(step - 3 * nb).start()

    if comm:

        @pl.when(step == pl.num_programs(0) - 1)
        def _():
            run_plan(acts, FEED_PLAN[-1])
            scat.finish()
            for r in range(pro):
                hand_low(r).wait()


def feed_back(d_out, slope, b_own, b_oth, i_own, i_oth, resid, norms, o_own, o_oth, a_two, g_back, n, comm, tm=256, blk=512):
    t, d = d_out.shape
    half = b_own.shape[0]
    nb = half // blk
    pro = t // tm
    oth = lambda i: jnp.minimum(i, nb - 1)
    own = lambda i: jnp.clip(i - nb, 0, nb - 1)
    row = lambda i: jnp.clip(i - 3 * nb, 0, pro - 1)
    rows = lambda w: pl.BlockSpec((tm, w), lambda i: (row(i), 0))
    whole = lambda s: pl.BlockSpec(s, lambda i: (0, 0))
    pieces, g_rows, g_cols = g_back.shape
    part = (pieces, g_rows // n, g_cols)
    per = half // PIECES
    extra = scatter_scratch(*g_back.shape) + [pltpu.VMEM(part, bf16), dma(pieces)] if comm else []
    sems = 1 + nb + pro + 6 * pieces
    outs = pl.pallas_call(
        functools.partial(feed_kernel, comm),
        grid=(3 * nb + pro,),
        out_shape=[sds((PIECES, d, per), bf16), sds((t, d), f32), sds((t, d), bf16), sds((t, d), bf16), sds((d // 64, 128), f32),
                   sds((t, d // 2), bf16), sds(part, bf16)],
        in_specs=[whole((t, d)), pl.BlockSpec((t, blk), lambda i: (0, jnp.where(i < nb, nb + i, own(i)))),
                  pl.BlockSpec((blk, d), lambda i: (own(i), 0)), pl.BlockSpec((blk, d), lambda i: (oth(i), 0)),
                  pl.BlockSpec((d, blk), lambda i: (0, own(i))), pl.BlockSpec((d, blk), lambda i: (0, oth(i))),
                  rows(d), rows(d), whole(norms.shape), ANY, ANY, ANY, ANY],
        out_specs=[pl.BlockSpec((blk // per, d, per), lambda i: (jnp.clip(i - 2 * nb, 0, nb - 1), 0, 0)), rows(d), rows(d), rows(d),
                   whole((d // 64, 128)), ANY, ANY],
        scratch_shapes=[pltpu.VMEM((2 * nb, t, blk), bf16), pltpu.VMEM((nb, t, blk), bf16), pltpu.VMEM((2, t, d), bf16),
                        pltpu.VMEM((t, d), f32), pltpu.VMEM((d, d), bf16), pltpu.VMEM((t, d // 2), bf16), dma(4), dma(sems), dma(sems)]
        + extra,
        compiler_params=comm_params(4 if comm else None, 62),
        cost_estimate=cost(12 * t * d * half + 2 * t * d * d, 60e6),
        name="feed_back",
    )(d_out, slope, b_own, b_oth, i_own, i_oth, resid, d_out, norms, o_own, o_oth, a_two, g_back)
    if comm:
        return outs
    core = lax.axis_index("core")
    other = lax.dynamic_slice_in_dim(outs[2], (1 - core) * (d // 2), d // 2, 1)
    d_pre = pre_values(d_out, slope, b_own, b_oth)
    g_in = dot_tn(a_two, d_pre[:, :half]) + dot_tn(swap_core(a_two), swap_core(d_pre[:, half:]))
    return [in_columns(g_in.astype(bf16)), *outs[1:5], swap_core(other), scatter_pieces(g_back)]


def pre_values(d_out, slope, own, oth):
    both = jnp.concatenate([dot_nt(d_out, own), dot_nt(d_out, oth)], axis=1)
    return (both * slope.astype(f32)).astype(bf16)


def scatter_pieces(g):
    return lax.psum_scatter(g, ("y", "x"), scatter_dimension=1, tiled=True)


def last_kernel(cfg, g1, g2, g3, theirs, low, low_p, dq, dk, dv, tok, d_resid, norms, h_own, h_oth, resid, doc, two_norm,
                a_one, a_one_p, att, att_p, w_own, w_oth, b_own, b_oth, part_in, *refs):
    d, comm = cfg
    out, mixed, red_in, red_in_p, red_at, red_at_p, sums, w, wb, parts, held, lsem, total = refs[:13]
    refs = refs[1:]
    step = pl.program_id(0)
    last = pl.num_programs(0) - 1
    np_ = held.shape[0]
    pro = (last - np_) // 2
    half = 3 * d // 2
    q = d // 2
    hb = b_own.shape[0]
    nb = d // 128
    core = lax.axis_index("core")
    early = [pltpu.make_async_copy(a, wb.at[pl.ds(i * d, d), :], lsem.at[i]) for i, a in enumerate((a_one, a_one_p, att, att_p))]
    mids = [
        pltpu.make_async_copy(w_own, w.at[:, pl.ds(0, half)], lsem.at[4]),
        pltpu.make_async_copy(w_oth, w.at[:, pl.ds(half, half)], lsem.at[5]),
    ]
    late = [
        pltpu.make_async_copy(b_own, wb.at[pl.ds(0, hb), :], lsem.at[6]),
        pltpu.make_async_copy(b_oth, wb.at[pl.ds(hb, hb), :], lsem.at[7]),
    ]
    if comm:
        send, recv, mine_in, fi, sc, fa, vec, box, k_in, k_at = (
            refs[12], refs[13], refs[14], refs[15:19], refs[19:22], refs[22:27], refs[27], refs[28], refs[29], refs[30]
        )
        fold_in = Fold(
            pieces_of(part_in), pieces_of(mine_in), *fi, red_in, red_in_p, k_in, send, recv, 0
        )
        scat = Scatter(held, held, *sc, fa[0], send, recv, 4 * PIECES)
        mine_at = pieces_of(fa[0])
        fold_at = Fold(mine_at, mine_at, *fa[1:5], red_at, red_at_p, k_at, send, recv, 4 * PIECES + 6 * np_)
        base = 4 * PIECES + 10 * np_

        def note(i, src, dst, to):
            return pltpu.make_async_remote_copy(
                src_ref=src, dst_ref=dst, send_sem=send.at[base + i], recv_sem=recv.at[base + i], device_id=to, device_id_type=MESH
            )

        near, far = Fold.peers()
        notes = [
            note(0, vec.at[0], box.at[0], peer("x")),
            note(1, vec.at[1], box.at[1], peer("y")),
            note(2, vec.at[2], box.at[2], peer("core")),
            note(3, vec.at[3], box.at[3], near),
            note(4, vec.at[4], box.at[4], far),
            note(5, vec.at[5], vec.at[5], near),
        ]

        def norm_sum(k):
            if k < 3:
                notes[k].wait_recv()
                vec[k + 1] = vec[k] + box[k]
                if k < 2:
                    notes[k + 1].start()
                else:
                    pl.when(fold_in.end)(notes[3].start)
            elif k < 5:

                @pl.when(fold_in.mid)
                def _():
                    notes[k].wait_recv()
                    vec[k + 1] = vec[k] + box[k]
                    notes[k + 1].start()

            else:
                pl.when(fold_in.end)(notes[5].wait_recv)

        def settle(s):
            scat.close(s)
            fold_at.begin(s)

        acts = (scat.begin, scat.turn, settle, fold_in.inner, fold_in.outer, fold_in.land, fold_at.inner, fold_at.outer,
                fold_at.land, norm_sum)

    @pl.when(step == 0)
    def _():
        for cp in early + mids:
            cp.start()
        if comm:
            load = pltpu.make_async_copy(part_in, mine_in, lsem.at[8])
            load.start()
            greet([peer("core"), peer("x"), peer("y")] + Fold.peers())
            for s in range(PIECES):
                fold_in.begin(s)
            load.wait()
        for cp in early:
            cp.wait()
        parts[0 : 2 * nb, :] = jnp.zeros((2 * nb, 128), f32)
        parts[2 * nb :, :] = two_norm[...]

    if comm:
        for k, codes in enumerate(LAST_PLAN[:-1]):
            if codes:
                pl.when(step == k)(functools.partial(run_plan, acts, codes))

    per = q // g1.shape[1]

    @pl.when(step < 3 * per)
    def _():
        g = pick(step < per, g1[...], pick(step < 2 * per, g2[...], g3[...]))
        acc = dot_tn(wb[0:d, :], g) + dot_tn(wb[d : 2 * d, :], theirs[...])
        held[step] = acc.astype(bf16)

    @pl.when((step >= 3 * per) & (step < np_))
    def _():
        lo = pl.ds(pl.multiple_of(core * q, q), q)
        hi = pl.ds(pl.multiple_of((1 - core) * q, q), q)
        own = dot_tn(wb[2 * d : 3 * d, :q], low[...]) + dot_tn(wb[3 * d :, q:], low_p[...])
        held[step, lo, :] = own.astype(bf16)
        other = dot_tn(wb[2 * d : 3 * d, q:], low[...]) + dot_tn(wb[3 * d :, :q], low_p[...])
        held[step, hi, :] = other.astype(bf16)

    @pl.when(step == np_)
    def _():
        for cp in late:
            cp.start()
        for cp in mids:
            cp.wait()

    @pl.when((step >= np_) & (step < np_ + pro))
    def _():
        both = jnp.concatenate([g[:, :q] for g in (dq, dk, dv)] + [g[:, q:] for g in (dq, dk, dv)], axis=1)
        dz = dot_nt(both, w[...])
        grad, g, b = layer_norm_back(tok[...].astype(f32), gain_row(norms, 0, d), dz)
        parts[0:nb, :] += flat_row(g)
        parts[nb : 2 * nb, :] += flat_row(b)
        out[...] = (d_resid[...] + grad).astype(bf16)

    @pl.when(step == np_ + pro)
    def _():
        for cp in late:
            cp.wait()
        if comm:
            vec[0] = parts[...]
            notes[0].start()

    @pl.when((step >= np_ + pro) & (step < last))
    def _():
        total[...] = resid[...]
        chunk = hb // 4

        @pl.loop(0, 4)
        def _(i):
            at = pl.ds(pl.multiple_of(i * chunk, chunk), chunk)
            beyond = pl.ds(pl.multiple_of(hb + i * chunk, chunk), chunk)
            total[...] += dot_nn(h_own[:, at], wb[at, :]) + dot_nn(h_oth[:, at], wb[beyond, :])

        mixed[...] = jnp.where(doc[...] >= 0, total[...], 0.0).astype(bf16)

    @pl.when(step == last)
    def _():
        if comm:
            run_plan(acts, LAST_PLAN[-1])
            fold_in.finish()
            scat.finish()
            fold_at.finish()
            for i in (0, 1, 2):
                notes[i].wait_send()
            pl.when(fold_in.end)(notes[3].wait_send)

            @pl.when(fold_in.mid)
            def _():
                notes[4].wait_send()
                notes[5].wait_send()

            sums[...] = vec[5]
        else:
            sums[...] = parts[...]
            cp = pltpu.make_async_copy(held, red_at, lsem.at[0])
            cp.start()
            cp.wait()


def flat_row(v):
    return jnp.concatenate([v[:, i * 128 : (i + 1) * 128] for i in range(v.shape[1] // 128)], axis=0)


def last_grad(grads3, theirs, low, low_p, tok, d_resid, norms, hidden, resid, doc_col, two_norm, a_one, a_one_p, att, att_p,
              own, oth, b_own, b_oth, part_in, n, comm, tm=256, wide=256):
    t, d = tok.shape
    pro = t // tm
    half = b_own.shape[0]
    q = d // 2
    per = q // wide
    np_ = 4 * per
    one = lambda w, c=0: pl.BlockSpec((tm, w), lambda i: (jnp.clip(i - np_, 0, pro - 1), c))
    two = lambda w, c=0: pl.BlockSpec((tm, w), lambda i: (jnp.clip(i - np_ - pro, 0, pro - 1), c))
    whole = lambda a: pl.BlockSpec(a.shape, lambda i: (0, 0))
    col = lambda k, count: pl.BlockSpec((t, wide), lambda i: (0, jnp.clip(i - k * per, 0, count - 1)))
    low_col = pl.BlockSpec((t, wide), lambda i: (0, lax.axis_index("core") * per + jnp.clip(i - 3 * per, 0, per - 1)))
    nv = 4 * d // 128
    pieced = part_in.shape
    share = (np_, d // n if comm else d, wide)
    slots = 4 * PIECES + 10 * np_ + 6
    extra = []
    if comm:
        extra = [dma(slots), dma(slots), pltpu.VMEM(part_in.shape, bf16)] + fold_scratch(*part_in.shape)
        extra += scatter_scratch(np_, d, wide)[1:] + [pltpu.VMEM(share, bf16)] * 5
        extra += [pltpu.VMEM((6, nv, 128), f32), pltpu.VMEM((5, nv, 128), f32), dma(PIECES), dma(np_)]
    return pl.pallas_call(
        functools.partial(last_kernel, (d, comm)),
        grid=(np_ + 2 * pro + 1,),
        out_shape=[sds((t, d), bf16), sds((t, d), bf16)] + [sds(pieced, bf16)] * 2 + [sds(share, bf16)] * 2 + [sds((nv, 128), f32)],
        in_specs=[col(0, per), col(1, per), col(2, per), col(0, 3 * per), low_col, col(3, per)]
        + [one(d)] * 5 + [whole(norms), two(half), two(half, 1), two(d), two(1), whole(two_norm)] + [ANY] * 9,
        out_specs=[one(d), two(d), ANY, ANY, ANY, ANY, pl.BlockSpec((nv, 128), lambda i: (0, 0))],
        scratch_shapes=[pltpu.VMEM((d, 3 * d), bf16), pltpu.VMEM((4 * d, d), bf16), pltpu.VMEM((nv, 128), f32),
                        pltpu.VMEM((np_, d, wide), bf16), dma(9), pltpu.VMEM((tm, d), f32)] + extra,
        compiler_params=comm_params(7 if comm else None, 63),
        cost_estimate=cost(14 * t * d * d + 4 * t * d * half, 60e6),
        name="last_grad",
    )(*grads3, theirs, low, low_p, *grads3, tok, d_resid, norms, hidden, hidden, resid, doc_col, two_norm,
      a_one, a_one_p, att, att_p, own, oth, b_own, b_oth, part_in)


def adam_update(g_ref, m1, m2, wg, st, mn):
    rows = g_ref.shape[0]
    step = min(rows, 256)

    @pl.loop(0, rows // step)
    def _(i):
        at = pl.ds(pl.multiple_of(i * step, 8), step)
        g = g_ref[at, :]
        first = BETA_ONE * m1[at, :] + (1.0 - BETA_ONE) * g
        second_hat = (BETA_TWO / (1.0 - BETA_TWO**STEPS)) * m2[at, :] + ((1.0 - BETA_TWO) / (1.0 - BETA_TWO**STEPS)) * g * g
        wg[at, :] = g
        st[at, :] = (-RATE / (1.0 - BETA_ONE**STEPS)) * first / (second_hat * lax.rsqrt(second_hat) + ADAM_EPS)
        mn[at, :] = first


def adam_kernel(plan, inv_root, own, oth, m1, m2, *refs):
    wg, st, mn, flat = refs[-4:]
    rows, stride, places = plan
    first = lax.axis_index("core") == 0
    wide = own.shape[2]
    for col, lo, hi in places:
        p, c = col // wide, col % wide
        a = own[p, :, c : c + 128].astype(f32) * inv_root
        b = oth[p, :, c : c + 128].astype(f32) * inv_root
        flat[pl.ds(lo, rows, stride=stride), :] = pick(first, a, b)
        flat[pl.ds(hi, rows, stride=stride), :] = pick(first, b, a)
    adam_update(flat, m1, m2, wg, st, mn)


def adam_columns(own, oth, at, count, m1, m2, prev, inv_root, first_row, rows, places):
    total, wide = own.shape[1:]
    nb = 2 * count * wide // 128
    blk = rows * nb
    assert first_row % blk == 0
    base = first_row // blk
    half = pl.BlockSpec((count, rows, wide), lambda i: (at, i, 0))
    flat = pl.BlockSpec((blk, 128), lambda i: (base + i, 0))
    kernel = functools.partial(adam_kernel, (rows, nb, places), inv_root)
    return adam_call(kernel, (total // rows,), own, oth, m1, m2, prev, half, flat, blk, "adam")


def adam_call(kernel, grid, own, oth, m1, m2, prev, half, flat, blk, name):
    return pl.pallas_call(
        kernel,
        grid=grid,
        out_shape=[sds(m1.shape, f32)] * 3,
        in_specs=[half, half, flat, flat] + [ANY] * len(prev),
        out_specs=[flat] * 3,
        scratch_shapes=[pltpu.VMEM((blk, 128), f32)],
        input_output_aliases={4 + i: i for i in range(len(prev))},
        compiler_params=params(),
        cost_estimate=cost(0, own.size * 2 * 22),
        name=name,
    )(own, oth, m1, m2, *prev)


def adam_rows_kernel(inv_root, own, oth, m1, m2, *refs):
    wg, st, mn, flat = refs[-4:]
    g = pick(pl.program_id(0) == lax.axis_index("core"), own[...], oth[...]).astype(f32) * inv_root
    rows, width = g.shape
    nb = width // 128
    for w in range(nb):
        flat[pl.ds(w, rows, stride=nb), :] = g[:, w * 128 : (w + 1) * 128]
    adam_update(flat, m1, m2, wg, st, mn)


def adam_rows_halves(own, oth, m1, m2, prev, inv_root, first_row):
    count, width = own.shape
    rows = count // 4
    blk = rows * width // 128
    base = first_row // blk
    half = pl.BlockSpec((rows, width), lambda h, i: (i, 0))
    flat = pl.BlockSpec((blk, 128), lambda h, i: (base + h * 4 + i, 0))
    kernel = functools.partial(adam_rows_kernel, inv_root)
    return adam_call(kernel, (2, 4), own, oth, m1, m2, prev, half, flat, blk, "adam_rows")


def adam_tail_kernel(g, m1, m2, p1, p2, p3, wg, st, mn):
    adam_update(g, m1, m2, wg, st, mn)


def adam_tail(g, m1, m2, prev, first_row):
    rows = 8
    assert first_row % rows == 0 and g.shape[0] <= rows
    g = jnp.pad(g, ((0, rows - g.shape[0]), (0, 0)))
    flat = pl.BlockSpec((rows, 128), lambda i: (first_row // rows, 0))
    return pl.pallas_call(
        adam_tail_kernel,
        grid=(1,),
        out_shape=[sds(m1.shape, f32)] * 3,
        in_specs=[pl.BlockSpec((rows, 128), lambda i: (0, 0)), flat, flat] + [ANY] * 3,
        out_specs=[flat] * 3,
        input_output_aliases={3: 0, 4: 1, 5: 2},
        name="adam_norms",
    )(g, m1, m2, *prev)


BLOCK = 4096


def adam_all_kernel(cfg, b_own, b_oth, i_own, i_oth, a_own, a_oth, norm, m1, m2, wg, st, mn, flat, later):
    inv_root, at_in, at_at, counts = cfg
    step = pl.program_id(0)
    core = lax.axis_index("core")
    first = core == 0
    n_back, n_in, n_at = counts

    @pl.when(step < n_back)
    def _():
        mine = step // (n_back // 2) == core
        pieces, rows, wide = b_own.shape
        for w in range(pieces * wide // 128):
            p, c = w * 128 // wide, w * 128 % wide
            g = pick(mine, b_own[p, :, c : c + 128], b_oth[p, :, c : c + 128])
            flat[pl.ds(w, rows, stride=pieces * wide // 128), :] = g.astype(f32) * inv_root

    def spread_columns(dst, own, oth, places):
        rows, wide = own.shape[1:]
        for col, lo, hi, stride in places:
            p, c = col // wide, col % wide
            a = own[p, :, c : c + 128].astype(f32) * inv_root
            b = oth[p, :, c : c + 128].astype(f32) * inv_root
            dst[pl.ds(lo, rows, stride=stride), :] = pick(first, a, b)
            dst[pl.ds(hi, rows, stride=stride), :] = pick(first, b, a)

    @pl.when((step >= n_back) & (step < n_back + n_in))
    def _():
        spread_columns(flat, i_own, i_oth, at_in)

    for k, places in enumerate(at_at):
        pl.when(step == k)(functools.partial(spread_columns, later, a_own, a_oth, places))

    @pl.when((step >= n_back + n_in) & (step < n_back + n_in + n_at))
    def _():
        at = pl.multiple_of((step - n_back - n_in) * BLOCK, BLOCK)
        flat[...] = later[pl.ds(at, BLOCK), :]

    @pl.when(step == n_back + n_in + n_at)
    def _():
        per = norm.shape[0] // 4
        at = pl.multiple_of(lax.axis_index(("y", "x")) * per, per)
        flat[0:per, :] = norm[pl.ds(at, per), :] * inv_root

    adam_update(flat, m1, m2, wg, st, mn)


def adam_all(back, inner, attention, norm, m1, m2, inv_root, places):
    at_in, at_qkv, at_out = places
    b_np, b_rows, b_wide = back[0].shape
    i_np, i_rows, i_wide = inner[0].shape
    np_, a_rows, wide = attention[0].shape
    n_back = 2 * b_np * b_rows * b_wide // 128 // BLOCK
    n_in = 2 * i_np * i_rows * i_wide // 128 // BLOCK
    n_at = 2 * np_ * a_rows * wide // 128 // BLOCK
    lots = np_ // (n_back + n_in)
    assert np_ == lots * (n_back + n_in) and m1.shape[0] == (n_back + n_in + n_at) * BLOCK + 8
    s_in, s_qkv, s_out = 2 * i_np * i_wide // 128, 2 * len(at_qkv), 2 * len(at_out)
    edge = a_rows * s_qkv
    at_at = [[] for _ in range(n_back + n_in)]
    for col, lo, hi in at_qkv:
        at_at[col // wide // lots].append((col % (wide * lots), lo, hi, s_qkv))
    for col, lo, hi in at_out:
        col += len(at_qkv) * 128
        at_at[col // wide // lots].append((col % (wide * lots), edge + lo, edge + hi, s_out))
    cfg = (inv_root, [(c, lo, hi, s_in) for c, lo, hi in at_in], at_at, (n_back, n_in, n_at))
    after_at, after_in = n_at, n_at + n_in

    def where(i):
        back_or_in = jnp.where(i < n_back, after_in + i, after_at + i - n_back)
        return jnp.where(i < n_back + n_in, back_or_in, jnp.where(i < n_back + n_in + n_at, i - n_back - n_in, i))

    flat = pl.BlockSpec((BLOCK, 128), lambda i: (where(i), 0))
    b_spec = pl.BlockSpec((b_np, 2 * b_rows // n_back, b_wide), lambda i: (0, jnp.minimum(i, n_back - 1) % (n_back // 2), 0))
    i_spec = pl.BlockSpec((i_np, i_rows // n_in, i_wide), lambda i: (0, jnp.clip(i - n_back, 0, n_in - 1), 0))
    a_spec = pl.BlockSpec((lots, a_rows, wide), lambda i: (jnp.minimum(i, n_back + n_in - 1), 0, 0))
    return pl.pallas_call(
        functools.partial(adam_all_kernel, cfg),
        grid=(n_back + n_in + n_at + 1,),
        out_shape=[sds(m1.shape, f32)] * 3,
        in_specs=[b_spec, b_spec, i_spec, i_spec, a_spec, a_spec, pl.BlockSpec(norm.shape, lambda i: (0, 0)), flat, flat],
        out_specs=[flat] * 3,
        scratch_shapes=[pltpu.VMEM((BLOCK, 128), f32), pltpu.VMEM((n_at * BLOCK, 128), f32)],
        compiler_params=params(),
        cost_estimate=cost(0, m1.size * 22),
        name="adam_all",
    )(*back, *inner, *attention, norm, m1, m2)


def after(x, *deps):
    return lax.optimization_barrier((x, deps))[0]


def body(n, nz, tokens, cotangent, doc_ids, master, moment_one, moment_two):
    t, d = tokens.shape
    ff = (master.shape[0] * n - 4 * d) // (2 * d) - 2 * d
    me = lax.axis_index(("y", "x"))
    rows = d // n
    comm = n == 4 and nz == 4

    lanes = master.reshape(-1, 128)
    w, o, norm_share = unpack_first(lanes, n, d, ff)
    doc_row = doc_ids.reshape(1, t)
    if not comm:
        w, o = spread(w), spread(o)
        norm_share = lax.all_gather(master[-(4 * d // n) :].astype(bf16), ("y", "x"), axis=0, tiled=True)
        norm_share = norm_share.astype(f32).reshape(-1, 128)
    a_one, qkv, in_own, bk_own, w_own, w_oth, o_own, o_oth, norms, d_out, doc_col = project_qkv(
        lanes, tokens, cotangent, doc_row, norm_share, w, o, n, ff, comm
    )
    att, lse, in_own, in_oth, a_one_p, d_out_p = attend(qkv, doc_row, doc_col, in_own, a_one, d_out, d, comm)
    resid, a_two, hidden, slope, bk_own, bk_oth, att_p, g_back = middle(
        att, tokens, norms, o_own, o_oth, in_own, in_oth, bk_own, d_out, d_out_p, comm
    )
    g_in, d_resid, low, d_att, two_norm, low_p, part_back = feed_back(
        d_out, slope, bk_own, bk_oth, in_own, in_oth, resid, norms, o_own, o_oth, a_two, g_back, n, comm
    )
    dq, dk, dv, dqkv_p, red_back, part_in = attend_back(qkv, d_att, att, lse, doc_row, doc_col, part_back, g_in, d, n, comm)
    input_grad, mixed, red_in, red_in_p, red_at, red_at_p, sums = last_grad(
        [dq, dk, dv], dqkv_p, low, low_p, tokens, d_resid, norms, hidden, resid, doc_col, two_norm, a_one, a_one_p, att, att_p,
        w_own, w_oth, bk_own, bk_oth, part_in, n, comm,
    )
    red_in, red_at = (red_in, red_in_p), (red_at, red_at_p)
    if not comm:
        red_in, red_at = both_halves(part_in), both_halves(scatter_pieces(red_at[0]))
        sums = lax.psum(sums, ("z", "core", "y", "x"))

    inv_root = float(t * n * nz * 2) ** (-0.5)
    m1, m2 = moment_one.reshape(-1, 128), moment_two.reshape(-1, 128)
    nb = d // 128
    half = nb // 2
    hs = ff // n // 2
    r_qkv, r_out, r_in = rows * 3 * nb, rows * nb, rows * ff // 128
    back_at = r_qkv + r_out + r_in
    at_in = [(hs * j + q * 128, (2 * hs * j) // 128 + q, (2 * hs * j + hs) // 128 + q) for j in range(n) for q in range(hs // 128)]
    at_qkv = [((p * half + w) * 128, p * nb + w, p * nb + w + half) for p in range(3) for w in range(half)]
    at_out = [(w * 128, w, w + half) for w in range(half)]
    if comm:
        outs = adam_all(red_back, red_in, red_at, sums, m1, m2, inv_root, (at_in, at_qkv, at_out))
    else:
        plain = lambda v: v.transpose(1, 0, 2).reshape(v.shape[1], -1)
        count = red_at[0].shape[0]
        outs = adam_rows_halves(plain(red_back[0]), plain(red_back[1]), m1, m2, [], inv_root, back_at)
        outs = adam_columns(*red_in, 0, red_in[0].shape[0], m1, m2, outs, inv_root, r_qkv + r_out, rows // 8, at_in)
        outs = adam_columns(*red_at, 0, 3 * count // 4, m1, m2, outs, inv_root, 0, rows // 8, at_qkv)
        outs = adam_columns(*red_at, 3, count // 4, m1, m2, outs, inv_root, r_qkv, rows // 2, at_out)
        per = 4 * nb // n
        norm_part = lax.dynamic_slice_in_dim(sums, group_index(n) * per, per, 0) * inv_root
        outs = adam_tail(norm_part, m1, m2, outs, back_at + ff // n * nb)
    weight_grad, step, moment = [o.reshape(-1) for o in outs]
    return mixed, input_grad, weight_grad, step, moment


def solution(mesh):
    dp, n = mesh.shape["dp"], mesh.shape["group"]
    fine = Mesh(mesh.devices.reshape(dp // 2, 2, n // 2, 2), ("z", "core", "y", "x"))
    tok = ("z", "core", "y", "x")
    flat = P(("y", "x"))
    in_specs = (P(tok, None), P(tok, None), P(tok), flat, flat, flat)
    out_specs = (P(tok, None), P(tok, None), flat, flat, flat)
    return jax.shard_map(
        functools.partial(body, n, dp // 2), mesh=fine, in_specs=in_specs, out_specs=out_specs, check_vma=False
    )
```

```python
import functools

import jax
import jax.numpy as jnp
from jax import lax
from jax.experimental import pallas as pl
from jax.experimental.pallas import tpu as pltpu
from jax.sharding import Mesh
from jax.sharding import PartitionSpec as P

HEADS = 16
EPS = 1e-05
FILL = -1e30
BETA_ONE = 0.9
BETA_TWO = 0.999
RATE = 0.001
ADAM_EPS = 1e-08
STEPS = 100.0
VMEM_MB = 60

f32 = jnp.float32
bf16 = jnp.bfloat16
ANY = pl.BlockSpec(memory_space=pl.ANY)


def params(limit=VMEM_MB):
    return pltpu.CompilerParams(vmem_limit_bytes=limit << 20)


def cost(flops, nbytes, trans=0):
    return pl.CostEstimate(flops=int(flops), bytes_accessed=int(nbytes), transcendentals=int(trans))


def sds(shape, dtype):
    return jax.ShapeDtypeStruct(shape, dtype)


def dot_nn(a, b):
    return jnp.dot(a, b, preferred_element_type=f32)


def dot_nt(a, b):
    return lax.dot_general(a, b, (((1,), (1,)), ((), ())), preferred_element_type=f32)


def dot_tn(a, b):
    return lax.dot_general(a, b, (((0,), (0,)), ((), ())), preferred_element_type=f32)


def pick(flag, a, b):
    return jnp.where(flag, a, b)


MESH = pl.DeviceIdType.MESH


def peer(*axes):
    return {a: 1 - lax.axis_index(a) for a in axes}


def greet_start(peers):
    barrier = pltpu.get_barrier_semaphore()
    for p in peers:
        pl.semaphore_signal(barrier, inc=1, device_id=p, device_id_type=MESH)


def greet_end(peers):
    pl.semaphore_wait(pltpu.get_barrier_semaphore(), len(peers))


def greet(peers):
    greet_start(peers)
    greet_end(peers)


def member():
    return lax.axis_index("y") * 2 + lax.axis_index("x")


class Gather:
    COUNT = 11

    def __init__(self, own, oth, send, recv, base, mine=None):
        rows = own.shape[0] // 4
        half = rows // 2
        x, y = lax.axis_index("x"), lax.axis_index("y")
        share = [y * 2 + x, y * 2 + 1 - x, (1 - y) * 2 + x, (1 - y) * 2 + 1 - x]
        self.rows = [pl.ds(pl.multiple_of(k * rows, 8), rows) for k in share]

        def move(i, k, off, count, dst, to):
            at = pl.ds(pl.multiple_of(share[k] * rows + off, 8), count)
            here = own.at[at, :] if mine is None or k else mine.at[pl.ds(off, count), :]
            return pltpu.make_async_remote_copy(
                src_ref=here, dst_ref=dst.at[at, :],
                send_sem=send.at[base + i], recv_sem=recv.at[base + i], device_id=peer(to), device_id_type=MESH,
            )

        self.moves = [
            move(0, 0, 0, half, own, "x"),
            move(1, 0, half, half, own, "x"),
            move(2, 0, half, half, own, "y"),
            move(3, 0, 0, half, own, "y"),
            move(4, 0, 0, rows, oth, "core"),
            move(5, 1, 0, half, own, "y"),
            move(6, 2, half, half, own, "x"),
            move(7, 1, 0, rows, oth, "core"),
            move(8, 2, 0, rows, oth, "core"),
            move(9, 3, 0, half, oth, "core"),
            move(10, 3, half, half, oth, "core"),
        ]

    def begin(self):
        for i in (0, 2, 1, 3, 4):
            self.moves[i].start()

    def relay(self):
        self.moves[0].wait_recv()
        self.moves[5].start()
        self.moves[2].wait_recv()
        self.moves[6].start()

    def forward(self):
        self.moves[1].wait_recv()
        self.moves[7].start()
        self.moves[3].wait_recv()
        self.moves[8].start()

    def close(self):
        self.moves[5].wait_recv()
        self.moves[9].start()
        self.moves[6].wait_recv()
        self.moves[10].start()

    def arrive(self, *which):
        for i in which:
            self.moves[i].wait_recv()

    def sent(self):
        for m in self.moves:
            m.wait_send()

    def finish(self):
        self.close()
        self.arrive(4, 7, 8, 9, 10)
        self.sent()


def hand_over(src, dst, send, recv):
    return pltpu.make_async_remote_copy(
        src_ref=src, dst_ref=dst, send_sem=send, recv_sem=recv, device_id=peer("core"), device_id_type=MESH
    )


def add_up(dst, a, b):
    dst[...] = a[...] + b[...]


class Fold:
    def __init__(self, source, mine, inbox, cross, stage, total, red, theirs, keep, send, recv, base):
        self.pieces = len(mine)
        self.out = [pltpu.make_async_copy(total.at[s], red.at[s], keep.at[s]) for s in range(self.pieces)]
        z = lax.axis_index("z")
        self.end = (z == 0) | (z == 3)
        self.mid = (z == 1) | (z == 2)
        near, far = self.peers()
        self.mine, self.inbox, self.across, self.stage, self.total = mine, inbox, cross, stage, total

        def move(s, kind, src, dst, to):
            i = base + 4 * s + kind
            return pltpu.make_async_remote_copy(
                src_ref=src, dst_ref=dst, send_sem=send.at[i], recv_sem=recv.at[i], device_id=to, device_id_type=MESH
            )

        every = range(self.pieces)
        self.fold = [move(s, 0, source[s], inbox.at[s], near) for s in every]
        self.cross = [move(s, 1, stage.at[s], cross.at[s], far) for s in every]
        self.unfold = [move(s, 2, total.at[s], total.at[s], near) for s in every]
        self.core = [move(s, 3, total.at[s], theirs.at[s], peer("core")) for s in every]

    @staticmethod
    def peers():
        z = lax.axis_index("z")
        return [{"z": z + 1 - 2 * (z % 2)}, {"z": 3 - z}]

    def begin(self, s):
        pl.when(self.end)(self.fold[s].start)

    def inner(self, s):
        @pl.when(self.mid)
        def _():
            self.fold[s].wait_recv()
            add_up(self.stage.at[s], self.mine[s], self.inbox.at[s])
            self.cross[s].start()

    def outer(self, s):
        @pl.when(self.mid)
        def _():
            self.cross[s].wait_recv()
            add_up(self.total.at[s], self.stage.at[s], self.across.at[s])
            self.unfold[s].start()
            self.core[s].start()
            self.out[s].start()

    def land(self, s):
        @pl.when(self.end)
        def _():
            self.unfold[s].wait_recv()
            self.core[s].start()
            self.out[s].start()

    def finish(self):
        @pl.when(self.end)
        def _():
            for m in self.fold:
                m.wait_send()

        @pl.when(self.mid)
        def _():
            for m in self.cross + self.unfold:
                m.wait_send()

        for m in self.core + self.out:
            m.wait()


def pieces_of(ref):
    return [ref.at[i] for i in range(ref.shape[0])]


def fold_scratch(pieces, rows, cols):
    return [pltpu.VMEM((pieces, rows, cols), bf16)] * 4


class Scatter:
    def __init__(self, source, held, far, near, mid, total, send, recv, base, out=None, keep=None):
        pieces, rows, _ = held.shape
        self.out = [] if out is None else [pltpu.make_async_copy(total.at[s], out.at[s], keep.at[s]) for s in range(pieces)]
        block = rows // 4
        half = block // 2
        x, y = lax.axis_index("x"), lax.axis_index("y")
        me, over_x, over_y, both = y * 2 + x, y * 2 + 1 - x, (1 - y) * 2 + x, (1 - y) * 2 + 1 - x
        self.pieces, self.held, self.far, self.near, self.mid, self.total, self.half = pieces, held, far, near, mid, total, half

        def at(share, part):
            return pl.ds(pl.multiple_of(share * block + part * half, half), half)

        def move(i, src, dst, to):
            return pltpu.make_async_remote_copy(
                src_ref=src, dst_ref=dst, send_sem=send.at[base + i], recv_sem=recv.at[base + i],
                device_id=peer(to), device_id_type=MESH,
            )

        self.first, self.second = [], []
        for s in range(pieces):
            b = 6 * s
            self.first.append([
                move(b, source.at[s, at(over_x, 0), :], far.at[s, 0], "x"),
                move(b + 1, source.at[s, at(both, 0), :], far.at[s, 1], "x"),
                move(b + 2, source.at[s, at(over_y, 1), :], far.at[s, 2], "y"),
                move(b + 3, source.at[s, at(both, 1), :], far.at[s, 3], "y"),
            ])
            self.second.append([move(b + 4, mid.at[s, 1], near.at[s, 0], "y"), move(b + 5, mid.at[s, 3], near.at[s, 1], "x")])
        self.keep = [at(me, 0), at(over_y, 0), at(me, 1), at(over_x, 1)]

    def begin(self, s):
        for k in (1, 3, 0, 2):
            self.first[s][k].start()

    def turn(self, s):
        for k in (1, 3, 0, 2):
            self.first[s][k].wait_recv()
            add_up(self.mid.at[s, k], self.held.at[s, self.keep[k], :], self.far.at[s, k])
            if k in (1, 3):
                self.second[s][k // 2].start()

    def close(self, s):
        for part in range(2):
            self.second[s][part].wait_recv()
            at = pl.ds(part * self.half, self.half)
            add_up(self.total.at[s, at, :], self.mid.at[s, 2 * part], self.near.at[s, part])
        if self.out:
            self.out[s].start()

    def finish(self):
        for s in range(self.pieces):
            for m in self.first[s] + self.second[s]:
                m.wait_send()
        for m in self.out:
            m.wait()


def scatter_scratch(pieces, rows, cols):
    half = rows // 8
    four = pltpu.VMEM((pieces, 4, half, cols), bf16)
    return [pltpu.VMEM((pieces, rows, cols), bf16), four, pltpu.VMEM((pieces, 2, half, cols), bf16), four]


def swap_core(v):
    return lax.ppermute(v, "core", [(0, 1), (1, 0)])


def comm_params(cid, limit=VMEM_MB):
    if cid is None:
        return params(limit)
    return pltpu.CompilerParams(vmem_limit_bytes=limit << 20, collective_id=cid, has_side_effects=True)


def dma(count):
    return pltpu.SemaphoreType.DMA((count,))


def gain_row(norms, r, d):
    nb = d // 128
    return jnp.concatenate([norms[r * nb + i : r * nb + i + 1, :] for i in range(nb)], axis=1)


def layer_norm_parts(v):
    centre = v - jnp.mean(v, axis=-1, keepdims=True)
    r = lax.rsqrt(jnp.mean(centre * centre, axis=-1, keepdims=True) + EPS)
    return centre * r, r


def layer_norm_back(v, gain, dz):
    xhat, r = layer_norm_parts(v)
    dg = jnp.sum(dz * xhat, axis=0, keepdims=True)
    db = jnp.sum(dz, axis=0, keepdims=True)
    t = dz * gain
    dv = r * (t - jnp.mean(t, axis=-1, keepdims=True) - xhat * jnp.mean(t * xhat, axis=-1, keepdims=True))
    return dv, dg, db


def unpack_kernel(dims, m_qkv, m_out, m_norm, own_qkv, own_out, norm):
    n, d = dims
    core = lax.axis_index("core")
    nb = d // 128
    half = nb // 2
    rows = own_qkv.shape[0]

    def put(ref, own, dst, lo, stride):
        own[:, dst : dst + 128] = ref[pl.ds(lo + core * half, rows, stride=stride), :].astype(bf16)

    for part in range(3):
        for w in range(half):
            put(m_qkv, own_qkv, (part * half + w) * 128, part * nb + w, 3 * nb)
    for w in range(half):
        put(m_out, own_out, w * 128, w, nb)
    norm[...] = m_norm[...].astype(bf16).astype(f32)


def group_index(n):
    return lax.axis_index(("y", "x"))


def unpack_first(lanes, n, d, ff):
    rows = d // n
    nb = d // 128
    r1, r2, r3, r4 = rows * 3 * nb, rows * nb, rows * ff // 128, ff // n * nb
    steps = 4 if n == 4 else 2
    sr = rows // steps
    me = lambda: group_index(n)
    return pl.pallas_call(
        functools.partial(unpack_kernel, (n, d)),
        grid=(steps,),
        out_shape=[sds((d, 3 * d // 2), bf16), sds((d, d // 2), bf16), sds((8, 128), f32)],
        in_specs=[
            pl.BlockSpec((r1 // steps, 128), lambda i: (i, 0)),
            pl.BlockSpec((r2 // steps, 128), lambda i: (r1 // (r2 // steps) + i, 0)),
            pl.BlockSpec((8, 128), lambda i: ((r1 + r2 + r3 + r4) // 8, 0)),
        ],
        out_specs=[
            pl.BlockSpec((sr, 3 * d // 2), lambda i: (me() * steps + i, 0)),
            pl.BlockSpec((sr, d // 2), lambda i: (me() * steps + i, 0)),
            pl.BlockSpec((8, 128), lambda i: (0, 0)),
        ],
        compiler_params=params(),
        name="unpack",
    )(lanes, lanes, lanes)


UNPACK_STEPS = 8


def qkv_kernel(cfg, tok, norm_share, m_in, m_back, w_own_in, w_oth_in, o_own_in, o_oth_in, cot, docs, *refs):
    n, comm, hd = cfg
    (a_hbm, qkv_hbm, in_own, own_bk, w_own, w_oth, o_own, o_oth, norms_out, d_hbm, doc_col, att, lse, in_oth, a_p, d_p,
     norms, w, toks, acc, cots, qkv, a_out, own_in, bias, lsem, send, recv) = refs
    if not comm:
        w_own, w_oth = w_own_in, w_oth_in
    t, d = toks.shape
    step = pl.program_id(0)
    nb = d // 128
    half = 3 * d // 2
    share = d // n
    tm = min(256, t)
    tok_copy = pltpu.make_async_copy(tok, toks, lsem.at[0])
    cot_copy = pltpu.make_async_copy(cot, cots, lsem.at[1 + 2 * n])
    a_copy = pltpu.make_async_copy(a_out, a_hbm, lsem.at[2 + 2 * n])
    d_copy = pltpu.make_async_copy(cots, d_hbm, lsem.at[3 + 2 * n])
    place = pl.ds(pl.multiple_of(group_index(n) * share, 8), share)
    in_copy = pltpu.make_async_copy(own_in, in_own.at[place, :], lsem.at[5 + 2 * n])
    out = pltpu.make_async_copy(qkv, qkv_hbm, lsem.at[4 + 2 * n])

    if comm:
        me = member()
        near = [peer("x"), peer("y"), peer("x", "y")]
        mine = pl.ds(pl.multiple_of(me * 8, 8), 8)
        notes = [
            pltpu.make_async_remote_copy(
                src_ref=norm_share, dst_ref=norms.at[mine, :], send_sem=send.at[22 + i], recv_sem=recv.at[22 + i],
                device_id=p, device_id_type=MESH,
            )
            for i, p in enumerate(near)
        ]
        first = Gather(w_own, w_oth, send, recv, 0)
        second = Gather(o_own, o_oth, send, recv, 11)
        third = Gather(in_own, in_oth, send, recv, 25, own_in)
        swaps = [hand_over(a_out, a_p, send.at[36], recv.at[36]), hand_over(cots, d_p, send.at[37], recv.at[37])]
        rows = first.rows
    else:
        rows = [pl.ds(k * share, share) for k in range(n)]

    @pl.when(step == 0)
    def _():
        tok_copy.start()
        cot_copy.start()
        if comm:
            greet(near + [peer("core")])
            for m in notes:
                m.start()
            first.begin()
            norms[mine, :] = norm_share[...]

    @pl.when(step < UNPACK_STEPS)
    def _():
        core = lax.axis_index("core")
        rows_in = own_in.shape[0] // UNPACK_STEPS
        there = pl.ds(pl.multiple_of(step * rows_in, 8), rows_in)
        hs = own_in.shape[1] // n
        stride = m_in.shape[0] // rows_in
        for j in range(n):
            for q in range(hs // 128):
                lo = (2 * hs * j) // 128 + q + core * (hs // 128)
                at = hs * j + q * 128
                own_in[there, at : at + 128] = m_in[pl.ds(lo, rows_in, stride=stride), :].astype(bf16)
        for q in range(nb):
            own_bk[:, q * 128 : (q + 1) * 128] = m_back[pl.ds(q, own_bk.shape[0], stride=nb), :].astype(bf16)

    def load(*which):
        cps = []
        for k in which:
            cps.append(pltpu.make_async_copy(w_own.at[rows[k], :], w.at[k, :, pl.ds(0, half)], lsem.at[1 + 2 * k]))
            cps.append(pltpu.make_async_copy(w_oth.at[rows[k], :], w.at[k, :, pl.ds(half, half)], lsem.at[2 + 2 * k]))
        for cp in cps:
            cp.start()
        for cp in cps:
            cp.wait()

    def product(at, *which):
        return sum(dot_nn(a_out[at, cols_of(k)], w[k]) for k in which)

    def cols_of(k):
        if comm:
            return rows[k]
        return slice(k * share, (k + 1) * share)

    def each_block(fn):
        @pl.loop(0, t // tm)
        def _(i):
            fn(pl.ds(pl.multiple_of(i * tm, tm), tm))

    @pl.when(step == UNPACK_STEPS)
    def _():
        if comm:
            for m in notes:
                m.wait()
            first.relay()
            second.begin()
        else:
            norms[...] = norm_share[...]
        norms_out[...] = norms[...]
        tok_copy.wait()
        gain, shift = gain_row(norms, 0, d), gain_row(norms, 1, d)

        def norm(at):
            xhat, _ = layer_norm_parts(toks[at, :].astype(f32))
            a_out[at, :] = (xhat * gain + shift).astype(bf16)

        each_block(norm)
        cot_copy.wait()
        doc_col[...] = jnp.broadcast_to(docs[...].astype(f32), (128, t)).T[:, :1].astype(jnp.int32)

        def mask(at):
            cots[at, :] = jnp.where(doc_col[at, :] >= 0, cots[at, :].astype(f32), 0.0).astype(bf16)

        each_block(mask)
        a_copy.start()
        d_copy.start()
        in_copy.start()
        fill_bias(bias, docs, doc_col)
        if comm:
            first.arrive(4)
        load(0)

        def start(at):
            acc[at, :] = product(at, 0)

        each_block(start)

    @pl.when(step == UNPACK_STEPS + 1)
    def _():
        if comm:
            first.forward()
            third.begin()
            first.arrive(7, 8)
        load(*range(1, n - 1))

        def more(at):
            acc[at, :] += product(at, *range(1, n - 1))

        each_block(more)

    @pl.when(step == UNPACK_STEPS + 2)
    def _():
        if comm:
            first.close()
            second.relay()
            first.arrive(9, 10)
        load(n - 1)
        scale = (d // HEADS) ** (-0.5)
        q = d // 2

        def last(at):
            total = acc[at, :] + product(at, n - 1)
            for o in (0, half):
                qkv[at, o : o + q] = (total[:, o : o + q].astype(bf16).astype(f32) * scale).astype(bf16)
                qkv[at, o + q : o + half] = total[:, o + q : o + half].astype(bf16)

        each_block(last)
        out.start()

    start = UNPACK_STEPS + 3
    if comm:

        @pl.when(step == start + 1)
        def _():
            second.forward()
            for m in swaps:
                m.start()

        @pl.when(step == start + 3)
        def _():
            third.relay()

        @pl.when(step == start + 6)
        def _():
            third.forward()
            second.close()

    @pl.when(step >= start)
    def _():
        pair = step - start
        pairs = d // 256
        first_col = (pair // pairs) * half + (pair % pairs) * 128

        def part(k):
            return qkv.at[:, pl.ds(pl.multiple_of(first_col + k * (d // 2), 128), 128)]

        attend_pair(hd, part(0), part(1), part(2), bias, att, lse)

    @pl.when(step == pl.num_programs(0) - 1)
    def _():
        if comm:
            third.finish()
            second.arrive(4, 7, 8, 9, 10)
            second.sent()
            first.sent()
            for m in swaps:
                m.wait()
        for cp in (a_copy, d_copy, in_copy, out):
            cp.wait()


def attend_pair(hd, q, k, v, bias, out, lse):
    t = q.shape[0]
    vt = v[...].T
    per = 128 // hd
    qs = [head_lanes(q[...], h, hd) for h in range(per)]
    for i in range(t // QB):
        n = (i + 1) * QB
        cols = slice(i * QB, n)
        outs = []
        for h in range(per):
            s = dot_nt(k[:n, :], qs[h][cols, :]) + bias[:n, cols]
            top = jnp.max(s, axis=0, keepdims=True)
            e = jnp.exp(s - top)
            total = jnp.sum(e, axis=0, keepdims=True)
            lse[0, h : h + 1, cols] = top + jnp.log(total)
            o = dot_nn(vt[h * hd : (h + 1) * hd, :n], e.astype(bf16))
            outs.append(o * (1.0 / total))
        out[cols, :] = jnp.concatenate(outs, axis=0).T.astype(bf16)


def project_qkv(lanes, tok, cot, docs, norm_share, w, o, n, ff, comm):
    t, d = tok.shape
    rows = d // n
    nb = d // 128
    hs = ff // n // 2
    r_in, r_bk = rows * ff // 128, ff // n * nb
    at_in, at_bk = rows * 4 * nb, rows * 4 * nb + r_in
    b_in, b_bk = r_in // UNPACK_STEPS, hs * nb // UNPACK_STEPS
    assert at_in % b_in == 0 and at_bk % b_bk == 0
    up = lambda i: jnp.minimum(i, UNPACK_STEPS - 1)
    me = lambda: group_index(n)
    whole = lambda s: pl.BlockSpec(s, lambda i: (0, 0))
    half = 3 * d // 2
    pairs, hd = d // 128, d // HEADS
    per = 128 // hd
    pair = lambda i: jnp.maximum(i - UNPACK_STEPS - 3, 0)
    shapes = [sds((t, d), bf16), sds((t, 3 * d), bf16), sds((d, ff // 2), bf16), sds((ff // 2, d), bf16),
              sds((d, half), bf16), sds((d, half), bf16), sds((d, d // 2), bf16), sds((d, d // 2), bf16), sds((4 * nb, 128), f32),
              sds((t, d), bf16), sds((t, 1), jnp.int32), sds((t, d), bf16), sds((pairs, per, t), f32), sds((d, ff // 2), bf16),
              sds((t, d), bf16), sds((t, d), bf16)]
    w_args = [w, norm_share, o, norm_share] if comm else [w[0], w[1], o[0], o[1]]
    outs = pl.pallas_call(
        functools.partial(qkv_kernel, (n, comm, hd)),
        grid=(UNPACK_STEPS + 3 + pairs,),
        out_shape=shapes,
        in_specs=[
            ANY, whole(norm_share.shape),
            pl.BlockSpec((b_in, 128), lambda i: (at_in // b_in + up(i), 0)),
            pl.BlockSpec((b_bk, 128), lambda i: (at_bk // b_bk + lax.axis_index("core") * UNPACK_STEPS + up(i), 0)),
            ANY, ANY, ANY, ANY, ANY, whole((1, t)),
        ],
        out_specs=[
            ANY, ANY, ANY,
            pl.BlockSpec((hs // UNPACK_STEPS, d), lambda i: (me() * UNPACK_STEPS + up(i), 0)),
            ANY, ANY, ANY, ANY, whole((4 * nb, 128)), ANY, whole((t, 1)),
            pl.BlockSpec((t, 128), lambda i: (0, pair(i))), pl.BlockSpec((1, per, t), lambda i: (pair(i), 0, 0)), ANY, ANY, ANY,
        ],
        scratch_shapes=[pltpu.VMEM((4 * nb, 128), f32), pltpu.VMEM((n, rows, 3 * d), bf16), pltpu.VMEM((t, d), bf16),
                        pltpu.VMEM((t, 3 * d), f32), pltpu.VMEM((t, d), bf16), pltpu.VMEM((t, 3 * d), bf16), pltpu.VMEM((t, d), bf16),
                        pltpu.VMEM((rows, ff // 2), bf16), pltpu.VMEM((t, t), f32), dma(6 + 2 * n), dma(38), dma(38)],
        input_output_aliases={4: 4, 6: 6},
        compiler_params=comm_params(1 if comm else None),
        cost_estimate=cost(2 * t * d * 3 * d + 8 * t * t * d, 50e6, t * t * HEADS),
        name="qkv_attend",
    )(tok, norm_share, lanes, lanes, *w_args, cot, docs)
    if comm:
        return outs
    full, oth = spread(outs[2])
    return [*outs[:2], full, outs[3], w[0], w[1], o[0], o[1], *outs[8:13], oth, swap_core(outs[0]), swap_core(outs[9])]


QB = 256


def fill_bias(bias, doc_row, doc_col):
    t = bias.shape[0]
    for r in range(0, t, QB):
        key = r + lax.broadcasted_iota(jnp.int32, (QB, t), 0)
        query = lax.broadcasted_iota(jnp.int32, (QB, t), 1)
        ok = (doc_col[r : r + QB, :] == doc_row[...]) & (key <= query)
        bias[r : r + QB, :] = jnp.where(ok, 0.0, FILL)


def head_lanes(v, h, hd):
    lane = lax.broadcasted_iota(jnp.int32, v.shape, 1)
    return jnp.where((lane >= h * hd) & (lane < (h + 1) * hd), v, jnp.zeros_like(v))


def head_column(d, part):
    pairs = d // 256
    return lambda p: (0, (p // pairs) * 3 * pairs + part * pairs + p % pairs)


def spread(own):
    n = lax.axis_size("y") * lax.axis_size("x")
    rows = own.shape[0] // n
    mine = lax.dynamic_slice_in_dim(own, lax.axis_index(("y", "x")) * rows, rows, 0)
    full = lax.all_gather(mine, ("y", "x"), axis=0, tiled=True)
    return full, swap_core(full)


def attend_back_kernel(cfg, q, k, v, dout, att, lse, doc_row, doc_col, part_sum, g_in, dq, dk, dv, sent, red, red_p, part_in, *refs):
    hd, comm = cfg
    bias, dk_acc, dv_acc, stage, lsem, send, recv = refs[:7]
    step = pl.program_id(0)
    pairs = stage.shape[0] // 3

    def hand(p, part):
        wide = 128 * pairs
        cols = pl.ds(pl.multiple_of(part * wide + p * 128, 128), 128)
        i = p * 3 + part
        return hand_over(stage.at[i], sent.at[:, cols], send.at[i], recv.at[i])

    if comm:

        base = 3 * pairs
        mine, keep, held, far, near, mid, total, keep_in = refs[7], refs[12], *refs[13:19]
        fold = Fold(pieces_of(part_sum), pieces_of(mine), *refs[8:12], red, red_p, keep, send, recv, base)
        scat = Scatter(g_in, held, far, near, mid, total, send, recv, base + 4 * PIECES, part_in, keep_in)
        acts = (scat.begin, scat.turn, scat.close, fold.inner, fold.outer, fold.land)

        @pl.when(step == 0)
        def _():
            loads = [pltpu.make_async_copy(part_sum, mine, lsem.at[0]), pltpu.make_async_copy(g_in, held, lsem.at[1])]
            for cp in loads:
                cp.start()
            greet([peer("core"), peer("x"), peer("y")] + Fold.peers())
            run_plan(acts, BACK_PLAN[0])
            for s in range(PIECES):
                fold.begin(s)
            for cp in loads:
                cp.wait()

        @pl.when((step > 0) & (step <= pairs))
        def _():
            for part in range(3):
                hand(step - 1, part).start()

    @pl.when(step == 0)
    def _():
        fill_bias(bias, doc_row, doc_col)

    if comm:
        for at, codes in enumerate(BACK_PLAN[:-1]):
            if codes and at > 0:
                pl.when(step == at)(functools.partial(run_plan, acts, codes))

    t = q.shape[0]
    per = 128 // hd
    scale = hd ** (-0.5)
    kt = k[...].T
    prod = (dout[...].astype(f32) * att[...].astype(f32)).T
    inner = [jnp.sum(prod[h * hd : (h + 1) * hd, :], axis=0, keepdims=True) for h in range(per)]
    qs = [head_lanes(q[...], h, hd) for h in range(per)]
    ds_ = [head_lanes(dout[...], h, hd) for h in range(per)]
    dk_acc[...] = jnp.zeros_like(dk_acc)
    dv_acc[...] = jnp.zeros_like(dv_acc)
    for i in range(t // QB):
        n = (i + 1) * QB
        cols = slice(i * QB, n)
        dqs = []
        for h in range(per):
            qh, dh = qs[h][cols, :], ds_[h][cols, :]
            s = dot_nt(k[:n, :], qh) + bias[:n, cols]
            p = jnp.exp(s - lse[0, h : h + 1, cols])
            dp = dot_nt(v[:n, :], dh)
            g = (p * (dp - inner[h][:, cols])).astype(bf16)
            dv_acc[:n, :] += dot_nn(p.astype(bf16), dh)
            dk_acc[:n, :] += dot_nn(g, qh)
            dqs.append(dot_nn(kt[h * hd : (h + 1) * hd, :n], g))
        dq[cols, :] = (jnp.concatenate(dqs, axis=0).T * scale).astype(bf16)
    dk[...] = dk_acc[...].astype(bf16)
    dv[...] = dv_acc[...].astype(bf16)

    if comm:

        @pl.when(step < pairs)
        def _():
            stage[step * 3] = dq[...]
            stage[step * 3 + 1] = dk[...]
            stage[step * 3 + 2] = dv[...]

        @pl.when(step == 2 * pairs - 1)
        def _():
            for p in range(pairs):
                for part in range(3):
                    hand(p, part).wait()
            run_plan(acts, BACK_PLAN[-1])
            fold.finish()
            scat.finish()


def run_plan(acts, codes):
    for code in codes:
        acts[code // 10](code % 10)


FEED_PLAN = (
    (0, 1),
    (),
    (),
    (10, 2),
    (),
    (11, 3, 20),
    (),
    (12, 4, 21),
    (),
    (13, 5, 22),
    (14, 6),
    (23, 15, 7),
    (24,),
    (16, 25, 17),
    (26, 27),
    (),
    (),
)
BACK_PLAN = (
    (0, 1, 2, 3),
    (),
    (30, 31, 10, 4, 11, 5),
    (32, 40, 33, 12, 6),
    (41, 20, 34, 13, 7, 42, 35),
    (43, 21, 50, 36, 14, 15, 44, 37),
    (45, 22, 51, 52, 16, 23, 46),
    (47, 24, 53, 54, 17),
    (25, 26, 27, 55, 56, 57),
)
LAST_PLAN = (
    (),
    (0,),
    (1,),
    (30,),
    (10, 2, 31),
    (11, 3, 32, 40),
    (20, 33, 41),
    (12, 4, 34, 42),
    (21, 35, 43, 50),
    (13, 5, 22, 36, 44, 45, 37, 51),
    (14, 6, 23, 60, 46, 52, 53),
    (15, 7, 24, 61, 62, 70, 47, 54),
    (16, 25, 63, 64, 71, 55),
    (17, 26, 65, 72, 73, 66, 56, 90),
    (27, 67, 74, 75, 80, 91),
    (76, 81, 57, 92),
    (77, 93, 82, 94, 83, 95, 84, 85, 86, 87),
)
PIECES = 8


def attend_back(qkv, dout, att, lse, doc_row, doc_col, part_sum, g_in, d, n, comm):
    t = qkv.shape[0]
    pairs = d // 128
    half = pairs // 2
    hd = d // HEADS
    per = 128 // hd
    turn = lambda p: (p + half) % pairs
    part_in = (g_in.shape[0], g_in.shape[1] // n, g_in.shape[2])
    col = lambda part: pl.BlockSpec((t, 128), lambda p: head_column(d, part)(turn(p)))
    one = pl.BlockSpec((t, 128), lambda p: (0, turn(p)))
    sems = 3 * half + 10 * PIECES
    extra = []
    if comm:
        extra = [pltpu.VMEM(part_sum.shape, bf16)] + fold_scratch(*part_sum.shape) + [dma(PIECES)]
        extra += scatter_scratch(*g_in.shape) + [pltpu.VMEM(part_in, bf16), dma(PIECES)]
    outs = pl.pallas_call(
        functools.partial(attend_back_kernel, (hd, comm)),
        grid=(pairs,),
        out_shape=[sds((t, d), bf16)] * 3 + [sds((t, 3 * d // 2), bf16)] + [sds(part_sum.shape, bf16)] * 2 + [sds(part_in, bf16)],
        in_specs=[col(0), col(1), col(2), one, one, pl.BlockSpec((1, per, t), lambda p: (turn(p), 0, 0)),
                  pl.BlockSpec((1, t), lambda p: (0, 0)), pl.BlockSpec((t, 1), lambda p: (0, 0)), ANY, ANY],
        out_specs=[one, one, one, ANY, ANY, ANY, ANY],
        scratch_shapes=[pltpu.VMEM((t, t), f32), pltpu.VMEM((t, 128), f32), pltpu.VMEM((t, 128), f32),
                        pltpu.VMEM((3 * half, t, 128), bf16), dma(2), dma(sems), dma(sems)] + extra,
        compiler_params=comm_params(6 if comm else None),
        cost_estimate=cost(20 * t * t * d, 16e6, t * t * HEADS),
        name="attend_back",
    )(qkv, qkv, qkv, dout, att, lse, doc_row, doc_col, part_sum, g_in)
    if comm:
        return outs[0], outs[1], outs[2], outs[3], (outs[4], outs[5]), outs[6]
    sent = swap_core(jnp.concatenate([g[:, d // 2 :] for g in outs[:3]], axis=1))
    return outs[0], outs[1], outs[2], sent, both_halves(part_sum), scatter_pieces(g_in)


def both_halves(part_sum):
    full = lax.psum(part_sum.astype(f32), "z").astype(bf16)
    return full, swap_core(full)


def middle_kernel(cfg, att_rows, tok, norms, o_own, o_oth, w_own, w_oth, att_all, bk_own_in, d_out, d_out_p, *refs):
    d, tm, blk, comm = cfg
    (resid, a_two_out, hidden, slope, bk_own, bk_oth, att_p, grad, w, a_two, stage, theirs, douts, lsem, send, recv) = refs
    step = pl.program_id(0)
    last = pl.num_programs(0) - 1
    t = a_two.shape[0]
    pro = t // tm
    half = d // 2
    nb = theirs.shape[0]
    core = lax.axis_index("core")
    loads = [pltpu.make_async_copy(v, douts.at[i], lsem.at[2 + i]) for i, v in enumerate((d_out, d_out_p))]

    def hand(j):
        return hand_over(stage.at[j], theirs.at[j], send.at[12 + j], recv.at[12 + j])

    if comm:
        gather = Gather(bk_own, bk_oth, send, recv, 0)
        swap = hand_over(att_all, att_p, send.at[11], recv.at[11])

        @pl.when(step == 0)
        def _():
            greet([peer("x"), peer("y"), peer("core")])
            gather.begin()
            swap.start()

        @pl.when(step == pro + 4)
        def _():
            gather.relay()

        @pl.when((step > pro) & (step <= pro + nb))
        def _():
            hand(step - pro - 1).start()

    @pl.when(step == 0)
    def _():
        lo = pl.multiple_of(core * half, half)
        hi = pl.multiple_of((1 - core) * half, half)
        cps = [
            pltpu.make_async_copy(o_own, w.at[:, pl.ds(lo, half)], lsem.at[0]),
            pltpu.make_async_copy(o_oth, w.at[:, pl.ds(hi, half)], lsem.at[1]),
        ]
        for cp in cps + loads:
            cp.start()
        for cp in cps:
            cp.wait()

    @pl.when(step < pro)
    def _():
        lo = pl.multiple_of(core * half, half)
        hi = pl.multiple_of((1 - core) * half, half)
        y = dot_nn(att_rows[:, :half], w[pl.ds(lo, half), :]) + dot_nn(att_rows[:, half:], w[pl.ds(hi, half), :])
        r = tok[...].astype(f32) + y
        resid[...] = r
        xhat, _ = layer_norm_parts(r)
        a = (xhat * gain_row(norms, 2, d) + gain_row(norms, 3, d)).astype(bf16)
        a_two_out[...] = a
        a_two[pl.ds(pl.multiple_of(step * tm, tm), tm), :] = a

    @pl.when((step >= pro) & (step < pro + 2 * nb))
    def _():
        pre = dot_nn(a_two[...], pick(step < pro + nb, w_oth[...], w_own[...]))
        cdf = 0.5 + 0.5 * lax.erf(pre * (0.5**0.5))
        pdf = jnp.exp(-0.5 * pre * pre) * 0.3989422804014327
        h = (pre * cdf).astype(bf16)
        hidden[...] = h
        slope[...] = (cdf + pre * pdf).astype(bf16)
        stage[step - pro] = h

    @pl.when(step == pro + 2 * nb)
    def _():
        for cp in loads:
            cp.wait()

    if comm:
        for j in range(nb):

            @pl.when(step == pro + 2 * nb + j)
            def _():
                hand(j).wait_recv()

        @pl.when(step == pro + 2 * nb)
        def _():
            gather.forward()

    @pl.when(step >= pro + 2 * nb)
    def _():
        j = step - pro - 2 * nb
        g = dot_tn(stage[nb + j], douts[0])
        if comm:
            g = g + dot_tn(theirs[j], douts[1])
        store_columns(grad, g)

    if comm:

        @pl.when(step == last)
        def _():
            gather.finish()
            swap.wait()
            for j in range(nb):
                hand(j).wait_send()


def store_columns(ref, g):
    wide = ref.shape[2]
    for p in range(ref.shape[0]):
        ref[p] = g[:, p * wide : (p + 1) * wide].astype(bf16)


def middle(att, tok, norms, o_own, o_oth, w_own, w_oth, bk_own, d_out, d_out_p, comm, tm=256, blk=512):
    t, d = tok.shape
    wide = w_own.shape[1]
    pro, nb = t // tm, wide // blk
    rowi = lambda i: jnp.minimum(i, pro - 1)
    oth = lambda i: jnp.clip(i - pro, 0, nb - 1)
    own = lambda i: jnp.clip(i - pro - nb, 0, nb - 1)
    both = lambda i: jnp.where(i < pro + nb, nb + oth(i), own(i))
    rows = lambda wd: pl.BlockSpec((tm, wd), lambda i: (rowi(i), 0))
    part = lambda count: pltpu.VMEM((count, t, blk), bf16)
    outs = pl.pallas_call(
        functools.partial(middle_kernel, (d, tm, blk, comm)),
        grid=(pro + 3 * nb,),
        out_shape=[sds((t, d), f32), sds((t, d), bf16), sds((t, 2 * wide), bf16), sds((t, 2 * wide), bf16),
                   sds(bk_own.shape, bf16), sds(bk_own.shape, bf16), sds((t, d), bf16), sds((PIECES, wide, d // PIECES), bf16)],
        in_specs=[rows(d), rows(d), pl.BlockSpec(norms.shape, lambda i: (0, 0)), ANY, ANY,
                  pl.BlockSpec((d, blk), lambda i: (0, own(i))), pl.BlockSpec((d, blk), lambda i: (0, oth(i))), ANY, ANY, ANY, ANY],
        out_specs=[rows(d), rows(d), pl.BlockSpec((t, blk), lambda i: (0, both(i))), pl.BlockSpec((t, blk), lambda i: (0, both(i))),
                   ANY, ANY, ANY, pl.BlockSpec((PIECES, blk, d // PIECES), lambda i: (0, jnp.maximum(i - pro - 2 * nb, 0), 0))],
        scratch_shapes=[pltpu.VMEM((d, d), bf16), pltpu.VMEM((t, d), bf16), part(2 * nb), part(nb), pltpu.VMEM((2, t, d), bf16),
                        dma(4), dma(12 + nb), dma(12 + nb)],
        input_output_aliases={8: 4},
        compiler_params=comm_params(3 if comm else None),
        cost_estimate=cost(2 * t * d * d + 8 * t * d * wide, 60e6, 4 * t * wide),
        name="middle",
    )(att, tok, norms, o_own, o_oth, w_own, w_oth, att, bk_own, d_out, d_out_p)
    if comm:
        return outs
    full, other = spread(bk_own)
    hid_p = swap_core(outs[2][:, wide:])
    grad = (dot_tn(outs[2][:, :wide], d_out) + dot_tn(hid_p, d_out_p)).astype(bf16)
    return [*outs[:4], full, other, swap_core(att), in_columns(grad)]


def in_columns(g):
    rows, cols = g.shape
    return g.reshape(rows, PIECES, cols // PIECES).transpose(1, 0, 2)


def feed_kernel(comm, d_out, slope, b_own, b_oth, i_own, i_oth, resid, dout_rows, norms, o_own, o_oth, a_two, g_back, *refs):
    (grad, d_resid, low, d_att, two_norm, sent, part_back, stage, theirs, lhs, wi, wo, lows, lsem, send, recv) = refs[:16]
    step = pl.program_id(0)
    nb = theirs.shape[0]
    tm, d = resid.shape
    pro = lows.shape[0] // tm
    half = d // 2
    wide = wi.shape[1] // 2
    np_ = d // 128
    core = lax.axis_index("core")
    lo = pl.multiple_of(core * half, half)
    hi = pl.multiple_of((1 - core) * half, half)
    loads = [
        pltpu.make_async_copy(a_two, lhs.at[0], lsem.at[0]),
        pltpu.make_async_copy(o_own, wo.at[:, pl.ds(lo, half)], lsem.at[1]),
        pltpu.make_async_copy(o_oth, wo.at[:, pl.ds(hi, half)], lsem.at[2]),
        pltpu.make_async_copy(i_oth, wi.at[:, pl.ds(0, wide)], lsem.at[4]),
        pltpu.make_async_copy(i_own, wi.at[:, pl.ds(wide, wide)], lsem.at[5]),
    ]

    def hand(j):
        return hand_over(stage.at[j], theirs.at[j], send.at[1 + j], recv.at[1 + j])

    def hand_low(r):
        at = pl.ds(pl.multiple_of(r * tm, tm), tm)
        return hand_over(lows.at[at, :], sent.at[at, :], send.at[1 + nb + r], recv.at[1 + nb + r])

    @pl.when(step == 1)
    def _():
        for cp in loads:
            cp.start()

    if comm:
        swap = hand_over(a_two, lhs.at[1], send.at[0], recv.at[0])
        held, far, near, mid, total, keep = refs[16:22]
        scat = Scatter(g_back, held, far, near, mid, total, send, recv, 1 + nb + pro, part_back, keep)
        acts = (scat.begin, scat.turn, scat.close)
        load = pltpu.make_async_copy(g_back, held, lsem.at[3])
        near_by = [peer("core"), peer("x"), peer("y")]

        @pl.when(step == 0)
        def _():
            load.start()
            greet_start(near_by)

    @pl.when(step < 2 * nb)
    def _():
        first = step < nb
        g = (dot_nt(d_out[...], pick(first, b_oth[...], b_own[...])) * slope[...].astype(f32)).astype(bf16)
        stage[step] = g

    if comm:

        @pl.when(step == 0)
        def _():
            greet_end(near_by)
            run_plan(acts, FEED_PLAN[0])
            swap.start()
            load.wait()

        for at, codes in enumerate(FEED_PLAN[:-1]):
            if codes and at > 0:
                pl.when(step == at)(functools.partial(run_plan, acts, codes))

        @pl.when((step > 0) & (step <= nb))
        def _():
            hand(step - 1).start()

    @pl.when(step == 2 * nb)
    def _():
        loads[0].wait()
        if comm:
            swap.wait()

    if comm:
        for j in range(nb):

            @pl.when(step == 2 * nb + j)
            def _():
                hand(j).wait()

    @pl.when((step >= 2 * nb) & (step < 3 * nb))
    def _():
        j = step - 2 * nb
        g = dot_tn(lhs[0], stage[nb + j])
        if comm:
            g = g + dot_tn(lhs[1], theirs[j])
        store_columns(grad, g)

    @pl.when(step == 3 * nb)
    def _():
        for cp in loads[1:]:
            cp.wait()
        two_norm[...] = jnp.zeros_like(two_norm)

    @pl.when(step >= 3 * nb)
    def _():
        here = pl.ds(pl.multiple_of((step - 3 * nb) * tm, tm), tm)
        dz = dot_nt(jnp.concatenate([stage[j, here, :] for j in range(2 * nb)], axis=1), wi[...])
        dv, g, b = layer_norm_back(resid[...], gain_row(norms, 2, d), dz)
        two_norm[0:np_, :] += flat_row(g)
        two_norm[np_:, :] += flat_row(b)
        dr = dout_rows[...].astype(f32) + dv
        d_resid[...] = dr
        dl = dr.astype(bf16)
        low[...] = dl
        lows[here, :] = pick(core == 0, dl[:, half:], dl[:, :half])
        d_att[:, :half] = dot_nt(dl, wo[pl.ds(lo, half), :]).astype(bf16)
        d_att[:, half:] = dot_nt(dl, wo[pl.ds(hi, half), :]).astype(bf16)
        if comm:
            hand_low(step - 3 * nb).start()

    if comm:

        @pl.when(step == pl.num_programs(0) - 1)
        def _():
            run_plan(acts, FEED_PLAN[-1])
            scat.finish()
            for r in range(pro):
                hand_low(r).wait()


def feed_back(d_out, slope, b_own, b_oth, i_own, i_oth, resid, norms, o_own, o_oth, a_two, g_back, n, comm, tm=256, blk=512):
    t, d = d_out.shape
    half = b_own.shape[0]
    nb = half // blk
    pro = t // tm
    oth = lambda i: jnp.minimum(i, nb - 1)
    own = lambda i: jnp.clip(i - nb, 0, nb - 1)
    row = lambda i: jnp.clip(i - 3 * nb, 0, pro - 1)
    rows = lambda w: pl.BlockSpec((tm, w), lambda i: (row(i), 0))
    whole = lambda s: pl.BlockSpec(s, lambda i: (0, 0))
    pieces, g_rows, g_cols = g_back.shape
    part = (pieces, g_rows // n, g_cols)
    per = half // PIECES
    extra = scatter_scratch(*g_back.shape) + [pltpu.VMEM(part, bf16), dma(pieces)] if comm else []
    sems = 1 + nb + pro + 6 * pieces
    outs = pl.pallas_call(
        functools.partial(feed_kernel, comm),
        grid=(3 * nb + pro,),
        out_shape=[sds((PIECES, d, per), bf16), sds((t, d), f32), sds((t, d), bf16), sds((t, d), bf16), sds((d // 64, 128), f32),
                   sds((t, d // 2), bf16), sds(part, bf16)],
        in_specs=[whole((t, d)), pl.BlockSpec((t, blk), lambda i: (0, jnp.where(i < nb, nb + i, own(i)))),
                  pl.BlockSpec((blk, d), lambda i: (own(i), 0)), pl.BlockSpec((blk, d), lambda i: (oth(i), 0)),
                  ANY, ANY, rows(d), rows(d), whole(norms.shape), ANY, ANY, ANY, ANY],
        out_specs=[pl.BlockSpec((blk // per, d, per), lambda i: (jnp.clip(i - 2 * nb, 0, nb - 1), 0, 0)), rows(d), rows(d), rows(d),
                   whole((d // 64, 128)), ANY, ANY],
        scratch_shapes=[pltpu.VMEM((2 * nb, t, blk), bf16), pltpu.VMEM((nb, t, blk), bf16), pltpu.VMEM((2, t, d), bf16),
                        pltpu.VMEM((d, 2 * half), bf16), pltpu.VMEM((d, d), bf16), pltpu.VMEM((t, d // 2), bf16), dma(6), dma(sems), dma(sems)]
        + extra,
        compiler_params=comm_params(4 if comm else None, 62),
        cost_estimate=cost(12 * t * d * half + 2 * t * d * d, 60e6),
        name="feed_back",
    )(d_out, slope, b_own, b_oth, i_own, i_oth, resid, d_out, norms, o_own, o_oth, a_two, g_back)
    if comm:
        return outs
    core = lax.axis_index("core")
    other = lax.dynamic_slice_in_dim(outs[2], (1 - core) * (d // 2), d // 2, 1)
    d_pre = pre_values(d_out, slope, b_own, b_oth)
    g_in = dot_tn(a_two, d_pre[:, :half]) + dot_tn(swap_core(a_two), swap_core(d_pre[:, half:]))
    return [in_columns(g_in.astype(bf16)), *outs[1:5], swap_core(other), scatter_pieces(g_back)]


def pre_values(d_out, slope, own, oth):
    both = jnp.concatenate([dot_nt(d_out, own), dot_nt(d_out, oth)], axis=1)
    return (both * slope.astype(f32)).astype(bf16)


def scatter_pieces(g):
    return lax.psum_scatter(g, ("y", "x"), scatter_dimension=1, tiled=True)


def last_kernel(cfg, g1, g2, g3, theirs, low, low_p, dq, dk, dv, tok, d_resid, norms, h_own, h_oth, resid, doc, two_norm,
                a_one, a_one_p, att, att_p, w_own, w_oth, b_own, b_oth, part_in, *refs):
    d, comm = cfg
    out, mixed, red_in, red_in_p, red_at, red_at_p, sums, w, wb, parts, held, lsem, total = refs[:13]
    refs = refs[1:]
    step = pl.program_id(0)
    last = pl.num_programs(0) - 1
    np_ = held.shape[0]
    pro = (last - np_) // 2
    half = 3 * d // 2
    q = d // 2
    hb = b_own.shape[0]
    nb = d // 128
    core = lax.axis_index("core")
    early = [pltpu.make_async_copy(a, wb.at[pl.ds(i * d, d), :], lsem.at[i]) for i, a in enumerate((a_one, a_one_p, att, att_p))]
    mids = [
        pltpu.make_async_copy(w_own, w.at[:, pl.ds(0, half)], lsem.at[4]),
        pltpu.make_async_copy(w_oth, w.at[:, pl.ds(half, half)], lsem.at[5]),
    ]
    late = [
        pltpu.make_async_copy(b_own, wb.at[pl.ds(0, hb), :], lsem.at[6]),
        pltpu.make_async_copy(b_oth, wb.at[pl.ds(hb, hb), :], lsem.at[7]),
    ]
    if comm:
        send, recv, mine_in, fi, sc, fa, vec, box, k_in, k_at = (
            refs[12], refs[13], refs[14], refs[15:19], refs[19:22], refs[22:27], refs[27], refs[28], refs[29], refs[30]
        )
        fold_in = Fold(
            pieces_of(part_in), pieces_of(mine_in), *fi, red_in, red_in_p, k_in, send, recv, 0
        )
        scat = Scatter(held, held, *sc, fa[0], send, recv, 4 * PIECES)
        mine_at = pieces_of(fa[0])
        fold_at = Fold(mine_at, mine_at, *fa[1:5], red_at, red_at_p, k_at, send, recv, 4 * PIECES + 6 * np_)
        base = 4 * PIECES + 10 * np_

        def note(i, src, dst, to):
            return pltpu.make_async_remote_copy(
                src_ref=src, dst_ref=dst, send_sem=send.at[base + i], recv_sem=recv.at[base + i], device_id=to, device_id_type=MESH
            )

        near, far = Fold.peers()
        notes = [
            note(0, vec.at[0], box.at[0], peer("x")),
            note(1, vec.at[1], box.at[1], peer("y")),
            note(2, vec.at[2], box.at[2], peer("core")),
            note(3, vec.at[3], box.at[3], near),
            note(4, vec.at[4], box.at[4], far),
            note(5, vec.at[5], vec.at[5], near),
        ]

        def norm_sum(k):
            if k < 3:
                notes[k].wait_recv()
                vec[k + 1] = vec[k] + box[k]
                if k < 2:
                    notes[k + 1].start()
                else:
                    pl.when(fold_in.end)(notes[3].start)
            elif k < 5:

                @pl.when(fold_in.mid)
                def _():
                    notes[k].wait_recv()
                    vec[k + 1] = vec[k] + box[k]
                    notes[k + 1].start()

            else:
                pl.when(fold_in.end)(notes[5].wait_recv)

        def settle(s):
            scat.close(s)
            fold_at.begin(s)

        acts = (scat.begin, scat.turn, settle, fold_in.inner, fold_in.outer, fold_in.land, fold_at.inner, fold_at.outer,
                fold_at.land, norm_sum)

    @pl.when(step == 0)
    def _():
        for cp in early:
            cp.start()
        if comm:
            load = pltpu.make_async_copy(part_in, mine_in, lsem.at[8])
            load.start()
            greet([peer("core"), peer("x"), peer("y")] + Fold.peers())
            for s in range(PIECES):
                fold_in.begin(s)
            load.wait()
        for cp in early[:2]:
            cp.wait()
        for cp in mids:
            cp.start()
        parts[0 : 2 * nb, :] = jnp.zeros((2 * nb, 128), f32)
        parts[2 * nb :, :] = two_norm[...]

    if comm:
        for k, codes in enumerate(LAST_PLAN[:-1]):
            if codes:
                pl.when(step == k)(functools.partial(run_plan, acts, codes))

    per = q // g1.shape[1]

    @pl.when(step < 3 * per)
    def _():
        g = pick(step < per, g1[...], pick(step < 2 * per, g2[...], g3[...]))
        acc = dot_tn(wb[0:d, :], g) + dot_tn(wb[d : 2 * d, :], theirs[...])
        held[step] = acc.astype(bf16)

    @pl.when(step == 3 * per)
    def _():
        for cp in early[2:]:
            cp.wait()

    @pl.when((step >= 3 * per) & (step < np_))
    def _():
        lo = pl.ds(pl.multiple_of(core * q, q), q)
        hi = pl.ds(pl.multiple_of((1 - core) * q, q), q)
        own = dot_tn(wb[2 * d : 3 * d, :q], low[...]) + dot_tn(wb[3 * d :, q:], low_p[...])
        held[step, lo, :] = own.astype(bf16)
        other = dot_tn(wb[2 * d : 3 * d, q:], low[...]) + dot_tn(wb[3 * d :, :q], low_p[...])
        held[step, hi, :] = other.astype(bf16)

    @pl.when(step == np_)
    def _():
        for cp in late:
            cp.start()
        for cp in mids:
            cp.wait()

    @pl.when((step >= np_) & (step < np_ + pro))
    def _():
        both = jnp.concatenate([g[:, :q] for g in (dq, dk, dv)] + [g[:, q:] for g in (dq, dk, dv)], axis=1)
        dz = dot_nt(both, w[...])
        grad, g, b = layer_norm_back(tok[...].astype(f32), gain_row(norms, 0, d), dz)
        parts[0:nb, :] += flat_row(g)
        parts[nb : 2 * nb, :] += flat_row(b)
        out[...] = (d_resid[...] + grad).astype(bf16)

    @pl.when(step == np_ + pro)
    def _():
        for cp in late:
            cp.wait()
        if comm:
            vec[0] = parts[...]
            notes[0].start()

    @pl.when((step >= np_ + pro) & (step < last))
    def _():
        total[...] = resid[...]
        chunk = hb // 4

        @pl.loop(0, 4)
        def _(i):
            at = pl.ds(pl.multiple_of(i * chunk, chunk), chunk)
            beyond = pl.ds(pl.multiple_of(hb + i * chunk, chunk), chunk)
            total[...] += dot_nn(h_own[:, at], wb[at, :]) + dot_nn(h_oth[:, at], wb[beyond, :])

        mixed[...] = jnp.where(doc[...] >= 0, total[...], 0.0).astype(bf16)

    @pl.when(step == last)
    def _():
        if comm:
            run_plan(acts, LAST_PLAN[-1])
            fold_in.finish()
            scat.finish()
            fold_at.finish()
            for i in (0, 1, 2):
                notes[i].wait_send()
            pl.when(fold_in.end)(notes[3].wait_send)

            @pl.when(fold_in.mid)
            def _():
                notes[4].wait_send()
                notes[5].wait_send()

            sums[...] = vec[5]
        else:
            sums[...] = parts[...]
            cp = pltpu.make_async_copy(held, red_at, lsem.at[0])
            cp.start()
            cp.wait()


def flat_row(v):
    return jnp.concatenate([v[:, i * 128 : (i + 1) * 128] for i in range(v.shape[1] // 128)], axis=0)


def last_grad(grads3, theirs, low, low_p, tok, d_resid, norms, hidden, resid, doc_col, two_norm, a_one, a_one_p, att, att_p,
              own, oth, b_own, b_oth, part_in, n, comm, tm=256, wide=256):
    t, d = tok.shape
    pro = t // tm
    half = b_own.shape[0]
    q = d // 2
    per = q // wide
    np_ = 4 * per
    one = lambda w, c=0: pl.BlockSpec((tm, w), lambda i: (jnp.clip(i - np_, 0, pro - 1), c))
    two = lambda w, c=0: pl.BlockSpec((tm, w), lambda i: (jnp.clip(i - np_ - pro, 0, pro - 1), c))
    whole = lambda a: pl.BlockSpec(a.shape, lambda i: (0, 0))
    col = lambda k, count: pl.BlockSpec((t, wide), lambda i: (0, jnp.clip(i - k * per, 0, count - 1)))
    low_col = pl.BlockSpec((t, wide), lambda i: (0, lax.axis_index("core") * per + jnp.clip(i - 3 * per, 0, per - 1)))
    nv = 4 * d // 128
    pieced = part_in.shape
    share = (np_, d // n if comm else d, wide)
    slots = 4 * PIECES + 10 * np_ + 6
    extra = []
    if comm:
        extra = [dma(slots), dma(slots), pltpu.VMEM(part_in.shape, bf16)] + fold_scratch(*part_in.shape)
        extra += scatter_scratch(np_, d, wide)[1:] + [pltpu.VMEM(share, bf16)] * 5
        extra += [pltpu.VMEM((6, nv, 128), f32), pltpu.VMEM((5, nv, 128), f32), dma(PIECES), dma(np_)]
    return pl.pallas_call(
        functools.partial(last_kernel, (d, comm)),
        grid=(np_ + 2 * pro + 1,),
        out_shape=[sds((t, d), bf16), sds((t, d), bf16)] + [sds(pieced, bf16)] * 2 + [sds(share, bf16)] * 2 + [sds((nv, 128), f32)],
        in_specs=[col(0, per), col(1, per), col(2, per), col(0, 3 * per), low_col, col(3, per)]
        + [one(d)] * 5 + [whole(norms), two(half), two(half, 1), two(d), two(1), whole(two_norm)] + [ANY] * 9,
        out_specs=[one(d), two(d), ANY, ANY, ANY, ANY, pl.BlockSpec((nv, 128), lambda i: (0, 0))],
        scratch_shapes=[pltpu.VMEM((d, 3 * d), bf16), pltpu.VMEM((4 * d, d), bf16), pltpu.VMEM((nv, 128), f32),
                        pltpu.VMEM((np_, d, wide), bf16), dma(9), pltpu.VMEM((tm, d), f32)] + extra,
        compiler_params=comm_params(7 if comm else None, 63),
        cost_estimate=cost(14 * t * d * d + 4 * t * d * half, 60e6),
        name="last_grad",
    )(*grads3, theirs, low, low_p, *grads3, tok, d_resid, norms, hidden, hidden, resid, doc_col, two_norm,
      a_one, a_one_p, att, att_p, own, oth, b_own, b_oth, part_in)


def adam_update(g_ref, m1, m2, wg, st, mn):
    rows = g_ref.shape[0]
    step = min(rows, 256)

    @pl.loop(0, rows // step)
    def _(i):
        at = pl.ds(pl.multiple_of(i * step, 8), step)
        g = g_ref[at, :]
        first = BETA_ONE * m1[at, :] + (1.0 - BETA_ONE) * g
        second_hat = (BETA_TWO / (1.0 - BETA_TWO**STEPS)) * m2[at, :] + ((1.0 - BETA_TWO) / (1.0 - BETA_TWO**STEPS)) * g * g
        wg[at, :] = g
        st[at, :] = (-RATE / (1.0 - BETA_ONE**STEPS)) * first / (second_hat * lax.rsqrt(second_hat) + ADAM_EPS)
        mn[at, :] = first


def adam_kernel(plan, inv_root, own, oth, m1, m2, *refs):
    wg, st, mn, flat = refs[-4:]
    rows, stride, places = plan
    first = lax.axis_index("core") == 0
    wide = own.shape[2]
    for col, lo, hi in places:
        p, c = col // wide, col % wide
        a = own[p, :, c : c + 128].astype(f32) * inv_root
        b = oth[p, :, c : c + 128].astype(f32) * inv_root
        flat[pl.ds(lo, rows, stride=stride), :] = pick(first, a, b)
        flat[pl.ds(hi, rows, stride=stride), :] = pick(first, b, a)
    adam_update(flat, m1, m2, wg, st, mn)


def adam_columns(own, oth, at, count, m1, m2, prev, inv_root, first_row, rows, places):
    total, wide = own.shape[1:]
    nb = 2 * count * wide // 128
    blk = rows * nb
    assert first_row % blk == 0
    base = first_row // blk
    half = pl.BlockSpec((count, rows, wide), lambda i: (at, i, 0))
    flat = pl.BlockSpec((blk, 128), lambda i: (base + i, 0))
    kernel = functools.partial(adam_kernel, (rows, nb, places), inv_root)
    return adam_call(kernel, (total // rows,), own, oth, m1, m2, prev, half, flat, blk, "adam")


def adam_call(kernel, grid, own, oth, m1, m2, prev, half, flat, blk, name):
    return pl.pallas_call(
        kernel,
        grid=grid,
        out_shape=[sds(m1.shape, f32)] * 3,
        in_specs=[half, half, flat, flat] + [ANY] * len(prev),
        out_specs=[flat] * 3,
        scratch_shapes=[pltpu.VMEM((blk, 128), f32)],
        input_output_aliases={4 + i: i for i in range(len(prev))},
        compiler_params=params(),
        cost_estimate=cost(0, own.size * 2 * 22),
        name=name,
    )(own, oth, m1, m2, *prev)


def adam_rows_kernel(inv_root, own, oth, m1, m2, *refs):
    wg, st, mn, flat = refs[-4:]
    g = pick(pl.program_id(0) == lax.axis_index("core"), own[...], oth[...]).astype(f32) * inv_root
    rows, width = g.shape
    nb = width // 128
    for w in range(nb):
        flat[pl.ds(w, rows, stride=nb), :] = g[:, w * 128 : (w + 1) * 128]
    adam_update(flat, m1, m2, wg, st, mn)


def adam_rows_halves(own, oth, m1, m2, prev, inv_root, first_row):
    count, width = own.shape
    rows = count // 4
    blk = rows * width // 128
    base = first_row // blk
    half = pl.BlockSpec((rows, width), lambda h, i: (i, 0))
    flat = pl.BlockSpec((blk, 128), lambda h, i: (base + h * 4 + i, 0))
    kernel = functools.partial(adam_rows_kernel, inv_root)
    return adam_call(kernel, (2, 4), own, oth, m1, m2, prev, half, flat, blk, "adam_rows")


def adam_tail_kernel(g, m1, m2, p1, p2, p3, wg, st, mn):
    adam_update(g, m1, m2, wg, st, mn)


def adam_tail(g, m1, m2, prev, first_row):
    rows = 8
    assert first_row % rows == 0 and g.shape[0] <= rows
    g = jnp.pad(g, ((0, rows - g.shape[0]), (0, 0)))
    flat = pl.BlockSpec((rows, 128), lambda i: (first_row // rows, 0))
    return pl.pallas_call(
        adam_tail_kernel,
        grid=(1,),
        out_shape=[sds(m1.shape, f32)] * 3,
        in_specs=[pl.BlockSpec((rows, 128), lambda i: (0, 0)), flat, flat] + [ANY] * 3,
        out_specs=[flat] * 3,
        input_output_aliases={3: 0, 4: 1, 5: 2},
        name="adam_norms",
    )(g, m1, m2, *prev)


BLOCK = 4096


def adam_all_kernel(cfg, b_own, b_oth, i_own, i_oth, a_own, a_oth, norm, m1, m2, wg, st, mn, flat, later):
    inv_root, at_in, at_at, counts = cfg
    step = pl.program_id(0)
    core = lax.axis_index("core")
    n_back, n_in, n_at = counts

    @pl.when(step < n_back)
    def _():
        mine = step // (n_back // 2) == core
        pieces, rows, wide = b_own.shape
        for w in range(pieces * wide // 128):
            p, c = w * 128 // wide, w * 128 % wide
            g = pick(mine, b_own[p, :, c : c + 128], b_oth[p, :, c : c + 128])
            flat[pl.ds(w, rows, stride=pieces * wide // 128), :] = g.astype(f32) * inv_root

    def spread_columns(dst, own, oth, places):
        rows, wide = own.shape[1:]
        for col, lo, hi, stride in places:
            p, c = col // wide, col % wide
            mine = lo + core * (hi - lo)
            dst[pl.ds(mine, rows, stride=stride), :] = own[p, :, c : c + 128].astype(f32) * inv_root
            dst[pl.ds(lo + hi - mine, rows, stride=stride), :] = oth[p, :, c : c + 128].astype(f32) * inv_root

    @pl.when((step >= n_back) & (step < n_back + n_in))
    def _():
        spread_columns(flat, i_own, i_oth, at_in)

    for k, places in enumerate(at_at):
        pl.when(step == k)(functools.partial(spread_columns, later, a_own, a_oth, places))

    @pl.when((step >= n_back + n_in) & (step < n_back + n_in + n_at))
    def _():
        at = pl.multiple_of((step - n_back - n_in) * BLOCK, BLOCK)
        flat[...] = later[pl.ds(at, BLOCK), :]

    @pl.when(step == n_back + n_in + n_at)
    def _():
        per = norm.shape[0] // 4
        at = pl.multiple_of(lax.axis_index(("y", "x")) * per, per)
        flat[0:per, :] = norm[pl.ds(at, per), :] * inv_root

    adam_update(flat, m1, m2, wg, st, mn)


def adam_all(back, inner, attention, norm, m1, m2, inv_root, places):
    at_in, at_qkv, at_out = places
    b_np, b_rows, b_wide = back[0].shape
    i_np, i_rows, i_wide = inner[0].shape
    np_, a_rows, wide = attention[0].shape
    n_back = 2 * b_np * b_rows * b_wide // 128 // BLOCK
    n_in = 2 * i_np * i_rows * i_wide // 128 // BLOCK
    n_at = 2 * np_ * a_rows * wide // 128 // BLOCK
    lots = np_ // (n_back + n_in)
    assert np_ == lots * (n_back + n_in) and m1.shape[0] == (n_back + n_in + n_at) * BLOCK + 8
    s_in, s_qkv, s_out = 2 * i_np * i_wide // 128, 2 * len(at_qkv), 2 * len(at_out)
    edge = a_rows * s_qkv
    at_at = [[] for _ in range(n_back + n_in)]
    for col, lo, hi in at_qkv:
        at_at[col // wide // lots].append((col % (wide * lots), lo, hi, s_qkv))
    for col, lo, hi in at_out:
        col += len(at_qkv) * 128
        at_at[col // wide // lots].append((col % (wide * lots), edge + lo, edge + hi, s_out))
    cfg = (inv_root, [(c, lo, hi, s_in) for c, lo, hi in at_in], at_at, (n_back, n_in, n_at))
    after_at, after_in = n_at, n_at + n_in

    def where(i):
        back_or_in = jnp.where(i < n_back, after_in + i, after_at + i - n_back)
        return jnp.where(i < n_back + n_in, back_or_in, jnp.where(i < n_back + n_in + n_at, i - n_back - n_in, i))

    flat = pl.BlockSpec((BLOCK, 128), lambda i: (where(i), 0))
    b_spec = pl.BlockSpec((b_np, 2 * b_rows // n_back, b_wide), lambda i: (0, jnp.minimum(i, n_back - 1) % (n_back // 2), 0))
    i_spec = pl.BlockSpec((i_np, i_rows // n_in, i_wide), lambda i: (0, jnp.clip(i - n_back, 0, n_in - 1), 0))
    a_spec = pl.BlockSpec((lots, a_rows, wide), lambda i: (jnp.minimum(i, n_back + n_in - 1), 0, 0))
    return pl.pallas_call(
        functools.partial(adam_all_kernel, cfg),
        grid=(n_back + n_in + n_at + 1,),
        out_shape=[sds(m1.shape, f32)] * 3,
        in_specs=[b_spec, b_spec, i_spec, i_spec, a_spec, a_spec, pl.BlockSpec(norm.shape, lambda i: (0, 0)), flat, flat],
        out_specs=[flat] * 3,
        scratch_shapes=[pltpu.VMEM((BLOCK, 128), f32), pltpu.VMEM((n_at * BLOCK, 128), f32)],
        compiler_params=params(),
        cost_estimate=cost(0, m1.size * 22),
        name="adam_all",
    )(*back, *inner, *attention, norm, m1, m2)


def after(x, *deps):
    return lax.optimization_barrier((x, deps))[0]


def body(n, nz, tokens, cotangent, doc_ids, master, moment_one, moment_two):
    t, d = tokens.shape
    ff = (master.shape[0] * n - 4 * d) // (2 * d) - 2 * d
    me = lax.axis_index(("y", "x"))
    rows = d // n
    comm = n == 4 and nz == 4

    lanes = master.reshape(-1, 128)
    w, o, norm_share = unpack_first(lanes, n, d, ff)
    doc_row = doc_ids.reshape(1, t)
    if not comm:
        w, o = spread(w), spread(o)
        norm_share = lax.all_gather(master[-(4 * d // n) :].astype(bf16), ("y", "x"), axis=0, tiled=True)
        norm_share = norm_share.astype(f32).reshape(-1, 128)
    (a_one, qkv, in_own, bk_own, w_own, w_oth, o_own, o_oth, norms, d_out, doc_col, att, lse, in_oth, a_one_p, d_out_p) = project_qkv(
        lanes, tokens, cotangent, doc_row, norm_share, w, o, n, ff, comm
    )
    resid, a_two, hidden, slope, bk_own, bk_oth, att_p, g_back = middle(
        att, tokens, norms, o_own, o_oth, in_own, in_oth, bk_own, d_out, d_out_p, comm
    )
    g_in, d_resid, low, d_att, two_norm, low_p, part_back = feed_back(
        d_out, slope, bk_own, bk_oth, in_own, in_oth, resid, norms, o_own, o_oth, a_two, g_back, n, comm
    )
    dq, dk, dv, dqkv_p, red_back, part_in = attend_back(qkv, d_att, att, lse, doc_row, doc_col, part_back, g_in, d, n, comm)
    input_grad, mixed, red_in, red_in_p, red_at, red_at_p, sums = last_grad(
        [dq, dk, dv], dqkv_p, low, low_p, tokens, d_resid, norms, hidden, resid, doc_col, two_norm, a_one, a_one_p, att, att_p,
        w_own, w_oth, bk_own, bk_oth, part_in, n, comm,
    )
    red_in, red_at = (red_in, red_in_p), (red_at, red_at_p)
    if not comm:
        red_in, red_at = both_halves(part_in), both_halves(scatter_pieces(red_at[0]))
        sums = lax.psum(sums, ("z", "core", "y", "x"))

    inv_root = float(t * n * nz * 2) ** (-0.5)
    m1, m2 = moment_one.reshape(-1, 128), moment_two.reshape(-1, 128)
    nb = d // 128
    half = nb // 2
    hs = ff // n // 2
    r_qkv, r_out, r_in = rows * 3 * nb, rows * nb, rows * ff // 128
    back_at = r_qkv + r_out + r_in
    at_in = [(hs * j + q * 128, (2 * hs * j) // 128 + q, (2 * hs * j + hs) // 128 + q) for j in range(n) for q in range(hs // 128)]
    at_qkv = [((p * half + w) * 128, p * nb + w, p * nb + w + half) for p in range(3) for w in range(half)]
    at_out = [(w * 128, w, w + half) for w in range(half)]
    if comm:
        outs = adam_all(red_back, red_in, red_at, sums, m1, m2, inv_root, (at_in, at_qkv, at_out))
    else:
        plain = lambda v: v.transpose(1, 0, 2).reshape(v.shape[1], -1)
        count = red_at[0].shape[0]
        outs = adam_rows_halves(plain(red_back[0]), plain(red_back[1]), m1, m2, [], inv_root, back_at)
        outs = adam_columns(*red_in, 0, red_in[0].shape[0], m1, m2, outs, inv_root, r_qkv + r_out, rows // 8, at_in)
        outs = adam_columns(*red_at, 0, 3 * count // 4, m1, m2, outs, inv_root, 0, rows // 8, at_qkv)
        outs = adam_columns(*red_at, 3, count // 4, m1, m2, outs, inv_root, r_qkv, rows // 2, at_out)
        per = 4 * nb // n
        norm_part = lax.dynamic_slice_in_dim(sums, group_index(n) * per, per, 0) * inv_root
        outs = adam_tail(norm_part, m1, m2, outs, back_at + ff // n * nb)
    weight_grad, step, moment = [o.reshape(-1) for o in outs]
    return mixed, input_grad, weight_grad, step, moment


def solution(mesh):
    dp, n = mesh.shape["dp"], mesh.shape["group"]
    fine = Mesh(mesh.devices.reshape(dp // 2, 2, n // 2, 2), ("z", "core", "y", "x"))
    tok = ("z", "core", "y", "x")
    flat = P(("y", "x"))
    in_specs = (P(tok, None), P(tok, None), P(tok), flat, flat, flat)
    out_specs = (P(tok, None), P(tok, None), flat, flat, flat)
    return jax.shard_map(
        functools.partial(body, n, dp // 2), mesh=fine, in_specs=in_specs, out_specs=out_specs, check_vma=False
    )
```

```python
import functools

import jax
import jax.numpy as jnp
from jax import lax
from jax.experimental import pallas as pl
from jax.experimental.pallas import tpu as pltpu
from jax.sharding import Mesh
from jax.sharding import PartitionSpec as P

HEADS = 16
EPS = 1e-05
FILL = -1e30
BETA_ONE = 0.9
BETA_TWO = 0.999
RATE = 0.001
ADAM_EPS = 1e-08
STEPS = 100.0
VMEM_MB = 60

f32 = jnp.float32
bf16 = jnp.bfloat16
ANY = pl.BlockSpec(memory_space=pl.ANY)


def params(limit=VMEM_MB):
    return pltpu.CompilerParams(vmem_limit_bytes=limit << 20)


def cost(flops, nbytes, trans=0):
    return pl.CostEstimate(flops=int(flops), bytes_accessed=int(nbytes), transcendentals=int(trans))


def sds(shape, dtype):
    return jax.ShapeDtypeStruct(shape, dtype)


def dot_nn(a, b):
    return jnp.dot(a, b, preferred_element_type=f32)


def dot_nt(a, b):
    return lax.dot_general(a, b, (((1,), (1,)), ((), ())), preferred_element_type=f32)


def dot_tn(a, b):
    return lax.dot_general(a, b, (((0,), (0,)), ((), ())), preferred_element_type=f32)


def pick(flag, a, b):
    return jnp.where(flag, a, b)


MESH = pl.DeviceIdType.MESH


def peer(*axes):
    return {a: 1 - lax.axis_index(a) for a in axes}


def greet_start(peers):
    barrier = pltpu.get_barrier_semaphore()
    for p in peers:
        pl.semaphore_signal(barrier, inc=1, device_id=p, device_id_type=MESH)


def greet_end(peers):
    pl.semaphore_wait(pltpu.get_barrier_semaphore(), len(peers))


def greet(peers):
    greet_start(peers)
    greet_end(peers)


def member():
    return lax.axis_index("y") * 2 + lax.axis_index("x")


class Gather:
    COUNT = 11

    def __init__(self, own, oth, send, recv, base, mine=None):
        rows = own.shape[0] // 4
        half = rows // 2
        x, y = lax.axis_index("x"), lax.axis_index("y")
        share = [y * 2 + x, y * 2 + 1 - x, (1 - y) * 2 + x, (1 - y) * 2 + 1 - x]
        self.rows = [pl.ds(pl.multiple_of(k * rows, 8), rows) for k in share]

        def move(i, k, off, count, dst, to):
            at = pl.ds(pl.multiple_of(share[k] * rows + off, 8), count)
            here = own.at[at, :] if mine is None or k else mine.at[pl.ds(off, count), :]
            return pltpu.make_async_remote_copy(
                src_ref=here, dst_ref=dst.at[at, :],
                send_sem=send.at[base + i], recv_sem=recv.at[base + i], device_id=peer(to), device_id_type=MESH,
            )

        self.moves = [
            move(0, 0, 0, half, own, "x"),
            move(1, 0, half, half, own, "x"),
            move(2, 0, half, half, own, "y"),
            move(3, 0, 0, half, own, "y"),
            move(4, 0, 0, rows, oth, "core"),
            move(5, 1, 0, half, own, "y"),
            move(6, 2, half, half, own, "x"),
            move(7, 1, 0, rows, oth, "core"),
            move(8, 2, 0, rows, oth, "core"),
            move(9, 3, 0, half, oth, "core"),
            move(10, 3, half, half, oth, "core"),
        ]

    def begin(self):
        for i in (0, 2, 1, 3, 4):
            self.moves[i].start()

    def relay(self):
        self.moves[0].wait_recv()
        self.moves[5].start()
        self.moves[2].wait_recv()
        self.moves[6].start()

    def forward(self):
        self.moves[1].wait_recv()
        self.moves[7].start()
        self.moves[3].wait_recv()
        self.moves[8].start()

    def close(self):
        self.moves[5].wait_recv()
        self.moves[9].start()
        self.moves[6].wait_recv()
        self.moves[10].start()

    def arrive(self, *which):
        for i in which:
            self.moves[i].wait_recv()

    def sent(self):
        for m in self.moves:
            m.wait_send()

    def finish(self):
        self.close()
        self.arrive(4, 7, 8, 9, 10)
        self.sent()


def hand_over(src, dst, send, recv):
    return pltpu.make_async_remote_copy(
        src_ref=src, dst_ref=dst, send_sem=send, recv_sem=recv, device_id=peer("core"), device_id_type=MESH
    )


def add_up(dst, a, b):
    dst[...] = a[...] + b[...]


class Fold:
    def __init__(self, source, mine, inbox, cross, stage, total, red, theirs, keep, send, recv, base):
        self.pieces = len(mine)
        self.out = [pltpu.make_async_copy(total.at[s], red.at[s], keep.at[s]) for s in range(self.pieces)]
        z = lax.axis_index("z")
        self.end = (z == 0) | (z == 3)
        self.mid = (z == 1) | (z == 2)
        near, far = self.peers()
        self.mine, self.inbox, self.across, self.stage, self.total = mine, inbox, cross, stage, total

        def move(s, kind, src, dst, to):
            i = base + 4 * s + kind
            return pltpu.make_async_remote_copy(
                src_ref=src, dst_ref=dst, send_sem=send.at[i], recv_sem=recv.at[i], device_id=to, device_id_type=MESH
            )

        every = range(self.pieces)
        self.fold = [move(s, 0, source[s], inbox.at[s], near) for s in every]
        self.cross = [move(s, 1, stage.at[s], cross.at[s], far) for s in every]
        self.unfold = [move(s, 2, total.at[s], total.at[s], near) for s in every]
        self.core = [move(s, 3, total.at[s], theirs.at[s], peer("core")) for s in every]

    @staticmethod
    def peers():
        z = lax.axis_index("z")
        return [{"z": z + 1 - 2 * (z % 2)}, {"z": 3 - z}]

    def begin(self, s):
        pl.when(self.end)(self.fold[s].start)

    def inner(self, s):
        @pl.when(self.mid)
        def _():
            self.fold[s].wait_recv()
            add_up(self.stage.at[s], self.mine[s], self.inbox.at[s])
            self.cross[s].start()

    def outer(self, s):
        @pl.when(self.mid)
        def _():
            self.cross[s].wait_recv()
            add_up(self.total.at[s], self.stage.at[s], self.across.at[s])
            self.unfold[s].start()
            self.core[s].start()
            self.out[s].start()

    def land(self, s):
        @pl.when(self.end)
        def _():
            self.unfold[s].wait_recv()
            self.core[s].start()
            self.out[s].start()

    def finish(self):
        @pl.when(self.end)
        def _():
            for m in self.fold:
                m.wait_send()

        @pl.when(self.mid)
        def _():
            for m in self.cross + self.unfold:
                m.wait_send()

        for m in self.core + self.out:
            m.wait()


def pieces_of(ref):
    return [ref.at[i] for i in range(ref.shape[0])]


def fold_scratch(pieces, rows, cols):
    return [pltpu.VMEM((pieces, rows, cols), bf16)] * 4


class Scatter:
    def __init__(self, source, held, far, near, mid, total, send, recv, base, out=None, keep=None):
        pieces, rows, _ = held.shape
        self.out = [] if out is None else [pltpu.make_async_copy(total.at[s], out.at[s], keep.at[s]) for s in range(pieces)]
        block = rows // 4
        half = block // 2
        x, y = lax.axis_index("x"), lax.axis_index("y")
        me, over_x, over_y, both = y * 2 + x, y * 2 + 1 - x, (1 - y) * 2 + x, (1 - y) * 2 + 1 - x
        self.pieces, self.held, self.far, self.near, self.mid, self.total, self.half = pieces, held, far, near, mid, total, half

        def at(share, part):
            return pl.ds(pl.multiple_of(share * block + part * half, half), half)

        def move(i, src, dst, to):
            return pltpu.make_async_remote_copy(
                src_ref=src, dst_ref=dst, send_sem=send.at[base + i], recv_sem=recv.at[base + i],
                device_id=peer(to), device_id_type=MESH,
            )

        self.first, self.second = [], []
        for s in range(pieces):
            b = 6 * s
            self.first.append([
                move(b, source.at[s, at(over_x, 0), :], far.at[s, 0], "x"),
                move(b + 1, source.at[s, at(both, 0), :], far.at[s, 1], "x"),
                move(b + 2, source.at[s, at(over_y, 1), :], far.at[s, 2], "y"),
                move(b + 3, source.at[s, at(both, 1), :], far.at[s, 3], "y"),
            ])
            self.second.append([move(b + 4, mid.at[s, 1], near.at[s, 0], "y"), move(b + 5, mid.at[s, 3], near.at[s, 1], "x")])
        self.keep = [at(me, 0), at(over_y, 0), at(me, 1), at(over_x, 1)]

    def begin(self, s):
        for k in (1, 3, 0, 2):
            self.first[s][k].start()

    def turn(self, s):
        for k in (1, 3, 0, 2):
            self.first[s][k].wait_recv()
            add_up(self.mid.at[s, k], self.held.at[s, self.keep[k], :], self.far.at[s, k])
            if k in (1, 3):
                self.second[s][k // 2].start()

    def close(self, s):
        for part in range(2):
            self.second[s][part].wait_recv()
            at = pl.ds(part * self.half, self.half)
            add_up(self.total.at[s, at, :], self.mid.at[s, 2 * part], self.near.at[s, part])
        if self.out:
            self.out[s].start()

    def finish(self):
        for s in range(self.pieces):
            for m in self.first[s] + self.second[s]:
                m.wait_send()
        for m in self.out:
            m.wait()


def scatter_scratch(pieces, rows, cols):
    half = rows // 8
    four = pltpu.VMEM((pieces, 4, half, cols), bf16)
    return [pltpu.VMEM((pieces, rows, cols), bf16), four, pltpu.VMEM((pieces, 2, half, cols), bf16), four]


def swap_core(v):
    return lax.ppermute(v, "core", [(0, 1), (1, 0)])


def comm_params(cid, limit=VMEM_MB):
    if cid is None:
        return params(limit)
    return pltpu.CompilerParams(vmem_limit_bytes=limit << 20, collective_id=cid, has_side_effects=True)


def dma(count):
    return pltpu.SemaphoreType.DMA((count,))


def gain_row(norms, r, d):
    nb = d // 128
    return jnp.concatenate([norms[r * nb + i : r * nb + i + 1, :] for i in range(nb)], axis=1)


def layer_norm_parts(v):
    centre = v - jnp.mean(v, axis=-1, keepdims=True)
    r = lax.rsqrt(jnp.mean(centre * centre, axis=-1, keepdims=True) + EPS)
    return centre * r, r


def layer_norm_back(v, gain, dz):
    xhat, r = layer_norm_parts(v)
    dg = jnp.sum(dz * xhat, axis=0, keepdims=True)
    db = jnp.sum(dz, axis=0, keepdims=True)
    t = dz * gain
    dv = r * (t - jnp.mean(t, axis=-1, keepdims=True) - xhat * jnp.mean(t * xhat, axis=-1, keepdims=True))
    return dv, dg, db


def unpack_kernel(dims, m_qkv, m_out, m_norm, own_qkv, own_out, norm):
    n, d = dims
    core = lax.axis_index("core")
    nb = d // 128
    half = nb // 2
    rows = own_qkv.shape[0]

    def put(ref, own, dst, lo, stride):
        own[:, dst : dst + 128] = ref[pl.ds(lo + core * half, rows, stride=stride), :].astype(bf16)

    for part in range(3):
        for w in range(half):
            put(m_qkv, own_qkv, (part * half + w) * 128, part * nb + w, 3 * nb)
    for w in range(half):
        put(m_out, own_out, w * 128, w, nb)
    norm[...] = m_norm[...].astype(bf16).astype(f32)


def group_index(n):
    return lax.axis_index(("y", "x"))


def unpack_first(lanes, n, d, ff):
    rows = d // n
    nb = d // 128
    r1, r2, r3, r4 = rows * 3 * nb, rows * nb, rows * ff // 128, ff // n * nb
    steps = 4 if n == 4 else 2
    sr = rows // steps
    me = lambda: group_index(n)
    return pl.pallas_call(
        functools.partial(unpack_kernel, (n, d)),
        grid=(steps,),
        out_shape=[sds((d, 3 * d // 2), bf16), sds((d, d // 2), bf16), sds((8, 128), f32)],
        in_specs=[
            pl.BlockSpec((r1 // steps, 128), lambda i: (i, 0)),
            pl.BlockSpec((r2 // steps, 128), lambda i: (r1 // (r2 // steps) + i, 0)),
            pl.BlockSpec((8, 128), lambda i: ((r1 + r2 + r3 + r4) // 8, 0)),
        ],
        out_specs=[
            pl.BlockSpec((sr, 3 * d // 2), lambda i: (me() * steps + i, 0)),
            pl.BlockSpec((sr, d // 2), lambda i: (me() * steps + i, 0)),
            pl.BlockSpec((8, 128), lambda i: (0, 0)),
        ],
        compiler_params=params(),
        name="unpack",
    )(lanes, lanes, lanes)


UNPACK_STEPS = 8


def qkv_kernel(cfg, tok, norm_share, m_in, m_back, w_own_in, w_oth_in, o_own_in, o_oth_in, cot, docs, *refs):
    n, comm, hd = cfg
    (a_hbm, qkv_hbm, in_own, own_bk, w_own, w_oth, o_own, o_oth, norms_out, d_hbm, doc_col, att, lse, in_oth, a_p, d_p,
     norms, w, toks, acc, cots, qkv, a_out, own_in, bias, raw, own_w, own_o, noted, lsem, send, recv) = refs
    if not comm:
        w_own, w_oth = w_own_in, w_oth_in
    t, d = toks.shape
    step = pl.program_id(0)
    nb = d // 128
    half = 3 * d // 2
    share = d // n
    tm = min(256, t)
    tok_copy = pltpu.make_async_copy(tok, toks, lsem.at[0])
    cot_copy = pltpu.make_async_copy(cot, cots, lsem.at[1 + 2 * n])
    a_copy = pltpu.make_async_copy(a_out, a_hbm, lsem.at[2 + 2 * n])
    d_copy = pltpu.make_async_copy(cots, d_hbm, lsem.at[3 + 2 * n])
    place = pl.ds(pl.multiple_of(group_index(n) * share, 8), share)
    in_copy = pltpu.make_async_copy(own_in, in_own.at[place, :], lsem.at[5 + 2 * n])
    if comm:
        own_copies = [
            pltpu.make_async_copy(own_w, w_own.at[place, :], lsem.at[7 + 2 * n]),
            pltpu.make_async_copy(own_o, o_own.at[place, :], lsem.at[8 + 2 * n]),
        ]
    out = pltpu.make_async_copy(qkv, qkv_hbm, lsem.at[4 + 2 * n])

    if comm:
        me = member()
        near = [peer("x"), peer("y"), peer("x", "y")]
        mine = pl.ds(pl.multiple_of(me * 8, 8), 8)
        notes = [
            pltpu.make_async_remote_copy(
                src_ref=noted, dst_ref=norms.at[mine, :], send_sem=send.at[22 + i], recv_sem=recv.at[22 + i],
                device_id=p, device_id_type=MESH,
            )
            for i, p in enumerate(near)
        ]
        first = Gather(w_own, w_oth, send, recv, 0, own_w)
        second = Gather(o_own, o_oth, send, recv, 11, own_o)
        third = Gather(in_own, in_oth, send, recv, 25, own_in)
        swaps = [hand_over(a_out, a_p, send.at[36], recv.at[36]), hand_over(cots, d_p, send.at[37], recv.at[37])]
        rows = first.rows
    else:
        rows = [pl.ds(k * share, share) for k in range(n)]

    @pl.when(step == 0)
    def _():
        tok_copy.start()
        cot_copy.start()
        if comm:
            fetch = pltpu.make_async_copy(w_own_in.at[pl.ds(0, raw.shape[0]), :], raw, lsem.at[6 + 2 * n])
            fetch.start()
            greet_start(near + [peer("core")])
            noted[...] = norm_share[...].astype(bf16).astype(f32)
            norms[mine, :] = noted[...]
            fetch.wait()
            core = lax.axis_index("core")
            hb = nb // 2

            @pl.loop(0, hb)
            def _(c):
                def put(base, own, dst, lo, stride):
                    cols = pl.ds(pl.multiple_of((dst + c) * 128, 128), 128)
                    own[:, cols] = raw[pl.ds(base + lo + c + core * hb, share, stride=stride), :].astype(bf16)

                for part in range(3):
                    put(0, own_w, part * hb, part * nb, 3 * nb)
                put(share * 3 * nb, own_o, 0, 0, nb)

            greet_end(near + [peer("core")])
            for m in notes:
                m.start()
            first.begin()
            own_copies[0].start()
            own_copies[1].start()

    @pl.when(step < UNPACK_STEPS)
    def _():
        core = lax.axis_index("core")
        rows_in = own_in.shape[0] // UNPACK_STEPS
        there = pl.ds(pl.multiple_of(step * rows_in, 8), rows_in)
        hs = own_in.shape[1] // n
        stride = m_in.shape[0] // rows_in
        for j in range(n):
            for q in range(hs // 128):
                lo = (2 * hs * j) // 128 + q + core * (hs // 128)
                at = hs * j + q * 128
                own_in[there, at : at + 128] = m_in[pl.ds(lo, rows_in, stride=stride), :].astype(bf16)
        for q in range(nb):
            own_bk[:, q * 128 : (q + 1) * 128] = m_back[pl.ds(q, own_bk.shape[0], stride=nb), :].astype(bf16)

    def load(*which):
        cps = []
        for k in which:
            cps.append(pltpu.make_async_copy(w_own.at[rows[k], :], w.at[k, :, pl.ds(0, half)], lsem.at[1 + 2 * k]))
            cps.append(pltpu.make_async_copy(w_oth.at[rows[k], :], w.at[k, :, pl.ds(half, half)], lsem.at[2 + 2 * k]))
        for cp in cps:
            cp.start()
        for cp in cps:
            cp.wait()

    def product(at, *which):
        return sum(dot_nn(a_out[at, cols_of(k)], w[k]) for k in which)

    def cols_of(k):
        if comm:
            return rows[k]
        return slice(k * share, (k + 1) * share)

    def each_block(fn):
        @pl.loop(0, t // tm)
        def _(i):
            fn(pl.ds(pl.multiple_of(i * tm, tm), tm))

    @pl.when(step == UNPACK_STEPS)
    def _():
        if comm:
            for m in notes:
                m.wait()
            first.relay()
            second.begin()
        else:
            norms[...] = norm_share[...]
        norms_out[...] = norms[...]
        tok_copy.wait()
        gain, shift = gain_row(norms, 0, d), gain_row(norms, 1, d)

        def norm(at):
            xhat, _ = layer_norm_parts(toks[at, :].astype(f32))
            a_out[at, :] = (xhat * gain + shift).astype(bf16)

        each_block(norm)
        cot_copy.wait()
        doc_col[...] = jnp.broadcast_to(docs[...].astype(f32), (128, t)).T[:, :1].astype(jnp.int32)

        def mask(at):
            cots[at, :] = jnp.where(doc_col[at, :] >= 0, cots[at, :].astype(f32), 0.0).astype(bf16)

        each_block(mask)
        a_copy.start()
        d_copy.start()
        in_copy.start()
        fill_bias(bias, docs, doc_col)
        if comm:
            own_copies[0].wait()
            first.arrive(4)
        load(0)

        def start(at):
            acc[at, :] = product(at, 0)

        each_block(start)

    @pl.when(step == UNPACK_STEPS + 1)
    def _():
        if comm:
            first.forward()
            third.begin()
            first.arrive(7, 8)
        load(*range(1, n - 1))

        def more(at):
            acc[at, :] += product(at, *range(1, n - 1))

        each_block(more)

    @pl.when(step == UNPACK_STEPS + 2)
    def _():
        if comm:
            first.close()
            second.relay()
            first.arrive(9, 10)
        load(n - 1)
        scale = (d // HEADS) ** (-0.5)
        q = d // 2

        def last(at):
            total = acc[at, :] + product(at, n - 1)
            for o in (0, half):
                qkv[at, o : o + q] = (total[:, o : o + q].astype(bf16).astype(f32) * scale).astype(bf16)
                qkv[at, o + q : o + half] = total[:, o + q : o + half].astype(bf16)

        each_block(last)
        out.start()

    start = UNPACK_STEPS + 3
    if comm:

        @pl.when(step == start + 1)
        def _():
            second.forward()
            for m in swaps:
                m.start()

        @pl.when(step == start + 3)
        def _():
            third.relay()

        @pl.when(step == start + 6)
        def _():
            third.forward()
            second.close()

    @pl.when(step >= start)
    def _():
        pair = step - start
        pairs = d // 256
        first_col = (pair // pairs) * half + (pair % pairs) * 128

        def part(k):
            return qkv.at[:, pl.ds(pl.multiple_of(first_col + k * (d // 2), 128), 128)]

        attend_pair(hd, part(0), part(1), part(2), bias, att, lse)

    @pl.when(step == pl.num_programs(0) - 1)
    def _():
        if comm:
            own_copies[1].wait()
            third.finish()
            second.arrive(4, 7, 8, 9, 10)
            second.sent()
            first.sent()
            for m in swaps:
                m.wait()
        for cp in (a_copy, d_copy, in_copy, out):
            cp.wait()


def attend_pair(hd, q, k, v, bias, out, lse):
    t = q.shape[0]
    vt = v[...].T
    per = 128 // hd
    qs = [head_lanes(q[...], h, hd) for h in range(per)]
    for i in range(t // QB):
        n = (i + 1) * QB
        cols = slice(i * QB, n)
        outs = []
        for h in range(per):
            s = dot_nt(k[:n, :], qs[h][cols, :]) + bias[:n, cols]
            top = jnp.max(s, axis=0, keepdims=True)
            e = jnp.exp(s - top)
            total = jnp.sum(e, axis=0, keepdims=True)
            lse[0, h : h + 1, cols] = top + jnp.log(total)
            o = dot_nn(vt[h * hd : (h + 1) * hd, :n], e.astype(bf16))
            outs.append(o * (1.0 / total))
        out[cols, :] = jnp.concatenate(outs, axis=0).T.astype(bf16)


def project_qkv(lanes, tok, cot, docs, norm_share, w, o, n, ff, comm):
    t, d = tok.shape
    rows = d // n
    nb = d // 128
    hs = ff // n // 2
    r_in, r_bk = rows * ff // 128, ff // n * nb
    at_in, at_bk = rows * 4 * nb, rows * 4 * nb + r_in
    b_in, b_bk = r_in // UNPACK_STEPS, hs * nb // UNPACK_STEPS
    assert at_in % b_in == 0 and at_bk % b_bk == 0
    up = lambda i: jnp.minimum(i, UNPACK_STEPS - 1)
    me = lambda: group_index(n)
    whole = lambda s: pl.BlockSpec(s, lambda i: (0, 0))
    half = 3 * d // 2
    pairs, hd = d // 128, d // HEADS
    per = 128 // hd
    pair = lambda i: jnp.maximum(i - UNPACK_STEPS - 3, 0)
    shapes = [sds((t, d), bf16), sds((t, 3 * d), bf16), sds((d, ff // 2), bf16), sds((ff // 2, d), bf16),
              sds((d, half), bf16), sds((d, half), bf16), sds((d, d // 2), bf16), sds((d, d // 2), bf16), sds((4 * nb, 128), f32),
              sds((t, d), bf16), sds((t, 1), jnp.int32), sds((t, d), bf16), sds((pairs, per, t), f32), sds((d, ff // 2), bf16),
              sds((t, d), bf16), sds((t, d), bf16)]
    w_args = [lanes] * 4 if comm else [w[0], w[1], o[0], o[1]]
    if comm:
        norm_share = lanes
        norm_spec = pl.BlockSpec((8, 128), lambda i: (lanes.shape[0] // 8 - 1, 0))
    else:
        norm_spec = whole(norm_share.shape)
    outs = pl.pallas_call(
        functools.partial(qkv_kernel, (n, comm, hd)),
        grid=(UNPACK_STEPS + 3 + pairs,),
        out_shape=shapes,
        in_specs=[
            ANY, norm_spec,
            pl.BlockSpec((b_in, 128), lambda i: (at_in // b_in + up(i), 0)),
            pl.BlockSpec((b_bk, 128), lambda i: (at_bk // b_bk + lax.axis_index("core") * UNPACK_STEPS + up(i), 0)),
            ANY, ANY, ANY, ANY, ANY, whole((1, t)),
        ],
        out_specs=[
            ANY, ANY, ANY,
            pl.BlockSpec((hs // UNPACK_STEPS, d), lambda i: (me() * UNPACK_STEPS + up(i), 0)),
            ANY, ANY, ANY, ANY, whole((4 * nb, 128)), ANY, whole((t, 1)),
            pl.BlockSpec((t, 128), lambda i: (0, pair(i))), pl.BlockSpec((1, per, t), lambda i: (pair(i), 0, 0)), ANY, ANY, ANY,
        ],
        scratch_shapes=[pltpu.VMEM((4 * nb, 128), f32), pltpu.VMEM((n, rows, 3 * d), bf16), pltpu.VMEM((t, d), bf16),
                        pltpu.VMEM((t, 3 * d), f32), pltpu.VMEM((t, d), bf16), pltpu.VMEM((t, 3 * d), bf16), pltpu.VMEM((t, d), bf16),
                        pltpu.VMEM((rows, ff // 2), bf16), pltpu.VMEM((t, t), f32), pltpu.VMEM((rows * 4 * nb, 128), f32),
                        pltpu.VMEM((rows, half), bf16), pltpu.VMEM((rows, d // 2), bf16), pltpu.VMEM((8, 128), f32),
                        dma(9 + 2 * n), dma(38), dma(38)],
        input_output_aliases={} if comm else {4: 4, 6: 6},
        compiler_params=comm_params(1 if comm else None),
        cost_estimate=cost(2 * t * d * 3 * d + 8 * t * t * d, 50e6, t * t * HEADS),
        name="qkv_attend",
    )(tok, norm_share, lanes, lanes, *w_args, cot, docs)
    if comm:
        return outs
    full, oth = spread(outs[2])
    return [*outs[:2], full, outs[3], w[0], w[1], o[0], o[1], *outs[8:13], oth, swap_core(outs[0]), swap_core(outs[9])]


QB = 256


def fill_bias(bias, doc_row, doc_col):
    t = bias.shape[0]
    for r in range(0, t, QB):
        key = r + lax.broadcasted_iota(jnp.int32, (QB, t), 0)
        query = lax.broadcasted_iota(jnp.int32, (QB, t), 1)
        ok = (doc_col[r : r + QB, :] == doc_row[...]) & (key <= query)
        bias[r : r + QB, :] = jnp.where(ok, 0.0, FILL)


def head_lanes(v, h, hd):
    lane = lax.broadcasted_iota(jnp.int32, v.shape, 1)
    return jnp.where((lane >= h * hd) & (lane < (h + 1) * hd), v, jnp.zeros_like(v))


def head_column(d, part):
    pairs = d // 256
    return lambda p: (0, (p // pairs) * 3 * pairs + part * pairs + p % pairs)


def spread(own):
    n = lax.axis_size("y") * lax.axis_size("x")
    rows = own.shape[0] // n
    mine = lax.dynamic_slice_in_dim(own, lax.axis_index(("y", "x")) * rows, rows, 0)
    full = lax.all_gather(mine, ("y", "x"), axis=0, tiled=True)
    return full, swap_core(full)


def attend_back_kernel(cfg, q, k, v, dout, att, lse, doc_row, doc_col, part_sum, g_in, dq, dk, dv, sent, red, red_p, part_in, *refs):
    hd, comm = cfg
    bias, dk_acc, dv_acc, stage, lsem, send, recv = refs[:7]
    step = pl.program_id(0)
    pairs = stage.shape[0] // 3

    def hand(p, part):
        wide = 128 * pairs
        cols = pl.ds(pl.multiple_of(part * wide + p * 128, 128), 128)
        i = p * 3 + part
        return hand_over(stage.at[i], sent.at[:, cols], send.at[i], recv.at[i])

    if comm:

        base = 3 * pairs
        mine, keep, held, far, near, mid, total, keep_in = refs[7], refs[12], *refs[13:19]
        fold = Fold(pieces_of(part_sum), pieces_of(mine), *refs[8:12], red, red_p, keep, send, recv, base)
        scat = Scatter(g_in, held, far, near, mid, total, send, recv, base + 4 * PIECES, part_in, keep_in)
        acts = (scat.begin, scat.turn, scat.close, fold.inner, fold.outer, fold.land)

        @pl.when(step == 0)
        def _():
            loads = [pltpu.make_async_copy(part_sum, mine, lsem.at[0]), pltpu.make_async_copy(g_in, held, lsem.at[1])]
            for cp in loads:
                cp.start()
            greet([peer("core"), peer("x"), peer("y")] + Fold.peers())
            run_plan(acts, BACK_PLAN[0])
            for s in range(PIECES):
                fold.begin(s)
            for cp in loads:
                cp.wait()

        @pl.when((step > 0) & (step <= pairs))
        def _():
            for part in range(3):
                hand(step - 1, part).start()

    @pl.when(step == 0)
    def _():
        fill_bias(bias, doc_row, doc_col)

    if comm:
        for at, codes in enumerate(BACK_PLAN[:-1]):
            if codes and at > 0:
                pl.when(step == at)(functools.partial(run_plan, acts, codes))

    t = q.shape[0]
    per = 128 // hd
    scale = hd ** (-0.5)
    kt = k[...].T
    prod = (dout[...].astype(f32) * att[...].astype(f32)).T
    inner = [jnp.sum(prod[h * hd : (h + 1) * hd, :], axis=0, keepdims=True) for h in range(per)]
    qs = [head_lanes(q[...], h, hd) for h in range(per)]
    ds_ = [head_lanes(dout[...], h, hd) for h in range(per)]
    dk_acc[...] = jnp.zeros_like(dk_acc)
    dv_acc[...] = jnp.zeros_like(dv_acc)
    for i in range(t // QB):
        n = (i + 1) * QB
        cols = slice(i * QB, n)
        dqs = []
        for h in range(per):
            qh, dh = qs[h][cols, :], ds_[h][cols, :]
            s = dot_nt(k[:n, :], qh) + bias[:n, cols]
            p = jnp.exp(s - lse[0, h : h + 1, cols])
            dp = dot_nt(v[:n, :], dh)
            g = (p * (dp - inner[h][:, cols])).astype(bf16)
            dv_acc[:n, :] += dot_nn(p.astype(bf16), dh)
            dk_acc[:n, :] += dot_nn(g, qh)
            dqs.append(dot_nn(kt[h * hd : (h + 1) * hd, :n], g))
        dq[cols, :] = (jnp.concatenate(dqs, axis=0).T * scale).astype(bf16)
    dk[...] = dk_acc[...].astype(bf16)
    dv[...] = dv_acc[...].astype(bf16)

    if comm:

        @pl.when(step < pairs)
        def _():
            stage[step * 3] = dq[...]
            stage[step * 3 + 1] = dk[...]
            stage[step * 3 + 2] = dv[...]

        @pl.when(step == 2 * pairs - 1)
        def _():
            for p in range(pairs):
                for part in range(3):
                    hand(p, part).wait()
            run_plan(acts, BACK_PLAN[-1])
            fold.finish()
            scat.finish()


def run_plan(acts, codes):
    for code in codes:
        acts[code // 10](code % 10)


FEED_PLAN = (
    (0, 1),
    (),
    (),
    (10, 2),
    (),
    (11, 3, 20),
    (),
    (12, 4, 21),
    (),
    (13, 5, 22),
    (14, 6),
    (23, 15, 7),
    (24,),
    (16, 25, 17),
    (26, 27),
    (),
    (),
)
BACK_PLAN = (
    (0, 1, 2, 3),
    (),
    (30, 31, 10, 4, 11, 5),
    (32, 40, 33, 12, 6),
    (41, 20, 34, 13, 7, 42, 35),
    (43, 21, 50, 36, 14, 15, 44, 37),
    (45, 22, 51, 52, 16, 23, 46),
    (47, 24, 53, 54, 17),
    (25, 26, 27, 55, 56, 57),
)
LAST_PLAN = (
    (),
    (0,),
    (1,),
    (30,),
    (10, 2, 31),
    (11, 3, 32, 40),
    (20, 33, 41),
    (12, 4, 34, 42),
    (21, 35, 43, 50),
    (13, 5, 22, 36, 44, 45, 37, 51),
    (14, 6, 23, 60, 46, 52, 53),
    (15, 7, 24, 61, 62, 70, 47, 54),
    (16, 25, 63, 64, 71, 55),
    (17, 26, 65, 72, 73, 66, 56, 90),
    (27, 67, 74, 75, 80, 91),
    (76, 81, 57, 92),
    (77, 93, 82, 94, 83, 95, 84, 85, 86, 87),
)
PIECES = 8


def attend_back(qkv, dout, att, lse, doc_row, doc_col, part_sum, g_in, d, n, comm):
    t = qkv.shape[0]
    pairs = d // 128
    half = pairs // 2
    hd = d // HEADS
    per = 128 // hd
    turn = lambda p: (p + half) % pairs
    part_in = (g_in.shape[0], g_in.shape[1] // n, g_in.shape[2])
    col = lambda part: pl.BlockSpec((t, 128), lambda p: head_column(d, part)(turn(p)))
    one = pl.BlockSpec((t, 128), lambda p: (0, turn(p)))
    sems = 3 * half + 10 * PIECES
    extra = []
    if comm:
        extra = [pltpu.VMEM(part_sum.shape, bf16)] + fold_scratch(*part_sum.shape) + [dma(PIECES)]
        extra += scatter_scratch(*g_in.shape) + [pltpu.VMEM(part_in, bf16), dma(PIECES)]
    outs = pl.pallas_call(
        functools.partial(attend_back_kernel, (hd, comm)),
        grid=(pairs,),
        out_shape=[sds((t, d), bf16)] * 3 + [sds((t, 3 * d // 2), bf16)] + [sds(part_sum.shape, bf16)] * 2 + [sds(part_in, bf16)],
        in_specs=[col(0), col(1), col(2), one, one, pl.BlockSpec((1, per, t), lambda p: (turn(p), 0, 0)),
                  pl.BlockSpec((1, t), lambda p: (0, 0)), pl.BlockSpec((t, 1), lambda p: (0, 0)), ANY, ANY],
        out_specs=[one, one, one, ANY, ANY, ANY, ANY],
        scratch_shapes=[pltpu.VMEM((t, t), f32), pltpu.VMEM((t, 128), f32), pltpu.VMEM((t, 128), f32),
                        pltpu.VMEM((3 * half, t, 128), bf16), dma(2), dma(sems), dma(sems)] + extra,
        compiler_params=comm_params(6 if comm else None),
        cost_estimate=cost(20 * t * t * d, 16e6, t * t * HEADS),
        name="attend_back",
    )(qkv, qkv, qkv, dout, att, lse, doc_row, doc_col, part_sum, g_in)
    if comm:
        return outs[0], outs[1], outs[2], outs[3], (outs[4], outs[5]), outs[6]
    sent = swap_core(jnp.concatenate([g[:, d // 2 :] for g in outs[:3]], axis=1))
    return outs[0], outs[1], outs[2], sent, both_halves(part_sum), scatter_pieces(g_in)


def both_halves(part_sum):
    full = lax.psum(part_sum.astype(f32), "z").astype(bf16)
    return full, swap_core(full)


def middle_kernel(cfg, att_rows, tok, norms, o_own, o_oth, w_own, w_oth, att_all, bk_own_in, d_out, d_out_p, *refs):
    d, tm, blk, comm = cfg
    (resid, a_two_out, hidden, slope, bk_own, bk_oth, att_p, grad, w, a_two, stage, theirs, douts, lsem, send, recv) = refs
    step = pl.program_id(0)
    last = pl.num_programs(0) - 1
    t = a_two.shape[0]
    pro = t // tm
    half = d // 2
    nb = theirs.shape[0]
    core = lax.axis_index("core")
    loads = [pltpu.make_async_copy(v, douts.at[i], lsem.at[2 + i]) for i, v in enumerate((d_out, d_out_p))]

    def hand(j):
        return hand_over(stage.at[j], theirs.at[j], send.at[12 + j], recv.at[12 + j])

    if comm:
        gather = Gather(bk_own, bk_oth, send, recv, 0)
        swap = hand_over(att_all, att_p, send.at[11], recv.at[11])

        @pl.when(step == 0)
        def _():
            greet([peer("x"), peer("y"), peer("core")])
            gather.begin()
            swap.start()

        @pl.when(step == pro + 4)
        def _():
            gather.relay()

        @pl.when((step > pro) & (step <= pro + nb))
        def _():
            hand(step - pro - 1).start()

    @pl.when(step == 0)
    def _():
        lo = pl.multiple_of(core * half, half)
        hi = pl.multiple_of((1 - core) * half, half)
        cps = [
            pltpu.make_async_copy(o_own, w.at[:, pl.ds(lo, half)], lsem.at[0]),
            pltpu.make_async_copy(o_oth, w.at[:, pl.ds(hi, half)], lsem.at[1]),
        ]
        for cp in cps + loads:
            cp.start()
        for cp in cps:
            cp.wait()

    @pl.when(step < pro)
    def _():
        lo = pl.multiple_of(core * half, half)
        hi = pl.multiple_of((1 - core) * half, half)
        y = dot_nn(att_rows[:, :half], w[pl.ds(lo, half), :]) + dot_nn(att_rows[:, half:], w[pl.ds(hi, half), :])
        r = tok[...].astype(f32) + y
        resid[...] = r
        xhat, _ = layer_norm_parts(r)
        a = (xhat * gain_row(norms, 2, d) + gain_row(norms, 3, d)).astype(bf16)
        a_two_out[...] = a
        a_two[pl.ds(pl.multiple_of(step * tm, tm), tm), :] = a

    @pl.when((step >= pro) & (step < pro + 2 * nb))
    def _():
        pre = dot_nn(a_two[...], pick(step < pro + nb, w_oth[...], w_own[...]))
        cdf = 0.5 + 0.5 * lax.erf(pre * (0.5**0.5))
        pdf = jnp.exp(-0.5 * pre * pre) * 0.3989422804014327
        h = (pre * cdf).astype(bf16)
        hidden[...] = h
        slope[...] = (cdf + pre * pdf).astype(bf16)
        stage[step - pro] = h

    @pl.when(step == pro + 2 * nb)
    def _():
        for cp in loads:
            cp.wait()

    if comm:
        for j in range(nb):

            @pl.when(step == pro + 2 * nb + j)
            def _():
                hand(j).wait_recv()

        @pl.when(step == pro + 2 * nb)
        def _():
            gather.forward()

    @pl.when(step >= pro + 2 * nb)
    def _():
        j = step - pro - 2 * nb
        g = dot_tn(stage[nb + j], douts[0])
        if comm:
            g = g + dot_tn(theirs[j], douts[1])
        store_columns(grad, g)

    if comm:

        @pl.when(step == last)
        def _():
            gather.finish()
            swap.wait()
            for j in range(nb):
                hand(j).wait_send()


def store_columns(ref, g):
    wide = ref.shape[2]
    for p in range(ref.shape[0]):
        ref[p] = g[:, p * wide : (p + 1) * wide].astype(bf16)


def middle(att, tok, norms, o_own, o_oth, w_own, w_oth, bk_own, d_out, d_out_p, comm, tm=256, blk=512):
    t, d = tok.shape
    wide = w_own.shape[1]
    pro, nb = t // tm, wide // blk
    rowi = lambda i: jnp.minimum(i, pro - 1)
    oth = lambda i: jnp.clip(i - pro, 0, nb - 1)
    own = lambda i: jnp.clip(i - pro - nb, 0, nb - 1)
    both = lambda i: jnp.where(i < pro + nb, nb + oth(i), own(i))
    rows = lambda wd: pl.BlockSpec((tm, wd), lambda i: (rowi(i), 0))
    part = lambda count: pltpu.VMEM((count, t, blk), bf16)
    outs = pl.pallas_call(
        functools.partial(middle_kernel, (d, tm, blk, comm)),
        grid=(pro + 3 * nb,),
        out_shape=[sds((t, d), f32), sds((t, d), bf16), sds((t, 2 * wide), bf16), sds((t, 2 * wide), bf16),
                   sds(bk_own.shape, bf16), sds(bk_own.shape, bf16), sds((t, d), bf16), sds((PIECES, wide, d // PIECES), bf16)],
        in_specs=[rows(d), rows(d), pl.BlockSpec(norms.shape, lambda i: (0, 0)), ANY, ANY,
                  pl.BlockSpec((d, blk), lambda i: (0, own(i))), pl.BlockSpec((d, blk), lambda i: (0, oth(i))), ANY, ANY, ANY, ANY],
        out_specs=[rows(d), rows(d), pl.BlockSpec((t, blk), lambda i: (0, both(i))), pl.BlockSpec((t, blk), lambda i: (0, both(i))),
                   ANY, ANY, ANY, pl.BlockSpec((PIECES, blk, d // PIECES), lambda i: (0, jnp.maximum(i - pro - 2 * nb, 0), 0))],
        scratch_shapes=[pltpu.VMEM((d, d), bf16), pltpu.VMEM((t, d), bf16), part(2 * nb), part(nb), pltpu.VMEM((2, t, d), bf16),
                        dma(4), dma(12 + nb), dma(12 + nb)],
        input_output_aliases={8: 4},
        compiler_params=comm_params(3 if comm else None),
        cost_estimate=cost(2 * t * d * d + 8 * t * d * wide, 60e6, 4 * t * wide),
        name="middle",
    )(att, tok, norms, o_own, o_oth, w_own, w_oth, att, bk_own, d_out, d_out_p)
    if comm:
        return outs
    full, other = spread(bk_own)
    hid_p = swap_core(outs[2][:, wide:])
    grad = (dot_tn(outs[2][:, :wide], d_out) + dot_tn(hid_p, d_out_p)).astype(bf16)
    return [*outs[:4], full, other, swap_core(att), in_columns(grad)]


def in_columns(g):
    rows, cols = g.shape
    return g.reshape(rows, PIECES, cols // PIECES).transpose(1, 0, 2)


def feed_kernel(comm, d_out, slope, b_own, b_oth, i_own, i_oth, resid, dout_rows, norms, o_own, o_oth, a_two, g_back, *refs):
    (grad, d_resid, low, d_att, two_norm, sent, part_back, stage, theirs, lhs, wi, wo, lows, lsem, send, recv) = refs[:16]
    step = pl.program_id(0)
    nb = theirs.shape[0]
    tm, d = resid.shape
    pro = lows.shape[0] // tm
    half = d // 2
    wide = wi.shape[1] // 2
    np_ = d // 128
    core = lax.axis_index("core")
    lo = pl.multiple_of(core * half, half)
    hi = pl.multiple_of((1 - core) * half, half)
    loads = [
        pltpu.make_async_copy(a_two, lhs.at[0], lsem.at[0]),
        pltpu.make_async_copy(o_own, wo.at[:, pl.ds(lo, half)], lsem.at[1]),
        pltpu.make_async_copy(o_oth, wo.at[:, pl.ds(hi, half)], lsem.at[2]),
        pltpu.make_async_copy(i_oth, wi.at[:, pl.ds(0, wide)], lsem.at[4]),
        pltpu.make_async_copy(i_own, wi.at[:, pl.ds(wide, wide)], lsem.at[5]),
    ]

    def hand(j):
        return hand_over(stage.at[j], theirs.at[j], send.at[1 + j], recv.at[1 + j])

    def hand_low(r):
        at = pl.ds(pl.multiple_of(r * tm, tm), tm)
        return hand_over(lows.at[at, :], sent.at[at, :], send.at[1 + nb + r], recv.at[1 + nb + r])

    @pl.when(step == 1)
    def _():
        for cp in loads:
            cp.start()

    if comm:
        swap = hand_over(a_two, lhs.at[1], send.at[0], recv.at[0])
        held, far, near, mid, total, keep = refs[16:22]
        scat = Scatter(g_back, held, far, near, mid, total, send, recv, 1 + nb + pro, part_back, keep)
        acts = (scat.begin, scat.turn, scat.close)
        load = pltpu.make_async_copy(g_back, held, lsem.at[3])
        near_by = [peer("core"), peer("x"), peer("y")]

        @pl.when(step == 0)
        def _():
            load.start()
            greet_start(near_by)

    @pl.when(step < 2 * nb)
    def _():
        first = step < nb
        g = (dot_nt(d_out[...], pick(first, b_oth[...], b_own[...])) * slope[...].astype(f32)).astype(bf16)
        stage[step] = g

    if comm:

        @pl.when(step == 0)
        def _():
            greet_end(near_by)
            run_plan(acts, FEED_PLAN[0])
            swap.start()
            load.wait()

        for at, codes in enumerate(FEED_PLAN[:-1]):
            if codes and at > 0:
                pl.when(step == at)(functools.partial(run_plan, acts, codes))

        @pl.when((step > 0) & (step <= nb))
        def _():
            hand(step - 1).start()

    @pl.when(step == 2 * nb)
    def _():
        loads[0].wait()
        if comm:
            swap.wait()

    if comm:
        for j in range(nb):

            @pl.when(step == 2 * nb + j)
            def _():
                hand(j).wait()

    @pl.when((step >= 2 * nb) & (step < 3 * nb))
    def _():
        j = step - 2 * nb
        g = dot_tn(lhs[0], stage[nb + j])
        if comm:
            g = g + dot_tn(lhs[1], theirs[j])
        store_columns(grad, g)

    @pl.when(step == 3 * nb)
    def _():
        for cp in loads[1:]:
            cp.wait()
        two_norm[...] = jnp.zeros_like(two_norm)

    @pl.when(step >= 3 * nb)
    def _():
        here = pl.ds(pl.multiple_of((step - 3 * nb) * tm, tm), tm)
        dz = dot_nt(jnp.concatenate([stage[j, here, :] for j in range(2 * nb)], axis=1), wi[...])
        dv, g, b = layer_norm_back(resid[...], gain_row(norms, 2, d), dz)
        two_norm[0:np_, :] += flat_row(g)
        two_norm[np_:, :] += flat_row(b)
        dr = dout_rows[...].astype(f32) + dv
        d_resid[...] = dr
        dl = dr.astype(bf16)
        low[...] = dl
        lows[here, :] = pick(core == 0, dl[:, half:], dl[:, :half])
        d_att[:, :half] = dot_nt(dl, wo[pl.ds(lo, half), :]).astype(bf16)
        d_att[:, half:] = dot_nt(dl, wo[pl.ds(hi, half), :]).astype(bf16)
        if comm:
            hand_low(step - 3 * nb).start()

    if comm:

        @pl.when(step == pl.num_programs(0) - 1)
        def _():
            run_plan(acts, FEED_PLAN[-1])
            scat.finish()
            for r in range(pro):
                hand_low(r).wait()


def feed_back(d_out, slope, b_own, b_oth, i_own, i_oth, resid, norms, o_own, o_oth, a_two, g_back, n, comm, tm=256, blk=512):
    t, d = d_out.shape
    half = b_own.shape[0]
    nb = half // blk
    pro = t // tm
    oth = lambda i: jnp.minimum(i, nb - 1)
    own = lambda i: jnp.clip(i - nb, 0, nb - 1)
    row = lambda i: jnp.clip(i - 3 * nb, 0, pro - 1)
    rows = lambda w: pl.BlockSpec((tm, w), lambda i: (row(i), 0))
    whole = lambda s: pl.BlockSpec(s, lambda i: (0, 0))
    pieces, g_rows, g_cols = g_back.shape
    part = (pieces, g_rows // n, g_cols)
    per = half // PIECES
    extra = scatter_scratch(*g_back.shape) + [pltpu.VMEM(part, bf16), dma(pieces)] if comm else []
    sems = 1 + nb + pro + 6 * pieces
    outs = pl.pallas_call(
        functools.partial(feed_kernel, comm),
        grid=(3 * nb + pro,),
        out_shape=[sds((PIECES, d, per), bf16), sds((t, d), f32), sds((t, d), bf16), sds((t, d), bf16), sds((d // 64, 128), f32),
                   sds((t, d // 2), bf16), sds(part, bf16)],
        in_specs=[whole((t, d)), pl.BlockSpec((t, blk), lambda i: (0, jnp.where(i < nb, nb + i, own(i)))),
                  pl.BlockSpec((blk, d), lambda i: (own(i), 0)), pl.BlockSpec((blk, d), lambda i: (oth(i), 0)),
                  ANY, ANY, rows(d), rows(d), whole(norms.shape), ANY, ANY, ANY, ANY],
        out_specs=[pl.BlockSpec((blk // per, d, per), lambda i: (jnp.clip(i - 2 * nb, 0, nb - 1), 0, 0)), rows(d), rows(d), rows(d),
                   whole((d // 64, 128)), ANY, ANY],
        scratch_shapes=[pltpu.VMEM((2 * nb, t, blk), bf16), pltpu.VMEM((nb, t, blk), bf16), pltpu.VMEM((2, t, d), bf16),
                        pltpu.VMEM((d, 2 * half), bf16), pltpu.VMEM((d, d), bf16), pltpu.VMEM((t, d // 2), bf16), dma(6), dma(sems), dma(sems)]
        + extra,
        compiler_params=comm_params(4 if comm else None, 62),
        cost_estimate=cost(12 * t * d * half + 2 * t * d * d, 60e6),
        name="feed_back",
    )(d_out, slope, b_own, b_oth, i_own, i_oth, resid, d_out, norms, o_own, o_oth, a_two, g_back)
    if comm:
        return outs
    core = lax.axis_index("core")
    other = lax.dynamic_slice_in_dim(outs[2], (1 - core) * (d // 2), d // 2, 1)
    d_pre = pre_values(d_out, slope, b_own, b_oth)
    g_in = dot_tn(a_two, d_pre[:, :half]) + dot_tn(swap_core(a_two), swap_core(d_pre[:, half:]))
    return [in_columns(g_in.astype(bf16)), *outs[1:5], swap_core(other), scatter_pieces(g_back)]


def pre_values(d_out, slope, own, oth):
    both = jnp.concatenate([dot_nt(d_out, own), dot_nt(d_out, oth)], axis=1)
    return (both * slope.astype(f32)).astype(bf16)


def scatter_pieces(g):
    return lax.psum_scatter(g, ("y", "x"), scatter_dimension=1, tiled=True)


def last_kernel(cfg, g1, g2, g3, theirs, low, low_p, dq, dk, dv, tok, d_resid, norms, h_own, h_oth, resid, doc, two_norm,
                a_one, a_one_p, att, att_p, w_own, w_oth, b_own, b_oth, part_in, *refs):
    d, comm = cfg
    out, mixed, red_in, red_in_p, red_at, red_at_p, sums, w, wb, parts, held, lsem, total = refs[:13]
    refs = refs[1:]
    step = pl.program_id(0)
    last = pl.num_programs(0) - 1
    np_ = held.shape[0]
    pro = (last - np_) // 2
    half = 3 * d // 2
    q = d // 2
    hb = b_own.shape[0]
    nb = d // 128
    core = lax.axis_index("core")
    early = [pltpu.make_async_copy(a, wb.at[pl.ds(i * d, d), :], lsem.at[i]) for i, a in enumerate((a_one, a_one_p, att, att_p))]
    mids = [
        pltpu.make_async_copy(w_own, w.at[:, pl.ds(0, half)], lsem.at[4]),
        pltpu.make_async_copy(w_oth, w.at[:, pl.ds(half, half)], lsem.at[5]),
    ]
    late = [
        pltpu.make_async_copy(b_own, wb.at[pl.ds(0, hb), :], lsem.at[6]),
        pltpu.make_async_copy(b_oth, wb.at[pl.ds(hb, hb), :], lsem.at[7]),
    ]
    if comm:
        send, recv, mine_in, fi, sc, fa, vec, box, k_in, k_at = (
            refs[12], refs[13], refs[14], refs[15:19], refs[19:22], refs[22:27], refs[27], refs[28], refs[29], refs[30]
        )
        fold_in = Fold(
            pieces_of(part_in), pieces_of(mine_in), *fi, red_in, red_in_p, k_in, send, recv, 0
        )
        scat = Scatter(held, held, *sc, fa[0], send, recv, 4 * PIECES)
        mine_at = pieces_of(fa[0])
        fold_at = Fold(mine_at, mine_at, *fa[1:5], red_at, red_at_p, k_at, send, recv, 4 * PIECES + 6 * np_)
        base = 4 * PIECES + 10 * np_

        def note(i, src, dst, to):
            return pltpu.make_async_remote_copy(
                src_ref=src, dst_ref=dst, send_sem=send.at[base + i], recv_sem=recv.at[base + i], device_id=to, device_id_type=MESH
            )

        near, far = Fold.peers()
        notes = [
            note(0, vec.at[0], box.at[0], peer("x")),
            note(1, vec.at[1], box.at[1], peer("y")),
            note(2, vec.at[2], box.at[2], peer("core")),
            note(3, vec.at[3], box.at[3], near),
            note(4, vec.at[4], box.at[4], far),
            note(5, vec.at[5], vec.at[5], near),
        ]

        def norm_sum(k):
            if k < 3:
                notes[k].wait_recv()
                vec[k + 1] = vec[k] + box[k]
                if k < 2:
                    notes[k + 1].start()
                else:
                    pl.when(fold_in.end)(notes[3].start)
            elif k < 5:

                @pl.when(fold_in.mid)
                def _():
                    notes[k].wait_recv()
                    vec[k + 1] = vec[k] + box[k]
                    notes[k + 1].start()

            else:
                pl.when(fold_in.end)(notes[5].wait_recv)

        def settle(s):
            scat.close(s)
            fold_at.begin(s)

        acts = (scat.begin, scat.turn, settle, fold_in.inner, fold_in.outer, fold_in.land, fold_at.inner, fold_at.outer,
                fold_at.land, norm_sum)

    @pl.when(step == 0)
    def _():
        for cp in early:
            cp.start()
        if comm:
            load = pltpu.make_async_copy(part_in, mine_in, lsem.at[8])
            load.start()
            greet([peer("core"), peer("x"), peer("y")] + Fold.peers())
            for s in range(PIECES):
                fold_in.begin(s)
            load.wait()
        for cp in early[:2]:
            cp.wait()
        for cp in mids:
            cp.start()
        parts[0 : 2 * nb, :] = jnp.zeros((2 * nb, 128), f32)
        parts[2 * nb :, :] = two_norm[...]

    if comm:
        for k, codes in enumerate(LAST_PLAN[:-1]):
            if codes:
                pl.when(step == k)(functools.partial(run_plan, acts, codes))

    per = q // g1.shape[1]

    @pl.when(step < 3 * per)
    def _():
        g = pick(step < per, g1[...], pick(step < 2 * per, g2[...], g3[...]))
        acc = dot_tn(wb[0:d, :], g) + dot_tn(wb[d : 2 * d, :], theirs[...])
        held[step] = acc.astype(bf16)

    @pl.when(step == 3 * per)
    def _():
        for cp in early[2:]:
            cp.wait()

    @pl.when((step >= 3 * per) & (step < np_))
    def _():
        lo = pl.ds(pl.multiple_of(core * q, q), q)
        hi = pl.ds(pl.multiple_of((1 - core) * q, q), q)
        own = dot_tn(wb[2 * d : 3 * d, :q], low[...]) + dot_tn(wb[3 * d :, q:], low_p[...])
        held[step, lo, :] = own.astype(bf16)
        other = dot_tn(wb[2 * d : 3 * d, q:], low[...]) + dot_tn(wb[3 * d :, :q], low_p[...])
        held[step, hi, :] = other.astype(bf16)

    @pl.when(step == np_)
    def _():
        for cp in late:
            cp.start()
        for cp in mids:
            cp.wait()

    @pl.when((step >= np_) & (step < np_ + pro))
    def _():
        both = jnp.concatenate([g[:, :q] for g in (dq, dk, dv)] + [g[:, q:] for g in (dq, dk, dv)], axis=1)
        dz = dot_nt(both, w[...])
        grad, g, b = layer_norm_back(tok[...].astype(f32), gain_row(norms, 0, d), dz)
        parts[0:nb, :] += flat_row(g)
        parts[nb : 2 * nb, :] += flat_row(b)
        out[...] = (d_resid[...] + grad).astype(bf16)

    @pl.when(step == np_ + pro)
    def _():
        for cp in late:
            cp.wait()
        if comm:
            vec[0] = parts[...]
            notes[0].start()

    @pl.when((step >= np_ + pro) & (step < last))
    def _():
        total[...] = resid[...]
        chunk = hb // 4

        @pl.loop(0, 4)
        def _(i):
            at = pl.ds(pl.multiple_of(i * chunk, chunk), chunk)
            beyond = pl.ds(pl.multiple_of(hb + i * chunk, chunk), chunk)
            total[...] += dot_nn(h_own[:, at], wb[at, :]) + dot_nn(h_oth[:, at], wb[beyond, :])

        mixed[...] = jnp.where(doc[...] >= 0, total[...], 0.0).astype(bf16)

    @pl.when(step == last)
    def _():
        if comm:
            run_plan(acts, LAST_PLAN[-1])
            fold_in.finish()
            scat.finish()
            fold_at.finish()
            for i in (0, 1, 2):
                notes[i].wait_send()
            pl.when(fold_in.end)(notes[3].wait_send)

            @pl.when(fold_in.mid)
            def _():
                notes[4].wait_send()
                notes[5].wait_send()

            sums[...] = vec[5]
        else:
            sums[...] = parts[...]
            cp = pltpu.make_async_copy(held, red_at, lsem.at[0])
            cp.start()
            cp.wait()


def flat_row(v):
    return jnp.concatenate([v[:, i * 128 : (i + 1) * 128] for i in range(v.shape[1] // 128)], axis=0)


def last_grad(grads3, theirs, low, low_p, tok, d_resid, norms, hidden, resid, doc_col, two_norm, a_one, a_one_p, att, att_p,
              own, oth, b_own, b_oth, part_in, n, comm, tm=256, wide=256):
    t, d = tok.shape
    pro = t // tm
    half = b_own.shape[0]
    q = d // 2
    per = q // wide
    np_ = 4 * per
    one = lambda w, c=0: pl.BlockSpec((tm, w), lambda i: (jnp.clip(i - np_, 0, pro - 1), c))
    two = lambda w, c=0: pl.BlockSpec((tm, w), lambda i: (jnp.clip(i - np_ - pro, 0, pro - 1), c))
    whole = lambda a: pl.BlockSpec(a.shape, lambda i: (0, 0))
    col = lambda k, count: pl.BlockSpec((t, wide), lambda i: (0, jnp.clip(i - k * per, 0, count - 1)))
    low_col = pl.BlockSpec((t, wide), lambda i: (0, lax.axis_index("core") * per + jnp.clip(i - 3 * per, 0, per - 1)))
    nv = 4 * d // 128
    pieced = part_in.shape
    share = (np_, d // n if comm else d, wide)
    slots = 4 * PIECES + 10 * np_ + 6
    extra = []
    if comm:
        extra = [dma(slots), dma(slots), pltpu.VMEM(part_in.shape, bf16)] + fold_scratch(*part_in.shape)
        extra += scatter_scratch(np_, d, wide)[1:] + [pltpu.VMEM(share, bf16)] * 5
        extra += [pltpu.VMEM((6, nv, 128), f32), pltpu.VMEM((5, nv, 128), f32), dma(PIECES), dma(np_)]
    return pl.pallas_call(
        functools.partial(last_kernel, (d, comm)),
        grid=(np_ + 2 * pro + 1,),
        out_shape=[sds((t, d), bf16), sds((t, d), bf16)] + [sds(pieced, bf16)] * 2 + [sds(share, bf16)] * 2 + [sds((nv, 128), f32)],
        in_specs=[col(0, per), col(1, per), col(2, per), col(0, 3 * per), low_col, col(3, per)]
        + [one(d)] * 5 + [whole(norms), two(half), two(half, 1), two(d), two(1), whole(two_norm)] + [ANY] * 9,
        out_specs=[one(d), two(d), ANY, ANY, ANY, ANY, pl.BlockSpec((nv, 128), lambda i: (0, 0))],
        scratch_shapes=[pltpu.VMEM((d, 3 * d), bf16), pltpu.VMEM((4 * d, d), bf16), pltpu.VMEM((nv, 128), f32),
                        pltpu.VMEM((np_, d, wide), bf16), dma(9), pltpu.VMEM((tm, d), f32)] + extra,
        compiler_params=comm_params(7 if comm else None, 63),
        cost_estimate=cost(14 * t * d * d + 4 * t * d * half, 60e6),
        name="last_grad",
    )(*grads3, theirs, low, low_p, *grads3, tok, d_resid, norms, hidden, hidden, resid, doc_col, two_norm,
      a_one, a_one_p, att, att_p, own, oth, b_own, b_oth, part_in)


def adam_update(g_ref, m1, m2, wg, st, mn):
    rows = g_ref.shape[0]
    step = min(rows, 256)

    @pl.loop(0, rows // step)
    def _(i):
        at = pl.ds(pl.multiple_of(i * step, 8), step)
        g = g_ref[at, :]
        first = BETA_ONE * m1[at, :] + (1.0 - BETA_ONE) * g
        second_hat = (BETA_TWO / (1.0 - BETA_TWO**STEPS)) * m2[at, :] + ((1.0 - BETA_TWO) / (1.0 - BETA_TWO**STEPS)) * g * g
        wg[at, :] = g
        st[at, :] = (-RATE / (1.0 - BETA_ONE**STEPS)) * first / (second_hat * lax.rsqrt(second_hat) + ADAM_EPS)
        mn[at, :] = first


def adam_kernel(plan, inv_root, own, oth, m1, m2, *refs):
    wg, st, mn, flat = refs[-4:]
    rows, stride, places = plan
    first = lax.axis_index("core") == 0
    wide = own.shape[2]
    for col, lo, hi in places:
        p, c = col // wide, col % wide
        a = own[p, :, c : c + 128].astype(f32) * inv_root
        b = oth[p, :, c : c + 128].astype(f32) * inv_root
        flat[pl.ds(lo, rows, stride=stride), :] = pick(first, a, b)
        flat[pl.ds(hi, rows, stride=stride), :] = pick(first, b, a)
    adam_update(flat, m1, m2, wg, st, mn)


def adam_columns(own, oth, at, count, m1, m2, prev, inv_root, first_row, rows, places):
    total, wide = own.shape[1:]
    nb = 2 * count * wide // 128
    blk = rows * nb
    assert first_row % blk == 0
    base = first_row // blk
    half = pl.BlockSpec((count, rows, wide), lambda i: (at, i, 0))
    flat = pl.BlockSpec((blk, 128), lambda i: (base + i, 0))
    kernel = functools.partial(adam_kernel, (rows, nb, places), inv_root)
    return adam_call(kernel, (total // rows,), own, oth, m1, m2, prev, half, flat, blk, "adam")


def adam_call(kernel, grid, own, oth, m1, m2, prev, half, flat, blk, name):
    return pl.pallas_call(
        kernel,
        grid=grid,
        out_shape=[sds(m1.shape, f32)] * 3,
        in_specs=[half, half, flat, flat] + [ANY] * len(prev),
        out_specs=[flat] * 3,
        scratch_shapes=[pltpu.VMEM((blk, 128), f32)],
        input_output_aliases={4 + i: i for i in range(len(prev))},
        compiler_params=params(),
        cost_estimate=cost(0, own.size * 2 * 22),
        name=name,
    )(own, oth, m1, m2, *prev)


def adam_rows_kernel(inv_root, own, oth, m1, m2, *refs):
    wg, st, mn, flat = refs[-4:]
    g = pick(pl.program_id(0) == lax.axis_index("core"), own[...], oth[...]).astype(f32) * inv_root
    rows, width = g.shape
    nb = width // 128
    for w in range(nb):
        flat[pl.ds(w, rows, stride=nb), :] = g[:, w * 128 : (w + 1) * 128]
    adam_update(flat, m1, m2, wg, st, mn)


def adam_rows_halves(own, oth, m1, m2, prev, inv_root, first_row):
    count, width = own.shape
    rows = count // 4
    blk = rows * width // 128
    base = first_row // blk
    half = pl.BlockSpec((rows, width), lambda h, i: (i, 0))
    flat = pl.BlockSpec((blk, 128), lambda h, i: (base + h * 4 + i, 0))
    kernel = functools.partial(adam_rows_kernel, inv_root)
    return adam_call(kernel, (2, 4), own, oth, m1, m2, prev, half, flat, blk, "adam_rows")


def adam_tail_kernel(g, m1, m2, p1, p2, p3, wg, st, mn):
    adam_update(g, m1, m2, wg, st, mn)


def adam_tail(g, m1, m2, prev, first_row):
    rows = 8
    assert first_row % rows == 0 and g.shape[0] <= rows
    g = jnp.pad(g, ((0, rows - g.shape[0]), (0, 0)))
    flat = pl.BlockSpec((rows, 128), lambda i: (first_row // rows, 0))
    return pl.pallas_call(
        adam_tail_kernel,
        grid=(1,),
        out_shape=[sds(m1.shape, f32)] * 3,
        in_specs=[pl.BlockSpec((rows, 128), lambda i: (0, 0)), flat, flat] + [ANY] * 3,
        out_specs=[flat] * 3,
        input_output_aliases={3: 0, 4: 1, 5: 2},
        name="adam_norms",
    )(g, m1, m2, *prev)


BLOCK = 4096


def adam_all_kernel(cfg, b_own, b_oth, i_own, i_oth, a_own, a_oth, norm, m1, m2, wg, st, mn, flat, later):
    inv_root, at_in, at_at, counts = cfg
    step = pl.program_id(0)
    core = lax.axis_index("core")
    n_back, n_in, n_at = counts

    @pl.when(step < n_back)
    def _():
        mine = step // (n_back // 2) == core
        pieces, rows, wide = b_own.shape
        for w in range(pieces * wide // 128):
            p, c = w * 128 // wide, w * 128 % wide
            g = pick(mine, b_own[p, :, c : c + 128], b_oth[p, :, c : c + 128])
            flat[pl.ds(w, rows, stride=pieces * wide // 128), :] = g.astype(f32) * inv_root

    def spread_columns(dst, own, oth, places):
        rows, wide = own.shape[1:]
        for col, lo, hi, stride in places:
            p, c = col // wide, col % wide
            mine = lo + core * (hi - lo)
            dst[pl.ds(mine, rows, stride=stride), :] = own[p, :, c : c + 128].astype(f32) * inv_root
            dst[pl.ds(lo + hi - mine, rows, stride=stride), :] = oth[p, :, c : c + 128].astype(f32) * inv_root

    @pl.when((step >= n_back) & (step < n_back + n_in))
    def _():
        spread_columns(flat, i_own, i_oth, at_in)

    for k, places in enumerate(at_at):
        pl.when(step == k)(functools.partial(spread_columns, later, a_own, a_oth, places))

    @pl.when((step >= n_back + n_in) & (step < n_back + n_in + n_at))
    def _():
        at = pl.multiple_of((step - n_back - n_in) * BLOCK, BLOCK)
        flat[...] = later[pl.ds(at, BLOCK), :]

    @pl.when(step == n_back + n_in + n_at)
    def _():
        per = norm.shape[0] // 4
        at = pl.multiple_of(lax.axis_index(("y", "x")) * per, per)
        flat[0:per, :] = norm[pl.ds(at, per), :] * inv_root

    adam_update(flat, m1, m2, wg, st, mn)


def adam_all(back, inner, attention, norm, m1, m2, inv_root, places):
    at_in, at_qkv, at_out = places
    b_np, b_rows, b_wide = back[0].shape
    i_np, i_rows, i_wide = inner[0].shape
    np_, a_rows, wide = attention[0].shape
    n_back = 2 * b_np * b_rows * b_wide // 128 // BLOCK
    n_in = 2 * i_np * i_rows * i_wide // 128 // BLOCK
    n_at = 2 * np_ * a_rows * wide // 128 // BLOCK
    lots = np_ // (n_back + n_in)
    assert np_ == lots * (n_back + n_in) and m1.shape[0] == (n_back + n_in + n_at) * BLOCK + 8
    s_in, s_qkv, s_out = 2 * i_np * i_wide // 128, 2 * len(at_qkv), 2 * len(at_out)
    edge = a_rows * s_qkv
    at_at = [[] for _ in range(n_back + n_in)]
    for col, lo, hi in at_qkv:
        at_at[col // wide // lots].append((col % (wide * lots), lo, hi, s_qkv))
    for col, lo, hi in at_out:
        col += len(at_qkv) * 128
        at_at[col // wide // lots].append((col % (wide * lots), edge + lo, edge + hi, s_out))
    cfg = (inv_root, [(c, lo, hi, s_in) for c, lo, hi in at_in], at_at, (n_back, n_in, n_at))
    after_at, after_in = n_at, n_at + n_in

    def where(i):
        back_or_in = jnp.where(i < n_back, after_in + i, after_at + i - n_back)
        return jnp.where(i < n_back + n_in, back_or_in, jnp.where(i < n_back + n_in + n_at, i - n_back - n_in, i))

    flat = pl.BlockSpec((BLOCK, 128), lambda i: (where(i), 0))
    b_spec = pl.BlockSpec((b_np, 2 * b_rows // n_back, b_wide), lambda i: (0, jnp.minimum(i, n_back - 1) % (n_back // 2), 0))
    i_spec = pl.BlockSpec((i_np, i_rows // n_in, i_wide), lambda i: (0, jnp.clip(i - n_back, 0, n_in - 1), 0))
    a_spec = pl.BlockSpec((lots, a_rows, wide), lambda i: (jnp.minimum(i, n_back + n_in - 1), 0, 0))
    return pl.pallas_call(
        functools.partial(adam_all_kernel, cfg),
        grid=(n_back + n_in + n_at + 1,),
        out_shape=[sds(m1.shape, f32)] * 3,
        in_specs=[b_spec, b_spec, i_spec, i_spec, a_spec, a_spec, pl.BlockSpec(norm.shape, lambda i: (0, 0)), flat, flat],
        out_specs=[flat] * 3,
        scratch_shapes=[pltpu.VMEM((BLOCK, 128), f32), pltpu.VMEM((n_at * BLOCK, 128), f32)],
        compiler_params=params(),
        cost_estimate=cost(0, m1.size * 22),
        name="adam_all",
    )(*back, *inner, *attention, norm, m1, m2)


def after(x, *deps):
    return lax.optimization_barrier((x, deps))[0]


def body(n, nz, tokens, cotangent, doc_ids, master, moment_one, moment_two):
    t, d = tokens.shape
    ff = (master.shape[0] * n - 4 * d) // (2 * d) - 2 * d
    me = lax.axis_index(("y", "x"))
    rows = d // n
    comm = n == 4 and nz == 4

    lanes = master.reshape(-1, 128)
    doc_row = doc_ids.reshape(1, t)
    w = o = norm_share = None
    if not comm:
        w, o, _ = unpack_first(lanes, n, d, ff)
        w, o = spread(w), spread(o)
        norm_share = lax.all_gather(master[-(4 * d // n) :].astype(bf16), ("y", "x"), axis=0, tiled=True)
        norm_share = norm_share.astype(f32).reshape(-1, 128)
    (a_one, qkv, in_own, bk_own, w_own, w_oth, o_own, o_oth, norms, d_out, doc_col, att, lse, in_oth, a_one_p, d_out_p) = project_qkv(
        lanes, tokens, cotangent, doc_row, norm_share, w, o, n, ff, comm
    )
    resid, a_two, hidden, slope, bk_own, bk_oth, att_p, g_back = middle(
        att, tokens, norms, o_own, o_oth, in_own, in_oth, bk_own, d_out, d_out_p, comm
    )
    g_in, d_resid, low, d_att, two_norm, low_p, part_back = feed_back(
        d_out, slope, bk_own, bk_oth, in_own, in_oth, resid, norms, o_own, o_oth, a_two, g_back, n, comm
    )
    dq, dk, dv, dqkv_p, red_back, part_in = attend_back(qkv, d_att, att, lse, doc_row, doc_col, part_back, g_in, d, n, comm)
    input_grad, mixed, red_in, red_in_p, red_at, red_at_p, sums = last_grad(
        [dq, dk, dv], dqkv_p, low, low_p, tokens, d_resid, norms, hidden, resid, doc_col, two_norm, a_one, a_one_p, att, att_p,
        w_own, w_oth, bk_own, bk_oth, part_in, n, comm,
    )
    red_in, red_at = (red_in, red_in_p), (red_at, red_at_p)
    if not comm:
        red_in, red_at = both_halves(part_in), both_halves(scatter_pieces(red_at[0]))
        sums = lax.psum(sums, ("z", "core", "y", "x"))

    inv_root = float(t * n * nz * 2) ** (-0.5)
    m1, m2 = moment_one.reshape(-1, 128), moment_two.reshape(-1, 128)
    nb = d // 128
    half = nb // 2
    hs = ff // n // 2
    r_qkv, r_out, r_in = rows * 3 * nb, rows * nb, rows * ff // 128
    back_at = r_qkv + r_out + r_in
    at_in = [(hs * j + q * 128, (2 * hs * j) // 128 + q, (2 * hs * j + hs) // 128 + q) for j in range(n) for q in range(hs // 128)]
    at_qkv = [((p * half + w) * 128, p * nb + w, p * nb + w + half) for p in range(3) for w in range(half)]
    at_out = [(w * 128, w, w + half) for w in range(half)]
    if comm:
        outs = adam_all(red_back, red_in, red_at, sums, m1, m2, inv_root, (at_in, at_qkv, at_out))
    else:
        plain = lambda v: v.transpose(1, 0, 2).reshape(v.shape[1], -1)
        count = red_at[0].shape[0]
        outs = adam_rows_halves(plain(red_back[0]), plain(red_back[1]), m1, m2, [], inv_root, back_at)
        outs = adam_columns(*red_in, 0, red_in[0].shape[0], m1, m2, outs, inv_root, r_qkv + r_out, rows // 8, at_in)
        outs = adam_columns(*red_at, 0, 3 * count // 4, m1, m2, outs, inv_root, 0, rows // 8, at_qkv)
        outs = adam_columns(*red_at, 3, count // 4, m1, m2, outs, inv_root, r_qkv, rows // 2, at_out)
        per = 4 * nb // n
        norm_part = lax.dynamic_slice_in_dim(sums, group_index(n) * per, per, 0) * inv_root
        outs = adam_tail(norm_part, m1, m2, outs, back_at + ff // n * nb)
    weight_grad, step, moment = [o.reshape(-1) for o in outs]
    return mixed, input_grad, weight_grad, step, moment


def solution(mesh):
    dp, n = mesh.shape["dp"], mesh.shape["group"]
    fine = Mesh(mesh.devices.reshape(dp // 2, 2, n // 2, 2), ("z", "core", "y", "x"))
    tok = ("z", "core", "y", "x")
    flat = P(("y", "x"))
    in_specs = (P(tok, None), P(tok, None), P(tok), flat, flat, flat)
    out_specs = (P(tok, None), P(tok, None), flat, flat, flat)
    return jax.shard_map(
        functools.partial(body, n, dp // 2), mesh=fine, in_specs=in_specs, out_specs=out_specs, check_vma=False
    )
```

```python
import functools

import jax
import jax.numpy as jnp
from jax import lax
from jax.experimental import pallas as pl
from jax.experimental.pallas import tpu as pltpu
from jax.sharding import Mesh
from jax.sharding import PartitionSpec as P

HEADS = 16
EPS = 1e-05
FILL = -1e30
BETA_ONE = 0.9
BETA_TWO = 0.999
RATE = 0.001
ADAM_EPS = 1e-08
STEPS = 100.0
VMEM_MB = 60

f32 = jnp.float32
bf16 = jnp.bfloat16
ANY = pl.BlockSpec(memory_space=pl.ANY)


def params(limit=VMEM_MB):
    return pltpu.CompilerParams(vmem_limit_bytes=limit << 20)


def cost(flops, nbytes, trans=0):
    return pl.CostEstimate(flops=int(flops), bytes_accessed=int(nbytes), transcendentals=int(trans))


def sds(shape, dtype):
    return jax.ShapeDtypeStruct(shape, dtype)


def dot_nn(a, b):
    return jnp.dot(a, b, preferred_element_type=f32)


def dot_nt(a, b):
    return lax.dot_general(a, b, (((1,), (1,)), ((), ())), preferred_element_type=f32)


def dot_tn(a, b):
    return lax.dot_general(a, b, (((0,), (0,)), ((), ())), preferred_element_type=f32)


def pick(flag, a, b):
    return jnp.where(flag, a, b)


MESH = pl.DeviceIdType.MESH


def peer(*axes):
    return {a: 1 - lax.axis_index(a) for a in axes}


def greet_start(peers):
    barrier = pltpu.get_barrier_semaphore()
    for p in peers:
        pl.semaphore_signal(barrier, inc=1, device_id=p, device_id_type=MESH)


def greet_end(peers):
    pl.semaphore_wait(pltpu.get_barrier_semaphore(), len(peers))


def greet(peers):
    greet_start(peers)
    greet_end(peers)


def member():
    return lax.axis_index("y") * 2 + lax.axis_index("x")


class Gather:
    COUNT = 11

    def __init__(self, own, oth, send, recv, base, mine=None):
        rows = own.shape[0] // 4
        half = rows // 2
        x, y = lax.axis_index("x"), lax.axis_index("y")
        share = [y * 2 + x, y * 2 + 1 - x, (1 - y) * 2 + x, (1 - y) * 2 + 1 - x]
        self.rows = [pl.ds(pl.multiple_of(k * rows, 8), rows) for k in share]

        def move(i, k, off, count, dst, to):
            at = pl.ds(pl.multiple_of(share[k] * rows + off, 8), count)
            here = own.at[at, :] if mine is None or k else mine.at[pl.ds(off, count), :]
            return pltpu.make_async_remote_copy(
                src_ref=here, dst_ref=dst.at[at, :],
                send_sem=send.at[base + i], recv_sem=recv.at[base + i], device_id=peer(to), device_id_type=MESH,
            )

        self.moves = [
            move(0, 0, 0, half, own, "x"),
            move(1, 0, half, half, own, "x"),
            move(2, 0, half, half, own, "y"),
            move(3, 0, 0, half, own, "y"),
            move(4, 0, 0, rows, oth, "core"),
            move(5, 1, 0, half, own, "y"),
            move(6, 2, half, half, own, "x"),
            move(7, 1, 0, rows, oth, "core"),
            move(8, 2, 0, rows, oth, "core"),
            move(9, 3, 0, half, oth, "core"),
            move(10, 3, half, half, oth, "core"),
        ]

    def begin(self):
        for i in (0, 2, 1, 3, 4):
            self.moves[i].start()

    def relay(self):
        self.moves[0].wait_recv()
        self.moves[5].start()
        self.moves[2].wait_recv()
        self.moves[6].start()

    def forward(self):
        self.moves[1].wait_recv()
        self.moves[7].start()
        self.moves[3].wait_recv()
        self.moves[8].start()

    def close(self):
        self.moves[5].wait_recv()
        self.moves[9].start()
        self.moves[6].wait_recv()
        self.moves[10].start()

    def arrive(self, *which):
        for i in which:
            self.moves[i].wait_recv()

    def sent(self):
        for m in self.moves:
            m.wait_send()

    def finish(self):
        self.close()
        self.arrive(4, 7, 8, 9, 10)
        self.sent()


def hand_over(src, dst, send, recv):
    return pltpu.make_async_remote_copy(
        src_ref=src, dst_ref=dst, send_sem=send, recv_sem=recv, device_id=peer("core"), device_id_type=MESH
    )


def add_up(dst, a, b):
    dst[...] = a[...] + b[...]


class Fold:
    def __init__(self, source, mine, inbox, cross, stage, total, red, theirs, keep, send, recv, base):
        self.pieces = len(mine)
        self.out = [pltpu.make_async_copy(total.at[s], red.at[s], keep.at[s]) for s in range(self.pieces)]
        z = lax.axis_index("z")
        self.end = (z == 0) | (z == 3)
        self.mid = (z == 1) | (z == 2)
        near, far = self.peers()
        self.mine, self.inbox, self.across, self.stage, self.total = mine, inbox, cross, stage, total

        def move(s, kind, src, dst, to):
            i = base + 4 * s + kind
            return pltpu.make_async_remote_copy(
                src_ref=src, dst_ref=dst, send_sem=send.at[i], recv_sem=recv.at[i], device_id=to, device_id_type=MESH
            )

        every = range(self.pieces)
        self.fold = [move(s, 0, source[s], inbox.at[s], near) for s in every]
        self.cross = [move(s, 1, stage.at[s], cross.at[s], far) for s in every]
        self.unfold = [move(s, 2, total.at[s], total.at[s], near) for s in every]
        self.core = [move(s, 3, total.at[s], theirs.at[s], peer("core")) for s in every]

    @staticmethod
    def peers():
        z = lax.axis_index("z")
        return [{"z": z + 1 - 2 * (z % 2)}, {"z": 3 - z}]

    def begin(self, s):
        pl.when(self.end)(self.fold[s].start)

    def inner(self, s):
        @pl.when(self.mid)
        def _():
            self.fold[s].wait_recv()
            add_up(self.stage.at[s], self.mine[s], self.inbox.at[s])
            self.cross[s].start()

    def outer(self, s):
        @pl.when(self.mid)
        def _():
            self.cross[s].wait_recv()
            add_up(self.total.at[s], self.stage.at[s], self.across.at[s])
            self.unfold[s].start()
            self.core[s].start()
            self.out[s].start()

    def land(self, s):
        @pl.when(self.end)
        def _():
            self.unfold[s].wait_recv()
            self.core[s].start()
            self.out[s].start()

    def finish(self):
        @pl.when(self.end)
        def _():
            for m in self.fold:
                m.wait_send()

        @pl.when(self.mid)
        def _():
            for m in self.cross + self.unfold:
                m.wait_send()

        for m in self.core + self.out:
            m.wait()


def pieces_of(ref):
    return [ref.at[i] for i in range(ref.shape[0])]


def fold_scratch(pieces, rows, cols):
    return [pltpu.VMEM((pieces, rows, cols), bf16)] * 4


class Scatter:
    def __init__(self, source, held, far, near, mid, total, send, recv, base, out=None, keep=None):
        pieces, rows, _ = held.shape
        self.out = [] if out is None else [pltpu.make_async_copy(total.at[s], out.at[s], keep.at[s]) for s in range(pieces)]
        block = rows // 4
        half = block // 2
        x, y = lax.axis_index("x"), lax.axis_index("y")
        me, over_x, over_y, both = y * 2 + x, y * 2 + 1 - x, (1 - y) * 2 + x, (1 - y) * 2 + 1 - x
        self.pieces, self.held, self.far, self.near, self.mid, self.total, self.half = pieces, held, far, near, mid, total, half

        def at(share, part):
            return pl.ds(pl.multiple_of(share * block + part * half, half), half)

        def move(i, src, dst, to):
            return pltpu.make_async_remote_copy(
                src_ref=src, dst_ref=dst, send_sem=send.at[base + i], recv_sem=recv.at[base + i],
                device_id=peer(to), device_id_type=MESH,
            )

        self.first, self.second = [], []
        for s in range(pieces):
            b = 6 * s
            self.first.append([
                move(b, source.at[s, at(over_x, 0), :], far.at[s, 0], "x"),
                move(b + 1, source.at[s, at(both, 0), :], far.at[s, 1], "x"),
                move(b + 2, source.at[s, at(over_y, 1), :], far.at[s, 2], "y"),
                move(b + 3, source.at[s, at(both, 1), :], far.at[s, 3], "y"),
            ])
            self.second.append([move(b + 4, mid.at[s, 1], near.at[s, 0], "y"), move(b + 5, mid.at[s, 3], near.at[s, 1], "x")])
        self.keep = [at(me, 0), at(over_y, 0), at(me, 1), at(over_x, 1)]

    def begin(self, s):
        for k in (1, 3, 0, 2):
            self.first[s][k].start()

    def turn(self, s):
        for k in (1, 3, 0, 2):
            self.first[s][k].wait_recv()
            add_up(self.mid.at[s, k], self.held.at[s, self.keep[k], :], self.far.at[s, k])
            if k in (1, 3):
                self.second[s][k // 2].start()

    def close(self, s):
        for part in range(2):
            self.second[s][part].wait_recv()
            at = pl.ds(part * self.half, self.half)
            add_up(self.total.at[s, at, :], self.mid.at[s, 2 * part], self.near.at[s, part])
        if self.out:
            self.out[s].start()

    def finish(self):
        for s in range(self.pieces):
            for m in self.first[s] + self.second[s]:
                m.wait_send()
        for m in self.out:
            m.wait()


def scatter_scratch(pieces, rows, cols):
    half = rows // 8
    four = pltpu.VMEM((pieces, 4, half, cols), bf16)
    return [pltpu.VMEM((pieces, rows, cols), bf16), four, pltpu.VMEM((pieces, 2, half, cols), bf16), four]


def swap_core(v):
    return lax.ppermute(v, "core", [(0, 1), (1, 0)])


def comm_params(cid, limit=VMEM_MB):
    if cid is None:
        return params(limit)
    return pltpu.CompilerParams(vmem_limit_bytes=limit << 20, collective_id=cid, has_side_effects=True)


def dma(count):
    return pltpu.SemaphoreType.DMA((count,))


def gain_row(norms, r, d):
    nb = d // 128
    return jnp.concatenate([norms[r * nb + i : r * nb + i + 1, :] for i in range(nb)], axis=1)


def layer_norm_parts(v):
    centre = v - jnp.mean(v, axis=-1, keepdims=True)
    r = lax.rsqrt(jnp.mean(centre * centre, axis=-1, keepdims=True) + EPS)
    return centre * r, r


def layer_norm_back(v, gain, dz):
    xhat, r = layer_norm_parts(v)
    dg = jnp.sum(dz * xhat, axis=0, keepdims=True)
    db = jnp.sum(dz, axis=0, keepdims=True)
    t = dz * gain
    dv = r * (t - jnp.mean(t, axis=-1, keepdims=True) - xhat * jnp.mean(t * xhat, axis=-1, keepdims=True))
    return dv, dg, db


def unpack_kernel(dims, m_qkv, m_out, m_norm, own_qkv, own_out, norm):
    n, d = dims
    core = lax.axis_index("core")
    nb = d // 128
    half = nb // 2
    rows = own_qkv.shape[0]

    def put(ref, own, dst, lo, stride):
        own[:, dst : dst + 128] = ref[pl.ds(lo + core * half, rows, stride=stride), :].astype(bf16)

    for part in range(3):
        for w in range(half):
            put(m_qkv, own_qkv, (part * half + w) * 128, part * nb + w, 3 * nb)
    for w in range(half):
        put(m_out, own_out, w * 128, w, nb)
    norm[...] = m_norm[...].astype(bf16).astype(f32)


def group_index(n):
    return lax.axis_index(("y", "x"))


def unpack_first(lanes, n, d, ff):
    rows = d // n
    nb = d // 128
    r1, r2, r3, r4 = rows * 3 * nb, rows * nb, rows * ff // 128, ff // n * nb
    steps = 4 if n == 4 else 2
    sr = rows // steps
    me = lambda: group_index(n)
    return pl.pallas_call(
        functools.partial(unpack_kernel, (n, d)),
        grid=(steps,),
        out_shape=[sds((d, 3 * d // 2), bf16), sds((d, d // 2), bf16), sds((8, 128), f32)],
        in_specs=[
            pl.BlockSpec((r1 // steps, 128), lambda i: (i, 0)),
            pl.BlockSpec((r2 // steps, 128), lambda i: (r1 // (r2 // steps) + i, 0)),
            pl.BlockSpec((8, 128), lambda i: ((r1 + r2 + r3 + r4) // 8, 0)),
        ],
        out_specs=[
            pl.BlockSpec((sr, 3 * d // 2), lambda i: (me() * steps + i, 0)),
            pl.BlockSpec((sr, d // 2), lambda i: (me() * steps + i, 0)),
            pl.BlockSpec((8, 128), lambda i: (0, 0)),
        ],
        compiler_params=params(),
        name="unpack",
    )(lanes, lanes, lanes)


UNPACK_STEPS = 8


def qkv_kernel(cfg, tok, norm_share, m_in, m_back, w_own_in, w_oth_in, o_own_in, o_oth_in, cot, docs, *refs):
    n, comm, hd = cfg
    (a_hbm, qkv_hbm, in_own, own_bk, w_own, w_oth, o_own, o_oth, norms_out, d_hbm, doc_col, att, lse, in_oth, a_p, d_p,
     norms, w, toks, acc, cots, qkv, a_out, own_in, bias, raw, own_w, own_o, noted, lsem, send, recv) = refs
    if not comm:
        w_own, w_oth = w_own_in, w_oth_in
    t, d = toks.shape
    step = pl.program_id(0)
    nb = d // 128
    half = 3 * d // 2
    share = d // n
    tm = min(256, t)
    tok_copy = pltpu.make_async_copy(tok, toks, lsem.at[0])
    cot_copy = pltpu.make_async_copy(cot, cots, lsem.at[1 + 2 * n])
    a_copy = pltpu.make_async_copy(a_out, a_hbm, lsem.at[2 + 2 * n])
    d_copy = pltpu.make_async_copy(cots, d_hbm, lsem.at[3 + 2 * n])
    place = pl.ds(pl.multiple_of(group_index(n) * share, 8), share)
    in_copy = pltpu.make_async_copy(own_in, in_own.at[place, :], lsem.at[5 + 2 * n])
    if comm:
        own_copies = [
            pltpu.make_async_copy(own_w, w_own.at[place, :], lsem.at[7 + 2 * n]),
            pltpu.make_async_copy(own_o, o_own.at[place, :], lsem.at[8 + 2 * n]),
        ]
    out = pltpu.make_async_copy(qkv, qkv_hbm, lsem.at[4 + 2 * n])

    if comm:
        me = member()
        near = [peer("x"), peer("y"), peer("x", "y")]
        mine = pl.ds(pl.multiple_of(me * 8, 8), 8)
        notes = [
            pltpu.make_async_remote_copy(
                src_ref=noted, dst_ref=norms.at[mine, :], send_sem=send.at[22 + i], recv_sem=recv.at[22 + i],
                device_id=p, device_id_type=MESH,
            )
            for i, p in enumerate(near)
        ]
        first = Gather(w_own, w_oth, send, recv, 0, own_w)
        second = Gather(o_own, o_oth, send, recv, 11, own_o)
        third = Gather(in_own, in_oth, send, recv, 25, own_in)
        swaps = [hand_over(a_out, a_p, send.at[36], recv.at[36]), hand_over(cots, d_p, send.at[37], recv.at[37])]
        rows = first.rows
    else:
        rows = [pl.ds(k * share, share) for k in range(n)]

    @pl.when(step == 0)
    def _():
        tok_copy.start()
        cot_copy.start()
        if comm:
            fetch = pltpu.make_async_copy(w_own_in.at[pl.ds(0, raw.shape[0]), :], raw, lsem.at[6 + 2 * n])
            fetch.start()
            greet_start(near + [peer("core")])
            noted[...] = norm_share[...].astype(bf16).astype(f32)
            norms[mine, :] = noted[...]
            fetch.wait()
            core = lax.axis_index("core")
            hb = nb // 2

            @pl.loop(0, hb)
            def _(c):
                def put(base, own, dst, lo, stride):
                    cols = pl.ds(pl.multiple_of((dst + c) * 128, 128), 128)
                    own[:, cols] = raw[pl.ds(base + lo + c + core * hb, share, stride=stride), :].astype(bf16)

                for part in range(3):
                    put(0, own_w, part * hb, part * nb, 3 * nb)
                put(share * 3 * nb, own_o, 0, 0, nb)

            greet_end(near + [peer("core")])
            for m in notes:
                m.start()
            first.begin()
            own_copies[0].start()
            own_copies[1].start()

    @pl.when(step < UNPACK_STEPS)
    def _():
        core = lax.axis_index("core")
        rows_in = own_in.shape[0] // UNPACK_STEPS
        there = pl.ds(pl.multiple_of(step * rows_in, 8), rows_in)
        hs = own_in.shape[1] // n
        stride = m_in.shape[0] // rows_in
        for j in range(n):
            for q in range(hs // 128):
                lo = (2 * hs * j) // 128 + q + core * (hs // 128)
                at = hs * j + q * 128
                own_in[there, at : at + 128] = m_in[pl.ds(lo, rows_in, stride=stride), :].astype(bf16)
        for q in range(nb):
            own_bk[:, q * 128 : (q + 1) * 128] = m_back[pl.ds(q, own_bk.shape[0], stride=nb), :].astype(bf16)

    def load(*which):
        cps = []
        for k in which:
            cps.append(pltpu.make_async_copy(w_own.at[rows[k], :], w.at[k, :, pl.ds(0, half)], lsem.at[1 + 2 * k]))
            cps.append(pltpu.make_async_copy(w_oth.at[rows[k], :], w.at[k, :, pl.ds(half, half)], lsem.at[2 + 2 * k]))
        for cp in cps:
            cp.start()
        for cp in cps:
            cp.wait()

    def product(at, *which):
        return sum(dot_nn(a_out[at, cols_of(k)], w[k]) for k in which)

    def cols_of(k):
        if comm:
            return rows[k]
        return slice(k * share, (k + 1) * share)

    def each_block(fn):
        @pl.loop(0, t // tm)
        def _(i):
            fn(pl.ds(pl.multiple_of(i * tm, tm), tm))

    @pl.when(step == UNPACK_STEPS)
    def _():
        if comm:
            for m in notes:
                m.wait()
            first.relay()
            second.begin()
        else:
            norms[...] = norm_share[...]
        norms_out[...] = norms[...]
        tok_copy.wait()
        gain, shift = gain_row(norms, 0, d), gain_row(norms, 1, d)

        def norm(at):
            xhat, _ = layer_norm_parts(toks[at, :].astype(f32))
            a_out[at, :] = (xhat * gain + shift).astype(bf16)

        each_block(norm)
        cot_copy.wait()
        doc_col[...] = jnp.broadcast_to(docs[...].astype(f32), (128, t)).T[:, :1].astype(jnp.int32)

        def mask(at):
            cots[at, :] = jnp.where(doc_col[at, :] >= 0, cots[at, :].astype(f32), 0.0).astype(bf16)

        each_block(mask)
        a_copy.start()
        d_copy.start()
        in_copy.start()
        fill_bias(bias, docs, doc_col)
        if comm:
            own_copies[0].wait()
            first.arrive(4)
        load(0)

        def start(at):
            acc[at, :] = product(at, 0)

        each_block(start)

    @pl.when(step == UNPACK_STEPS + 1)
    def _():
        if comm:
            first.forward()
            third.begin()
            first.arrive(7, 8)
        load(*range(1, n - 1))

        def more(at):
            acc[at, :] += product(at, *range(1, n - 1))

        each_block(more)

    @pl.when(step == UNPACK_STEPS + 2)
    def _():
        if comm:
            first.close()
            second.relay()
            first.arrive(9, 10)
        load(n - 1)
        scale = (d // HEADS) ** (-0.5)
        q = d // 2

        def last(at):
            total = acc[at, :] + product(at, n - 1)
            for o in (0, half):
                qkv[at, o : o + q] = (total[:, o : o + q].astype(bf16).astype(f32) * scale).astype(bf16)
                qkv[at, o + q : o + half] = total[:, o + q : o + half].astype(bf16)

        each_block(last)
        out.start()

    start = UNPACK_STEPS + 3
    if comm:

        @pl.when(step == start + 1)
        def _():
            second.forward()
            for m in swaps:
                m.start()

        @pl.when(step == start + 3)
        def _():
            third.relay()

        @pl.when(step == start + 6)
        def _():
            third.forward()
            second.close()

        @pl.when(step == start + 7)
        def _():
            third.close()

    @pl.when(step >= start)
    def _():
        pair = step - start
        pairs = d // 256
        first_col = (pair // pairs) * half + (pair % pairs) * 128

        def part(k):
            return qkv.at[:, pl.ds(pl.multiple_of(first_col + k * (d // 2), 128), 128)]

        attend_pair(hd, part(0), part(1), part(2), bias, att, lse)

    @pl.when(step == pl.num_programs(0) - 1)
    def _():
        if comm:
            own_copies[1].wait()
            third.arrive(4, 7, 8, 9, 10)
            third.sent()
            second.arrive(4, 7, 8, 9, 10)
            second.sent()
            first.sent()
            for m in swaps:
                m.wait()
        for cp in (a_copy, d_copy, in_copy, out):
            cp.wait()


def attend_pair(hd, q, k, v, bias, out, lse):
    t = q.shape[0]
    vt = v[...].T
    per = 128 // hd
    qs = [head_lanes(q[...], h, hd) for h in range(per)]
    for i in range(t // QB):
        n = (i + 1) * QB
        cols = slice(i * QB, n)
        outs = []
        for h in range(per):
            s = dot_nt(k[:n, :], qs[h][cols, :]) + bias[:n, cols]
            top = jnp.max(s, axis=0, keepdims=True)
            e = jnp.exp(s - top)
            total = jnp.sum(e, axis=0, keepdims=True)
            lse[0, h : h + 1, cols] = top + jnp.log(total)
            o = dot_nn(vt[h * hd : (h + 1) * hd, :n], e.astype(bf16))
            outs.append(o * (1.0 / total))
        out[cols, :] = jnp.concatenate(outs, axis=0).T.astype(bf16)


def project_qkv(lanes, tok, cot, docs, norm_share, w, o, n, ff, comm):
    t, d = tok.shape
    rows = d // n
    nb = d // 128
    hs = ff // n // 2
    r_in, r_bk = rows * ff // 128, ff // n * nb
    at_in, at_bk = rows * 4 * nb, rows * 4 * nb + r_in
    b_in, b_bk = r_in // UNPACK_STEPS, hs * nb // UNPACK_STEPS
    assert at_in % b_in == 0 and at_bk % b_bk == 0
    up = lambda i: jnp.minimum(i, UNPACK_STEPS - 1)
    me = lambda: group_index(n)
    whole = lambda s: pl.BlockSpec(s, lambda i: (0, 0))
    half = 3 * d // 2
    pairs, hd = d // 128, d // HEADS
    per = 128 // hd
    pair = lambda i: jnp.maximum(i - UNPACK_STEPS - 3, 0)
    shapes = [sds((t, d), bf16), sds((t, 3 * d), bf16), sds((d, ff // 2), bf16), sds((ff // 2, d), bf16),
              sds((d, half), bf16), sds((d, half), bf16), sds((d, d // 2), bf16), sds((d, d // 2), bf16), sds((4 * nb, 128), f32),
              sds((t, d), bf16), sds((t, 1), jnp.int32), sds((t, d), bf16), sds((pairs, per, t), f32), sds((d, ff // 2), bf16),
              sds((t, d), bf16), sds((t, d), bf16)]
    w_args = [lanes] * 4 if comm else [w[0], w[1], o[0], o[1]]
    if comm:
        norm_share = lanes
        norm_spec = pl.BlockSpec((8, 128), lambda i: (lanes.shape[0] // 8 - 1, 0))
    else:
        norm_spec = whole(norm_share.shape)
    outs = pl.pallas_call(
        functools.partial(qkv_kernel, (n, comm, hd)),
        grid=(UNPACK_STEPS + 3 + pairs,),
        out_shape=shapes,
        in_specs=[
            ANY, norm_spec,
            pl.BlockSpec((b_in, 128), lambda i: (at_in // b_in + up(i), 0)),
            pl.BlockSpec((b_bk, 128), lambda i: (at_bk // b_bk + lax.axis_index("core") * UNPACK_STEPS + up(i), 0)),
            ANY, ANY, ANY, ANY, ANY, whole((1, t)),
        ],
        out_specs=[
            ANY, ANY, ANY,
            pl.BlockSpec((hs // UNPACK_STEPS, d), lambda i: (me() * UNPACK_STEPS + up(i), 0)),
            ANY, ANY, ANY, ANY, whole((4 * nb, 128)), ANY, whole((t, 1)),
            pl.BlockSpec((t, 128), lambda i: (0, pair(i))), pl.BlockSpec((1, per, t), lambda i: (pair(i), 0, 0)), ANY, ANY, ANY,
        ],
        scratch_shapes=[pltpu.VMEM((4 * nb, 128), f32), pltpu.VMEM((n, rows, 3 * d), bf16), pltpu.VMEM((t, d), bf16),
                        pltpu.VMEM((t, 3 * d), f32), pltpu.VMEM((t, d), bf16), pltpu.VMEM((t, 3 * d), bf16), pltpu.VMEM((t, d), bf16),
                        pltpu.VMEM((rows, ff // 2), bf16), pltpu.VMEM((t, t), f32), pltpu.VMEM((rows * 4 * nb, 128), f32),
                        pltpu.VMEM((rows, half), bf16), pltpu.VMEM((rows, d // 2), bf16), pltpu.VMEM((8, 128), f32),
                        dma(9 + 2 * n), dma(38), dma(38)],
        input_output_aliases={} if comm else {4: 4, 6: 6},
        compiler_params=comm_params(1 if comm else None),
        cost_estimate=cost(2 * t * d * 3 * d + 8 * t * t * d, 50e6, t * t * HEADS),
        name="qkv_attend",
    )(tok, norm_share, lanes, lanes, *w_args, cot, docs)
    if comm:
        return outs
    full, oth = spread(outs[2])
    return [*outs[:2], full, outs[3], w[0], w[1], o[0], o[1], *outs[8:13], oth, swap_core(outs[0]), swap_core(outs[9])]


QB = 256


def fill_bias(bias, doc_row, doc_col):
    t = bias.shape[0]
    for r in range(0, t, QB):
        key = r + lax.broadcasted_iota(jnp.int32, (QB, t), 0)
        query = lax.broadcasted_iota(jnp.int32, (QB, t), 1)
        ok = (doc_col[r : r + QB, :] == doc_row[...]) & (key <= query)
        bias[r : r + QB, :] = jnp.where(ok, 0.0, FILL)


def head_lanes(v, h, hd):
    lane = lax.broadcasted_iota(jnp.int32, v.shape, 1)
    return jnp.where((lane >= h * hd) & (lane < (h + 1) * hd), v, jnp.zeros_like(v))


def head_column(d, part):
    pairs = d // 256
    return lambda p: (0, (p // pairs) * 3 * pairs + part * pairs + p % pairs)


def spread(own):
    n = lax.axis_size("y") * lax.axis_size("x")
    rows = own.shape[0] // n
    mine = lax.dynamic_slice_in_dim(own, lax.axis_index(("y", "x")) * rows, rows, 0)
    full = lax.all_gather(mine, ("y", "x"), axis=0, tiled=True)
    return full, swap_core(full)


def attend_back_kernel(cfg, q, k, v, dout, att, lse, doc_row, doc_col, part_sum, g_in, dq, dk, dv, sent, red, red_p, part_in, *refs):
    hd, comm = cfg
    bias, dk_acc, dv_acc, stage, lsem, send, recv = refs[:7]
    step = pl.program_id(0)
    pairs = stage.shape[0] // 3

    def hand(p, part):
        wide = 128 * pairs
        cols = pl.ds(pl.multiple_of(part * wide + p * 128, 128), 128)
        i = p * 3 + part
        return hand_over(stage.at[i], sent.at[:, cols], send.at[i], recv.at[i])

    if comm:

        base = 3 * pairs
        mine, keep, held, far, near, mid, total, keep_in = refs[7], refs[12], *refs[13:19]
        fold = Fold(pieces_of(part_sum), pieces_of(mine), *refs[8:12], red, red_p, keep, send, recv, base)
        scat = Scatter(g_in, held, far, near, mid, total, send, recv, base + 4 * PIECES, part_in, keep_in)
        acts = (scat.begin, scat.turn, scat.close, fold.inner, fold.outer, fold.land)

        @pl.when(step == 0)
        def _():
            loads = [pltpu.make_async_copy(part_sum, mine, lsem.at[0]), pltpu.make_async_copy(g_in, held, lsem.at[1])]
            for cp in loads:
                cp.start()
            greet([peer("core"), peer("x"), peer("y")] + Fold.peers())
            run_plan(acts, BACK_PLAN[0])
            for s in range(PIECES):
                fold.begin(s)
            for cp in loads:
                cp.wait()

        @pl.when((step > 0) & (step <= pairs))
        def _():
            for part in range(3):
                hand(step - 1, part).start()

    @pl.when(step == 0)
    def _():
        fill_bias(bias, doc_row, doc_col)

    if comm:
        for at, codes in enumerate(BACK_PLAN[:-1]):
            if codes and at > 0:
                pl.when(step == at)(functools.partial(run_plan, acts, codes))

    t = q.shape[0]
    per = 128 // hd
    scale = hd ** (-0.5)
    kt = k[...].T
    prod = (dout[...].astype(f32) * att[...].astype(f32)).T
    inner = [jnp.sum(prod[h * hd : (h + 1) * hd, :], axis=0, keepdims=True) for h in range(per)]
    qs = [head_lanes(q[...], h, hd) for h in range(per)]
    ds_ = [head_lanes(dout[...], h, hd) for h in range(per)]
    dk_acc[...] = jnp.zeros_like(dk_acc)
    dv_acc[...] = jnp.zeros_like(dv_acc)
    for i in range(t // QB):
        n = (i + 1) * QB
        cols = slice(i * QB, n)
        dqs = []
        for h in range(per):
            qh, dh = qs[h][cols, :], ds_[h][cols, :]
            s = dot_nt(k[:n, :], qh) + bias[:n, cols]
            p = jnp.exp(s - lse[0, h : h + 1, cols])
            dp = dot_nt(v[:n, :], dh)
            g = (p * (dp - inner[h][:, cols])).astype(bf16)
            dv_acc[:n, :] += dot_nn(p.astype(bf16), dh)
            dk_acc[:n, :] += dot_nn(g, qh)
            dqs.append(dot_nn(kt[h * hd : (h + 1) * hd, :n], g))
        dq[cols, :] = (jnp.concatenate(dqs, axis=0).T * scale).astype(bf16)
    dk[...] = dk_acc[...].astype(bf16)
    dv[...] = dv_acc[...].astype(bf16)

    if comm:

        @pl.when(step < pairs)
        def _():
            stage[step * 3] = dq[...]
            stage[step * 3 + 1] = dk[...]
            stage[step * 3 + 2] = dv[...]

        @pl.when(step == 2 * pairs - 1)
        def _():
            for p in range(pairs):
                for part in range(3):
                    hand(p, part).wait()
            run_plan(acts, BACK_PLAN[-1])
            fold.finish()
            scat.finish()


def run_plan(acts, codes):
    for code in codes:
        acts[code // 10](code % 10)


FEED_PLAN = (
    (0, 1),
    (),
    (),
    (10, 2),
    (),
    (11, 3, 20),
    (),
    (12, 4, 21),
    (),
    (13, 5, 22),
    (14, 6),
    (23, 15, 7),
    (24,),
    (16, 25, 17),
    (26, 27),
    (),
    (),
)
BACK_PLAN = (
    (0, 1, 2, 3),
    (),
    (30, 31, 10, 4, 11, 5),
    (32, 40, 33, 12, 6),
    (41, 20, 34, 13, 7, 42, 35),
    (43, 21, 50, 36, 14, 15, 44, 37),
    (45, 22, 51, 52, 16, 23, 46),
    (47, 24, 53, 54, 17),
    (25, 26, 27, 55, 56, 57),
)
LAST_PLAN = (
    (),
    (0,),
    (1,),
    (30,),
    (10, 2, 31),
    (11, 3, 32, 40),
    (20, 33, 41),
    (12, 4, 34, 42),
    (21, 35, 43, 50),
    (13, 5, 22, 36, 44, 45, 37, 51),
    (14, 6, 23, 60, 46, 52, 53),
    (15, 7, 24, 61, 62, 70, 47, 54),
    (16, 25, 63, 64, 71, 55),
    (17, 26, 65, 72, 73, 66, 56, 90),
    (27, 67, 74, 75, 80, 91),
    (76, 81, 57, 92),
    (77, 93, 82, 94, 83, 95, 84, 85, 86, 87),
)
PIECES = 8


def attend_back(qkv, dout, att, lse, doc_row, doc_col, part_sum, g_in, d, n, comm):
    t = qkv.shape[0]
    pairs = d // 128
    half = pairs // 2
    hd = d // HEADS
    per = 128 // hd
    turn = lambda p: (p + half) % pairs
    part_in = (g_in.shape[0], g_in.shape[1] // n, g_in.shape[2])
    col = lambda part: pl.BlockSpec((t, 128), lambda p: head_column(d, part)(turn(p)))
    one = pl.BlockSpec((t, 128), lambda p: (0, turn(p)))
    sems = 3 * half + 10 * PIECES
    extra = []
    if comm:
        extra = [pltpu.VMEM(part_sum.shape, bf16)] + fold_scratch(*part_sum.shape) + [dma(PIECES)]
        extra += scatter_scratch(*g_in.shape) + [pltpu.VMEM(part_in, bf16), dma(PIECES)]
    outs = pl.pallas_call(
        functools.partial(attend_back_kernel, (hd, comm)),
        grid=(pairs,),
        out_shape=[sds((t, d), bf16)] * 3 + [sds((t, 3 * d // 2), bf16)] + [sds(part_sum.shape, bf16)] * 2 + [sds(part_in, bf16)],
        in_specs=[col(0), col(1), col(2), one, one, pl.BlockSpec((1, per, t), lambda p: (turn(p), 0, 0)),
                  pl.BlockSpec((1, t), lambda p: (0, 0)), pl.BlockSpec((t, 1), lambda p: (0, 0)), ANY, ANY],
        out_specs=[one, one, one, ANY, ANY, ANY, ANY],
        scratch_shapes=[pltpu.VMEM((t, t), f32), pltpu.VMEM((t, 128), f32), pltpu.VMEM((t, 128), f32),
                        pltpu.VMEM((3 * half, t, 128), bf16), dma(2), dma(sems), dma(sems)] + extra,
        compiler_params=comm_params(6 if comm else None),
        cost_estimate=cost(20 * t * t * d, 16e6, t * t * HEADS),
        name="attend_back",
    )(qkv, qkv, qkv, dout, att, lse, doc_row, doc_col, part_sum, g_in)
    if comm:
        return outs[0], outs[1], outs[2], outs[3], (outs[4], outs[5]), outs[6]
    sent = swap_core(jnp.concatenate([g[:, d // 2 :] for g in outs[:3]], axis=1))
    return outs[0], outs[1], outs[2], sent, both_halves(part_sum), scatter_pieces(g_in)


def both_halves(part_sum):
    full = lax.psum(part_sum.astype(f32), "z").astype(bf16)
    return full, swap_core(full)


def middle_kernel(cfg, att_rows, tok, norms, o_own, o_oth, w_own, w_oth, att_all, bk_own_in, d_out, d_out_p, *refs):
    d, tm, blk, comm = cfg
    (resid, a_two_out, hidden, slope, bk_own, bk_oth, att_p, grad, w, a_two, stage, theirs, douts, lsem, send, recv) = refs
    step = pl.program_id(0)
    last = pl.num_programs(0) - 1
    t = a_two.shape[0]
    pro = t // tm
    half = d // 2
    nb = theirs.shape[0]
    core = lax.axis_index("core")
    loads = [pltpu.make_async_copy(v, douts.at[i], lsem.at[2 + i]) for i, v in enumerate((d_out, d_out_p))]

    def hand(j):
        return hand_over(stage.at[j], theirs.at[j], send.at[12 + j], recv.at[12 + j])

    if comm:
        gather = Gather(bk_own, bk_oth, send, recv, 0)
        swap = hand_over(att_all, att_p, send.at[11], recv.at[11])

        @pl.when(step == 0)
        def _():
            greet([peer("x"), peer("y"), peer("core")])
            gather.begin()
            swap.start()

        @pl.when(step == pro + 4)
        def _():
            gather.relay()

        @pl.when((step > pro) & (step <= pro + nb))
        def _():
            hand(step - pro - 1).start()

    @pl.when(step == 0)
    def _():
        lo = pl.multiple_of(core * half, half)
        hi = pl.multiple_of((1 - core) * half, half)
        cps = [
            pltpu.make_async_copy(o_own, w.at[:, pl.ds(lo, half)], lsem.at[0]),
            pltpu.make_async_copy(o_oth, w.at[:, pl.ds(hi, half)], lsem.at[1]),
        ]
        for cp in cps + loads:
            cp.start()
        for cp in cps:
            cp.wait()

    @pl.when(step < pro)
    def _():
        lo = pl.multiple_of(core * half, half)
        hi = pl.multiple_of((1 - core) * half, half)
        y = dot_nn(att_rows[:, :half], w[pl.ds(lo, half), :]) + dot_nn(att_rows[:, half:], w[pl.ds(hi, half), :])
        r = tok[...].astype(f32) + y
        resid[...] = r
        xhat, _ = layer_norm_parts(r)
        a = (xhat * gain_row(norms, 2, d) + gain_row(norms, 3, d)).astype(bf16)
        a_two_out[...] = a
        a_two[pl.ds(pl.multiple_of(step * tm, tm), tm), :] = a

    @pl.when((step >= pro) & (step < pro + 2 * nb))
    def _():
        pre = dot_nn(a_two[...], pick(step < pro + nb, w_oth[...], w_own[...]))
        cdf = 0.5 + 0.5 * lax.erf(pre * (0.5**0.5))
        pdf = jnp.exp(-0.5 * pre * pre) * 0.3989422804014327
        h = (pre * cdf).astype(bf16)
        hidden[...] = h
        slope[...] = (cdf + pre * pdf).astype(bf16)
        stage[step - pro] = h

    @pl.when(step == pro + 2 * nb)
    def _():
        for cp in loads:
            cp.wait()

    if comm:
        for j in range(nb):

            @pl.when(step == pro + 2 * nb + j)
            def _():
                hand(j).wait_recv()

        @pl.when(step == pro + 2 * nb)
        def _():
            gather.forward()

        @pl.when(step == last)
        def _():
            gather.close()

    @pl.when(step >= pro + 2 * nb)
    def _():
        j = step - pro - 2 * nb
        g = dot_tn(stage[nb + j], douts[0])
        if comm:
            g = g + dot_tn(theirs[j], douts[1])
        store_columns(grad, g)

    if comm:

        @pl.when(step == last)
        def _():
            gather.arrive(4, 7, 8, 9, 10)
            gather.sent()
            swap.wait()
            for j in range(nb):
                hand(j).wait_send()


def store_columns(ref, g):
    wide = ref.shape[2]
    for p in range(ref.shape[0]):
        ref[p] = g[:, p * wide : (p + 1) * wide].astype(bf16)


def middle(att, tok, norms, o_own, o_oth, w_own, w_oth, bk_own, d_out, d_out_p, comm, tm=256, blk=512):
    t, d = tok.shape
    wide = w_own.shape[1]
    pro, nb = t // tm, wide // blk
    rowi = lambda i: jnp.minimum(i, pro - 1)
    oth = lambda i: jnp.clip(i - pro, 0, nb - 1)
    own = lambda i: jnp.clip(i - pro - nb, 0, nb - 1)
    both = lambda i: jnp.where(i < pro + nb, nb + oth(i), own(i))
    rows = lambda wd: pl.BlockSpec((tm, wd), lambda i: (rowi(i), 0))
    part = lambda count: pltpu.VMEM((count, t, blk), bf16)
    outs = pl.pallas_call(
        functools.partial(middle_kernel, (d, tm, blk, comm)),
        grid=(pro + 3 * nb,),
        out_shape=[sds((t, d), f32), sds((t, d), bf16), sds((t, 2 * wide), bf16), sds((t, 2 * wide), bf16),
                   sds(bk_own.shape, bf16), sds(bk_own.shape, bf16), sds((t, d), bf16), sds((PIECES, wide, d // PIECES), bf16)],
        in_specs=[rows(d), rows(d), pl.BlockSpec(norms.shape, lambda i: (0, 0)), ANY, ANY,
                  pl.BlockSpec((d, blk), lambda i: (0, own(i))), pl.BlockSpec((d, blk), lambda i: (0, oth(i))), ANY, ANY, ANY, ANY],
        out_specs=[rows(d), rows(d), pl.BlockSpec((t, blk), lambda i: (0, both(i))), pl.BlockSpec((t, blk), lambda i: (0, both(i))),
                   ANY, ANY, ANY, pl.BlockSpec((PIECES, blk, d // PIECES), lambda i: (0, jnp.maximum(i - pro - 2 * nb, 0), 0))],
        scratch_shapes=[pltpu.VMEM((d, d), bf16), pltpu.VMEM((t, d), bf16), part(2 * nb), part(nb), pltpu.VMEM((2, t, d), bf16),
                        dma(4), dma(12 + nb), dma(12 + nb)],
        input_output_aliases={8: 4},
        compiler_params=comm_params(3 if comm else None),
        cost_estimate=cost(2 * t * d * d + 8 * t * d * wide, 60e6, 4 * t * wide),
        name="middle",
    )(att, tok, norms, o_own, o_oth, w_own, w_oth, att, bk_own, d_out, d_out_p)
    if comm:
        return outs
    full, other = spread(bk_own)
    hid_p = swap_core(outs[2][:, wide:])
    grad = (dot_tn(outs[2][:, :wide], d_out) + dot_tn(hid_p, d_out_p)).astype(bf16)
    return [*outs[:4], full, other, swap_core(att), in_columns(grad)]


def in_columns(g):
    rows, cols = g.shape
    return g.reshape(rows, PIECES, cols // PIECES).transpose(1, 0, 2)


def feed_kernel(comm, d_out, slope, b_own, b_oth, i_own, i_oth, resid, dout_rows, norms, o_own, o_oth, a_two, g_back, *refs):
    (grad, d_resid, low, d_att, two_norm, sent, part_back, stage, theirs, lhs, wi, wo, lows, lsem, send, recv) = refs[:16]
    step = pl.program_id(0)
    nb = theirs.shape[0]
    tm, d = resid.shape
    pro = lows.shape[0] // tm
    half = d // 2
    wide = wi.shape[1] // 2
    np_ = d // 128
    core = lax.axis_index("core")
    lo = pl.multiple_of(core * half, half)
    hi = pl.multiple_of((1 - core) * half, half)
    loads = [
        pltpu.make_async_copy(a_two, lhs.at[0], lsem.at[0]),
        pltpu.make_async_copy(o_own, wo.at[:, pl.ds(lo, half)], lsem.at[1]),
        pltpu.make_async_copy(o_oth, wo.at[:, pl.ds(hi, half)], lsem.at[2]),
        pltpu.make_async_copy(i_oth, wi.at[:, pl.ds(0, wide)], lsem.at[4]),
        pltpu.make_async_copy(i_own, wi.at[:, pl.ds(wide, wide)], lsem.at[5]),
    ]

    def hand(j):
        return hand_over(stage.at[j], theirs.at[j], send.at[1 + j], recv.at[1 + j])

    def hand_low(r):
        at = pl.ds(pl.multiple_of(r * tm, tm), tm)
        return hand_over(lows.at[at, :], sent.at[at, :], send.at[1 + nb + r], recv.at[1 + nb + r])

    @pl.when(step == 1)
    def _():
        for cp in loads:
            cp.start()

    if comm:
        swap = hand_over(a_two, lhs.at[1], send.at[0], recv.at[0])
        held, far, near, mid, total, keep = refs[16:22]
        scat = Scatter(g_back, held, far, near, mid, total, send, recv, 1 + nb + pro, part_back, keep)
        acts = (scat.begin, scat.turn, scat.close)
        load = pltpu.make_async_copy(g_back, held, lsem.at[3])
        near_by = [peer("core"), peer("x"), peer("y")]

        @pl.when(step == 0)
        def _():
            load.start()
            greet_start(near_by)

    @pl.when(step < 2 * nb)
    def _():
        first = step < nb
        g = (dot_nt(d_out[...], pick(first, b_oth[...], b_own[...])) * slope[...].astype(f32)).astype(bf16)
        stage[step] = g

    if comm:

        @pl.when(step == 0)
        def _():
            greet_end(near_by)
            run_plan(acts, FEED_PLAN[0])
            swap.start()
            load.wait()

        for at, codes in enumerate(FEED_PLAN[:-1]):
            if codes and at > 0:
                pl.when(step == at)(functools.partial(run_plan, acts, codes))

        @pl.when((step > 0) & (step <= nb))
        def _():
            hand(step - 1).start()

    @pl.when(step == 2 * nb)
    def _():
        loads[0].wait()
        if comm:
            swap.wait()

    if comm:
        for j in range(nb):

            @pl.when(step == 2 * nb + j)
            def _():
                hand(j).wait()

    @pl.when((step >= 2 * nb) & (step < 3 * nb))
    def _():
        j = step - 2 * nb
        g = dot_tn(lhs[0], stage[nb + j])
        if comm:
            g = g + dot_tn(lhs[1], theirs[j])
        store_columns(grad, g)

    @pl.when(step == 3 * nb)
    def _():
        for cp in loads[1:]:
            cp.wait()
        two_norm[...] = jnp.zeros_like(two_norm)

    @pl.when(step >= 3 * nb)
    def _():
        here = pl.ds(pl.multiple_of((step - 3 * nb) * tm, tm), tm)
        dz = dot_nt(jnp.concatenate([stage[j, here, :] for j in range(2 * nb)], axis=1), wi[...])
        dv, g, b = layer_norm_back(resid[...], gain_row(norms, 2, d), dz)
        two_norm[0:np_, :] += flat_row(g)
        two_norm[np_:, :] += flat_row(b)
        dr = dout_rows[...].astype(f32) + dv
        d_resid[...] = dr
        dl = dr.astype(bf16)
        low[...] = dl
        lows[here, :] = pick(core == 0, dl[:, half:], dl[:, :half])
        d_att[:, :half] = dot_nt(dl, wo[pl.ds(lo, half), :]).astype(bf16)
        d_att[:, half:] = dot_nt(dl, wo[pl.ds(hi, half), :]).astype(bf16)
        if comm:
            hand_low(step - 3 * nb).start()

    if comm:

        @pl.when(step == pl.num_programs(0) - 1)
        def _():
            run_plan(acts, FEED_PLAN[-1])
            scat.finish()
            for r in range(pro):
                hand_low(r).wait()


def feed_back(d_out, slope, b_own, b_oth, i_own, i_oth, resid, norms, o_own, o_oth, a_two, g_back, n, comm, tm=256, blk=512):
    t, d = d_out.shape
    half = b_own.shape[0]
    nb = half // blk
    pro = t // tm
    oth = lambda i: jnp.minimum(i, nb - 1)
    own = lambda i: jnp.clip(i - nb, 0, nb - 1)
    row = lambda i: jnp.clip(i - 3 * nb, 0, pro - 1)
    rows = lambda w: pl.BlockSpec((tm, w), lambda i: (row(i), 0))
    whole = lambda s: pl.BlockSpec(s, lambda i: (0, 0))
    pieces, g_rows, g_cols = g_back.shape
    part = (pieces, g_rows // n, g_cols)
    per = half // PIECES
    extra = scatter_scratch(*g_back.shape) + [pltpu.VMEM(part, bf16), dma(pieces)] if comm else []
    sems = 1 + nb + pro + 6 * pieces
    outs = pl.pallas_call(
        functools.partial(feed_kernel, comm),
        grid=(3 * nb + pro,),
        out_shape=[sds((PIECES, d, per), bf16), sds((t, d), f32), sds((t, d), bf16), sds((t, d), bf16), sds((d // 64, 128), f32),
                   sds((t, d // 2), bf16), sds(part, bf16)],
        in_specs=[whole((t, d)), pl.BlockSpec((t, blk), lambda i: (0, jnp.where(i < nb, nb + i, own(i)))),
                  pl.BlockSpec((blk, d), lambda i: (own(i), 0)), pl.BlockSpec((blk, d), lambda i: (oth(i), 0)),
                  ANY, ANY, rows(d), rows(d), whole(norms.shape), ANY, ANY, ANY, ANY],
        out_specs=[pl.BlockSpec((blk // per, d, per), lambda i: (jnp.clip(i - 2 * nb, 0, nb - 1), 0, 0)), rows(d), rows(d), rows(d),
                   whole((d // 64, 128)), ANY, ANY],
        scratch_shapes=[pltpu.VMEM((2 * nb, t, blk), bf16), pltpu.VMEM((nb, t, blk), bf16), pltpu.VMEM((2, t, d), bf16),
                        pltpu.VMEM((d, 2 * half), bf16), pltpu.VMEM((d, d), bf16), pltpu.VMEM((t, d // 2), bf16), dma(6), dma(sems), dma(sems)]
        + extra,
        compiler_params=comm_params(4 if comm else None, 62),
        cost_estimate=cost(12 * t * d * half + 2 * t * d * d, 60e6),
        name="feed_back",
    )(d_out, slope, b_own, b_oth, i_own, i_oth, resid, d_out, norms, o_own, o_oth, a_two, g_back)
    if comm:
        return outs
    core = lax.axis_index("core")
    other = lax.dynamic_slice_in_dim(outs[2], (1 - core) * (d // 2), d // 2, 1)
    d_pre = pre_values(d_out, slope, b_own, b_oth)
    g_in = dot_tn(a_two, d_pre[:, :half]) + dot_tn(swap_core(a_two), swap_core(d_pre[:, half:]))
    return [in_columns(g_in.astype(bf16)), *outs[1:5], swap_core(other), scatter_pieces(g_back)]


def pre_values(d_out, slope, own, oth):
    both = jnp.concatenate([dot_nt(d_out, own), dot_nt(d_out, oth)], axis=1)
    return (both * slope.astype(f32)).astype(bf16)


def scatter_pieces(g):
    return lax.psum_scatter(g, ("y", "x"), scatter_dimension=1, tiled=True)


def last_kernel(cfg, g1, g2, g3, theirs, low, low_p, dq, dk, dv, tok, d_resid, norms, h_own, h_oth, resid, doc, two_norm,
                a_one, a_one_p, att, att_p, w_own, w_oth, b_own, b_oth, part_in, *refs):
    d, comm = cfg
    out, mixed, red_in, red_in_p, red_at, red_at_p, sums, w, wb, parts, held, lsem, total = refs[:13]
    refs = refs[1:]
    step = pl.program_id(0)
    last = pl.num_programs(0) - 1
    np_ = held.shape[0]
    pro = (last - np_) // 2
    half = 3 * d // 2
    q = d // 2
    hb = b_own.shape[0]
    nb = d // 128
    core = lax.axis_index("core")
    early = [pltpu.make_async_copy(a, wb.at[pl.ds(i * d, d), :], lsem.at[i]) for i, a in enumerate((a_one, a_one_p, att, att_p))]
    mids = [
        pltpu.make_async_copy(w_own, w.at[:, pl.ds(0, half)], lsem.at[4]),
        pltpu.make_async_copy(w_oth, w.at[:, pl.ds(half, half)], lsem.at[5]),
    ]
    late = [
        pltpu.make_async_copy(b_own, wb.at[pl.ds(0, hb), :], lsem.at[6]),
        pltpu.make_async_copy(b_oth, wb.at[pl.ds(hb, hb), :], lsem.at[7]),
    ]
    if comm:
        send, recv, mine_in, fi, sc, fa, vec, box, k_in, k_at = (
            refs[12], refs[13], refs[14], refs[15:19], refs[19:22], refs[22:27], refs[27], refs[28], refs[29], refs[30]
        )
        fold_in = Fold(
            pieces_of(part_in), pieces_of(mine_in), *fi, red_in, red_in_p, k_in, send, recv, 0
        )
        scat = Scatter(held, held, *sc, fa[0], send, recv, 4 * PIECES)
        mine_at = pieces_of(fa[0])
        fold_at = Fold(mine_at, mine_at, *fa[1:5], red_at, red_at_p, k_at, send, recv, 4 * PIECES + 6 * np_)
        base = 4 * PIECES + 10 * np_

        def note(i, src, dst, to):
            return pltpu.make_async_remote_copy(
                src_ref=src, dst_ref=dst, send_sem=send.at[base + i], recv_sem=recv.at[base + i], device_id=to, device_id_type=MESH
            )

        near, far = Fold.peers()
        notes = [
            note(0, vec.at[0], box.at[0], peer("x")),
            note(1, vec.at[1], box.at[1], peer("y")),
            note(2, vec.at[2], box.at[2], peer("core")),
            note(3, vec.at[3], box.at[3], near),
            note(4, vec.at[4], box.at[4], far),
            note(5, vec.at[5], vec.at[5], near),
        ]

        def norm_sum(k):
            if k < 3:
                notes[k].wait_recv()
                vec[k + 1] = vec[k] + box[k]
                if k < 2:
                    notes[k + 1].start()
                else:
                    pl.when(fold_in.end)(notes[3].start)
            elif k < 5:

                @pl.when(fold_in.mid)
                def _():
                    notes[k].wait_recv()
                    vec[k + 1] = vec[k] + box[k]
                    notes[k + 1].start()

            else:
                pl.when(fold_in.end)(notes[5].wait_recv)

        def settle(s):
            scat.close(s)
            fold_at.begin(s)

        acts = (scat.begin, scat.turn, settle, fold_in.inner, fold_in.outer, fold_in.land, fold_at.inner, fold_at.outer,
                fold_at.land, norm_sum)

    @pl.when(step == 0)
    def _():
        for cp in early:
            cp.start()
        if comm:
            load = pltpu.make_async_copy(part_in, mine_in, lsem.at[8])
            load.start()
            greet([peer("core"), peer("x"), peer("y")] + Fold.peers())
            for s in range(PIECES):
                fold_in.begin(s)
            load.wait()
        for cp in early[:2]:
            cp.wait()
        for cp in mids:
            cp.start()
        parts[0 : 2 * nb, :] = jnp.zeros((2 * nb, 128), f32)
        parts[2 * nb :, :] = two_norm[...]

    if comm:
        for k, codes in enumerate(LAST_PLAN[:-1]):
            if codes:
                pl.when(step == k)(functools.partial(run_plan, acts, codes))

    per = q // g1.shape[1]

    @pl.when(step < 3 * per)
    def _():
        g = pick(step < per, g1[...], pick(step < 2 * per, g2[...], g3[...]))
        acc = dot_tn(wb[0:d, :], g) + dot_tn(wb[d : 2 * d, :], theirs[...])
        held[step] = acc.astype(bf16)

    @pl.when(step == 3 * per)
    def _():
        for cp in early[2:]:
            cp.wait()

    @pl.when((step >= 3 * per) & (step < np_))
    def _():
        lo = pl.ds(pl.multiple_of(core * q, q), q)
        hi = pl.ds(pl.multiple_of((1 - core) * q, q), q)
        own = dot_tn(wb[2 * d : 3 * d, :q], low[...]) + dot_tn(wb[3 * d :, q:], low_p[...])
        held[step, lo, :] = own.astype(bf16)
        other = dot_tn(wb[2 * d : 3 * d, q:], low[...]) + dot_tn(wb[3 * d :, :q], low_p[...])
        held[step, hi, :] = other.astype(bf16)

    @pl.when(step == np_)
    def _():
        for cp in late:
            cp.start()
        for cp in mids:
            cp.wait()

    @pl.when((step >= np_) & (step < np_ + pro))
    def _():
        both = jnp.concatenate([g[:, :q] for g in (dq, dk, dv)] + [g[:, q:] for g in (dq, dk, dv)], axis=1)
        dz = dot_nt(both, w[...])
        grad, g, b = layer_norm_back(tok[...].astype(f32), gain_row(norms, 0, d), dz)
        parts[0:nb, :] += flat_row(g)
        parts[nb : 2 * nb, :] += flat_row(b)
        out[...] = (d_resid[...] + grad).astype(bf16)

    @pl.when(step == np_ + pro)
    def _():
        for cp in late:
            cp.wait()
        if comm:
            vec[0] = parts[...]
            notes[0].start()

    @pl.when((step >= np_ + pro) & (step < last))
    def _():
        total[...] = resid[...]
        chunk = hb // 4

        @pl.loop(0, 4)
        def _(i):
            at = pl.ds(pl.multiple_of(i * chunk, chunk), chunk)
            beyond = pl.ds(pl.multiple_of(hb + i * chunk, chunk), chunk)
            total[...] += dot_nn(h_own[:, at], wb[at, :]) + dot_nn(h_oth[:, at], wb[beyond, :])

        mixed[...] = jnp.where(doc[...] >= 0, total[...], 0.0).astype(bf16)

    @pl.when(step == last)
    def _():
        if comm:
            run_plan(acts, LAST_PLAN[-1])
            fold_in.finish()
            scat.finish()
            fold_at.finish()
            for i in (0, 1, 2):
                notes[i].wait_send()
            pl.when(fold_in.end)(notes[3].wait_send)

            @pl.when(fold_in.mid)
            def _():
                notes[4].wait_send()
                notes[5].wait_send()

            sums[...] = vec[5]
        else:
            sums[...] = parts[...]
            cp = pltpu.make_async_copy(held, red_at, lsem.at[0])
            cp.start()
            cp.wait()


def flat_row(v):
    return jnp.concatenate([v[:, i * 128 : (i + 1) * 128] for i in range(v.shape[1] // 128)], axis=0)


def last_grad(grads3, theirs, low, low_p, tok, d_resid, norms, hidden, resid, doc_col, two_norm, a_one, a_one_p, att, att_p,
              own, oth, b_own, b_oth, part_in, n, comm, tm=256, wide=256):
    t, d = tok.shape
    pro = t // tm
    half = b_own.shape[0]
    q = d // 2
    per = q // wide
    np_ = 4 * per
    one = lambda w, c=0: pl.BlockSpec((tm, w), lambda i: (jnp.clip(i - np_, 0, pro - 1), c))
    two = lambda w, c=0: pl.BlockSpec((tm, w), lambda i: (jnp.clip(i - np_ - pro, 0, pro - 1), c))
    whole = lambda a: pl.BlockSpec(a.shape, lambda i: (0, 0))
    col = lambda k, count: pl.BlockSpec((t, wide), lambda i: (0, jnp.clip(i - k * per, 0, count - 1)))
    low_col = pl.BlockSpec((t, wide), lambda i: (0, lax.axis_index("core") * per + jnp.clip(i - 3 * per, 0, per - 1)))
    nv = 4 * d // 128
    pieced = part_in.shape
    share = (np_, d // n if comm else d, wide)
    slots = 4 * PIECES + 10 * np_ + 6
    extra = []
    if comm:
        extra = [dma(slots), dma(slots), pltpu.VMEM(part_in.shape, bf16)] + fold_scratch(*part_in.shape)
        extra += scatter_scratch(np_, d, wide)[1:] + [pltpu.VMEM(share, bf16)] * 5
        extra += [pltpu.VMEM((6, nv, 128), f32), pltpu.VMEM((5, nv, 128), f32), dma(PIECES), dma(np_)]
    return pl.pallas_call(
        functools.partial(last_kernel, (d, comm)),
        grid=(np_ + 2 * pro + 1,),
        out_shape=[sds((t, d), bf16), sds((t, d), bf16)] + [sds(pieced, bf16)] * 2 + [sds(share, bf16)] * 2 + [sds((nv, 128), f32)],
        in_specs=[col(0, per), col(1, per), col(2, per), col(0, 3 * per), low_col, col(3, per)]
        + [one(d)] * 5 + [whole(norms), two(half), two(half, 1), two(d), two(1), whole(two_norm)] + [ANY] * 9,
        out_specs=[one(d), two(d), ANY, ANY, ANY, ANY, pl.BlockSpec((nv, 128), lambda i: (0, 0))],
        scratch_shapes=[pltpu.VMEM((d, 3 * d), bf16), pltpu.VMEM((4 * d, d), bf16), pltpu.VMEM((nv, 128), f32),
                        pltpu.VMEM((np_, d, wide), bf16), dma(9), pltpu.VMEM((tm, d), f32)] + extra,
        compiler_params=comm_params(7 if comm else None, 63),
        cost_estimate=cost(14 * t * d * d + 4 * t * d * half, 60e6),
        name="last_grad",
    )(*grads3, theirs, low, low_p, *grads3, tok, d_resid, norms, hidden, hidden, resid, doc_col, two_norm,
      a_one, a_one_p, att, att_p, own, oth, b_own, b_oth, part_in)


def adam_update(g_ref, m1, m2, wg, st, mn):
    rows = g_ref.shape[0]
    step = min(rows, 256)

    @pl.loop(0, rows // step)
    def _(i):
        at = pl.ds(pl.multiple_of(i * step, 8), step)
        g = g_ref[at, :]
        first = BETA_ONE * m1[at, :] + (1.0 - BETA_ONE) * g
        second_hat = (BETA_TWO / (1.0 - BETA_TWO**STEPS)) * m2[at, :] + ((1.0 - BETA_TWO) / (1.0 - BETA_TWO**STEPS)) * g * g
        wg[at, :] = g
        st[at, :] = (-RATE / (1.0 - BETA_ONE**STEPS)) * first / (second_hat * lax.rsqrt(second_hat) + ADAM_EPS)
        mn[at, :] = first


def adam_kernel(plan, inv_root, own, oth, m1, m2, *refs):
    wg, st, mn, flat = refs[-4:]
    rows, stride, places = plan
    first = lax.axis_index("core") == 0
    wide = own.shape[2]
    for col, lo, hi in places:
        p, c = col // wide, col % wide
        a = own[p, :, c : c + 128].astype(f32) * inv_root
        b = oth[p, :, c : c + 128].astype(f32) * inv_root
        flat[pl.ds(lo, rows, stride=stride), :] = pick(first, a, b)
        flat[pl.ds(hi, rows, stride=stride), :] = pick(first, b, a)
    adam_update(flat, m1, m2, wg, st, mn)


def adam_columns(own, oth, at, count, m1, m2, prev, inv_root, first_row, rows, places):
    total, wide = own.shape[1:]
    nb = 2 * count * wide // 128
    blk = rows * nb
    assert first_row % blk == 0
    base = first_row // blk
    half = pl.BlockSpec((count, rows, wide), lambda i: (at, i, 0))
    flat = pl.BlockSpec((blk, 128), lambda i: (base + i, 0))
    kernel = functools.partial(adam_kernel, (rows, nb, places), inv_root)
    return adam_call(kernel, (total // rows,), own, oth, m1, m2, prev, half, flat, blk, "adam")


def adam_call(kernel, grid, own, oth, m1, m2, prev, half, flat, blk, name):
    return pl.pallas_call(
        kernel,
        grid=grid,
        out_shape=[sds(m1.shape, f32)] * 3,
        in_specs=[half, half, flat, flat] + [ANY] * len(prev),
        out_specs=[flat] * 3,
        scratch_shapes=[pltpu.VMEM((blk, 128), f32)],
        input_output_aliases={4 + i: i for i in range(len(prev))},
        compiler_params=params(),
        cost_estimate=cost(0, own.size * 2 * 22),
        name=name,
    )(own, oth, m1, m2, *prev)


def adam_rows_kernel(inv_root, own, oth, m1, m2, *refs):
    wg, st, mn, flat = refs[-4:]
    g = pick(pl.program_id(0) == lax.axis_index("core"), own[...], oth[...]).astype(f32) * inv_root
    rows, width = g.shape
    nb = width // 128
    for w in range(nb):
        flat[pl.ds(w, rows, stride=nb), :] = g[:, w * 128 : (w + 1) * 128]
    adam_update(flat, m1, m2, wg, st, mn)


def adam_rows_halves(own, oth, m1, m2, prev, inv_root, first_row):
    count, width = own.shape
    rows = count // 4
    blk = rows * width // 128
    base = first_row // blk
    half = pl.BlockSpec((rows, width), lambda h, i: (i, 0))
    flat = pl.BlockSpec((blk, 128), lambda h, i: (base + h * 4 + i, 0))
    kernel = functools.partial(adam_rows_kernel, inv_root)
    return adam_call(kernel, (2, 4), own, oth, m1, m2, prev, half, flat, blk, "adam_rows")


def adam_tail_kernel(g, m1, m2, p1, p2, p3, wg, st, mn):
    adam_update(g, m1, m2, wg, st, mn)


def adam_tail(g, m1, m2, prev, first_row):
    rows = 8
    assert first_row % rows == 0 and g.shape[0] <= rows
    g = jnp.pad(g, ((0, rows - g.shape[0]), (0, 0)))
    flat = pl.BlockSpec((rows, 128), lambda i: (first_row // rows, 0))
    return pl.pallas_call(
        adam_tail_kernel,
        grid=(1,),
        out_shape=[sds(m1.shape, f32)] * 3,
        in_specs=[pl.BlockSpec((rows, 128), lambda i: (0, 0)), flat, flat] + [ANY] * 3,
        out_specs=[flat] * 3,
        input_output_aliases={3: 0, 4: 1, 5: 2},
        name="adam_norms",
    )(g, m1, m2, *prev)


BLOCK = 4096


def adam_all_kernel(cfg, b_own, b_oth, i_own, i_oth, a_own, a_oth, norm, m1, m2, wg, st, mn, flat, later):
    inv_root, at_in, at_at, counts = cfg
    step = pl.program_id(0)
    core = lax.axis_index("core")
    n_back, n_in, n_at = counts

    @pl.when(step < n_back)
    def _():
        mine = step // (n_back // 2) == core
        pieces, rows, wide = b_own.shape
        for w in range(pieces * wide // 128):
            p, c = w * 128 // wide, w * 128 % wide
            g = pick(mine, b_own[p, :, c : c + 128], b_oth[p, :, c : c + 128])
            flat[pl.ds(w, rows, stride=pieces * wide // 128), :] = g.astype(f32) * inv_root

    def spread_columns(dst, own, oth, places):
        rows, wide = own.shape[1:]
        for col, lo, hi, stride in places:
            p, c = col // wide, col % wide
            mine = lo + core * (hi - lo)
            dst[pl.ds(mine, rows, stride=stride), :] = own[p, :, c : c + 128].astype(f32) * inv_root
            dst[pl.ds(lo + hi - mine, rows, stride=stride), :] = oth[p, :, c : c + 128].astype(f32) * inv_root

    @pl.when((step >= n_back) & (step < n_back + n_in))
    def _():
        spread_columns(flat, i_own, i_oth, at_in)

    for k, places in enumerate(at_at):
        pl.when(step == k)(functools.partial(spread_columns, later, a_own, a_oth, places))

    @pl.when((step >= n_back + n_in) & (step < n_back + n_in + n_at))
    def _():
        at = pl.multiple_of((step - n_back - n_in) * BLOCK, BLOCK)
        flat[...] = later[pl.ds(at, BLOCK), :]

    @pl.when(step == n_back + n_in + n_at)
    def _():
        per = norm.shape[0] // 4
        at = pl.multiple_of(lax.axis_index(("y", "x")) * per, per)
        flat[0:per, :] = norm[pl.ds(at, per), :] * inv_root

    adam_update(flat, m1, m2, wg, st, mn)


def adam_all(back, inner, attention, norm, m1, m2, inv_root, places):
    at_in, at_qkv, at_out = places
    b_np, b_rows, b_wide = back[0].shape
    i_np, i_rows, i_wide = inner[0].shape
    np_, a_rows, wide = attention[0].shape
    n_back = 2 * b_np * b_rows * b_wide // 128 // BLOCK
    n_in = 2 * i_np * i_rows * i_wide // 128 // BLOCK
    n_at = 2 * np_ * a_rows * wide // 128 // BLOCK
    lots = np_ // (n_back + n_in)
    assert np_ == lots * (n_back + n_in) and m1.shape[0] == (n_back + n_in + n_at) * BLOCK + 8
    s_in, s_qkv, s_out = 2 * i_np * i_wide // 128, 2 * len(at_qkv), 2 * len(at_out)
    edge = a_rows * s_qkv
    at_at = [[] for _ in range(n_back + n_in)]
    for col, lo, hi in at_qkv:
        at_at[col // wide // lots].append((col % (wide * lots), lo, hi, s_qkv))
    for col, lo, hi in at_out:
        col += len(at_qkv) * 128
        at_at[col // wide // lots].append((col % (wide * lots), edge + lo, edge + hi, s_out))
    cfg = (inv_root, [(c, lo, hi, s_in) for c, lo, hi in at_in], at_at, (n_back, n_in, n_at))
    after_at, after_in = n_at, n_at + n_in

    def where(i):
        back_or_in = jnp.where(i < n_back, after_in + i, after_at + i - n_back)
        return jnp.where(i < n_back + n_in, back_or_in, jnp.where(i < n_back + n_in + n_at, i - n_back - n_in, i))

    flat = pl.BlockSpec((BLOCK, 128), lambda i: (where(i), 0))
    b_spec = pl.BlockSpec((b_np, 2 * b_rows // n_back, b_wide), lambda i: (0, jnp.minimum(i, n_back - 1) % (n_back // 2), 0))
    i_spec = pl.BlockSpec((i_np, i_rows // n_in, i_wide), lambda i: (0, jnp.clip(i - n_back, 0, n_in - 1), 0))
    a_spec = pl.BlockSpec((lots, a_rows, wide), lambda i: (jnp.minimum(i, n_back + n_in - 1), 0, 0))
    return pl.pallas_call(
        functools.partial(adam_all_kernel, cfg),
        grid=(n_back + n_in + n_at + 1,),
        out_shape=[sds(m1.shape, f32)] * 3,
        in_specs=[b_spec, b_spec, i_spec, i_spec, a_spec, a_spec, pl.BlockSpec(norm.shape, lambda i: (0, 0)), flat, flat],
        out_specs=[flat] * 3,
        scratch_shapes=[pltpu.VMEM((BLOCK, 128), f32), pltpu.VMEM((n_at * BLOCK, 128), f32)],
        compiler_params=params(),
        cost_estimate=cost(0, m1.size * 22),
        name="adam_all",
    )(*back, *inner, *attention, norm, m1, m2)


def after(x, *deps):
    return lax.optimization_barrier((x, deps))[0]


def body(n, nz, tokens, cotangent, doc_ids, master, moment_one, moment_two):
    t, d = tokens.shape
    ff = (master.shape[0] * n - 4 * d) // (2 * d) - 2 * d
    me = lax.axis_index(("y", "x"))
    rows = d // n
    comm = n == 4 and nz == 4

    lanes = master.reshape(-1, 128)
    doc_row = doc_ids.reshape(1, t)
    w = o = norm_share = None
    if not comm:
        w, o, _ = unpack_first(lanes, n, d, ff)
        w, o = spread(w), spread(o)
        norm_share = lax.all_gather(master[-(4 * d // n) :].astype(bf16), ("y", "x"), axis=0, tiled=True)
        norm_share = norm_share.astype(f32).reshape(-1, 128)
    (a_one, qkv, in_own, bk_own, w_own, w_oth, o_own, o_oth, norms, d_out, doc_col, att, lse, in_oth, a_one_p, d_out_p) = project_qkv(
        lanes, tokens, cotangent, doc_row, norm_share, w, o, n, ff, comm
    )
    resid, a_two, hidden, slope, bk_own, bk_oth, att_p, g_back = middle(
        att, tokens, norms, o_own, o_oth, in_own, in_oth, bk_own, d_out, d_out_p, comm
    )
    g_in, d_resid, low, d_att, two_norm, low_p, part_back = feed_back(
        d_out, slope, bk_own, bk_oth, in_own, in_oth, resid, norms, o_own, o_oth, a_two, g_back, n, comm
    )
    dq, dk, dv, dqkv_p, red_back, part_in = attend_back(qkv, d_att, att, lse, doc_row, doc_col, part_back, g_in, d, n, comm)
    input_grad, mixed, red_in, red_in_p, red_at, red_at_p, sums = last_grad(
        [dq, dk, dv], dqkv_p, low, low_p, tokens, d_resid, norms, hidden, resid, doc_col, two_norm, a_one, a_one_p, att, att_p,
        w_own, w_oth, bk_own, bk_oth, part_in, n, comm,
    )
    red_in, red_at = (red_in, red_in_p), (red_at, red_at_p)
    if not comm:
        red_in, red_at = both_halves(part_in), both_halves(scatter_pieces(red_at[0]))
        sums = lax.psum(sums, ("z", "core", "y", "x"))

    inv_root = float(t * n * nz * 2) ** (-0.5)
    m1, m2 = moment_one.reshape(-1, 128), moment_two.reshape(-1, 128)
    nb = d // 128
    half = nb // 2
    hs = ff // n // 2
    r_qkv, r_out, r_in = rows * 3 * nb, rows * nb, rows * ff // 128
    back_at = r_qkv + r_out + r_in
    at_in = [(hs * j + q * 128, (2 * hs * j) // 128 + q, (2 * hs * j + hs) // 128 + q) for j in range(n) for q in range(hs // 128)]
    at_qkv = [((p * half + w) * 128, p * nb + w, p * nb + w + half) for p in range(3) for w in range(half)]
    at_out = [(w * 128, w, w + half) for w in range(half)]
    if comm:
        outs = adam_all(red_back, red_in, red_at, sums, m1, m2, inv_root, (at_in, at_qkv, at_out))
    else:
        plain = lambda v: v.transpose(1, 0, 2).reshape(v.shape[1], -1)
        count = red_at[0].shape[0]
        outs = adam_rows_halves(plain(red_back[0]), plain(red_back[1]), m1, m2, [], inv_root, back_at)
        outs = adam_columns(*red_in, 0, red_in[0].shape[0], m1, m2, outs, inv_root, r_qkv + r_out, rows // 8, at_in)
        outs = adam_columns(*red_at, 0, 3 * count // 4, m1, m2, outs, inv_root, 0, rows // 8, at_qkv)
        outs = adam_columns(*red_at, 3, count // 4, m1, m2, outs, inv_root, r_qkv, rows // 2, at_out)
        per = 4 * nb // n
        norm_part = lax.dynamic_slice_in_dim(sums, group_index(n) * per, per, 0) * inv_root
        outs = adam_tail(norm_part, m1, m2, outs, back_at + ff // n * nb)
    weight_grad, step, moment = [o.reshape(-1) for o in outs]
    return mixed, input_grad, weight_grad, step, moment


def solution(mesh):
    dp, n = mesh.shape["dp"], mesh.shape["group"]
    fine = Mesh(mesh.devices.reshape(dp // 2, 2, n // 2, 2), ("z", "core", "y", "x"))
    tok = ("z", "core", "y", "x")
    flat = P(("y", "x"))
    in_specs = (P(tok, None), P(tok, None), P(tok), flat, flat, flat)
    out_specs = (P(tok, None), P(tok, None), flat, flat, flat)
    return jax.shard_map(
        functools.partial(body, n, dp // 2), mesh=fine, in_specs=in_specs, out_specs=out_specs, check_vma=False
    )
```
